128 devices in a mesh: dom: 32 (over x, z, core), feat: 4 (over y).
Axes of the slice: x: 4, y: 4, z: 4, core: 2. Of those that a mesh axis runs over, the one named last changes fastest.
Arguments:
- features: bfloat16 [32768, 512], P('dom'), may hold values from -96 to 96
- w_query: bfloat16 [512, 512], P(None, 'feat'), may hold values from -0.25 to 0.25
- w_key: bfloat16 [512, 512], P(None, 'feat'), may hold values from -0.25 to 0.25
- w_value: bfloat16 [512, 512], P(None, 'feat'), may hold values from -0.25 to 0.25
- cotangent: bfloat16 [32768, 512], P('dom', 'feat'), may hold values from -6 to 6
- send_rows: int32 [32, 32, 128], P('dom'), may hold values from 0 to 1023, as said below
- halo_count: int32 [32, 32], P(None, 'dom'), may hold values from 0 to 128, as said below
- block_mask: int32 [256, 40], P('dom'), may hold values 0 or 1
- exp_rows: int32 [4, 32768], P(None, 'dom'), may hold values from 0 to 1023, as said below
- global_ids: int32 [128], replicated, may hold values from 0 to 32767, as said below
Outputs:
- attended: bfloat16 [32768, 512], P('dom', 'feat')
- input_grad: bfloat16 [32768, 512], P('dom', 'feat')
The draws below stay inside these ranges and needn't reach their ends.
Inputs may be any that keep to these rules, and one draw needn't show every extreme that they name: `send_rows`: local row numbers on the sending slab, distinct within each list. `halo_count`: zero from a slab to itself; some receiver gets 128 live slots from every other slab. `exp_rows`: each slab's part of each matching is a permutation of 0 to 1023. `global_ids`: distinct node ids.
All inputs are finite; a program needn't handle non-finite values. No bound on the sum of `block_mask` on one device may be relied on, other than what follows from the above.
Results may differ from the reference program's by a relative error of at most 0.013.
The reference program's roundings to bfloat16 on the way count: a program that leaves them out, or rounds other values in their place, can miss the bound.
Values may be sent and summed in bfloat16 or wider, within the bound.
No kernel may reach another device: no remote copies, remote signals or barrier semaphores. Data moves between devices by JAX's collectives and lax.ppermute only.
A program may use at most 128 MiB of HBM per device.

```python
import math
import jax
import jax.numpy as jnp
from jax import lax

D = 512
HEADS = 8
HEAD = 64
NODE_DEV = 1024
BLOCK = 128
EXPANDERS = 4
GLOBALS = 128
NODES = 32768
KEYS = 5120
N_DOM = 32


def draw_features(key, part):
    base = jnp.clip(jax.random.normal(key, (NODES, D), jnp.float32), -6.0, 6.0)
    return base.astype(jnp.bfloat16)


def draw_halo_count(key, part):
    base = jax.random.randint(key, (N_DOM, N_DOM), BLOCK // 4, BLOCK + 1)
    level = jax.random.randint(jax.random.fold_in(key, 3), (1, N_DOM), 1, 5)
    counts = jnp.minimum(BLOCK, base * level // 2)
    full = jax.random.randint(jax.random.fold_in(key, 5), (), 0, N_DOM)
    column = jnp.arange(N_DOM, dtype=jnp.int32)[None, :]
    row_ids = jnp.arange(N_DOM, dtype=jnp.int32)[:, None]
    counts = jnp.where(column == full, BLOCK, counts)
    counts = jnp.where(row_ids == column, 0, counts)
    return counts.astype(jnp.int32)


def draw_send_rows(key, part):
    keys = jax.random.split(key, N_DOM * N_DOM)
    row_lists = jax.vmap(lambda single: jax.random.permutation(single, NODE_DEV)[:BLOCK])(keys)
    return row_lists.reshape(N_DOM, N_DOM, BLOCK).astype(jnp.int32)


def draw_exp_rows(key, part):
    keys = jax.random.split(key, EXPANDERS * N_DOM)
    row_lists = jax.vmap(lambda single: jax.random.permutation(single, NODE_DEV))(keys)
    return row_lists.reshape(EXPANDERS, NODES).astype(jnp.int32)


def draw_global_ids(key, part):
    middle = jax.random.permutation(key, NODES - 2)[:GLOBALS - 2].astype(jnp.int32) + 1
    first = jnp.zeros((1,), jnp.int32)
    last = jnp.full((1,), NODES - 1, jnp.int32)
    return jnp.concatenate([first, middle, last]).astype(jnp.int32)


def plant(result, key, low, high):
    longest = result.shape.index(max(result.shape))
    spots = []
    for shift in (0, 1):
        where = [jax.random.randint(jax.random.fold_in(key, axis), (), 0, length) for axis, length in enumerate(result.shape)]
        where[longest] = (where[longest] + shift) % result.shape[longest]
        spots.append(tuple(where))
    return result.at[spots[0]].set(low).at[spots[1]].set(high)


def level_of(own_key, shape, cuts, smallest, high):
    gain, own = 1.0, jax.random.fold_in(own_key, 6)
    for dim, parts in cuts:
        steps = jnp.exp(jax.random.uniform(jax.random.fold_in(own, dim), (parts,), jnp.float32, smallest / len(cuts), high / len(cuts)))
        gain = gain * jnp.repeat(steps, shape[dim] // parts).reshape([-1 if axis == dim else 1 for axis in range(len(shape))])
    return gain


def normal_values(stream_key, dims, width, most, cuts=(), kind=jnp.bfloat16):
    drawn = jax.random.normal(stream_key, dims, jnp.float32) * width
    if len(cuts) > 0:
        drawn = level_of(stream_key, dims, cuts, -0.22, 0.18) * drawn
    return jnp.clip(drawn, min=-most, max=most).astype(kind)


def setup_inputs(seed: int = 0) -> dict:
    seeds = jax.random.split(jax.random.key(seed), 11)
    return {
        "features": draw_features(jax.random.fold_in(seeds[10], 71), 0),
        "w_query": normal_values(seeds[1], (D, D), D ** -0.5, 0.25, ((1, 4),)),
        "w_key": normal_values(seeds[2], (D, D), D ** -0.5, 0.25, ((1, 4),)),
        "w_value": normal_values(seeds[3], (D, D), D ** -0.5, 0.25, ((1, 4),)),
        "cotangent": normal_values(seeds[4], (NODES, D), 1.0, 6.0, ((0, 32), (1, 4))),
        "send_rows": draw_send_rows(jax.random.fold_in(seeds[10], 71), 0),
        "halo_count": draw_halo_count(jax.random.fold_in(seeds[10], 71), 0),
        "block_mask": plant((jax.random.randint(seeds[7], (NODES // BLOCK, KEYS // BLOCK), 0, 2) < 1).astype(jnp.int32), jax.random.fold_in(seeds[7], 1), 0, 1),
        "exp_rows": draw_exp_rows(jax.random.fold_in(seeds[10], 71), 0),
        "global_ids": draw_global_ids(jax.random.fold_in(seeds[10], 71), 0),
    }


def round_half(value):
    return lax.optimization_barrier(value.astype(jnp.bfloat16)).astype(jnp.float32)

def reference(features, w_query, w_key, w_value, cotangent, send_rows, halo_count, block_mask, exp_rows, global_ids):
    levels = int(N_DOM).bit_length() - 1
    score_scale = 1.0 / math.sqrt(HEAD)
    query = jnp.dot(features, w_query, preferred_element_type=jnp.float32).astype(jnp.bfloat16)
    key_rows = jnp.dot(features, w_key, preferred_element_type=jnp.float32).astype(jnp.bfloat16)
    value_rows = jnp.dot(features, w_value, preferred_element_type=jnp.float32).astype(jnp.bfloat16)
    query_dev = query.reshape(N_DOM, NODE_DEV, D)
    key_dev = key_rows.reshape(N_DOM, NODE_DEV, D)
    value_dev = value_rows.reshape(N_DOM, NODE_DEV, D)
    grad_dev = cotangent.reshape(N_DOM, NODE_DEV, D)
    global_key = key_rows[global_ids].astype(jnp.float32).reshape(GLOBALS, HEADS, HEAD)
    global_value = value_rows[global_ids].astype(jnp.float32).reshape(GLOBALS, HEADS, HEAD)
    senders = jnp.arange(N_DOM, dtype=jnp.int32)
    slot_ids = jnp.arange(BLOCK, dtype=jnp.int32)
    own_ids = jnp.arange(NODE_DEV, dtype=jnp.int32)

    def per_device(totals, device):
        grad_key, grad_value = totals
        query_here = query_dev[device].astype(jnp.float32).reshape(NODE_DEV, HEADS, HEAD)
        grad_here = grad_dev[device].astype(jnp.float32).reshape(NODE_DEV, HEADS, HEAD)
        row_list = send_rows[:, device, :]
        halo_key = key_dev[senders[:, None], row_list].reshape(N_DOM * BLOCK, D)
        halo_value = value_dev[senders[:, None], row_list].reshape(N_DOM * BLOCK, D)
        cand_key = jnp.concatenate([key_dev[device], halo_key], 0).astype(jnp.float32).reshape(-1, HEADS, HEAD)
        cand_value = jnp.concatenate([value_dev[device], halo_value], 0).astype(jnp.float32).reshape(-1, HEADS, HEAD)
        slot_live = (slot_ids[None, :] < halo_count[:, device][:, None]).reshape(-1)
        key_live = jnp.concatenate([jnp.ones((NODE_DEV,), dtype=bool), slot_live])
        mask_rows = lax.dynamic_slice_in_dim(block_mask, device * (NODE_DEV // BLOCK), NODE_DEV // BLOCK, 0)
        allowed = jnp.repeat(jnp.repeat(mask_rows > 0, BLOCK, axis=0), BLOCK, axis=1) & key_live[None, :]
        partner_rows = lax.dynamic_slice_in_dim(exp_rows, device * NODE_DEV, NODE_DEV, 1)
        partners = jnp.stack([jnp.bitwise_xor(device, 2 ** (matching % levels)) for matching in range(EXPANDERS)])
        partner_key = key_dev[partners[:, None], partner_rows].astype(jnp.float32).reshape(EXPANDERS, NODE_DEV, HEADS, HEAD)
        partner_value = value_dev[partners[:, None], partner_rows].astype(jnp.float32).reshape(EXPANDERS, NODE_DEV, HEADS, HEAD)
        local_score = jnp.einsum('nhe,khe->nhk', query_here, cand_key) * score_scale
        local_score = jnp.where(allowed[:, None, :], local_score, -jnp.inf)
        partner_score = jnp.einsum('nhe,mnhe->nhm', query_here, partner_key) * score_scale
        global_score = jnp.einsum('nhe,ghe->nhg', query_here, global_key) * score_scale
        top_score = jnp.maximum(jnp.maximum(local_score.max(-1), partner_score.max(-1)), global_score.max(-1))[..., None]
        local_exp = jnp.exp(local_score - top_score)
        partner_exp = jnp.exp(partner_score - top_score)
        global_exp = jnp.exp(global_score - top_score)
        denominator = local_exp.sum(-1, keepdims=True) + partner_exp.sum(-1, keepdims=True) + global_exp.sum(-1, keepdims=True)
        local_prob = local_exp / denominator
        partner_prob = partner_exp / denominator
        global_prob = global_exp / denominator
        local_weight = round_half(local_prob)
        partner_weight = round_half(partner_prob)
        global_weight = round_half(global_prob)
        attended_here = (jnp.einsum('nhk,khe->nhe', local_weight, cand_value) + jnp.einsum('nhm,mnhe->nhe', partner_weight, partner_value) + jnp.einsum('nhg,ghe->nhe', global_weight, global_value)).astype(jnp.bfloat16).reshape(NODE_DEV, D)
        local_dp = jnp.einsum('nhe,khe->nhk', grad_here, cand_value)
        partner_dp = jnp.einsum('nhe,mnhe->nhm', grad_here, partner_value)
        global_dp = jnp.einsum('nhe,ghe->nhg', grad_here, global_value)
        delta = (local_prob * local_dp).sum(-1, keepdims=True) + (partner_prob * partner_dp).sum(-1, keepdims=True) + (global_prob * global_dp).sum(-1, keepdims=True)
        local_ds = round_half(local_prob * (local_dp - delta) * score_scale)
        partner_ds = round_half(partner_prob * (partner_dp - delta) * score_scale)
        global_ds = round_half(global_prob * (global_dp - delta) * score_scale)
        grad_query = jnp.einsum('nhk,khe->nhe', local_ds, cand_key) + jnp.einsum('nhm,mnhe->nhe', partner_ds, partner_key) + jnp.einsum('nhg,ghe->nhe', global_ds, global_key)
        cand_gk = jnp.einsum('nhk,nhe->khe', local_ds, query_here).reshape(-1, D)
        cand_gv = jnp.einsum('nhk,nhe->khe', local_weight, grad_here).reshape(-1, D)
        cand_gk = jnp.concatenate([cand_gk[:NODE_DEV], round_half(cand_gk[NODE_DEV:])], 0)
        cand_gv = jnp.concatenate([cand_gv[:NODE_DEV], round_half(cand_gv[NODE_DEV:])], 0)
        partner_gk = jnp.einsum('nhm,nhe->mnhe', partner_ds, query_here).reshape(EXPANDERS * NODE_DEV, D)
        partner_gv = jnp.einsum('nhm,nhe->mnhe', partner_weight, grad_here).reshape(EXPANDERS * NODE_DEV, D)
        global_gk = jnp.einsum('nhg,nhe->ghe', global_ds, query_here).reshape(GLOBALS, D)
        global_gv = jnp.einsum('nhg,nhe->ghe', global_weight, grad_here).reshape(GLOBALS, D)
        cand_index = jnp.concatenate([device * NODE_DEV + own_ids, (senders[:, None] * NODE_DEV + row_list).reshape(-1)])
        partner_index = (partners[:, None] * NODE_DEV + partner_rows).reshape(-1)
        all_index = jnp.concatenate([cand_index, partner_index, global_ids]).astype(jnp.int32)
        grad_key = grad_key.at[all_index].add(jnp.concatenate([cand_gk, partner_gk, global_gk], 0))
        grad_value = grad_value.at[all_index].add(jnp.concatenate([cand_gv, partner_gv, global_gv], 0))
        return ((grad_key, grad_value), (attended_here, grad_query.reshape(NODE_DEV, D)))
    zero_rows = jnp.zeros((NODES, D), jnp.float32)
    totals, outputs = lax.scan(per_device, (zero_rows, zero_rows), senders)
    grad_key, grad_value = totals
    attended, grad_query = outputs
    attended = attended.reshape(NODES, D)
    query_grad = grad_query.reshape(NODES, D).astype(jnp.bfloat16)
    input_grad = (jnp.dot(query_grad, w_query.T, preferred_element_type=jnp.float32) + jnp.dot(grad_key.astype(jnp.bfloat16), w_key.T, preferred_element_type=jnp.float32) + jnp.dot(grad_value.astype(jnp.bfloat16), w_value.T, preferred_element_type=jnp.float32)).astype(jnp.bfloat16)
    return (attended, input_grad)
```

```python
import math

import jax
import jax.numpy as jnp
from jax import lax
from jax.experimental import pallas as pl
from jax.experimental.pallas import tpu as pltpu
from jax.sharding import PartitionSpec as P

HEAD = 64
BLOCK = 128
EXPANDERS = 4
COLS = 128
NODES_HERE = 1024
Q_BLOCKS = NODES_HERE // BLOCK
SENDERS = 32
GLOBAL_BLOCK = Q_BLOCKS + SENDERS
EMPTY_BLOCK = GLOBAL_BLOCK + 1
KEY_BLOCKS = EMPTY_BLOCK + 1
GROUP = 4
LIST = 48
NEG = -1e30
F32 = jnp.float32
BF16 = jnp.bfloat16


def params():
    return pltpu.CompilerParams(vmem_limit_bytes=56 * 1024 * 1024)


def vmem():
    return pl.BlockSpec(memory_space=pltpu.VMEM)


def smem():
    return pl.BlockSpec(memory_space=pltpu.SMEM)


def iota(shape, dim):
    return lax.broadcasted_iota(jnp.int32, shape, dim)


def dot(a, b):
    return jnp.dot(a, b, preferred_element_type=F32)


def dot_nt(a, b):
    return lax.dot_general(a, b, (((1,), (1,)), ((), ())), preferred_element_type=F32)


def one_hot_rows(row, table_rows):
    column = jnp.broadcast_to(row, (BLOCK, BLOCK)).T
    lanes = iota((BLOCK, BLOCK), 1)
    return jnp.concatenate(
        [(column == lanes + c * BLOCK).astype(F32).astype(BF16) for c in range(table_rows // BLOCK)],
        axis=1,
    )


def project_kernel(x_ref, wq_ref, wk_ref, wv_ref, rows_ref, gid_ref, q_ref, kv_ref, outk_ref, outv_ref, glob_ref):
    x = x_ref[...]
    q_ref[...] = (dot(x, wq_ref[...]).astype(BF16).astype(F32) * (1.0 / math.sqrt(HEAD))).astype(BF16)
    kv_ref[:, :COLS] = dot(x, wk_ref[...]).astype(BF16)
    kv_ref[:, COLS:] = dot(x, wv_ref[...]).astype(BF16)

    def gather(d, carry):
        got = dot(one_hot_rows(rows_ref[pl.ds(d, 1), :], NODES_HERE), kv_ref[...]).astype(BF16)
        outk_ref[d] = got[:, :COLS]
        outv_ref[d] = got[:, COLS:]
        return carry

    lax.fori_loop(0, SENDERS, gather, 0)
    glob_ref[...] = dot(one_hot_rows(gid_ref[...], NODES_HERE), kv_ref[...]).astype(BF16)


def partner_kernel(exp_ref, t0_ref, t1_ref, t2_ref, t3_ref, out_ref):
    for m, table in enumerate((t0_ref, t1_ref, t2_ref, t3_ref)):

        def gather(i, carry):
            b = m * Q_BLOCKS + i
            out_ref[b] = dot(one_hot_rows(exp_ref[pl.ds(b, 1), :], NODES_HERE), table[...]).astype(BF16)
            return carry

        lax.fori_loop(0, Q_BLOCKS, gather, 0)


def plan_kernel(mask_ref, count_ref, list_ref, groups_ref, live_ref):
    for j in range(Q_BLOCKS):
        live_ref[j] = BLOCK
    live_ref[GLOBAL_BLOCK] = BLOCK
    live_ref[EMPTY_BLOCK] = 0

    def copy_count(s, carry):
        live_ref[Q_BLOCKS + s] = count_ref[s]
        return carry

    lax.fori_loop(0, SENDERS, copy_count, 0)

    def per_block(i, carry):
        list_ref[i * LIST] = GLOBAL_BLOCK

        def put(j, n):
            list_ref[i * LIST + n] = j
            used = jnp.logical_and(mask_ref[i * GLOBAL_BLOCK + j] > 0, live_ref[j] > 0)
            return n + used.astype(jnp.int32)

        n = lax.fori_loop(0, GLOBAL_BLOCK, put, 1)
        for extra in range(GROUP):
            list_ref[i * LIST + n + extra] = EMPTY_BLOCK
        groups_ref[i] = (n + GROUP - 1) // GROUP
        return carry

    lax.fori_loop(0, Q_BLOCKS, per_block, 0)


def fill(dst, own_ref, first_col, halo_ref, glob_ref, transposed=False):
    def turn(x):
        return x.T if transposed else x

    def own(j, carry):
        dst[j] = turn(own_ref[pl.ds(pl.multiple_of(j * BLOCK, BLOCK), BLOCK), first_col : first_col + COLS])
        return carry

    def halo(j, carry):
        dst[Q_BLOCKS + j] = turn(halo_ref[j])
        return carry

    lax.fori_loop(0, Q_BLOCKS, own, 0)
    lax.fori_loop(0, SENDERS, halo, 0)
    dst[GLOBAL_BLOCK] = turn(glob_ref[:, first_col : first_col + COLS])
    dst[EMPTY_BLOCK] = jnp.zeros((BLOCK, COLS), BF16)


def stacked(rows):
    lanes = iota((BLOCK, COLS), 1)
    zero = jnp.zeros_like(rows)
    return jnp.concatenate([jnp.where(lanes < HEAD, rows, zero), jnp.where(lanes < HEAD, zero, rows)], axis=0)


def stacked_t(rows):
    turned = rows.T
    subs = iota((COLS, BLOCK), 0)
    zero = jnp.zeros_like(turned)
    return jnp.concatenate([jnp.where(subs < HEAD, turned, zero), jnp.where(subs < HEAD, zero, turned)], axis=1)


def partner_rows(rows, pair_ref, i, first_col):
    total = jnp.zeros((16, BLOCK), F32)
    row_id = iota((16, COLS), 0)
    lane = iota((16, COLS), 1)
    for m in range(EXPANDERS):
        other = pair_ref[m * Q_BLOCKS + i][:, first_col : first_col + COLS]
        prod = rows.astype(F32) * other.astype(F32)
        high = prod.astype(BF16)
        low = (prod - high.astype(F32)).astype(BF16)
        picks = (row_id == jnp.where(lane < HEAD, m, 8 + m)).astype(F32).astype(BF16)
        total = total + dot_nt(picks, high) + dot_nt(picks, low)
    return jnp.concatenate([total[:8], total[8:]], axis=1)


def tall(weights):
    return jnp.concatenate([weights[:, :BLOCK], weights[:, BLOCK:]], axis=0)


def spread(tall_weights):
    turned = tall_weights.T.astype(BF16)
    row_id = iota((16, EXPANDERS * COLS), 0)
    col = iota((16, EXPANDERS * COLS), 1)
    picks = (row_id == (col // COLS) + jnp.where(col % COLS < HEAD, 0, 8)).astype(F32).astype(BF16)
    return dot(turned, picks)


def head_rows(turned):
    return jnp.concatenate([turned[:HEAD, :BLOCK], turned[HEAD:, BLOCK:]], axis=0)


def masked_scores(blocks, k_s, turned_q, live_ref):
    keys = jnp.concatenate([k_s[b] for b in blocks], axis=0)
    scores = dot(keys, turned_q)
    row_id = iota((BLOCK, 2 * BLOCK), 0)
    return jnp.concatenate(
        [
            jnp.where(row_id < live_ref[b], scores[u * BLOCK : (u + 1) * BLOCK], NEG)
            for u, b in enumerate(blocks)
        ],
        axis=0,
    )


def block_ids(list_ref, i, g):
    return [list_ref[i * LIST + g * GROUP + u] for u in range(GROUP)]


def q_rows(i):
    return pl.ds(pl.multiple_of(i * BLOCK, BLOCK), BLOCK)


def score_kernel(list_ref, groups_ref, live_ref, q_ref, kv_ref, hk_ref, glob_ref, pair_ref, lse_ref, sp_ref, k_s):
    fill(k_s, kv_ref, 0, hk_ref, glob_ref)

    def per_block(i, carry):
        rows = q_ref[q_rows(i), :]
        turned_q = stacked_t(rows)
        partner = partner_rows(rows, pair_ref, i, 0)
        partner = jnp.where(iota((8, 2 * BLOCK), 0) < EXPANDERS, partner, NEG)
        sp_ref[i] = partner

        def step(g, state):
            top, total = state
            scores = masked_scores(block_ids(list_ref, i, g), k_s, turned_q, live_ref)
            scores = scores.reshape(GROUP * BLOCK // 8, 8, 2 * BLOCK)
            new_top = jnp.maximum(top, jnp.max(scores, axis=0))
            total = total * jnp.exp(top - new_top) + jnp.sum(jnp.exp(scores - new_top[None]), axis=0)
            return new_top, total

        top, total = lax.fori_loop(0, groups_ref[i], step, (partner, jnp.ones((8, 2 * BLOCK), F32)))
        best = jnp.max(top, axis=0, keepdims=True)
        denominator = jnp.sum(total * jnp.exp(top - best), axis=0, keepdims=True)
        lse_ref[pl.ds(i, 1), :] = best + jnp.log(denominator)
        return carry

    lax.fori_loop(0, Q_BLOCKS, per_block, 0)


def value_kernel(
    list_ref, groups_ref, live_ref, q_ref, kv_ref, hk_ref, hv_ref, glob_ref, pair_ref, cot_ref, lse_ref, sp_ref,
    att_ref, own_ref, halo_ref, gout_ref, wp_ref, dp_ref, delta_ref, k_s, vt_s, acc_s, out_s,
):
    fill(k_s, kv_ref, 0, hk_ref, glob_ref)
    fill(vt_s, kv_ref, COLS, hv_ref, glob_ref, transposed=True)

    def clear(j, carry):
        acc_s[j] = jnp.zeros((BLOCK, COLS), F32)
        return carry

    lax.fori_loop(0, KEY_BLOCKS, clear, 0)

    def per_block(i, carry):
        turned_q = stacked_t(q_ref[q_rows(i), :])
        cot = cot_ref[q_rows(i), :]
        cot_stack = stacked(cot)
        lse = lse_ref[pl.ds(i, 1), :]
        out_s[...] = jnp.zeros((COLS, 2 * BLOCK), F32)

        def step(g, carry):
            blocks = block_ids(list_ref, i, g)
            scores = masked_scores(blocks, k_s, turned_q, live_ref)
            weight = jnp.exp(scores - lse).astype(BF16)
            turned_v = jnp.concatenate([vt_s[b] for b in blocks], axis=1)
            out_s[...] += dot(turned_v, weight)
            grads = dot(weight, cot_stack)
            for u, b in enumerate(blocks):
                acc_s[b] += grads[u * BLOCK : (u + 1) * BLOCK]
            return carry

        lax.fori_loop(0, groups_ref[i], step, 0)
        dprob = partner_rows(cot, pair_ref, i, COLS)
        dp_ref[i] = dprob
        prob = jnp.exp(sp_ref[i] - lse)
        weight = prob.astype(BF16).astype(F32)
        wide = spread(tall(weight))
        wp_ref[i] = tall(weight).astype(BF16)
        attended_t = head_rows(out_s[...])
        prod = attended_t * cot.T.astype(F32)
        delta = jnp.concatenate(
            [jnp.sum(prod[:HEAD], axis=0, keepdims=True), jnp.sum(prod[HEAD:], axis=0, keepdims=True)], axis=1
        )
        delta_ref[pl.ds(i, 1), :] = delta + jnp.sum(prob * dprob, axis=0, keepdims=True)
        attended = attended_t.T
        for m in range(EXPANDERS):
            attended += wide[:, m * COLS : (m + 1) * COLS] * pair_ref[m * Q_BLOCKS + i][:, COLS:].astype(F32)
        att_ref[q_rows(i), :] = attended.astype(BF16)
        return carry

    lax.fori_loop(0, Q_BLOCKS, per_block, 0)
    store_parts(acc_s, own_ref, halo_ref, gout_ref)


def store_parts(acc_s, own_ref, halo_ref, gout_ref):
    def own(j, carry):
        own_ref[q_rows(j), :] = acc_s[j]
        return carry

    def halo(j, carry):
        halo_ref[j] = acc_s[Q_BLOCKS + j].astype(BF16)
        return carry

    lax.fori_loop(0, Q_BLOCKS, own, 0)
    lax.fori_loop(0, SENDERS, halo, 0)
    gout_ref[...] = acc_s[GLOBAL_BLOCK].astype(BF16)


def key_kernel(
    list_ref, groups_ref, live_ref, q_ref, kv_ref, hk_ref, hv_ref, glob_ref, pair_ref, cot_ref, lse_ref, sp_ref,
    dp_ref, delta_ref, gq_ref, own_ref, halo_ref, gout_ref, dsp_ref, k_s, v_s, kt_s, acc_s, out_s,
):
    fill(k_s, kv_ref, 0, hk_ref, glob_ref)
    fill(v_s, kv_ref, COLS, hv_ref, glob_ref)
    fill(kt_s, kv_ref, 0, hk_ref, glob_ref, transposed=True)

    def clear(j, carry):
        acc_s[j] = jnp.zeros((BLOCK, COLS), F32)
        return carry

    lax.fori_loop(0, KEY_BLOCKS, clear, 0)

    def per_block(i, carry):
        rows = q_ref[q_rows(i), :]
        turned_q = stacked_t(rows)
        q_stack = stacked(rows)
        turned_cot = stacked_t(cot_ref[q_rows(i), :])
        lse = lse_ref[pl.ds(i, 1), :]
        delta = delta_ref[pl.ds(i, 1), :]
        out_s[...] = jnp.zeros((COLS, 2 * BLOCK), F32)

        def step(g, carry):
            blocks = block_ids(list_ref, i, g)
            scores = masked_scores(blocks, k_s, turned_q, live_ref)
            values = jnp.concatenate([v_s[b] for b in blocks], axis=0)
            dprob = dot(values, turned_cot)
            dscore = (jnp.exp(scores - lse) * (dprob - delta)).astype(BF16)
            turned_k = jnp.concatenate([kt_s[b] for b in blocks], axis=1)
            out_s[...] += dot(turned_k, dscore)
            grads = dot(dscore, q_stack)
            for u, b in enumerate(blocks):
                acc_s[b] += grads[u * BLOCK : (u + 1) * BLOCK]
            return carry

        lax.fori_loop(0, groups_ref[i], step, 0)
        partner = jnp.exp(sp_ref[i] - lse) * (dp_ref[i] - delta)
        partner = tall(partner.astype(BF16).astype(F32))
        dsp_ref[i] = partner.astype(BF16)
        wide = spread(partner)
        grad_query = head_rows(out_s[...]).T
        for m in range(EXPANDERS):
            grad_query += wide[:, m * COLS : (m + 1) * COLS] * pair_ref[m * Q_BLOCKS + i][:, :COLS].astype(F32)
        gq_ref[q_rows(i), :] = (grad_query * (1.0 / math.sqrt(HEAD))).astype(BF16)
        return carry

    lax.fori_loop(0, Q_BLOCKS, per_block, 0)
    store_parts(acc_s, own_ref, halo_ref, gout_ref)


def scatter_into(acc_s, index_rows, data):
    subs = iota((NODES_HERE, BLOCK), 0)
    hot = jnp.concatenate([(subs == row).astype(F32).astype(BF16) for row in index_rows], axis=1)
    acc_s[...] += dot(hot, data)


def gather_grads(own_ref, ret_ref, rows_ref, part_ref, pexp_ref, others, first_col, gsum_ref, gid_ref, acc_s, term_s):
    acc_s[...] = own_ref[...]

    def halo(t, carry):
        index_rows = [rows_ref[pl.ds(t * GROUP + u, 1), :] for u in range(GROUP)]
        data = jnp.concatenate([ret_ref[t * GROUP + u] for u in range(GROUP)], axis=0)
        scatter_into(acc_s, index_rows, data)
        return carry

    lax.fori_loop(0, SENDERS // GROUP, halo, 0)
    for m, other in enumerate(others):
        row_id = iota((16, COLS), 0)
        lane = iota((16, COLS), 1)
        picks = (row_id == jnp.where(lane < HEAD, m, 8 + m)).astype(F32).astype(BF16)

        def partner(t, carry):
            index_rows, data = [], []
            for u in range(GROUP):
                i = t * GROUP + u
                index_rows.append(pexp_ref[pl.ds(m * Q_BLOCKS + i, 1), :])
                wide = dot(part_ref[m, i].astype(F32).T.astype(BF16), picks)
                rows = other[q_rows(i), first_col : first_col + COLS].astype(F32)
                data.append((wide * rows).astype(BF16))
            scatter_into(acc_s, index_rows, jnp.concatenate(data, axis=0))
            return carry

        lax.fori_loop(0, Q_BLOCKS // GROUP, partner, 0)
    scatter_into(acc_s, [gid_ref[...]], gsum_ref[...])


def value_back_kernel(
    own_ref, ret_ref, rows_ref, part_ref, pexp_ref, o0_ref, o1_ref, o2_ref, o3_ref, gsum_ref, gid_ref, wv_ref,
    grad_ref, acc_s,
):
    gather_grads(
        own_ref, ret_ref, rows_ref, part_ref, pexp_ref, (o0_ref, o1_ref, o2_ref, o3_ref), COLS, gsum_ref, gid_ref,
        acc_s, None,
    )
    grad_ref[...] = acc_s[...].astype(BF16)


def key_back_kernel(
    feat_ref, own_ref, ret_ref, rows_ref, part_ref, pexp_ref, o0_ref, o1_ref, o2_ref, o3_ref, gsum_ref, gid_ref,
    wq_ref, wk_ref, wv_ref, gq_ref, gv_ref, t0_ref, t1_ref, t2_ref, t3_ref, acc_s,
):
    gather_grads(
        own_ref, ret_ref, rows_ref, part_ref, pexp_ref, (o0_ref, o1_ref, o2_ref, o3_ref), 0, gsum_ref, gid_ref,
        acc_s, None,
    )
    grad_key = acc_s[...].astype(BF16)
    for k, out in enumerate((t0_ref, t1_ref, t2_ref, t3_ref)):
        part = pl.ds(pl.multiple_of(((feat_ref[0] + k) % 4) * COLS, COLS), COLS)
        term = dot_nt(gq_ref[...], wq_ref[part, :]) + dot_nt(gv_ref[...], wv_ref[part, :])
        term = term + dot_nt(grad_key, wk_ref[part, :])
        out[...] = term.astype(out.dtype)


def shape(dims, kind=BF16):
    return jax.ShapeDtypeStruct(dims, kind)


def call(kernel, ins, outs, args, scratch=(), name=None, flops=0, out_spaces=None):
    cost = pl.CostEstimate(flops=flops, transcendentals=0, bytes_accessed=4_000_000)
    return pl.pallas_call(
        kernel,
        out_shape=outs,
        in_specs=ins,
        out_specs=out_spaces or tuple(vmem() for _ in outs),
        scratch_shapes=list(scratch),
        compiler_params=params(),
        cost_estimate=cost,
        name=name,
    )(*args)


def reduce_rows(part):
    width = part.shape[1]
    own = lax.all_to_all(part.reshape(SENDERS, 4, width), "dom", 0, 0, tiled=True)
    return own.astype(F32).sum(0).astype(BF16)


def spread_rows(rows):
    width = rows.shape[1]
    copies = jnp.broadcast_to(rows[None], (SENDERS, 4, width))
    return lax.all_to_all(copies, "dom", 0, 0, tiled=True).reshape(BLOCK, width)


def on_device(
    features,
    w_query,
    w_key,
    w_value,
    cotangent,
    send_rows,
    halo_count,
    block_mask,
    exp_rows,
    global_ids,
):
    dom_count = lax.axis_size("dom")
    my_index = lax.axis_index("dom")

    def swapped(value, bit):
        return lax.ppermute(value, "dom", [(i, i ^ (1 << bit)) for i in range(dom_count)])

    rows = send_rows[0]
    local = jnp.where(global_ids // NODES_HERE == my_index, global_ids % NODES_HERE, -1).reshape(1, BLOCK)
    exp_list = exp_rows.reshape(EXPANDERS * Q_BLOCKS, BLOCK)
    pexp = jnp.concatenate(
        [swapped(exp_list[m * Q_BLOCKS : (m + 1) * Q_BLOCKS], m) for m in range(EXPANDERS)], axis=0
    )

    query, paired, out_k, out_v, glob_part = call(
        project_kernel,
        [vmem()] * 6,
        (
            shape((NODES_HERE, COLS)),
            shape((NODES_HERE, 2 * COLS)),
            shape((SENDERS, BLOCK, COLS)),
            shape((SENDERS, BLOCK, COLS)),
            shape((BLOCK, 2 * COLS)),
        ),
        (features, w_query, w_key, w_value, rows, local),
        name="project",
        flops=3_000_000_000,
    )
    halo_k = lax.all_to_all(out_k, "dom", 0, 0, tiled=True)
    glob = spread_rows(reduce_rows(glob_part))
    swaps = [swapped(paired, m) for m in range(EXPANDERS)]
    halo_v = lax.all_to_all(out_v, "dom", 0, 0, tiled=True)
    others = [swapped(jnp.concatenate([query, cotangent], axis=1), m) for m in range(EXPANDERS)]

    plan = call(
        plan_kernel,
        [smem()] * 2,
        (shape((Q_BLOCKS * LIST,), jnp.int32), shape((Q_BLOCKS,), jnp.int32), shape((LIST,), jnp.int32)),
        (block_mask.reshape(-1), halo_count.reshape(-1)),
        name="plan",
        out_spaces=(smem(), smem(), smem()),
    )
    (pairs,) = call(
        partner_kernel,
        [vmem()] * 5,
        (shape((EXPANDERS * Q_BLOCKS, BLOCK, 2 * COLS)),),
        (exp_list, *swaps),
        name="partners",
        flops=2_000_000_000,
    )
    blocks_f = pltpu.VMEM((KEY_BLOCKS, BLOCK, COLS), F32)
    blocks_b = pltpu.VMEM((KEY_BLOCKS, BLOCK, COLS), BF16)
    lse, partner_scores = call(
        score_kernel,
        [smem()] * 3 + [vmem()] * 5,
        (shape((Q_BLOCKS, 2 * BLOCK), F32), shape((Q_BLOCKS, 8, 2 * BLOCK), F32)),
        (*plan, query, paired, halo_k, glob, pairs),
        scratch=[blocks_b],
        name="scores",
        flops=6_000_000_000,
    )
    attended, own_v, back_v, glob_v, weight_p, dprob_p, delta = call(
        value_kernel,
        [smem()] * 3 + [vmem()] * 9,
        (
            shape((NODES_HERE, COLS)),
            shape((NODES_HERE, COLS), F32),
            shape((SENDERS, BLOCK, COLS)),
            shape((BLOCK, COLS)),
            shape((Q_BLOCKS, 16, BLOCK)),
            shape((Q_BLOCKS, 8, 2 * BLOCK), F32),
            shape((Q_BLOCKS, 2 * BLOCK), F32),
        ),
        (*plan, query, paired, halo_k, halo_v, glob, pairs, cotangent, lse, partner_scores),
        scratch=[blocks_b, blocks_b, blocks_f, pltpu.VMEM((COLS, 2 * BLOCK), F32)],
        name="values",
        flops=15_000_000_000,
    )
    returned_v = lax.all_to_all(back_v, "dom", 0, 0, tiled=True)
    wp_back = jnp.stack([swapped(weight_p, m) for m in range(EXPANDERS)])
    gsum_v = spread_rows(reduce_rows(glob_v))
    grad_query, own_k, back_k, glob_k, dscore_p = call(
        key_kernel,
        [smem()] * 3 + [vmem()] * 11,
        (
            shape((NODES_HERE, COLS)),
            shape((NODES_HERE, COLS), F32),
            shape((SENDERS, BLOCK, COLS)),
            shape((BLOCK, COLS)),
            shape((Q_BLOCKS, 16, BLOCK)),
        ),
        (*plan, query, paired, halo_k, halo_v, glob, pairs, cotangent, lse, partner_scores, dprob_p, delta),
        scratch=[blocks_b, blocks_b, blocks_b, blocks_f, pltpu.VMEM((COLS, 2 * BLOCK), F32)],
        name="keys",
        flops=18_000_000_000,
    )
    returned_k = lax.all_to_all(back_k, "dom", 0, 0, tiled=True)
    ds_back = jnp.stack([swapped(dscore_p, m) for m in range(EXPANDERS)])
    gsum_k = spread_rows(reduce_rows(glob_k))
    acc = [pltpu.VMEM((NODES_HERE, COLS), F32)]
    (grad_value,) = call(
        value_back_kernel,
        [vmem()] * 12,
        (shape((NODES_HERE, COLS)),),
        (own_v, returned_v, rows, wp_back, pexp, *others, gsum_v, local, w_value),
        scratch=acc,
        name="value_back",
        flops=5_000_000_000,
    )
    mine, *away = call(
        key_back_kernel,
        [smem()] + [vmem()] * 16,
        (shape((NODES_HERE, COLS), F32),) + tuple(shape((NODES_HERE, COLS)) for _ in range(3)),
        (
            lax.axis_index("feat").reshape(1).astype(jnp.int32), own_k, returned_k, rows, ds_back, pexp, *others,
            gsum_k, local, w_query, w_key, w_value, grad_query, grad_value,
        ),
        scratch=acc,
        name="key_back",
        flops=5_000_000_000,
    )
    for k, term in enumerate(away, 1):
        mine = mine + lax.ppermute(term, "feat", [(i, (i + k) % 4) for i in range(4)]).astype(F32)
    return (attended, mine.astype(BF16))


def solution(mesh):
    return jax.shard_map(
        on_device,
        mesh=mesh,
        in_specs=(
            P("dom", None),
            P(None, "feat"),
            P(None, "feat"),
            P(None, "feat"),
            P("dom", "feat"),
            P("dom", None, None),
            P(None, "dom"),
            P("dom", None),
            P(None, "dom"),
            P(),
        ),
        out_specs=(P("dom", "feat"), P("dom", "feat")),
        check_vma=False,
    )
```

```python
import math

import jax
import jax.numpy as jnp
from jax import lax
from jax.experimental import pallas as pl
from jax.experimental.pallas import tpu as pltpu
from jax.sharding import PartitionSpec as P

HEAD = 64
BLOCK = 128
EXPANDERS = 4
COLS = 128
NODES_HERE = 1024
Q_BLOCKS = NODES_HERE // BLOCK
SENDERS = 32
GLOBAL_BLOCK = Q_BLOCKS + SENDERS
EMPTY_BLOCK = GLOBAL_BLOCK + 1
KEY_BLOCKS = EMPTY_BLOCK + 1
GROUP = 4
PAIR = 2
LIST = 56
EXTRA = 16
SLOTS = BLOCK + EXTRA
NEG = -1e30
F32 = jnp.float32
BF16 = jnp.bfloat16


def params():
    return pltpu.CompilerParams(vmem_limit_bytes=56 * 1024 * 1024)


def vmem():
    return pl.BlockSpec(memory_space=pltpu.VMEM)


def smem():
    return pl.BlockSpec(memory_space=pltpu.SMEM)


def iota(shape, dim):
    return lax.broadcasted_iota(jnp.int32, shape, dim)


def dot(a, b):
    return jnp.dot(a, b, preferred_element_type=F32)


def dot_nt(a, b):
    return lax.dot_general(a, b, (((1,), (1,)), ((), ())), preferred_element_type=F32)


def split_index(index):
    return (index & (BLOCK - 1)).astype(F32).astype(BF16), (index >> 7).astype(F32).astype(BF16)


def packed_iota(dim):
    return iota((BLOCK, BLOCK), dim).astype(F32).astype(BF16)


def one_hot_columns(column):
    low, high = split_index(column)
    lanes = jnp.concatenate([packed_iota(1)] * (column.shape[0] // BLOCK), axis=0)
    one, zero = jnp.ones((), BF16), jnp.zeros((), BF16)
    base = jnp.where(low == lanes, one, zero)
    return jnp.concatenate(
        [jnp.where(high == jnp.asarray(c, BF16), base, zero) for c in range(NODES_HERE // BLOCK)], axis=1
    )


def one_hot_of_rows(index_rows):
    columns = [jnp.broadcast_to(row, (BLOCK, BLOCK)).T for row in index_rows]
    return one_hot_columns(jnp.concatenate(columns, axis=0))


def owner_ranks(gid_row):
    owner = jnp.broadcast_to(gid_row >> 10, (BLOCK, BLOCK))
    owner_t = owner.T
    same = owner == owner_t
    subs, lanes = iota((BLOCK, BLOCK), 0), iota((BLOCK, BLOCK), 1)
    row = jnp.sum(jnp.where(jnp.logical_and(same, subs < lanes), 1.0, 0.0), axis=0, keepdims=True)
    col = jnp.sum(jnp.where(jnp.logical_and(same, lanes < subs), 1.0, 0.0), axis=1, keepdims=True)
    row, col = row.astype(jnp.int32), jnp.broadcast_to(col, (BLOCK, BLOCK)).astype(jnp.int32)
    slot_row = jnp.where(row < EXTRA, (gid_row >> 10) * EXTRA + row, -1)
    slot_col = jnp.where(col < EXTRA, owner_t * EXTRA + col, -1)
    return row, slot_row, slot_col


def mine_columns(gid_row, me):
    row, _, _ = owner_ranks(gid_row)
    mine = (gid_row >> 10) == me
    slots = iota((EXTRA, BLOCK), 0)
    hit = jnp.logical_and(jnp.broadcast_to(mine, (EXTRA, BLOCK)), slots == row)
    local = jnp.broadcast_to(gid_row & (NODES_HERE - 1), (EXTRA, BLOCK)) + 1
    return jnp.sum(jnp.where(hit, local, 0).astype(F32), axis=1, keepdims=True).astype(jnp.int32) - 1


def project_kernel(
    me_ref, x_ref, wq_ref, wk_ref, wv_ref, cot_ref, rows_ref, exp_ref, gid_ref, q_ref, kv_ref, outk_ref, outv_ref, away_ref
):
    x = x_ref[...]
    kv_ref[:, :COLS] = dot(x, wk_ref[...]).astype(BF16)
    kv_ref[:, COLS:] = dot(x, wv_ref[...]).astype(BF16)
    query = (dot(x, wq_ref[...]).astype(BF16).astype(F32) * (1.0 / math.sqrt(HEAD))).astype(BF16)
    q_ref[...] = query
    away_ref[:NODES_HERE, :COLS] = query
    away_ref[:NODES_HERE, COLS:] = cot_ref[...]
    low, high = split_index(exp_ref[...])
    away_ref[NODES_HERE:, :COLS] = low
    away_ref[NODES_HERE:, COLS:] = high
    mine = jnp.broadcast_to(mine_columns(gid_ref[...], me_ref[0]), (EXTRA, BLOCK))
    lanes = iota((EXTRA, NODES_HERE), 1)
    hot = (jnp.concatenate([mine] * (NODES_HERE // BLOCK), axis=1) == lanes).astype(F32).astype(BF16)
    extra = dot(hot, kv_ref[...]).astype(BF16)

    def gather(t, carry):
        hot = one_hot_of_rows([rows_ref[pl.ds(t * GROUP + u, 1), :] for u in range(GROUP)])
        got = dot(hot, kv_ref[...]).astype(BF16)
        for u in range(GROUP):
            outk_ref[t * GROUP + u, :BLOCK] = got[u * BLOCK : (u + 1) * BLOCK, :COLS]
            outv_ref[t * GROUP + u, :BLOCK] = got[u * BLOCK : (u + 1) * BLOCK, COLS:]
            outk_ref[t * GROUP + u, BLOCK:] = extra[:, :COLS]
            outv_ref[t * GROUP + u, BLOCK:] = extra[:, COLS:]
        return carry

    lax.fori_loop(0, SENDERS // GROUP, gather, 0)


def partner_kernel(exp_ref, t0_ref, t1_ref, t2_ref, t3_ref, out_ref):
    for m, table in enumerate((t0_ref, t1_ref, t2_ref, t3_ref)):

        def gather(t, carry):
            b = m * Q_BLOCKS + t * GROUP
            got = dot(one_hot_of_rows([exp_ref[pl.ds(b + u, 1), :] for u in range(GROUP)]), table[...]).astype(BF16)
            for u in range(GROUP):
                out_ref[b + u] = got[u * BLOCK : (u + 1) * BLOCK]
            return carry

        lax.fori_loop(0, Q_BLOCKS // GROUP, gather, 0)


def plan_kernel(mask_ref, count_ref, list_ref, groups_ref, live_ref):
    for j in range(Q_BLOCKS):
        live_ref[j] = BLOCK
    live_ref[GLOBAL_BLOCK] = BLOCK
    live_ref[EMPTY_BLOCK] = 0

    def copy_count(s, carry):
        live_ref[Q_BLOCKS + s] = count_ref[s]
        return carry

    lax.fori_loop(0, SENDERS, copy_count, 0)

    def per_block(i, carry):
        list_ref[i * LIST] = GLOBAL_BLOCK

        def put(j, n):
            list_ref[i * LIST + n] = j
            used = jnp.logical_and(mask_ref[i * GLOBAL_BLOCK + j] > 0, live_ref[j] > 0)
            return n + used.astype(jnp.int32)

        n = lax.fori_loop(0, GLOBAL_BLOCK, put, 1)
        for extra in range(GROUP):
            list_ref[i * LIST + n + extra] = EMPTY_BLOCK
        groups_ref[i] = (n + GROUP - 1) // GROUP
        return carry

    lax.fori_loop(0, Q_BLOCKS, per_block, 0)


def fill(dst, own_ref, first_col, halo_ref, gid_ref, glob_ref, transposed=False):
    def turn(x):
        return x.T if transposed else x

    def own(j, carry):
        dst[j] = turn(own_ref[q_rows(j), first_col : first_col + COLS])
        return carry

    def halo(j, carry):
        dst[Q_BLOCKS + j] = turn(halo_ref[j, :BLOCK])
        return carry

    lax.fori_loop(0, Q_BLOCKS, own, 0, unroll=4)
    lax.fori_loop(0, SENDERS, halo, 0, unroll=4)
    slot_col = owner_ranks(gid_ref[...])[2]
    wide = jnp.concatenate([slot_col] * (SENDERS * EXTRA // BLOCK), axis=1)
    hot = (wide == iota((BLOCK, SENDERS * EXTRA), 1)).astype(F32).astype(BF16)
    extra = jnp.concatenate([halo_ref[s, BLOCK:] for s in range(SENDERS)], axis=0)
    rows = dot(hot, extra) + glob_ref[:, first_col : first_col + COLS].astype(F32)
    dst[GLOBAL_BLOCK] = turn(rows.astype(BF16))
    dst[EMPTY_BLOCK] = jnp.zeros((BLOCK, COLS), BF16)


def stacked(rows):
    lanes = iota((BLOCK, COLS), 1)
    zero = jnp.zeros_like(rows)
    return jnp.concatenate([jnp.where(lanes < HEAD, rows, zero), jnp.where(lanes < HEAD, zero, rows)], axis=0)


def stacked_t(rows):
    turned = rows.T
    subs = iota((COLS, BLOCK), 0)
    zero = jnp.zeros_like(turned)
    return jnp.concatenate([jnp.where(subs < HEAD, turned, zero), jnp.where(subs < HEAD, zero, turned)], axis=1)


def partner_rows(rows, pair_ref, i, first_col):
    total = jnp.zeros((16, BLOCK), F32)
    row_id = iota((16, COLS), 0)
    lane = iota((16, COLS), 1)
    for m in range(EXPANDERS):
        other = pair_ref[m * Q_BLOCKS + i][:, first_col : first_col + COLS]
        prod = rows.astype(F32) * other.astype(F32)
        high = prod.astype(BF16)
        low = (prod - high.astype(F32)).astype(BF16)
        picks = (row_id == jnp.where(lane < HEAD, m, 8 + m)).astype(F32).astype(BF16)
        total = total + dot_nt(picks, high) + dot_nt(picks, low)
    return jnp.concatenate([total[:8], total[8:]], axis=1)


def tall(weights):
    return jnp.concatenate([weights[:, :BLOCK], weights[:, BLOCK:]], axis=0)


def spread(tall_weights):
    turned = tall_weights.T.astype(BF16)
    row_id = iota((16, EXPANDERS * COLS), 0)
    col = iota((16, EXPANDERS * COLS), 1)
    picks = (row_id == (col // COLS) + jnp.where(col % COLS < HEAD, 0, 8)).astype(F32).astype(BF16)
    return dot(turned, picks)


def head_rows(turned):
    return jnp.concatenate([turned[:HEAD, :BLOCK], turned[HEAD:, BLOCK:]], axis=0)


def masked_scores(blocks, k_s, turned_q, live_ref):
    keys = jnp.concatenate([k_s[b] for b in blocks], axis=0)
    scores = dot(keys, turned_q)
    row_id = iota((BLOCK, 2 * BLOCK), 0)
    return jnp.concatenate(
        [
            jnp.where(row_id < live_ref[b], scores[u * BLOCK : (u + 1) * BLOCK], NEG)
            for u, b in enumerate(blocks)
        ],
        axis=0,
    )


def score_rows(rows, pair_ref, i):
    partner = partner_rows(rows, pair_ref, i, 0)
    return jnp.where(iota((8, 2 * BLOCK), 0) < EXPANDERS, partner, NEG)


def block_ids(list_ref, i, g):
    return [list_ref[i * LIST + g * GROUP + u] for u in range(GROUP)]


def q_rows(i):
    return pl.ds(pl.multiple_of(i * BLOCK, BLOCK), BLOCK)


def score_kernel(list_ref, groups_ref, live_ref, q_ref, kv_ref, hk_ref, gid_ref, glob_ref, lse_ref, k_s):
    fill(k_s, kv_ref, 0, hk_ref, gid_ref, glob_ref)

    def per_block(i, carry):
        turned_q = stacked_t(q_ref[q_rows(i), :])

        def step(g, state):
            blocks = block_ids(list_ref, i, g)
            new_state = []
            for u in range(GROUP // PAIR):
                top, total = state[u]
                scores = masked_scores(blocks[u * PAIR : (u + 1) * PAIR], k_s, turned_q, live_ref)
                scores = scores.reshape(PAIR * BLOCK // 8, 8, 2 * BLOCK)
                new_top = jnp.maximum(top, jnp.max(scores, axis=0))
                total = total * jnp.exp(top - new_top) + jnp.sum(jnp.exp(scores - new_top[None]), axis=0)
                new_state.append((new_top, total))
            return tuple(new_state)

        init = (jnp.full((8, 2 * BLOCK), NEG, F32), jnp.zeros((8, 2 * BLOCK), F32))
        state = lax.fori_loop(0, groups_ref[i], step, tuple(init for _ in range(GROUP // PAIR)))
        top = jnp.concatenate([t for t, _ in state], axis=0)
        total = jnp.concatenate([t for _, t in state], axis=0)
        best = jnp.max(top, axis=0, keepdims=True)
        denominator = jnp.sum(total * jnp.exp(top - best), axis=0, keepdims=True)
        lse_ref[pl.ds(i, 1), :] = best + jnp.log(denominator)
        return carry

    lax.fori_loop(0, Q_BLOCKS, per_block, 0)


def clear_blocks(acc_s):
    def clear(j, carry):
        acc_s[j] = jnp.zeros((BLOCK, COLS), F32)
        return carry

    lax.fori_loop(0, KEY_BLOCKS, clear, 0)


def value_kernel(
    list_ref, groups_ref, live_ref, q_ref, kv_ref, hk_ref, hv_ref, gid_ref, glob_ref, pair_ref, cot_ref, part_ref,
    att_ref, own_ref, halo_ref, gout_ref, wp_ref, pdp_ref, delta_ref, lse_ref, k_s, vt_s, acc_s, out_s,
):
    fill(k_s, kv_ref, 0, hk_ref, gid_ref, glob_ref)
    fill(vt_s, kv_ref, COLS, hv_ref, gid_ref, glob_ref, transposed=True)
    clear_blocks(acc_s)

    def per_block(i, carry):
        rows = q_ref[q_rows(i), :]
        turned_q = stacked_t(rows)
        cot = cot_ref[q_rows(i), :]
        cot_stack = stacked(cot)
        partner = score_rows(rows, pair_ref, i)
        part = part_ref[pl.ds(i, 1), :]
        best = jnp.maximum(part, jnp.max(partner, axis=0, keepdims=True))
        lse = best + jnp.log(jnp.exp(part - best) + jnp.sum(jnp.exp(partner - best), axis=0, keepdims=True))
        lse_ref[pl.ds(i, 1), :] = lse
        out_s[...] = jnp.zeros((COLS, 2 * BLOCK), F32)

        def step(g, carry):
            blocks = block_ids(list_ref, i, g)
            total = None
            for u in range(0, GROUP, PAIR):
                pair = blocks[u : u + PAIR]
                scores = masked_scores(pair, k_s, turned_q, live_ref)
                weight = jnp.exp(scores - lse).astype(BF16)
                term = dot(jnp.concatenate([vt_s[b] for b in pair], axis=1), weight)
                total = term if total is None else total + term
                grads = dot(weight, cot_stack)
                for w, b in enumerate(pair):
                    acc_s[b] += grads[w * BLOCK : (w + 1) * BLOCK]
            out_s[...] += total
            return carry

        lax.fori_loop(0, groups_ref[i], step, 0)
        dprob = partner_rows(cot, pair_ref, i, COLS)
        prob = jnp.exp(partner - lse)
        weight = prob.astype(BF16).astype(F32)
        wide = spread(tall(weight))
        wp_ref[i] = tall(weight).astype(BF16)
        attended_t = head_rows(out_s[...])
        prod = attended_t * cot.T.astype(F32)
        delta = jnp.concatenate(
            [jnp.sum(prod[:HEAD], axis=0, keepdims=True), jnp.sum(prod[HEAD:], axis=0, keepdims=True)], axis=1
        )
        delta = delta + jnp.sum(prob * dprob, axis=0, keepdims=True)
        delta_ref[pl.ds(i, 1), :] = delta
        pdp_ref[i] = prob * (dprob - delta)
        attended = attended_t.T
        for m in range(EXPANDERS):
            attended += wide[:, m * COLS : (m + 1) * COLS] * pair_ref[m * Q_BLOCKS + i][:, COLS:].astype(F32)
        att_ref[q_rows(i), :] = attended.astype(BF16)
        return carry

    lax.fori_loop(0, Q_BLOCKS, per_block, 0)
    store_parts(acc_s, own_ref, halo_ref, gid_ref, gout_ref)


def store_parts(acc_s, own_ref, halo_ref, gid_ref, gout_ref):
    def own(j, carry):
        own_ref[q_rows(j), :] = acc_s[j]
        return carry

    def halo(j, carry):
        halo_ref[j, :BLOCK] = acc_s[Q_BLOCKS + j].astype(BF16)
        return carry

    lax.fori_loop(0, Q_BLOCKS, own, 0, unroll=2)
    lax.fori_loop(0, SENDERS, halo, 0, unroll=4)
    grads = acc_s[GLOBAL_BLOCK].astype(BF16)
    gout_ref[...] = grads
    slot_row = owner_ranks(gid_ref[...])[1]
    hot = (iota((SENDERS * EXTRA, BLOCK), 0) == slot_row).astype(F32).astype(BF16)
    extra = dot(hot, grads).astype(BF16)
    for s in range(SENDERS):
        halo_ref[s, BLOCK:] = extra[s * EXTRA : (s + 1) * EXTRA]


def key_kernel(
    list_ref, groups_ref, live_ref, q_ref, kv_ref, hk_ref, hv_ref, gid_ref, glob_ref, pair_ref, cot_ref, lse_ref,
    pdp_ref, delta_ref, gq_ref, own_ref, halo_ref, gout_ref, dsp_ref, k_s, v_s, kt_s, acc_s, out_s,
):
    fill(k_s, kv_ref, 0, hk_ref, gid_ref, glob_ref)
    fill(v_s, kv_ref, COLS, hv_ref, gid_ref, glob_ref)
    fill(kt_s, kv_ref, 0, hk_ref, gid_ref, glob_ref, transposed=True)
    clear_blocks(acc_s)

    def per_block(i, carry):
        rows = q_ref[q_rows(i), :]
        turned_q = stacked_t(rows)
        q_stack = stacked(rows)
        turned_cot = stacked_t(cot_ref[q_rows(i), :])
        lse = lse_ref[pl.ds(i, 1), :]
        delta = delta_ref[pl.ds(i, 1), :]
        out_s[...] = jnp.zeros((COLS, 2 * BLOCK), F32)

        def step(g, carry):
            blocks = block_ids(list_ref, i, g)
            total = None
            for u in range(0, GROUP, PAIR):
                pair = blocks[u : u + PAIR]
                scores = masked_scores(pair, k_s, turned_q, live_ref)
                dprob = dot(jnp.concatenate([v_s[b] for b in pair], axis=0), turned_cot)
                dscore = (jnp.exp(scores - lse) * (dprob - delta)).astype(BF16)
                term = dot(jnp.concatenate([kt_s[b] for b in pair], axis=1), dscore)
                total = term if total is None else total + term
                grads = dot(dscore, q_stack)
                for w, b in enumerate(pair):
                    acc_s[b] += grads[w * BLOCK : (w + 1) * BLOCK]
            out_s[...] += total
            return carry

        lax.fori_loop(0, groups_ref[i], step, 0)
        partner = tall(pdp_ref[i].astype(BF16).astype(F32))
        dsp_ref[i] = partner.astype(BF16)
        wide = spread(partner)
        grad_query = head_rows(out_s[...]).T
        for m in range(EXPANDERS):
            grad_query += wide[:, m * COLS : (m + 1) * COLS] * pair_ref[m * Q_BLOCKS + i][:, :COLS].astype(F32)
        gq_ref[q_rows(i), :] = (grad_query * (1.0 / math.sqrt(HEAD))).astype(BF16)
        return carry

    lax.fori_loop(0, Q_BLOCKS, per_block, 0)
    store_parts(acc_s, own_ref, halo_ref, gid_ref, gout_ref)


def scatter_into(acc_s, splits, data):
    subs = packed_iota(0)
    one, zero = jnp.ones((), BF16), jnp.zeros((), BF16)
    bases = [(jnp.where(subs == low, one, zero), jnp.broadcast_to(high, (BLOCK, BLOCK))) for low, high in splits]
    for c in range(NODES_HERE // BLOCK):
        hot = jnp.concatenate([jnp.where(high == jnp.asarray(c, BF16), base, zero) for base, high in bases], axis=1)
        acc_s[c * BLOCK : (c + 1) * BLOCK, :] += dot(hot, data)


def gather_grads(me_ref, own_ref, ret_ref, rows_ref, parts, others, first_col, gid_ref, acc_s):
    acc_s[...] = own_ref[...]

    def halo(t, carry):
        splits = [split_index(rows_ref[pl.ds(t * GROUP + u, 1), :]) for u in range(GROUP)]
        data = jnp.concatenate([ret_ref[t * GROUP + u, :BLOCK] for u in range(GROUP)], axis=0)
        scatter_into(acc_s, splits, data)
        return carry

    lax.fori_loop(0, SENDERS // GROUP, halo, 0)
    row_id = iota((16, COLS), 0)
    lane = iota((16, COLS), 1)
    for m, (part, other) in enumerate(zip(parts, others)):
        picks = (row_id == jnp.where(lane < HEAD, m, 8 + m)).astype(F32).astype(BF16)
        index_low = other[NODES_HERE + m * Q_BLOCKS : NODES_HERE + (m + 1) * Q_BLOCKS, :COLS]
        index_high = other[NODES_HERE + m * Q_BLOCKS : NODES_HERE + (m + 1) * Q_BLOCKS, COLS:]
        for t in range(Q_BLOCKS // GROUP):
            splits, data = [], []
            for u in range(GROUP):
                i = t * GROUP + u
                splits.append((index_low[i : i + 1], index_high[i : i + 1]))
                wide = dot(part[1 if first_col else 0, i].astype(F32).T.astype(BF16), picks)
                rows = other[i * BLOCK : (i + 1) * BLOCK, first_col : first_col + COLS].astype(F32)
                data.append((wide * rows).astype(BF16))
            scatter_into(acc_s, splits, jnp.concatenate(data, axis=0))
    extra = ret_ref[0, BLOCK:].astype(F32)
    for s in range(1, SENDERS):
        extra += ret_ref[s, BLOCK:].astype(F32)
    high = extra.astype(BF16)
    data = jnp.concatenate([high, (extra - high.astype(F32)).astype(BF16)], axis=0)
    mine = jnp.broadcast_to(mine_columns(gid_ref[...], me_ref[0]), (EXTRA, NODES_HERE))
    hot = (mine == iota((EXTRA, NODES_HERE), 1)).astype(F32)
    hot = jnp.concatenate([hot, hot], axis=0).T.astype(BF16)
    acc_s[...] += dot(hot, data)


def value_back_kernel(
    me_ref, own_ref, ret_ref, rows_ref, p0_ref, p1_ref, p2_ref, p3_ref, o0_ref, o1_ref, o2_ref, o3_ref, gid_ref,
    grad_ref, acc_s,
):
    parts, others = (p0_ref, p1_ref, p2_ref, p3_ref), (o0_ref, o1_ref, o2_ref, o3_ref)
    gather_grads(me_ref, own_ref, ret_ref, rows_ref, parts, others, COLS, gid_ref, acc_s)
    grad_ref[...] = acc_s[...].astype(BF16)


def key_back_kernel(
    me_ref, own_ref, ret_ref, rows_ref, p0_ref, p1_ref, p2_ref, p3_ref, o0_ref, o1_ref, o2_ref, o3_ref, gid_ref,
    wq_ref, wk_ref, wv_ref, gq_ref, gv_ref, t0_ref, t1_ref, t2_ref, t3_ref, acc_s,
):
    parts, others = (p0_ref, p1_ref, p2_ref, p3_ref), (o0_ref, o1_ref, o2_ref, o3_ref)
    gather_grads(me_ref, own_ref, ret_ref, rows_ref, parts, others, 0, gid_ref, acc_s)
    grad_key = acc_s[...].astype(BF16)
    for k, out in enumerate((t0_ref, t1_ref, t2_ref, t3_ref)):
        part = pl.ds(pl.multiple_of(((me_ref[1] + k) % 4) * COLS, COLS), COLS)
        term = dot_nt(gq_ref[...], wq_ref[part, :]) + dot_nt(gv_ref[...], wv_ref[part, :])
        term = term + dot_nt(grad_key, wk_ref[part, :])
        out[...] = term.astype(out.dtype)


def shape(dims, kind=BF16):
    return jax.ShapeDtypeStruct(dims, kind)


def call(kernel, ins, outs, args, scratch=(), name=None, flops=0, out_spaces=None):
    cost = pl.CostEstimate(flops=flops, transcendentals=0, bytes_accessed=4_000_000)
    return pl.pallas_call(
        kernel,
        out_shape=outs,
        in_specs=ins,
        out_specs=out_spaces or tuple(vmem() for _ in outs),
        scratch_shapes=list(scratch),
        compiler_params=params(),
        cost_estimate=cost,
        name=name,
    )(*args)


def blocks_of(kind):
    return pltpu.VMEM((KEY_BLOCKS, BLOCK, COLS), kind)


def run_project(me, features, w_query, w_key, w_value, cotangent, rows, exp_list, gids):
    return call(
        project_kernel,
        [smem()] + [vmem()] * 8,
        (
            shape((NODES_HERE, COLS)),
            shape((NODES_HERE, 2 * COLS)),
            shape((SENDERS, SLOTS, COLS)),
            shape((SENDERS, SLOTS, COLS)),
            shape((NODES_HERE + EXPANDERS * Q_BLOCKS, 2 * COLS)),
        ),
        (me, features, w_query, w_key, w_value, cotangent, rows, exp_list, gids),
        name="project",
        flops=3_000_000_000,
    )


def run_plan(block_mask, halo_count):
    return call(
        plan_kernel,
        [smem()] * 2,
        (shape((Q_BLOCKS * LIST,), jnp.int32), shape((Q_BLOCKS,), jnp.int32), shape((LIST,), jnp.int32)),
        (block_mask.reshape(-1), halo_count.reshape(-1)),
        name="plan",
        out_spaces=(smem(), smem(), smem()),
    )


def run_partners(exp_list, swaps):
    return call(
        partner_kernel,
        [vmem()] * 5,
        (shape((EXPANDERS * Q_BLOCKS, BLOCK, 2 * COLS)),),
        (exp_list, *swaps),
        name="partners",
        flops=5_000_000_000,
    )[0]


def run_scores(plan, query, paired, halo_k, gids, glob):
    return call(
        score_kernel,
        [smem()] * 3 + [vmem()] * 5,
        (shape((Q_BLOCKS, 2 * BLOCK), F32),),
        (*plan, query, paired, halo_k, gids, glob),
        scratch=[blocks_of(BF16)],
        name="scores",
        flops=12_000_000_000,
    )[0]


def run_values(plan, query, paired, halo_k, halo_v, gids, glob, pairs, cotangent, part):
    return call(
        value_kernel,
        [smem()] * 3 + [vmem()] * 9,
        (
            shape((NODES_HERE, COLS)),
            shape((NODES_HERE, COLS), F32),
            shape((SENDERS, SLOTS, COLS)),
            shape((BLOCK, COLS)),
            shape((Q_BLOCKS, 16, BLOCK)),
            shape((Q_BLOCKS, 8, 2 * BLOCK), F32),
            shape((Q_BLOCKS, 2 * BLOCK), F32),
            shape((Q_BLOCKS, 2 * BLOCK), F32),
        ),
        (*plan, query, paired, halo_k, halo_v, gids, glob, pairs, cotangent, part),
        scratch=[blocks_of(BF16), blocks_of(BF16), blocks_of(F32), pltpu.VMEM((COLS, 2 * BLOCK), F32)],
        name="values",
        flops=20_000_000_000,
    )


def run_keys(plan, query, paired, halo_k, halo_v, gids, glob, pairs, cotangent, lse, pdp, delta):
    return call(
        key_kernel,
        [smem()] * 3 + [vmem()] * 11,
        (
            shape((NODES_HERE, COLS)),
            shape((NODES_HERE, COLS), F32),
            shape((SENDERS, SLOTS, COLS)),
            shape((BLOCK, COLS)),
            shape((Q_BLOCKS, 16, BLOCK)),
        ),
        (*plan, query, paired, halo_k, halo_v, gids, glob, pairs, cotangent, lse, pdp, delta),
        scratch=[blocks_of(BF16), blocks_of(BF16), blocks_of(BF16), blocks_of(F32), pltpu.VMEM((COLS, 2 * BLOCK), F32)],
        name="keys",
        flops=25_000_000_000,
    )


def run_value_back(me, own_v, returned_v, rows, parts, others, gids):
    return call(
        value_back_kernel,
        [smem()] + [vmem()] * 12,
        (shape((NODES_HERE, COLS)),),
        (me, own_v, returned_v, rows, *parts, *others, gids),
        scratch=[pltpu.VMEM((NODES_HERE, COLS), F32)],
        name="value_back",
        flops=8_000_000_000,
    )[0]


def run_key_back(me, own_k, returned_k, rows, parts, others, gids, w_query, w_key, w_value, grad_query, grad_value):
    return call(
        key_back_kernel,
        [smem()] + [vmem()] * 17,
        (shape((NODES_HERE, COLS), F32),) + tuple(shape((NODES_HERE, COLS)) for _ in range(3)),
        (me, own_k, returned_k, rows, *parts, *others, gids, w_query, w_key, w_value, grad_query, grad_value),
        scratch=[pltpu.VMEM((NODES_HERE, COLS), F32)],
        name="key_back",
        flops=8_000_000_000,
    )


def more_rounds(global_ids):
    owned = (global_ids[None, :] // NODES_HERE == jnp.arange(SENDERS)[:, None]).sum(1)
    return (owned.max() + EXTRA - 1) // EXTRA


def ranks(global_ids):
    owner = global_ids // NODES_HERE
    ids = jnp.arange(BLOCK)
    return owner, ((owner[:, None] == owner[None, :]) & (ids[None, :] < ids[:, None])).sum(1)


def more_globals(rounds, global_ids, my_index, paired):
    def body(state):
        r, glob = state
        owner, rank = ranks(global_ids)
        slot = rank - r * EXTRA
        here = (slot >= 0) & (slot < EXTRA)
        place = jnp.where((owner == my_index) & here, slot, EXTRA)
        rows = jnp.zeros((EXTRA + 1, paired.shape[1]), BF16).at[place].set(paired[global_ids % NODES_HERE])[:EXTRA]
        got = lax.all_to_all(jnp.broadcast_to(rows[None], (SENDERS, *rows.shape)), "dom", 0, 0, tiled=True)
        found = got.reshape(SENDERS * EXTRA, -1)[jnp.clip(owner * EXTRA + slot, 0, SENDERS * EXTRA - 1)]
        return r + 1, jnp.where(here[:, None], found, glob)

    start = (jnp.asarray(1, jnp.int32), jnp.zeros((BLOCK, paired.shape[1]), BF16))
    return lax.while_loop(lambda state: state[0] < rounds, body, start)[1]


def more_grads(rounds, global_ids, my_index, part_k, part_v, own_k, own_v):
    def body(state):
        r, own_k, own_v = state
        owner, rank = ranks(global_ids)
        slot = rank - r * EXTRA
        here = (slot >= 0) & (slot < EXTRA)
        part = jnp.concatenate([part_k, part_v], axis=1)
        place = jnp.where(here, owner * EXTRA + slot, SENDERS * EXTRA)
        rows = jnp.zeros((SENDERS * EXTRA + 1, part.shape[1]), BF16).at[place].set(part)[: SENDERS * EXTRA]
        got = lax.all_to_all(rows.reshape(SENDERS, EXTRA, -1), "dom", 0, 0, tiled=True).astype(F32).sum(0)
        take = (owner == my_index) & here
        add = jnp.where(take[:, None], got[jnp.clip(slot, 0, EXTRA - 1)], 0.0)
        local = global_ids % NODES_HERE
        return r + 1, own_k.at[local].add(add[:, :COLS]), own_v.at[local].add(add[:, COLS:])

    start = (jnp.asarray(1, jnp.int32), own_k, own_v)
    return lax.while_loop(lambda state: state[0] < rounds, body, start)[1:]


def on_device(
    features,
    w_query,
    w_key,
    w_value,
    cotangent,
    send_rows,
    halo_count,
    block_mask,
    exp_rows,
    global_ids,
):
    dom_count = lax.axis_size("dom")
    my_index = lax.axis_index("dom")

    def swapped(value, bit):
        return lax.ppermute(value, "dom", [(i, i ^ (1 << bit)) for i in range(dom_count)])

    rows = send_rows[0]
    gids = global_ids.reshape(1, BLOCK)
    exp_list = exp_rows.reshape(EXPANDERS * Q_BLOCKS, BLOCK)
    me = jnp.stack([my_index, lax.axis_index("feat")]).astype(jnp.int32)
    rounds = more_rounds(global_ids)

    query, paired, out_k, out_v, away = run_project(
        me, features, w_query, w_key, w_value, cotangent, rows, exp_list, gids
    )
    glob = more_globals(rounds, global_ids, my_index, paired)
    out_k, out_v, glob = lax.optimization_barrier((out_k, out_v, glob))
    halo_k = lax.all_to_all(out_k, "dom", 0, 0, tiled=True)
    swaps = [swapped(paired, m) for m in range(EXPANDERS)]
    plan = run_plan(block_mask, halo_count)
    halo_v = lax.all_to_all(out_v, "dom", 0, 0, tiled=True)
    part = run_scores(plan, query, paired, halo_k, gids, glob)
    pairs = run_partners(exp_list, swaps)
    away, part = lax.optimization_barrier((away, part))
    others = [swapped(away, m) for m in range(EXPANDERS)]
    attended, own_v, back_v, glob_v, weight_p, pdp, delta, lse = run_values(
        plan, query, paired, halo_k, halo_v, gids, glob, pairs, cotangent, part
    )
    *others, lse = lax.optimization_barrier((*others, lse))
    returned_v = lax.all_to_all(back_v, "dom", 0, 0, tiled=True)
    grad_query, own_k, back_k, glob_k, dscore_p = run_keys(
        plan, query, paired, halo_k, halo_v, gids, glob, pairs, cotangent, lse, pdp, delta
    )
    own_k, own_v = more_grads(rounds, global_ids, my_index, glob_k, glob_v, own_k, own_v)
    back_k, own_k, own_v = lax.optimization_barrier((back_k, own_k, own_v))
    returned_k = lax.all_to_all(back_k, "dom", 0, 0, tiled=True)
    both = jnp.stack([dscore_p, weight_p])
    parts = [swapped(both, m) for m in range(EXPANDERS)]
    grad_value = run_value_back(me, own_v, returned_v, rows, parts, others, gids)
    mine, *away = run_key_back(
        me, own_k, returned_k, rows, parts, others, gids, w_query, w_key, w_value, grad_query, grad_value
    )
    for k, term in enumerate(away, 1):
        mine = mine + lax.ppermute(term, "feat", [(i, (i + k) % 4) for i in range(4)]).astype(F32)
    return (attended, mine.astype(BF16))


def solution(mesh):
    return jax.shard_map(
        on_device,
        mesh=mesh,
        in_specs=(
            P("dom", None),
            P(None, "feat"),
            P(None, "feat"),
            P(None, "feat"),
            P("dom", "feat"),
            P("dom", None, None),
            P(None, "dom"),
            P("dom", None),
            P(None, "dom"),
            P(),
        ),
        out_specs=(P("dom", "feat"), P("dom", "feat")),
        check_vma=False,
    )
```

```python
import math

import jax
import jax.numpy as jnp
from jax import lax
from jax.experimental import pallas as pl
from jax.experimental.pallas import tpu as pltpu
from jax.sharding import PartitionSpec as P

HEAD = 64
BLOCK = 128
EXPANDERS = 4
COLS = 128
NODES_HERE = 1024
Q_BLOCKS = NODES_HERE // BLOCK
SENDERS = 32
GLOBAL_BLOCK = Q_BLOCKS + SENDERS
EMPTY_BLOCK = GLOBAL_BLOCK + 1
KEY_BLOCKS = EMPTY_BLOCK + 1
GROUP = 8
PAIR = 4
LIST = 56
EXTRA = 16
SLOTS = BLOCK + EXTRA
NEG = -1e30
F32 = jnp.float32
BF16 = jnp.bfloat16


def params():
    return pltpu.CompilerParams(vmem_limit_bytes=56 * 1024 * 1024)


def vmem():
    return pl.BlockSpec(memory_space=pltpu.VMEM)


def smem():
    return pl.BlockSpec(memory_space=pltpu.SMEM)


def iota(shape, dim):
    return lax.broadcasted_iota(jnp.int32, shape, dim)


def dot(a, b):
    return jnp.dot(a, b, preferred_element_type=F32)


def dot_nt(a, b):
    return lax.dot_general(a, b, (((1,), (1,)), ((), ())), preferred_element_type=F32)


def split_index(index):
    return (index & (BLOCK - 1)).astype(F32).astype(BF16), (index >> 7).astype(F32).astype(BF16)


def packed_iota(dim):
    return iota((BLOCK, BLOCK), dim).astype(F32).astype(BF16)


def one_hot_columns(column):
    low, high = split_index(column)
    lanes = jnp.concatenate([packed_iota(1)] * (column.shape[0] // BLOCK), axis=0)
    one, zero = jnp.ones((), BF16), jnp.zeros((), BF16)
    base = jnp.where(low == lanes, one, zero)
    return jnp.concatenate(
        [jnp.where(high == jnp.asarray(c, BF16), base, zero) for c in range(NODES_HERE // BLOCK)], axis=1
    )


def one_hot_of_rows(index_rows):
    columns = [jnp.broadcast_to(row, (BLOCK, BLOCK)).T for row in index_rows]
    return one_hot_columns(jnp.concatenate(columns, axis=0))


def owner_ranks(gid_row):
    owner = jnp.broadcast_to(gid_row >> 10, (BLOCK, BLOCK))
    owner_t = owner.T
    same = owner == owner_t
    subs, lanes = iota((BLOCK, BLOCK), 0), iota((BLOCK, BLOCK), 1)
    row = jnp.sum(jnp.where(jnp.logical_and(same, subs < lanes), 1.0, 0.0), axis=0, keepdims=True)
    col = jnp.sum(jnp.where(jnp.logical_and(same, lanes < subs), 1.0, 0.0), axis=1, keepdims=True)
    row, col = row.astype(jnp.int32), jnp.broadcast_to(col, (BLOCK, BLOCK)).astype(jnp.int32)
    slot_row = jnp.where(row < EXTRA, (gid_row >> 10) * EXTRA + row, -1)
    slot_col = jnp.where(col < EXTRA, owner_t * EXTRA + col, -1)
    return row, slot_row, slot_col


def mine_columns(gid_row, me):
    row, _, _ = owner_ranks(gid_row)
    mine = (gid_row >> 10) == me
    slots = iota((EXTRA, BLOCK), 0)
    hit = jnp.logical_and(jnp.broadcast_to(mine, (EXTRA, BLOCK)), slots == row)
    local = jnp.broadcast_to(gid_row & (NODES_HERE - 1), (EXTRA, BLOCK)) + 1
    return jnp.sum(jnp.where(hit, local, 0).astype(F32), axis=1, keepdims=True).astype(jnp.int32) - 1


def exp_row(exp_ref, m, i):
    return exp_ref[m : m + 1, i * BLOCK : (i + 1) * BLOCK]


def project_kernel(
    me_ref, x_ref, wq_ref, wk_ref, wv_ref, cot_ref, rows_ref, exp_ref, gid_ref, q_ref, kv_ref, outk_ref, outv_ref, away_ref
):
    x = x_ref[...]
    kv_ref[:, :COLS] = dot(x, wk_ref[...]).astype(BF16)
    kv_ref[:, COLS:] = dot(x, wv_ref[...]).astype(BF16)
    query = (dot(x, wq_ref[...]).astype(BF16).astype(F32) * (1.0 / math.sqrt(HEAD))).astype(BF16)
    q_ref[...] = query
    away_ref[:NODES_HERE, :COLS] = query
    away_ref[:NODES_HERE, COLS:] = cot_ref[...]
    for m in range(EXPANDERS):
        low, high = split_index(jnp.concatenate([exp_row(exp_ref, m, i) for i in range(Q_BLOCKS)], axis=0))
        away_ref[NODES_HERE + m * Q_BLOCKS : NODES_HERE + (m + 1) * Q_BLOCKS, :COLS] = low
        away_ref[NODES_HERE + m * Q_BLOCKS : NODES_HERE + (m + 1) * Q_BLOCKS, COLS:] = high
    mine = jnp.broadcast_to(mine_columns(gid_ref[...], me_ref[0]), (EXTRA, BLOCK))
    lanes = iota((EXTRA, NODES_HERE), 1)
    hot = (jnp.concatenate([mine] * (NODES_HERE // BLOCK), axis=1) == lanes).astype(F32).astype(BF16)
    extra = dot(hot, kv_ref[...]).astype(BF16)

    def gather(t, carry):
        hot = one_hot_of_rows([rows_ref[pl.ds(t * GROUP + u, 1), :] for u in range(GROUP)])
        got = dot(hot, kv_ref[...]).astype(BF16)
        for u in range(GROUP):
            outk_ref[t * GROUP + u, :BLOCK] = got[u * BLOCK : (u + 1) * BLOCK, :COLS]
            outv_ref[t * GROUP + u, :BLOCK] = got[u * BLOCK : (u + 1) * BLOCK, COLS:]
            outk_ref[t * GROUP + u, BLOCK:] = extra[:, :COLS]
            outv_ref[t * GROUP + u, BLOCK:] = extra[:, COLS:]
        return carry

    lax.fori_loop(0, SENDERS // GROUP, gather, 0)


def partner_kernel(exp_ref, t0_ref, t1_ref, t2_ref, t3_ref, out_ref):
    for m, table in enumerate((t0_ref, t1_ref, t2_ref, t3_ref)):
        for t in range(0, Q_BLOCKS, 4):
            hot = one_hot_of_rows([exp_row(exp_ref, m, t + u) for u in range(4)])
            got = dot(hot, table[...]).astype(BF16)
            for u in range(4):
                out_ref[m * Q_BLOCKS + t + u] = got[u * BLOCK : (u + 1) * BLOCK]


def plan_kernel(mask_ref, count_ref, list_ref, groups_ref, live_ref):
    for j in range(Q_BLOCKS):
        live_ref[j] = BLOCK
    live_ref[GLOBAL_BLOCK] = BLOCK
    live_ref[EMPTY_BLOCK] = 0

    def copy_count(s, carry):
        live_ref[Q_BLOCKS + s] = count_ref[s]
        return carry

    lax.fori_loop(0, SENDERS, copy_count, 0)

    def per_block(i, carry):
        list_ref[i * LIST] = GLOBAL_BLOCK

        def put(j, n):
            list_ref[i * LIST + n] = j
            used = jnp.logical_and(mask_ref[i * GLOBAL_BLOCK + j] > 0, live_ref[j] > 0)
            return n + used.astype(jnp.int32)

        n = lax.fori_loop(0, GLOBAL_BLOCK, put, 1)
        for extra in range(GROUP):
            list_ref[i * LIST + n + extra] = EMPTY_BLOCK
        groups_ref[i] = (n + GROUP - 1) // GROUP
        return carry

    lax.fori_loop(0, Q_BLOCKS, per_block, 0)


def fill(dst, own_ref, first_col, halo_ref, gid_ref, glob_ref, transposed=False):
    def turn(x):
        return x.T if transposed else x

    def own(j, carry):
        dst[j] = turn(own_ref[q_rows(j), first_col : first_col + COLS])
        return carry

    def halo(j, carry):
        dst[Q_BLOCKS + j] = turn(halo_ref[j, :BLOCK])
        return carry

    lax.fori_loop(0, Q_BLOCKS, own, 0, unroll=4)
    lax.fori_loop(0, SENDERS, halo, 0, unroll=4)
    slot_col = owner_ranks(gid_ref[...])[2]
    wide = jnp.concatenate([slot_col] * (SENDERS * EXTRA // BLOCK), axis=1)
    hot = (wide == iota((BLOCK, SENDERS * EXTRA), 1)).astype(F32).astype(BF16)
    extra = jnp.concatenate([halo_ref[s, BLOCK:] for s in range(SENDERS)], axis=0)
    rows = dot(hot, extra) + glob_ref[:, first_col : first_col + COLS].astype(F32)
    dst[GLOBAL_BLOCK] = turn(rows.astype(BF16))
    dst[EMPTY_BLOCK] = jnp.zeros((BLOCK, COLS), BF16)


def stacked(rows):
    lanes = iota((BLOCK, COLS), 1)
    zero = jnp.zeros_like(rows)
    return jnp.concatenate([jnp.where(lanes < HEAD, rows, zero), jnp.where(lanes < HEAD, zero, rows)], axis=0)


def stacked_t(rows):
    turned = rows.T
    subs = iota((COLS, BLOCK), 0)
    zero = jnp.zeros_like(turned)
    return jnp.concatenate([jnp.where(subs < HEAD, turned, zero), jnp.where(subs < HEAD, zero, turned)], axis=1)


def partner_rows(rows, pair_ref, i, first_col):
    total = jnp.zeros((16, BLOCK), F32)
    row_id = iota((16, COLS), 0)
    lane = iota((16, COLS), 1)
    for m in range(EXPANDERS):
        other = pair_ref[m * Q_BLOCKS + i][:, first_col : first_col + COLS]
        prod = rows.astype(F32) * other.astype(F32)
        high = prod.astype(BF16)
        low = (prod - high.astype(F32)).astype(BF16)
        picks = (row_id == jnp.where(lane < HEAD, m, 8 + m)).astype(F32).astype(BF16)
        total = total + dot_nt(picks, high) + dot_nt(picks, low)
    return jnp.concatenate([total[:8], total[8:]], axis=1)


def tall(weights):
    return jnp.concatenate([weights[:, :BLOCK], weights[:, BLOCK:]], axis=0)


def spread(tall_weights):
    turned = tall_weights.T.astype(BF16)
    row_id = iota((16, EXPANDERS * COLS), 0)
    col = iota((16, EXPANDERS * COLS), 1)
    picks = (row_id == (col // COLS) + jnp.where(col % COLS < HEAD, 0, 8)).astype(F32).astype(BF16)
    return dot(turned, picks)


def head_rows(turned):
    return jnp.concatenate([turned[:HEAD, :BLOCK], turned[HEAD:, BLOCK:]], axis=0)


def masked_scores(blocks, k_s, turned_q, live_ref):
    keys = jnp.concatenate([k_s[b] for b in blocks], axis=0)
    scores = dot(keys, turned_q)
    row_id = iota((BLOCK, 2 * BLOCK), 0)
    return jnp.concatenate(
        [
            jnp.where(row_id < live_ref[b], scores[u * BLOCK : (u + 1) * BLOCK], NEG)
            for u, b in enumerate(blocks)
        ],
        axis=0,
    )


def score_rows(rows, pair_ref, i):
    partner = partner_rows(rows, pair_ref, i, 0)
    return jnp.where(iota((8, 2 * BLOCK), 0) < EXPANDERS, partner, NEG)


def block_ids(list_ref, i, g):
    return [list_ref[i * LIST + g * GROUP + u] for u in range(GROUP)]


def q_rows(i):
    return pl.ds(pl.multiple_of(i * BLOCK, BLOCK), BLOCK)


def score_kernel(list_ref, groups_ref, live_ref, q_ref, kv_ref, hk_ref, gid_ref, glob_ref, lse_ref, k_s):
    fill(k_s, kv_ref, 0, hk_ref, gid_ref, glob_ref)

    def per_block(i, carry):
        turned_q = stacked_t(q_ref[q_rows(i), :])

        def step(g, state):
            blocks = block_ids(list_ref, i, g)
            new_state = []
            for u in range(GROUP // PAIR):
                top, total = state[u]
                scores = masked_scores(blocks[u * PAIR : (u + 1) * PAIR], k_s, turned_q, live_ref)
                scores = scores.reshape(PAIR * BLOCK // 8, 8, 2 * BLOCK)
                new_top = jnp.maximum(top, jnp.max(scores, axis=0))
                total = total * jnp.exp(top - new_top) + jnp.sum(jnp.exp(scores - new_top[None]), axis=0)
                new_state.append((new_top, total))
            return tuple(new_state)

        init = (jnp.full((8, 2 * BLOCK), NEG, F32), jnp.zeros((8, 2 * BLOCK), F32))
        state = lax.fori_loop(0, groups_ref[i], step, tuple(init for _ in range(GROUP // PAIR)))
        top = jnp.concatenate([t for t, _ in state], axis=0)
        total = jnp.concatenate([t for _, t in state], axis=0)
        best = jnp.max(top, axis=0, keepdims=True)
        denominator = jnp.sum(total * jnp.exp(top - best), axis=0, keepdims=True)
        lse_ref[pl.ds(i, 1), :] = best + jnp.log(denominator)
        return carry

    lax.fori_loop(0, Q_BLOCKS, per_block, 0)


def clear_blocks(acc_s):
    def clear(j, carry):
        acc_s[j] = jnp.zeros((BLOCK, COLS), F32)
        return carry

    lax.fori_loop(0, KEY_BLOCKS, clear, 0)


def value_kernel(
    list_ref, groups_ref, live_ref, q_ref, kv_ref, hk_ref, hv_ref, gid_ref, glob_ref, pair_ref, cot_ref, part_ref,
    att_ref, own_ref, halo_ref, gout_ref, wp_ref, pdp_ref, delta_ref, lse_ref, k_s, vt_s, acc_s, out_s,
):
    fill(k_s, kv_ref, 0, hk_ref, gid_ref, glob_ref)
    fill(vt_s, kv_ref, COLS, hv_ref, gid_ref, glob_ref, transposed=True)
    clear_blocks(acc_s)

    def per_block(i, carry):
        rows = q_ref[q_rows(i), :]
        turned_q = stacked_t(rows)
        cot = cot_ref[q_rows(i), :]
        cot_stack = stacked(cot)
        partner = score_rows(rows, pair_ref, i)
        part = part_ref[pl.ds(i, 1), :]
        best = jnp.maximum(part, jnp.max(partner, axis=0, keepdims=True))
        lse = best + jnp.log(jnp.exp(part - best) + jnp.sum(jnp.exp(partner - best), axis=0, keepdims=True))
        lse_ref[pl.ds(i, 1), :] = lse
        out_s[...] = jnp.zeros((COLS, 2 * BLOCK), F32)

        def step(g, carry):
            blocks = block_ids(list_ref, i, g)
            total = None
            for u in range(0, GROUP, PAIR):
                pair = blocks[u : u + PAIR]
                scores = masked_scores(pair, k_s, turned_q, live_ref)
                weight = jnp.exp(scores - lse).astype(BF16)
                term = dot(jnp.concatenate([vt_s[b] for b in pair], axis=1), weight)
                total = term if total is None else total + term
                grads = dot(weight, cot_stack)
                for w, b in enumerate(pair):
                    acc_s[b] += grads[w * BLOCK : (w + 1) * BLOCK]
            out_s[...] += total
            return carry

        lax.fori_loop(0, groups_ref[i], step, 0)
        dprob = partner_rows(cot, pair_ref, i, COLS)
        prob = jnp.exp(partner - lse)
        weight = prob.astype(BF16).astype(F32)
        wide = spread(tall(weight))
        wp_ref[i] = tall(weight).astype(BF16)
        attended_t = head_rows(out_s[...])
        prod = attended_t * cot.T.astype(F32)
        delta = jnp.concatenate(
            [jnp.sum(prod[:HEAD], axis=0, keepdims=True), jnp.sum(prod[HEAD:], axis=0, keepdims=True)], axis=1
        )
        delta = delta + jnp.sum(prob * dprob, axis=0, keepdims=True)
        delta_ref[pl.ds(i, 1), :] = delta
        pdp_ref[i] = prob * (dprob - delta)
        attended = attended_t.T
        for m in range(EXPANDERS):
            attended += wide[:, m * COLS : (m + 1) * COLS] * pair_ref[m * Q_BLOCKS + i][:, COLS:].astype(F32)
        att_ref[q_rows(i), :] = attended.astype(BF16)
        return carry

    lax.fori_loop(0, Q_BLOCKS, per_block, 0)
    store_parts(acc_s, own_ref, halo_ref, gid_ref, gout_ref)


def store_parts(acc_s, own_ref, halo_ref, gid_ref, gout_ref):
    def own(j, carry):
        own_ref[q_rows(j), :] = acc_s[j]
        return carry

    def halo(j, carry):
        halo_ref[j, :BLOCK] = acc_s[Q_BLOCKS + j].astype(BF16)
        return carry

    lax.fori_loop(0, Q_BLOCKS, own, 0, unroll=2)
    lax.fori_loop(0, SENDERS, halo, 0, unroll=4)
    grads = acc_s[GLOBAL_BLOCK].astype(BF16)
    gout_ref[...] = grads
    slot_row = owner_ranks(gid_ref[...])[1]
    hot = (iota((SENDERS * EXTRA, BLOCK), 0) == slot_row).astype(F32).astype(BF16)
    extra = dot(hot, grads).astype(BF16)
    for s in range(SENDERS):
        halo_ref[s, BLOCK:] = extra[s * EXTRA : (s + 1) * EXTRA]


def key_kernel(
    list_ref, groups_ref, live_ref, q_ref, kv_ref, hk_ref, hv_ref, gid_ref, glob_ref, pair_ref, cot_ref, lse_ref,
    pdp_ref, delta_ref, gq_ref, own_ref, halo_ref, gout_ref, dsp_ref, k_s, v_s, kt_s, acc_s, out_s,
):
    fill(k_s, kv_ref, 0, hk_ref, gid_ref, glob_ref)
    fill(v_s, kv_ref, COLS, hv_ref, gid_ref, glob_ref)
    fill(kt_s, kv_ref, 0, hk_ref, gid_ref, glob_ref, transposed=True)
    clear_blocks(acc_s)

    def per_block(i, carry):
        rows = q_ref[q_rows(i), :]
        turned_q = stacked_t(rows)
        q_stack = stacked(rows)
        turned_cot = stacked_t(cot_ref[q_rows(i), :])
        lse = lse_ref[pl.ds(i, 1), :]
        delta = delta_ref[pl.ds(i, 1), :]
        out_s[...] = jnp.zeros((COLS, 2 * BLOCK), F32)

        def step(g, carry):
            blocks = block_ids(list_ref, i, g)
            total = None
            for u in range(0, GROUP, PAIR):
                pair = blocks[u : u + PAIR]
                scores = masked_scores(pair, k_s, turned_q, live_ref)
                dprob = dot(jnp.concatenate([v_s[b] for b in pair], axis=0), turned_cot)
                dscore = (jnp.exp(scores - lse) * (dprob - delta)).astype(BF16)
                term = dot(jnp.concatenate([kt_s[b] for b in pair], axis=1), dscore)
                total = term if total is None else total + term
                grads = dot(dscore, q_stack)
                for w, b in enumerate(pair):
                    acc_s[b] += grads[w * BLOCK : (w + 1) * BLOCK]
            out_s[...] += total
            return carry

        lax.fori_loop(0, groups_ref[i], step, 0)
        partner = tall(pdp_ref[i].astype(BF16).astype(F32))
        dsp_ref[i] = partner.astype(BF16)
        wide = spread(partner)
        grad_query = head_rows(out_s[...]).T
        for m in range(EXPANDERS):
            grad_query += wide[:, m * COLS : (m + 1) * COLS] * pair_ref[m * Q_BLOCKS + i][:, :COLS].astype(F32)
        gq_ref[q_rows(i), :] = (grad_query * (1.0 / math.sqrt(HEAD))).astype(BF16)
        return carry

    lax.fori_loop(0, Q_BLOCKS, per_block, 0)
    store_parts(acc_s, own_ref, halo_ref, gid_ref, gout_ref)


def scatter_into(acc_s, splits, data):
    subs = packed_iota(0)
    one, zero = jnp.ones((), BF16), jnp.zeros((), BF16)
    bases = [(jnp.where(subs == low, one, zero), jnp.broadcast_to(high, (BLOCK, BLOCK))) for low, high in splits]
    for c in range(NODES_HERE // BLOCK):
        hot = jnp.concatenate([jnp.where(high == jnp.asarray(c, BF16), base, zero) for base, high in bases], axis=1)
        acc_s[c * BLOCK : (c + 1) * BLOCK, :] += dot(hot, data)


def gather_grads(me_ref, own_ref, ret_ref, rows_ref, parts, others, first_col, gid_ref, acc_s):
    acc_s[...] = own_ref[...]

    def halo(t, carry):
        splits = [split_index(rows_ref[pl.ds(t * GROUP + u, 1), :]) for u in range(GROUP)]
        data = jnp.concatenate([ret_ref[t * GROUP + u, :BLOCK] for u in range(GROUP)], axis=0)
        scatter_into(acc_s, splits, data)
        return carry

    lax.fori_loop(0, SENDERS // GROUP, halo, 0)
    row_id = iota((16, COLS), 0)
    lane = iota((16, COLS), 1)
    for m, (part, other) in enumerate(zip(parts, others)):
        picks = (row_id == jnp.where(lane < HEAD, m, 8 + m)).astype(F32).astype(BF16)
        index_low = other[NODES_HERE + m * Q_BLOCKS : NODES_HERE + (m + 1) * Q_BLOCKS, :COLS]
        index_high = other[NODES_HERE + m * Q_BLOCKS : NODES_HERE + (m + 1) * Q_BLOCKS, COLS:]
        for t in range(Q_BLOCKS // GROUP):
            splits, data = [], []
            for u in range(GROUP):
                i = t * GROUP + u
                splits.append((index_low[i : i + 1], index_high[i : i + 1]))
                wide = dot(part[i].astype(F32).T.astype(BF16), picks)
                rows = other[i * BLOCK : (i + 1) * BLOCK, first_col : first_col + COLS].astype(F32)
                data.append((wide * rows).astype(BF16))
            scatter_into(acc_s, splits, jnp.concatenate(data, axis=0))
    extra = ret_ref[0, BLOCK:].astype(F32)
    for s in range(1, SENDERS):
        extra += ret_ref[s, BLOCK:].astype(F32)
    high = extra.astype(BF16)
    data = jnp.concatenate([high, (extra - high.astype(F32)).astype(BF16)], axis=0)
    mine = jnp.broadcast_to(mine_columns(gid_ref[...], me_ref[0]), (EXTRA, NODES_HERE))
    hot = (mine == iota((EXTRA, NODES_HERE), 1)).astype(F32)
    hot = jnp.concatenate([hot, hot], axis=0).T.astype(BF16)
    acc_s[...] += dot(hot, data)


def value_back_kernel(
    me_ref, own_ref, ret_ref, rows_ref, p0_ref, p1_ref, p2_ref, p3_ref, o0_ref, o1_ref, o2_ref, o3_ref, gid_ref,
    grad_ref, acc_s,
):
    parts, others = (p0_ref, p1_ref, p2_ref, p3_ref), (o0_ref, o1_ref, o2_ref, o3_ref)
    gather_grads(me_ref, own_ref, ret_ref, rows_ref, parts, others, COLS, gid_ref, acc_s)
    grad_ref[...] = acc_s[...].astype(BF16)


def key_back_kernel(
    me_ref, feat_ref, own_ref, ret_ref, rows_ref, p0_ref, p1_ref, p2_ref, p3_ref, o0_ref, o1_ref, o2_ref, o3_ref, gid_ref,
    wq_ref, wk_ref, wv_ref, gq_ref, gv_ref, t0_ref, t1_ref, t2_ref, t3_ref, acc_s,
):
    parts, others = (p0_ref, p1_ref, p2_ref, p3_ref), (o0_ref, o1_ref, o2_ref, o3_ref)
    gather_grads(me_ref, own_ref, ret_ref, rows_ref, parts, others, 0, gid_ref, acc_s)
    grad_key = acc_s[...].astype(BF16)
    for k, out in enumerate((t0_ref, t1_ref, t2_ref, t3_ref)):
        part = pl.ds(pl.multiple_of(((feat_ref[0] + k) % 4) * COLS, COLS), COLS)
        term = dot_nt(gq_ref[...], wq_ref[part, :]) + dot_nt(gv_ref[...], wv_ref[part, :])
        term = term + dot_nt(grad_key, wk_ref[part, :])
        out[...] = term.astype(out.dtype)


def shape(dims, kind=BF16):
    return jax.ShapeDtypeStruct(dims, kind)


def call(kernel, ins, outs, args, scratch=(), name=None, flops=0, out_spaces=None):
    cost = pl.CostEstimate(flops=flops, transcendentals=0, bytes_accessed=4_000_000)
    return pl.pallas_call(
        kernel,
        out_shape=outs,
        in_specs=ins,
        out_specs=out_spaces or tuple(vmem() for _ in outs),
        scratch_shapes=list(scratch),
        compiler_params=params(),
        cost_estimate=cost,
        name=name,
    )(*args)


def blocks_of(kind):
    return pltpu.VMEM((KEY_BLOCKS, BLOCK, COLS), kind)


def run_project(me, features, w_query, w_key, w_value, cotangent, rows, exp_list, gids):
    return call(
        project_kernel,
        [smem()] + [vmem()] * 8,
        (
            shape((NODES_HERE, COLS)),
            shape((NODES_HERE, 2 * COLS)),
            shape((SENDERS, SLOTS, COLS)),
            shape((SENDERS, SLOTS, COLS)),
            shape((NODES_HERE + EXPANDERS * Q_BLOCKS, 2 * COLS)),
        ),
        (me, features, w_query, w_key, w_value, cotangent, rows, exp_list, gids),
        name="project",
        flops=3_000_000_000,
    )


def run_plan(block_mask, halo_count):
    return call(
        plan_kernel,
        [smem()] * 2,
        (shape((Q_BLOCKS * LIST,), jnp.int32), shape((Q_BLOCKS,), jnp.int32), shape((LIST,), jnp.int32)),
        (block_mask.reshape(-1), halo_count.reshape(-1)),
        name="plan",
        out_spaces=(smem(), smem(), smem()),
    )


def run_partners(exp_list, swaps):
    return call(
        partner_kernel,
        [vmem()] * 5,
        (shape((EXPANDERS * Q_BLOCKS, BLOCK, 2 * COLS)),),
        (exp_list, *swaps),
        name="partners",
        flops=5_000_000_000,
    )[0]


def run_scores(plan, query, paired, halo_k, gids, glob):
    return call(
        score_kernel,
        [smem()] * 3 + [vmem()] * 5,
        (shape((Q_BLOCKS, 2 * BLOCK), F32),),
        (*plan, query, paired, halo_k, gids, glob),
        scratch=[blocks_of(BF16)],
        name="scores",
        flops=12_000_000_000,
    )[0]


def run_values(plan, query, paired, halo_k, halo_v, gids, glob, pairs, cotangent, part):
    return call(
        value_kernel,
        [smem()] * 3 + [vmem()] * 9,
        (
            shape((NODES_HERE, COLS)),
            shape((NODES_HERE, COLS), F32),
            shape((SENDERS, SLOTS, COLS)),
            shape((BLOCK, COLS)),
            shape((Q_BLOCKS, 16, BLOCK)),
            shape((Q_BLOCKS, 8, 2 * BLOCK), F32),
            shape((Q_BLOCKS, 2 * BLOCK), F32),
            shape((Q_BLOCKS, 2 * BLOCK), F32),
        ),
        (*plan, query, paired, halo_k, halo_v, gids, glob, pairs, cotangent, part),
        scratch=[blocks_of(BF16), blocks_of(BF16), blocks_of(F32), pltpu.VMEM((COLS, 2 * BLOCK), F32)],
        name="values",
        flops=20_000_000_000,
    )


def run_keys(plan, query, paired, halo_k, halo_v, gids, glob, pairs, cotangent, lse, pdp, delta):
    return call(
        key_kernel,
        [smem()] * 3 + [vmem()] * 11,
        (
            shape((NODES_HERE, COLS)),
            shape((NODES_HERE, COLS), F32),
            shape((SENDERS, SLOTS, COLS)),
            shape((BLOCK, COLS)),
            shape((Q_BLOCKS, 16, BLOCK)),
        ),
        (*plan, query, paired, halo_k, halo_v, gids, glob, pairs, cotangent, lse, pdp, delta),
        scratch=[blocks_of(BF16), blocks_of(BF16), blocks_of(BF16), blocks_of(F32), pltpu.VMEM((COLS, 2 * BLOCK), F32)],
        name="keys",
        flops=25_000_000_000,
    )


def run_value_back(me, own_v, returned_v, rows, parts, others, gids):
    return call(
        value_back_kernel,
        [smem()] + [vmem()] * 12,
        (shape((NODES_HERE, COLS)),),
        (me, own_v, returned_v, rows, *parts, *others, gids),
        scratch=[pltpu.VMEM((NODES_HERE, COLS), F32)],
        name="value_back",
        flops=8_000_000_000,
    )[0]


def run_key_back(me, feat, own_k, returned_k, rows, parts, others, gids, w_query, w_key, w_value, grad_query, grad_value):
    return call(
        key_back_kernel,
        [smem()] * 2 + [vmem()] * 17,
        (shape((NODES_HERE, COLS), F32),) + tuple(shape((NODES_HERE, COLS)) for _ in range(3)),
        (me, feat, own_k, returned_k, rows, *parts, *others, gids, w_query, w_key, w_value, grad_query, grad_value),
        scratch=[pltpu.VMEM((NODES_HERE, COLS), F32)],
        name="key_back",
        flops=8_000_000_000,
    )


def more_rounds(global_ids):
    owned = (global_ids[None, :] // NODES_HERE == jnp.arange(SENDERS)[:, None]).sum(1)
    return (owned.max() + EXTRA - 1) // EXTRA


def ranks(global_ids):
    owner = global_ids // NODES_HERE
    ids = jnp.arange(BLOCK)
    return owner, ((owner[:, None] == owner[None, :]) & (ids[None, :] < ids[:, None])).sum(1)


def more_globals(rounds, global_ids, my_index, paired):
    def body(state):
        r, glob = state
        owner, rank = ranks(global_ids)
        slot = rank - r * EXTRA
        here = (slot >= 0) & (slot < EXTRA)
        place = jnp.where((owner == my_index) & here, slot, EXTRA)
        rows = jnp.zeros((EXTRA + 1, paired.shape[1]), BF16).at[place].set(paired[jnp.where(here, global_ids % NODES_HERE, 0)])[:EXTRA]
        got = lax.all_to_all(jnp.broadcast_to(rows[None], (SENDERS, *rows.shape)), "dom", 0, 0, tiled=True)
        found = got.reshape(SENDERS * EXTRA, -1)[jnp.clip(owner * EXTRA + slot, 0, SENDERS * EXTRA - 1)]
        return r + 1, jnp.where(here[:, None], found, glob)

    start = (jnp.asarray(1, jnp.int32), jnp.zeros((BLOCK, paired.shape[1]), BF16))
    return lax.while_loop(lambda state: state[0] < rounds, body, start)[1]


def more_grads(rounds, global_ids, my_index, part_k, part_v, own_k, own_v):
    def body(state):
        r, own_k, own_v = state
        owner, rank = ranks(global_ids)
        slot = rank - r * EXTRA
        here = (slot >= 0) & (slot < EXTRA)
        part = jnp.concatenate([part_k, part_v], axis=1)
        place = jnp.where(here, owner * EXTRA + slot, SENDERS * EXTRA)
        rows = jnp.zeros((SENDERS * EXTRA + 1, part.shape[1]), BF16).at[place].set(part)[: SENDERS * EXTRA]
        got = lax.all_to_all(rows.reshape(SENDERS, EXTRA, -1), "dom", 0, 0, tiled=True).astype(F32).sum(0)
        take = (owner == my_index) & here
        add = jnp.where(take[:, None], got[jnp.clip(slot, 0, EXTRA - 1)], 0.0)
        local = global_ids % NODES_HERE
        return r + 1, own_k.at[local].add(add[:, :COLS]), own_v.at[local].add(add[:, COLS:])

    start = (jnp.asarray(1, jnp.int32), own_k, own_v)
    return lax.while_loop(lambda state: state[0] < rounds, body, start)[1:]


def on_device(
    features,
    w_query,
    w_key,
    w_value,
    cotangent,
    send_rows,
    halo_count,
    block_mask,
    exp_rows,
    global_ids,
):
    dom_count = lax.axis_size("dom")
    my_index = lax.axis_index("dom")

    def swapped(value, bit):
        return lax.ppermute(value, "dom", [(i, i ^ (1 << bit)) for i in range(dom_count)])

    rows = send_rows[0]
    gids = global_ids.reshape(1, BLOCK)
    me = my_index.reshape(1).astype(jnp.int32)
    feat = lax.axis_index("feat").reshape(1).astype(jnp.int32)

    query, paired, out_k, out_v, away = run_project(
        me, features, w_query, w_key, w_value, cotangent, rows, exp_rows, gids
    )
    rounds = more_rounds(global_ids)
    glob = more_globals(rounds, global_ids, my_index, paired)
    out_k, out_v, glob = lax.optimization_barrier((out_k, out_v, glob))
    halo_k = lax.all_to_all(out_k, "dom", 0, 0, tiled=True)
    swaps = [swapped(paired, m) for m in range(EXPANDERS)]
    plan = run_plan(block_mask, halo_count)
    halo_v = lax.all_to_all(out_v, "dom", 0, 0, tiled=True)
    part = run_scores(plan, query, paired, halo_k, gids, glob)
    away, part, *swaps = lax.optimization_barrier((away, part, *swaps))
    pairs = run_partners(exp_rows, swaps)
    others = [swapped(away, m) for m in range(EXPANDERS)]
    attended, own_v, back_v, glob_v, weight_p, pdp, delta, lse = run_values(
        plan, query, paired, halo_k, halo_v, gids, glob, pairs, cotangent, part
    )
    *others, lse = lax.optimization_barrier((*others, lse))
    parts_v = [swapped(weight_p, m) for m in range(EXPANDERS)]
    returned_v = lax.all_to_all(back_v, "dom", 0, 0, tiled=True)
    grad_query, own_k, back_k, glob_k, dscore_p = run_keys(
        plan, query, paired, halo_k, halo_v, gids, glob, pairs, cotangent, lse, pdp, delta
    )
    own_k, returned_v = lax.optimization_barrier((own_k, returned_v))
    own_k, own_v = more_grads(rounds, global_ids, my_index, glob_k, glob_v, own_k, own_v)
    back_k, own_k, own_v = lax.optimization_barrier((back_k, own_k, own_v))
    returned_k = lax.all_to_all(back_k, "dom", 0, 0, tiled=True)
    parts_k = [swapped(dscore_p, m) for m in range(EXPANDERS)]
    grad_value = run_value_back(me, own_v, returned_v, rows, parts_v, others, gids)
    mine, *away = run_key_back(
        me, feat, own_k, returned_k, rows, parts_k, others, gids, w_query, w_key, w_value, grad_query, grad_value
    )
    for k, term in enumerate(away, 1):
        mine = mine + lax.ppermute(term, "feat", [(i, (i + k) % 4) for i in range(4)]).astype(F32)
    return (attended, mine.astype(BF16))


def solution(mesh):
    return jax.shard_map(
        on_device,
        mesh=mesh,
        in_specs=(
            P("dom", None),
            P(None, "feat"),
            P(None, "feat"),
            P(None, "feat"),
            P("dom", "feat"),
            P("dom", None, None),
            P(None, "dom"),
            P("dom", None),
            P(None, "dom"),
            P(),
        ),
        out_specs=(P("dom", "feat"), P("dom", "feat")),
        check_vma=False,
    )
```

```python
import math

import jax
import jax.numpy as jnp
from jax import lax
from jax.experimental import pallas as pl
from jax.experimental.pallas import tpu as pltpu
from jax.sharding import PartitionSpec as P

HEAD = 64
BLOCK = 128
EXPANDERS = 4
COLS = 128
NODES_HERE = 1024
Q_BLOCKS = NODES_HERE // BLOCK
SENDERS = 32
GLOBAL_BLOCK = Q_BLOCKS + SENDERS
EMPTY_BLOCK = GLOBAL_BLOCK + 1
KEY_BLOCKS = EMPTY_BLOCK + 1
GROUP = 8
PAIR = 4
LIST = 56
EXTRA = 16
SLOTS = BLOCK + EXTRA
NEG = -1e30
F32 = jnp.float32
BF16 = jnp.bfloat16


def params():
    return pltpu.CompilerParams(vmem_limit_bytes=56 * 1024 * 1024)


def vmem():
    return pl.BlockSpec(memory_space=pltpu.VMEM)


def smem():
    return pl.BlockSpec(memory_space=pltpu.SMEM)


def iota(shape, dim):
    return lax.broadcasted_iota(jnp.int32, shape, dim)


def dot(a, b):
    return jnp.dot(a, b, preferred_element_type=F32)


def dot_nt(a, b):
    return lax.dot_general(a, b, (((1,), (1,)), ((), ())), preferred_element_type=F32)


def split_index(index):
    return (index & (BLOCK - 1)).astype(F32).astype(BF16), (index >> 7).astype(F32).astype(BF16)


def packed_iota(dim):
    return iota((BLOCK, BLOCK), dim).astype(F32).astype(BF16)


def one_hot_columns(column):
    low, high = split_index(column)
    lanes = jnp.concatenate([packed_iota(1)] * (column.shape[0] // BLOCK), axis=0)
    one, zero = jnp.ones((), BF16), jnp.zeros((), BF16)
    base = jnp.where(low == lanes, one, zero)
    return jnp.concatenate(
        [jnp.where(high == jnp.asarray(c, BF16), base, zero) for c in range(NODES_HERE // BLOCK)], axis=1
    )


def one_hot_of_rows(index_rows):
    columns = [jnp.broadcast_to(row, (BLOCK, BLOCK)).T for row in index_rows]
    return one_hot_columns(jnp.concatenate(columns, axis=0))


def owner_ranks(gid_row):
    owner = jnp.broadcast_to(gid_row >> 10, (BLOCK, BLOCK))
    owner_t = owner.T
    same = owner == owner_t
    subs, lanes = iota((BLOCK, BLOCK), 0), iota((BLOCK, BLOCK), 1)
    row = jnp.sum(jnp.where(jnp.logical_and(same, subs < lanes), 1.0, 0.0), axis=0, keepdims=True)
    col = jnp.sum(jnp.where(jnp.logical_and(same, lanes < subs), 1.0, 0.0), axis=1, keepdims=True)
    row, col = row.astype(jnp.int32), jnp.broadcast_to(col, (BLOCK, BLOCK)).astype(jnp.int32)
    slot_row = jnp.where(row < EXTRA, (gid_row >> 10) * EXTRA + row, -1)
    slot_col = jnp.where(col < EXTRA, owner_t * EXTRA + col, -1)
    return row, slot_row, slot_col


def mine_columns(gid_row, me):
    row, _, _ = owner_ranks(gid_row)
    mine = (gid_row >> 10) == me
    slots = iota((EXTRA, BLOCK), 0)
    hit = jnp.logical_and(jnp.broadcast_to(mine, (EXTRA, BLOCK)), slots == row)
    local = jnp.broadcast_to(gid_row & (NODES_HERE - 1), (EXTRA, BLOCK)) + 1
    return jnp.sum(jnp.where(hit, local, 0).astype(F32), axis=1, keepdims=True).astype(jnp.int32) - 1


def exp_row(exp_ref, m, i):
    return exp_ref[m : m + 1, i * BLOCK : (i + 1) * BLOCK]


def project_kernel(
    me_ref, x_ref, wq_ref, wk_ref, wv_ref, cot_ref, rows_ref, exp_ref, gid_ref, q_ref, kv_ref, outk_ref, outv_ref, away_ref,
    rounds_ref,
):
    most = jnp.max(owner_ranks(gid_ref[...])[0].astype(F32)).astype(jnp.int32)
    rounds_ref[0] = (most + EXTRA) // EXTRA
    x = x_ref[...]
    kv_ref[:, :COLS] = dot(x, wk_ref[...]).astype(BF16)
    kv_ref[:, COLS:] = dot(x, wv_ref[...]).astype(BF16)
    query = (dot(x, wq_ref[...]).astype(BF16).astype(F32) * (1.0 / math.sqrt(HEAD))).astype(BF16)
    q_ref[...] = query
    away_ref[:NODES_HERE, :COLS] = query
    away_ref[:NODES_HERE, COLS:] = cot_ref[...]
    for m in range(EXPANDERS):
        low, high = split_index(jnp.concatenate([exp_row(exp_ref, m, i) for i in range(Q_BLOCKS)], axis=0))
        away_ref[NODES_HERE + m * Q_BLOCKS : NODES_HERE + (m + 1) * Q_BLOCKS, :COLS] = low
        away_ref[NODES_HERE + m * Q_BLOCKS : NODES_HERE + (m + 1) * Q_BLOCKS, COLS:] = high
    mine = jnp.broadcast_to(mine_columns(gid_ref[...], me_ref[0]), (EXTRA, BLOCK))
    lanes = iota((EXTRA, NODES_HERE), 1)
    hot = (jnp.concatenate([mine] * (NODES_HERE // BLOCK), axis=1) == lanes).astype(F32).astype(BF16)
    extra = dot(hot, kv_ref[...]).astype(BF16)

    def gather(t, carry):
        hot = one_hot_of_rows([rows_ref[pl.ds(t * GROUP + u, 1), :] for u in range(GROUP)])
        got = dot(hot, kv_ref[...]).astype(BF16)
        for u in range(GROUP):
            outk_ref[t * GROUP + u, :BLOCK] = got[u * BLOCK : (u + 1) * BLOCK, :COLS]
            outv_ref[t * GROUP + u, :BLOCK] = got[u * BLOCK : (u + 1) * BLOCK, COLS:]
            outk_ref[t * GROUP + u, BLOCK:] = extra[:, :COLS]
            outv_ref[t * GROUP + u, BLOCK:] = extra[:, COLS:]
        return carry

    lax.fori_loop(0, SENDERS // GROUP, gather, 0)


def partner_kernel(m, exp_ref, table, q_ref, cot_ref, out_ref, sp_ref, dp_ref):
    sums = [jnp.zeros((16, BLOCK), F32), jnp.zeros((16, BLOCK), F32)]
    for t in range(0, Q_BLOCKS, 4):
        hot = one_hot_of_rows([exp_row(exp_ref, m, t + u) for u in range(4)])
        got = dot(hot, table[...]).astype(BF16)
        for u in range(4):
            i = t + u
            pair = got[u * BLOCK : (u + 1) * BLOCK]
            out_ref[i] = pair
            here = slice(i * BLOCK, (i + 1) * BLOCK)
            sums[0] += head_sums(q_ref[here, :], pair[:, :COLS], i)
            sums[1] += head_sums(cot_ref[here, :], pair[:, COLS:], i)
    sp_ref[...] = flat(sums[0])
    dp_ref[...] = flat(sums[1])


def head_picks(i):
    return (iota((16, COLS), 0) == jnp.where(iota((16, COLS), 1) < HEAD, i, 8 + i)).astype(F32).astype(BF16)


def head_sums(a, b, i):
    prod = a.astype(F32) * b.astype(F32)
    high = prod.astype(BF16)
    low = (prod - high.astype(F32)).astype(BF16)
    return dot_nt(head_picks(i), high) + dot_nt(head_picks(i), low)


def flat(x):
    return jnp.concatenate([x[:8], x[8:]], axis=1)


def tall(x):
    return jnp.concatenate([x[:, :BLOCK], x[:, BLOCK:]], axis=0)


def turned_weights(tall_rows):
    return tall_rows.astype(F32).T.astype(BF16)


def prepare_kernel(q_ref, cot_ref, qt_ref, qs_ref, ct_ref, cs_ref):
    def one(i, carry):
        q = q_ref[q_rows(i), :]
        cot = cot_ref[q_rows(i), :]
        qt_ref[i] = stacked_t(q)
        qs_ref[i] = stacked(q)
        ct_ref[i] = stacked_t(cot)
        cs_ref[i] = stacked(cot)
        return carry

    lax.fori_loop(0, Q_BLOCKS, one, 0, unroll=2)


def plan_kernel(mask_ref, count_ref, list_ref, groups_ref, live_ref):
    for j in range(Q_BLOCKS):
        live_ref[j] = BLOCK
    live_ref[GLOBAL_BLOCK] = BLOCK
    live_ref[EMPTY_BLOCK] = 0

    def copy_count(s, carry):
        live_ref[Q_BLOCKS + s] = count_ref[s]
        return carry

    lax.fori_loop(0, SENDERS, copy_count, 0)

    def per_block(i, carry):
        list_ref[i * LIST] = GLOBAL_BLOCK

        def put(j, n):
            list_ref[i * LIST + n] = j
            used = jnp.logical_and(mask_ref[i * GLOBAL_BLOCK + j] > 0, live_ref[j] > 0)
            return n + used.astype(jnp.int32)

        n = lax.fori_loop(0, GLOBAL_BLOCK, put, 1)
        for extra in range(GROUP):
            list_ref[i * LIST + n + extra] = EMPTY_BLOCK
        groups_ref[i] = (n + GROUP - 1) // GROUP
        return carry

    lax.fori_loop(0, Q_BLOCKS, per_block, 0)


def fill(dst, dst_t, own_ref, first_col, halo_ref, gid_ref, glob_ref):
    def own(j, carry):
        block = own_ref[q_rows(j), first_col : first_col + COLS]
        dst[j] = block
        dst_t[j] = block.T
        return carry

    def halo(j, carry):
        block = halo_ref[j, :BLOCK]
        dst[Q_BLOCKS + j] = block
        dst_t[Q_BLOCKS + j] = block.T
        return carry

    lax.fori_loop(0, Q_BLOCKS, own, 0, unroll=4)
    lax.fori_loop(0, SENDERS, halo, 0, unroll=4)
    slot_col = owner_ranks(gid_ref[...])[2]
    wide = jnp.concatenate([slot_col] * (SENDERS * EXTRA // BLOCK), axis=1)
    hot = (wide == iota((BLOCK, SENDERS * EXTRA), 1)).astype(F32).astype(BF16)
    extra = jnp.concatenate([halo_ref[s, BLOCK:] for s in range(SENDERS)], axis=0)
    rows = (dot(hot, extra) + glob_ref[:, first_col : first_col + COLS].astype(F32)).astype(BF16)
    dst[GLOBAL_BLOCK] = rows
    dst_t[GLOBAL_BLOCK] = rows.T
    dst[EMPTY_BLOCK] = jnp.zeros((BLOCK, COLS), BF16)
    dst_t[EMPTY_BLOCK] = jnp.zeros((BLOCK, COLS), BF16)


def turn_kernel(kv_ref, hv_ref, gid_ref, glob_ref, v_ref, vt_ref):
    fill(v_ref, vt_ref, kv_ref, COLS, hv_ref, gid_ref, glob_ref)


def stacked(rows):
    lanes = iota((BLOCK, COLS), 1)
    zero = jnp.zeros_like(rows)
    return jnp.concatenate([jnp.where(lanes < HEAD, rows, zero), jnp.where(lanes < HEAD, zero, rows)], axis=0)


def stacked_t(rows):
    turned = rows.T
    subs = iota((COLS, BLOCK), 0)
    zero = jnp.zeros_like(turned)
    return jnp.concatenate([jnp.where(subs < HEAD, turned, zero), jnp.where(subs < HEAD, zero, turned)], axis=1)


def head_rows(turned):
    return jnp.concatenate([turned[:HEAD, :BLOCK], turned[HEAD:, BLOCK:]], axis=0)


def masked_scores(blocks, k_s, turned_q, live_ref):
    keys = jnp.concatenate([k_s[b] for b in blocks], axis=0)
    scores = dot(keys, turned_q)
    row_id = iota((BLOCK, 2 * BLOCK), 0)
    return jnp.concatenate(
        [
            jnp.where(row_id < live_ref[b], scores[u * BLOCK : (u + 1) * BLOCK], NEG)
            for u, b in enumerate(blocks)
        ],
        axis=0,
    )


def block_ids(list_ref, i, g):
    return [list_ref[i * LIST + g * GROUP + u] for u in range(GROUP)]


def q_rows(i):
    return pl.ds(pl.multiple_of(i * BLOCK, BLOCK), BLOCK)


def score_kernel(
    list_ref, groups_ref, live_ref, qt_ref, kv_ref, hk_ref, gid_ref, glob_ref, lse_ref, k_s, kt_ref
):
    fill(k_s, kt_ref, kv_ref, 0, hk_ref, gid_ref, glob_ref)

    def per_block(i, carry):
        turned_q = qt_ref[i]

        def step(g, state):
            blocks = block_ids(list_ref, i, g)
            new_state = []
            for u in range(GROUP // PAIR):
                top, total = state[u]
                scores = masked_scores(blocks[u * PAIR : (u + 1) * PAIR], k_s, turned_q, live_ref)
                scores = scores.reshape(PAIR * BLOCK // 8, 8, 2 * BLOCK)
                new_top = jnp.maximum(top, jnp.max(scores, axis=0))
                total = total * jnp.exp(top - new_top) + jnp.sum(jnp.exp(scores - new_top[None]), axis=0)
                new_state.append((new_top, total))
            return tuple(new_state)

        init = (jnp.full((8, 2 * BLOCK), NEG, F32), jnp.zeros((8, 2 * BLOCK), F32))
        state = lax.fori_loop(0, groups_ref[i], step, tuple(init for _ in range(GROUP // PAIR)))
        top = jnp.concatenate([t for t, _ in state], axis=0)
        total = jnp.concatenate([t for _, t in state], axis=0)
        best = jnp.max(top, axis=0, keepdims=True)
        denominator = jnp.sum(total * jnp.exp(top - best), axis=0, keepdims=True)
        lse_ref[pl.ds(i, 1), :] = best + jnp.log(denominator)
        return carry

    lax.fori_loop(0, Q_BLOCKS, per_block, 0)


def clear_blocks(acc_s):
    def clear(j, carry):
        acc_s[j] = jnp.zeros((BLOCK, COLS), F32)
        return carry

    lax.fori_loop(0, KEY_BLOCKS, clear, 0)


def value_kernel(
    list_ref, groups_ref, live_ref, k_s, vt_s, qt_ref, ct_ref, cs_ref, part_ref, sp_ref, dp_ref,
    p0_ref, p1_ref, p2_ref, p3_ref, gid_ref,
    att_ref, own_ref, halo_ref, gout_ref, back_ref, delta_ref, lse_ref, acc_s, out_s,
):
    clear_blocks(acc_s)
    part = part_ref[...]
    best = part
    for m in range(EXPANDERS):
        best = jnp.maximum(best, sp_ref[m])
    total = jnp.exp(part - best)
    for m in range(EXPANDERS):
        total += jnp.exp(sp_ref[m] - best)
    lse_ref[...] = best + jnp.log(total)

    def per_block(i, carry):
        turned_q = qt_ref[i]
        cot_stack = cs_ref[i]
        lse = lse_ref[pl.ds(i, 1), :]
        out_s[i] = jnp.zeros((COLS, 2 * BLOCK), F32)

        def step(g, carry):
            blocks = block_ids(list_ref, i, g)
            total = None
            for u in range(0, GROUP, PAIR):
                pair = blocks[u : u + PAIR]
                scores = masked_scores(pair, k_s, turned_q, live_ref)
                weight = jnp.exp(scores - lse).astype(BF16)
                term = dot(jnp.concatenate([vt_s[b] for b in pair], axis=1), weight)
                total = term if total is None else total + term
                grads = dot(weight, cot_stack)
                for w, b in enumerate(pair):
                    acc_s[b] += grads[w * BLOCK : (w + 1) * BLOCK]
            out_s[i] += total
            return carry

        lax.fori_loop(0, groups_ref[i], step, 0)
        delta_ref[pl.ds(i, 1), :] = jnp.sum(out_s[i] * ct_ref[i].astype(F32), axis=0, keepdims=True)
        return carry

    lax.fori_loop(0, Q_BLOCKS, per_block, 0)
    lse = lse_ref[...]
    probs = [jnp.exp(sp_ref[m] - lse) for m in range(EXPANDERS)]
    delta = delta_ref[...]
    for m in range(EXPANDERS):
        delta += probs[m] * dp_ref[m]
    delta_ref[...] = delta
    turned = []
    for m in range(EXPANDERS):
        weight = tall(probs[m]).astype(BF16)
        turned.append(turned_weights(weight))
        back_ref[m, 0] = tall(probs[m] * (dp_ref[m] - delta)).astype(BF16)
        back_ref[m, 1] = weight
    for i in range(Q_BLOCKS):
        attended = head_rows(out_s[i]).T
        for m, pair_ref in enumerate((p0_ref, p1_ref, p2_ref, p3_ref)):
            attended += dot(turned[m], head_picks(i)) * pair_ref[i][:, COLS:].astype(F32)
        att_ref[i * BLOCK : (i + 1) * BLOCK, :] = attended.astype(BF16)
    store_parts(acc_s, own_ref, halo_ref, gid_ref, gout_ref)


def clear_blocks(acc_s):
    def clear(j, carry):
        acc_s[j] = jnp.zeros((BLOCK, COLS), F32)
        return carry

    lax.fori_loop(0, KEY_BLOCKS, clear, 0, unroll=2)


def store_parts(acc_s, own_ref, halo_ref, gid_ref, gout_ref):
    def own(j, carry):
        own_ref[q_rows(j), :] = acc_s[j]
        return carry

    def halo(j, carry):
        halo_ref[j, :BLOCK] = acc_s[Q_BLOCKS + j].astype(BF16)
        return carry

    lax.fori_loop(0, Q_BLOCKS, own, 0, unroll=2)
    lax.fori_loop(0, SENDERS, halo, 0, unroll=4)
    grads = acc_s[GLOBAL_BLOCK].astype(BF16)
    gout_ref[...] = grads
    slot_row = owner_ranks(gid_ref[...])[1]
    hot = (iota((SENDERS * EXTRA, BLOCK), 0) == slot_row).astype(F32).astype(BF16)
    extra = dot(hot, grads).astype(BF16)
    for s in range(SENDERS):
        halo_ref[s, BLOCK:] = extra[s * EXTRA : (s + 1) * EXTRA]


def key_kernel(
    list_ref, groups_ref, live_ref, k_s, kt_s, v_s, qt_ref, qs_ref, ct_ref, lse_ref, delta_ref, back_ref,
    p0_ref, p1_ref, p2_ref, p3_ref, gid_ref,
    gq_ref, own_ref, halo_ref, gout_ref, acc_s, out_s,
):
    clear_blocks(acc_s)

    def per_block(i, carry):
        turned_q = qt_ref[i]
        q_stack = qs_ref[i]
        turned_cot = ct_ref[i]
        lse = lse_ref[pl.ds(i, 1), :]
        delta = delta_ref[pl.ds(i, 1), :]
        out_s[i] = jnp.zeros((COLS, 2 * BLOCK), F32)

        def step(g, carry):
            blocks = block_ids(list_ref, i, g)
            total = None
            for u in range(0, GROUP, PAIR):
                pair = blocks[u : u + PAIR]
                scores = masked_scores(pair, k_s, turned_q, live_ref)
                dprob = dot(jnp.concatenate([v_s[b] for b in pair], axis=0), turned_cot)
                dscore = (jnp.exp(scores - lse) * (dprob - delta)).astype(BF16)
                term = dot(jnp.concatenate([kt_s[b] for b in pair], axis=1), dscore)
                total = term if total is None else total + term
                grads = dot(dscore, q_stack)
                for w, b in enumerate(pair):
                    acc_s[b] += grads[w * BLOCK : (w + 1) * BLOCK]
            out_s[i] += total
            return carry

        lax.fori_loop(0, groups_ref[i], step, 0)
        return carry

    lax.fori_loop(0, Q_BLOCKS, per_block, 0)
    turned = [turned_weights(back_ref[m, 0]) for m in range(EXPANDERS)]
    for i in range(Q_BLOCKS):
        grad_query = head_rows(out_s[i]).T
        for m, pair_ref in enumerate((p0_ref, p1_ref, p2_ref, p3_ref)):
            grad_query += dot(turned[m], head_picks(i)) * pair_ref[i][:, :COLS].astype(F32)
        gq_ref[i * BLOCK : (i + 1) * BLOCK, :] = (grad_query * (1.0 / math.sqrt(HEAD))).astype(BF16)
    store_parts(acc_s, own_ref, halo_ref, gid_ref, gout_ref)


def scatter_into(acc_s, splits, data):
    subs = packed_iota(0)
    one, zero = jnp.ones((), BF16), jnp.zeros((), BF16)
    bases = [(jnp.where(subs == low, one, zero), jnp.broadcast_to(high, (BLOCK, BLOCK))) for low, high in splits]
    for c in range(NODES_HERE // BLOCK):
        hot = jnp.concatenate([jnp.where(high == jnp.asarray(c, BF16), base, zero) for base, high in bases], axis=1)
        acc_s[c * BLOCK : (c + 1) * BLOCK, :] += dot(hot, data)


def gather_grads(me_ref, own_ref, ret_ref, rows_ref, parts, others, first_col, gid_ref, acc_s):
    acc_s[...] = own_ref[...]

    def halo(t, carry):
        splits = [split_index(rows_ref[pl.ds(t * GROUP + u, 1), :]) for u in range(GROUP)]
        data = jnp.concatenate([ret_ref[t * GROUP + u, :BLOCK] for u in range(GROUP)], axis=0)
        scatter_into(acc_s, splits, data)
        return carry

    lax.fori_loop(0, SENDERS // GROUP, halo, 0)
    for m, (part, other) in enumerate(zip(parts, others)):
        turned = turned_weights(part[1 if first_col else 0])
        index_low = other[NODES_HERE + m * Q_BLOCKS : NODES_HERE + (m + 1) * Q_BLOCKS, :COLS]
        index_high = other[NODES_HERE + m * Q_BLOCKS : NODES_HERE + (m + 1) * Q_BLOCKS, COLS:]
        for t in range(Q_BLOCKS // GROUP):
            splits, data = [], []
            for u in range(GROUP):
                i = t * GROUP + u
                splits.append((index_low[i : i + 1], index_high[i : i + 1]))
                wide = dot(turned, head_picks(i))
                rows = other[i * BLOCK : (i + 1) * BLOCK, first_col : first_col + COLS].astype(F32)
                data.append((wide * rows).astype(BF16))
            scatter_into(acc_s, splits, jnp.concatenate(data, axis=0))
    extra = ret_ref[0, BLOCK:].astype(F32)
    for s in range(1, SENDERS):
        extra += ret_ref[s, BLOCK:].astype(F32)
    high = extra.astype(BF16)
    data = jnp.concatenate([high, (extra - high.astype(F32)).astype(BF16)], axis=0)
    mine = jnp.broadcast_to(mine_columns(gid_ref[...], me_ref[0]), (EXTRA, NODES_HERE))
    hot = (mine == iota((EXTRA, NODES_HERE), 1)).astype(F32)
    hot = jnp.concatenate([hot, hot], axis=0).T.astype(BF16)
    acc_s[...] += dot(hot, data)


def value_back_kernel(
    me_ref, own_ref, ret_ref, rows_ref, p0_ref, p1_ref, p2_ref, p3_ref, o0_ref, o1_ref, o2_ref, o3_ref, gid_ref,
    grad_ref, acc_s,
):
    parts, others = (p0_ref, p1_ref, p2_ref, p3_ref), (o0_ref, o1_ref, o2_ref, o3_ref)
    gather_grads(me_ref, own_ref, ret_ref, rows_ref, parts, others, COLS, gid_ref, acc_s)
    grad_ref[...] = acc_s[...].astype(BF16)


def key_back_kernel(
    me_ref, feat_ref, own_ref, ret_ref, rows_ref, p0_ref, p1_ref, p2_ref, p3_ref, o0_ref, o1_ref, o2_ref, o3_ref, gid_ref,
    wq_ref, wk_ref, wv_ref, gq_ref, gv_ref, t0_ref, t1_ref, t2_ref, t3_ref, acc_s,
):
    parts, others = (p0_ref, p1_ref, p2_ref, p3_ref), (o0_ref, o1_ref, o2_ref, o3_ref)
    gather_grads(me_ref, own_ref, ret_ref, rows_ref, parts, others, 0, gid_ref, acc_s)
    grad_key = acc_s[...].astype(BF16)
    for k, out in enumerate((t0_ref, t1_ref, t2_ref, t3_ref)):
        part = pl.ds(pl.multiple_of(((feat_ref[0] + k) % 4) * COLS, COLS), COLS)
        term = dot_nt(gq_ref[...], wq_ref[part, :]) + dot_nt(gv_ref[...], wv_ref[part, :])
        term = term + dot_nt(grad_key, wk_ref[part, :])
        out[...] = term.astype(out.dtype)


def shape(dims, kind=BF16):
    return jax.ShapeDtypeStruct(dims, kind)


def call(kernel, ins, outs, args, scratch=(), name=None, flops=0, out_spaces=None):
    cost = pl.CostEstimate(flops=flops, transcendentals=0, bytes_accessed=4_000_000)
    return pl.pallas_call(
        kernel,
        out_shape=outs,
        in_specs=ins,
        out_specs=out_spaces or tuple(vmem() for _ in outs),
        scratch_shapes=list(scratch),
        compiler_params=params(),
        cost_estimate=cost,
        name=name,
    )(*args)


def blocks_of(kind):
    return pltpu.VMEM((KEY_BLOCKS, BLOCK, COLS), kind)


def run_project(me, features, w_query, w_key, w_value, cotangent, rows, exp_list, gids):
    return call(
        project_kernel,
        [smem()] + [vmem()] * 8,
        (
            shape((NODES_HERE, COLS)),
            shape((NODES_HERE, 2 * COLS)),
            shape((SENDERS, SLOTS, COLS)),
            shape((SENDERS, SLOTS, COLS)),
            shape((NODES_HERE + EXPANDERS * Q_BLOCKS, 2 * COLS)),
            shape((1,), jnp.int32),
        ),
        (me, features, w_query, w_key, w_value, cotangent, rows, exp_list, gids),
        name="project",
        flops=3_000_000_000,
        out_spaces=(*(vmem() for _ in range(5)), smem()),
    )


def run_plan(block_mask, halo_count):
    return call(
        plan_kernel,
        [smem()] * 2,
        (shape((Q_BLOCKS * LIST,), jnp.int32), shape((Q_BLOCKS,), jnp.int32), shape((LIST,), jnp.int32)),
        (block_mask.reshape(-1), halo_count.reshape(-1)),
        name="plan",
        out_spaces=(smem(), smem(), smem()),
    )


def run_partner(m, exp_rows, swap, query, cotangent):
    return call(
        lambda *refs: partner_kernel(m, *refs),
        [vmem()] * 4,
        (
            shape((Q_BLOCKS, BLOCK, 2 * COLS)),
            shape((Q_BLOCKS, 2 * BLOCK), F32),
            shape((Q_BLOCKS, 2 * BLOCK), F32),
        ),
        (exp_rows, swap, query, cotangent),
        name="partner%d" % m,
        flops=1_500_000_000,
    )


def run_prepare(query, cotangent):
    wide, high = shape((Q_BLOCKS, COLS, 2 * BLOCK)), shape((Q_BLOCKS, 2 * BLOCK, COLS))
    return call(
        prepare_kernel, [vmem()] * 2, (wide, high, wide, high), (query, cotangent), name="prepare", flops=2_000_000_000
    )


def run_scores(plan, turned_q, paired, halo_k, gids, glob):
    return call(
        score_kernel,
        [smem()] * 3 + [vmem()] * 5,
        (
            shape((Q_BLOCKS, 2 * BLOCK), F32),
            shape((KEY_BLOCKS, BLOCK, COLS)),
            shape((KEY_BLOCKS, COLS, BLOCK)),
        ),
        (*plan, turned_q, paired, halo_k, gids, glob),
        name="scores",
        flops=12_000_000_000,
    )


def run_turn(paired, halo_v, gids, glob):
    return call(
        turn_kernel,
        [vmem()] * 4,
        (shape((KEY_BLOCKS, BLOCK, COLS)), shape((KEY_BLOCKS, COLS, BLOCK))),
        (paired, halo_v, gids, glob),
        name="turn",
        flops=2_000_000_000,
    )


def run_values(plan, keys, turned_v, prepared, part, scores, dprobs, pairs, gids):
    turned_q, _, turned_cot, cot_stack = prepared
    return call(
        value_kernel,
        [smem()] * 3 + [vmem()] * 13,
        (
            shape((NODES_HERE, COLS)),
            shape((NODES_HERE, COLS), F32),
            shape((SENDERS, SLOTS, COLS)),
            shape((BLOCK, COLS)),
            shape((EXPANDERS, 2, 16, BLOCK)),
            shape((Q_BLOCKS, 2 * BLOCK), F32),
            shape((Q_BLOCKS, 2 * BLOCK), F32),
        ),
        (*plan, keys, turned_v, turned_q, turned_cot, cot_stack, part, scores, dprobs, *pairs, gids),
        scratch=[blocks_of(F32), pltpu.VMEM((Q_BLOCKS, COLS, 2 * BLOCK), F32)],
        name="values",
        flops=20_000_000_000,
    )


def run_keys(plan, keys, turned_k, values, prepared, lse, delta, back, pairs, gids):
    turned_q, q_stack, turned_cot, _ = prepared
    return call(
        key_kernel,
        [smem()] * 3 + [vmem()] * 14,
        (
            shape((NODES_HERE, COLS)),
            shape((NODES_HERE, COLS), F32),
            shape((SENDERS, SLOTS, COLS)),
            shape((BLOCK, COLS)),
        ),
        (*plan, keys, turned_k, values, turned_q, q_stack, turned_cot, lse, delta, back, *pairs, gids),
        scratch=[blocks_of(F32), pltpu.VMEM((Q_BLOCKS, COLS, 2 * BLOCK), F32)],
        name="keys",
        flops=25_000_000_000,
    )


def run_value_back(me, own_v, returned_v, rows, parts, others, gids):
    return call(
        value_back_kernel,
        [smem()] + [vmem()] * 12,
        (shape((NODES_HERE, COLS)),),
        (me, own_v, returned_v, rows, *parts, *others, gids),
        scratch=[pltpu.VMEM((NODES_HERE, COLS), F32)],
        name="value_back",
        flops=8_000_000_000,
    )[0]


def run_key_back(me, feat, own_k, returned_k, rows, parts, others, gids, w_query, w_key, w_value, grad_query, grad_value):
    return call(
        key_back_kernel,
        [smem()] * 2 + [vmem()] * 17,
        (shape((NODES_HERE, COLS), F32),) + tuple(shape((NODES_HERE, COLS)) for _ in range(3)),
        (me, feat, own_k, returned_k, rows, *parts, *others, gids, w_query, w_key, w_value, grad_query, grad_value),
        scratch=[pltpu.VMEM((NODES_HERE, COLS), F32)],
        name="key_back",
        flops=8_000_000_000,
    )


def ranks(global_ids):
    owner = global_ids // NODES_HERE
    ids = jnp.arange(BLOCK)
    return owner, ((owner[:, None] == owner[None, :]) & (ids[None, :] < ids[:, None])).sum(1)


def more_globals(rounds, global_ids, my_index, paired):
    def body(state):
        r, glob = state
        owner, rank = ranks(global_ids)
        slot = rank - r * EXTRA
        here = (slot >= 0) & (slot < EXTRA)
        place = jnp.where((owner == my_index) & here, slot, EXTRA)
        rows = jnp.zeros((EXTRA + 1, paired.shape[1]), BF16).at[place].set(paired[jnp.where(here, global_ids % NODES_HERE, 0)])[:EXTRA]
        got = lax.all_to_all(jnp.broadcast_to(rows[None], (SENDERS, *rows.shape)), "dom", 0, 0, tiled=True)
        found = got.reshape(SENDERS * EXTRA, -1)[jnp.clip(owner * EXTRA + slot, 0, SENDERS * EXTRA - 1)]
        return r + 1, jnp.where(here[:, None], found, glob)

    start = (jnp.asarray(1, jnp.int32), jnp.zeros((BLOCK, paired.shape[1]), BF16))
    return lax.while_loop(lambda state: state[0] < rounds, body, start)[1]


def more_grads(rounds, global_ids, my_index, part_k, part_v, own_k, own_v):
    def body(state):
        r, own_k, own_v = state
        owner, rank = ranks(global_ids)
        slot = rank - r * EXTRA
        here = (slot >= 0) & (slot < EXTRA)
        part = jnp.concatenate([part_k, part_v], axis=1)
        place = jnp.where(here, owner * EXTRA + slot, SENDERS * EXTRA)
        rows = jnp.zeros((SENDERS * EXTRA + 1, part.shape[1]), BF16).at[place].set(part)[: SENDERS * EXTRA]
        got = lax.all_to_all(rows.reshape(SENDERS, EXTRA, -1), "dom", 0, 0, tiled=True).astype(F32).sum(0)
        take = (owner == my_index) & here
        add = jnp.where(take[:, None], got[jnp.clip(slot, 0, EXTRA - 1)], 0.0)
        local = global_ids % NODES_HERE
        return r + 1, own_k.at[local].add(add[:, :COLS]), own_v.at[local].add(add[:, COLS:])

    start = (jnp.asarray(1, jnp.int32), own_k, own_v)
    return lax.while_loop(lambda state: state[0] < rounds, body, start)[1:]


def on_device(
    features,
    w_query,
    w_key,
    w_value,
    cotangent,
    send_rows,
    halo_count,
    block_mask,
    exp_rows,
    global_ids,
):
    dom_count = lax.axis_size("dom")
    my_index = lax.axis_index("dom")

    def swapped(value, bit):
        return lax.ppermute(value, "dom", [(i, i ^ (1 << bit)) for i in range(dom_count)])

    rows = send_rows[0]
    gids = global_ids.reshape(1, BLOCK)
    me = my_index.reshape(1).astype(jnp.int32)
    feat = lax.axis_index("feat").reshape(1).astype(jnp.int32)

    query, paired, out_k, out_v, away, rounds = run_project(
        me, features, w_query, w_key, w_value, cotangent, rows, exp_rows, gids
    )
    rounds = rounds[0]
    glob = more_globals(rounds, global_ids, my_index, paired)
    out_k, out_v, glob = lax.optimization_barrier((out_k, out_v, glob))
    halo_k = lax.all_to_all(out_k, "dom", 0, 0, tiled=True)
    swaps = [swapped(paired, m) for m in range(EXPANDERS)]
    plan = run_plan(block_mask, halo_count)
    prepared = run_prepare(query, cotangent)
    halo_v = lax.all_to_all(out_v, "dom", 0, 0, tiled=True)
    part, keys, turned_k = run_scores(plan, prepared[0], paired, halo_k, gids, glob)
    away, part, *swaps = lax.optimization_barrier((away, part, *swaps))
    joined = {m: run_partner(m, exp_rows, swaps[m], query, cotangent) for m in (0, 1, 3)}
    values, turned_v = run_turn(paired, halo_v, gids, glob)
    swaps[2], values, joined = lax.optimization_barrier((swaps[2], values, joined))
    joined[2] = run_partner(2, exp_rows, swaps[2], query, cotangent)
    pairs, scores, dprobs = zip(*[joined[m] for m in range(EXPANDERS)])
    others = [swapped(away, m) for m in range(EXPANDERS)]
    attended, own_v, back_v, glob_v, back, delta, lse = run_values(
        plan, keys, turned_v, prepared, part, jnp.stack(scores), jnp.stack(dprobs), pairs, gids
    )
    *others, lse = lax.optimization_barrier((*others, lse))
    parts = [swapped(back[m], m) for m in range(EXPANDERS)]
    returned_v = lax.all_to_all(back_v, "dom", 0, 0, tiled=True)
    grad_query, own_k, back_k, glob_k = run_keys(
        plan, keys, turned_k, values, prepared, lse, delta, back, pairs, gids
    )
    own_k, returned_v, *parts = lax.optimization_barrier((own_k, returned_v, *parts))
    own_k, own_v = more_grads(rounds, global_ids, my_index, glob_k, glob_v, own_k, own_v)
    back_k, own_k, own_v = lax.optimization_barrier((back_k, own_k, own_v))
    returned_k = lax.all_to_all(back_k, "dom", 0, 0, tiled=True)
    grad_value = run_value_back(me, own_v, returned_v, rows, parts, others, gids)
    mine, *away = run_key_back(
        me, feat, own_k, returned_k, rows, parts, others, gids, w_query, w_key, w_value, grad_query, grad_value
    )
    for k, term in enumerate(away, 1):
        mine = mine + lax.ppermute(term, "feat", [(i, (i + k) % 4) for i in range(4)]).astype(F32)
    return (attended, mine.astype(BF16))


def solution(mesh):
    return jax.shard_map(
        on_device,
        mesh=mesh,
        in_specs=(
            P("dom", None),
            P(None, "feat"),
            P(None, "feat"),
            P(None, "feat"),
            P("dom", "feat"),
            P("dom", None, None),
            P(None, "dom"),
            P("dom", None),
            P(None, "dom"),
            P(),
        ),
        out_specs=(P("dom", "feat"), P("dom", "feat")),
        check_vma=False,
    )
```

```python
import math

import jax
import jax.numpy as jnp
from jax import lax
from jax.experimental import pallas as pl
from jax.experimental.pallas import tpu as pltpu
from jax.sharding import PartitionSpec as P

HEAD = 64
BLOCK = 128
EXPANDERS = 4
COLS = 128
NODES_HERE = 1024
Q_BLOCKS = NODES_HERE // BLOCK
SENDERS = 32
GLOBAL_BLOCK = Q_BLOCKS + SENDERS
EMPTY_BLOCK = GLOBAL_BLOCK + 1
KEY_BLOCKS = EMPTY_BLOCK + 1
GROUP = 8
PAIR = 4
LIST = 56
EXTRA = 16
SLOTS = BLOCK + EXTRA
PART_ROWS = 32
BACK = SLOTS + PART_ROWS
NEG = -1e30
F32 = jnp.float32
BF16 = jnp.bfloat16


def params():
    return pltpu.CompilerParams(vmem_limit_bytes=56 * 1024 * 1024)


def vmem():
    return pl.BlockSpec(memory_space=pltpu.VMEM)


def smem():
    return pl.BlockSpec(memory_space=pltpu.SMEM)


def iota(shape, dim):
    return lax.broadcasted_iota(jnp.int32, shape, dim)


def dot(a, b):
    return jnp.dot(a, b, preferred_element_type=F32)


def dot_nt(a, b):
    return lax.dot_general(a, b, (((1,), (1,)), ((), ())), preferred_element_type=F32)


def split_index(index):
    return (index & (BLOCK - 1)).astype(F32).astype(BF16), (index >> 7).astype(F32).astype(BF16)


def packed_iota(dim):
    return iota((BLOCK, BLOCK), dim).astype(F32).astype(BF16)


def one_hot_columns(column):
    low, high = split_index(column)
    lanes = jnp.concatenate([packed_iota(1)] * (column.shape[0] // BLOCK), axis=0)
    one, zero = jnp.ones((), BF16), jnp.zeros((), BF16)
    base = jnp.where(low == lanes, one, zero)
    return jnp.concatenate(
        [jnp.where(high == jnp.asarray(c, BF16), base, zero) for c in range(NODES_HERE // BLOCK)], axis=1
    )


def one_hot_of_rows(index_rows):
    columns = [jnp.broadcast_to(row, (BLOCK, BLOCK)).T for row in index_rows]
    return one_hot_columns(jnp.concatenate(columns, axis=0))


def owner_ranks(gid_row):
    owner = jnp.broadcast_to(gid_row >> 10, (BLOCK, BLOCK))
    owner_t = owner.T
    same = owner == owner_t
    subs, lanes = iota((BLOCK, BLOCK), 0), iota((BLOCK, BLOCK), 1)
    row = jnp.sum(jnp.where(jnp.logical_and(same, subs < lanes), 1.0, 0.0), axis=0, keepdims=True)
    col = jnp.sum(jnp.where(jnp.logical_and(same, lanes < subs), 1.0, 0.0), axis=1, keepdims=True)
    row, col = row.astype(jnp.int32), jnp.broadcast_to(col, (BLOCK, BLOCK)).astype(jnp.int32)
    slot_row = jnp.where(row < EXTRA, (gid_row >> 10) * EXTRA + row, -1)
    slot_col = jnp.where(col < EXTRA, owner_t * EXTRA + col, -1)
    return row, slot_row, slot_col


def mine_columns(gid_row, me):
    row, _, _ = owner_ranks(gid_row)
    mine = (gid_row >> 10) == me
    slots = iota((EXTRA, BLOCK), 0)
    hit = jnp.logical_and(jnp.broadcast_to(mine, (EXTRA, BLOCK)), slots == row)
    local = jnp.broadcast_to(gid_row & (NODES_HERE - 1), (EXTRA, BLOCK)) + 1
    return jnp.sum(jnp.where(hit, local, 0).astype(F32), axis=1, keepdims=True).astype(jnp.int32) - 1


def exp_row(exp_ref, m, i):
    return exp_ref[m : m + 1, i * BLOCK : (i + 1) * BLOCK]


def project_kernel(
    me_ref, x_ref, wq_ref, wk_ref, wv_ref, cot_ref, rows_ref, exp_ref, gid_ref, q_ref, k_ref, v_ref, outk_ref, outv_ref,
    away_ref, rounds_ref, kv_ref,
):
    most = jnp.max(owner_ranks(gid_ref[...])[0].astype(F32)).astype(jnp.int32)
    rounds_ref[0] = (most + EXTRA) // EXTRA
    x = x_ref[...]
    keys = dot(x, wk_ref[...]).astype(BF16)
    values = dot(x, wv_ref[...]).astype(BF16)
    k_ref[...] = keys
    v_ref[...] = values
    kv_ref[:, :COLS] = keys
    kv_ref[:, COLS:] = values
    query = (dot(x, wq_ref[...]).astype(BF16).astype(F32) * (1.0 / math.sqrt(HEAD))).astype(BF16)
    q_ref[...] = query
    away_ref[:NODES_HERE, :COLS] = query
    away_ref[:NODES_HERE, COLS:] = cot_ref[...]
    for m in range(EXPANDERS):
        low, high = split_index(jnp.concatenate([exp_row(exp_ref, m, i) for i in range(Q_BLOCKS)], axis=0))
        away_ref[NODES_HERE + m * Q_BLOCKS : NODES_HERE + (m + 1) * Q_BLOCKS, :COLS] = low
        away_ref[NODES_HERE + m * Q_BLOCKS : NODES_HERE + (m + 1) * Q_BLOCKS, COLS:] = high
    mine = jnp.broadcast_to(mine_columns(gid_ref[...], me_ref[0]), (EXTRA, BLOCK))
    lanes = iota((EXTRA, NODES_HERE), 1)
    hot = (jnp.concatenate([mine] * (NODES_HERE // BLOCK), axis=1) == lanes).astype(F32).astype(BF16)
    extra = dot(hot, kv_ref[...]).astype(BF16)

    def gather(t, carry):
        hot = one_hot_of_rows([rows_ref[pl.ds(t * GROUP + u, 1), :] for u in range(GROUP)])
        got = dot(hot, kv_ref[...]).astype(BF16)
        for u in range(GROUP):
            outk_ref[t * GROUP + u, :BLOCK] = got[u * BLOCK : (u + 1) * BLOCK, :COLS]
            outv_ref[t * GROUP + u, :BLOCK] = got[u * BLOCK : (u + 1) * BLOCK, COLS:]
            outk_ref[t * GROUP + u, BLOCK:] = extra[:, :COLS]
            outv_ref[t * GROUP + u, BLOCK:] = extra[:, COLS:]
        return carry

    lax.fori_loop(0, SENDERS // GROUP, gather, 0)


def gather_partner(exp_ref, m, table):
    blocks = []
    for t in range(0, Q_BLOCKS, 4):
        hot = one_hot_of_rows([exp_row(exp_ref, m, t + u) for u in range(4)])
        got = dot(hot, table[...]).astype(BF16)
        blocks += [got[u * BLOCK : (u + 1) * BLOCK] for u in range(4)]
    return blocks


def sum_picks():
    sub = iota((2 * Q_BLOCKS * COLS, 16), 0)
    col = iota((2 * Q_BLOCKS * COLS, 16), 1)
    return (col == (sub >> 8) + jnp.where((sub & (COLS - 1)) < HEAD, 0, 8)).astype(F32).astype(BF16)


def head_sums(a_ref, blocks, picks):
    parts = []
    for i, b in enumerate(blocks):
        prod = a_ref[i * BLOCK : (i + 1) * BLOCK, :].astype(F32) * b.astype(F32)
        high = prod.astype(BF16)
        parts += [high, (prod - high.astype(F32)).astype(BF16)]
    return flat(dot(jnp.concatenate(parts, axis=1), picks).T)


def partner_key_kernel(exp_ref, t0_ref, t1_ref, t2_ref, t3_ref, q_ref, out_ref, sp_ref):
    picks = sum_picks()
    for m, table in enumerate((t0_ref, t1_ref, t2_ref, t3_ref)):
        blocks = gather_partner(exp_ref, m, table)
        for i, block in enumerate(blocks):
            out_ref[m * Q_BLOCKS + i] = block
        sp_ref[m] = head_sums(q_ref, blocks, picks)


def head_picks(i):
    return (iota((16, COLS), 0) == jnp.where(iota((16, COLS), 1) < HEAD, i, 8 + i)).astype(F32).astype(BF16)


def finish_kernel(
    me_ref, exp_ref, t0_ref, t1_ref, t2_ref, t3_ref, cot_ref, out_t_ref, sp_ref, lse_ref, local_ref, _, att_ref, back_ref,
    delta_ref, message_ref, sems,
):
    picks = sum_picks()
    lse = lse_ref[...]
    delta = local_ref[...]
    totals = [head_rows(out_t_ref[i]).T for i in range(Q_BLOCKS)]
    probs, dprobs = [], []
    for m, table in enumerate((t0_ref, t1_ref, t2_ref, t3_ref)):
        blocks = gather_partner(exp_ref, m, table)
        prob = jnp.exp(sp_ref[m] - lse)
        dprob = head_sums(cot_ref, blocks, picks)
        delta += prob * dprob
        weight = tall(prob).astype(BF16)
        back_ref[m, 16:] = weight
        turned = turned_weights(weight)
        for i, block in enumerate(blocks):
            totals[i] += dot(turned, head_picks(i)) * block.astype(F32)
        probs.append(prob)
        dprobs.append(dprob)
    delta_ref[...] = delta
    for m in range(EXPANDERS):
        back_ref[m, :16] = tall(probs[m] * (dprobs[m] - delta)).astype(BF16)
    copies = [
        pltpu.make_async_copy(
            back_ref.at[m], message_ref.at[me_ref[0] ^ (1 << m), pl.ds(SLOTS, PART_ROWS)], sems.at[m]
        )
        for m in range(EXPANDERS)
    ]
    for copy in copies:
        copy.start()
    for i in range(Q_BLOCKS):
        att_ref[i * BLOCK : (i + 1) * BLOCK, :] = totals[i].astype(BF16)
    for copy in copies:
        copy.wait()


def flat(x):
    return jnp.concatenate([x[:8], x[8:]], axis=1)


def tall(x):
    return jnp.concatenate([x[:, :BLOCK], x[:, BLOCK:]], axis=0)


def turned_weights(tall_rows):
    return tall_rows.astype(F32).T.astype(BF16)


def prepare_kernel(q_ref, cot_ref, qt_ref, qs_ref, ct_ref, cs_ref):
    def one(i, carry):
        q = q_ref[q_rows(i), :]
        cot = cot_ref[q_rows(i), :]
        qt_ref[i] = stacked_t(q)
        qs_ref[i] = stacked(q)
        ct_ref[i] = stacked_t(cot)
        cs_ref[i] = stacked(cot)
        return carry

    lax.fori_loop(0, Q_BLOCKS, one, 0, unroll=2)


def plan_kernel(mask_ref, count_ref, list_ref, groups_ref, live_ref):
    for j in range(Q_BLOCKS):
        live_ref[j] = BLOCK
    live_ref[GLOBAL_BLOCK] = BLOCK
    live_ref[EMPTY_BLOCK] = 0

    def copy_count(s, carry):
        live_ref[Q_BLOCKS + s] = count_ref[s]
        return carry

    lax.fori_loop(0, SENDERS, copy_count, 0)

    def per_block(i, carry):
        list_ref[i * LIST] = GLOBAL_BLOCK

        def put(j, n):
            list_ref[i * LIST + n] = j
            used = jnp.logical_and(mask_ref[i * GLOBAL_BLOCK + j] > 0, live_ref[j] > 0)
            return n + used.astype(jnp.int32)

        n = lax.fori_loop(0, GLOBAL_BLOCK, put, 1)
        for extra in range(GROUP):
            list_ref[i * LIST + n + extra] = EMPTY_BLOCK
        groups_ref[i] = (n + GROUP - 1) // GROUP
        return carry

    lax.fori_loop(0, Q_BLOCKS, per_block, 0)


def fill(dst, dst_t, first_col, own_ref, halo_ref, gid_ref, glob_ref):
    def own(j, carry):
        block = own_ref[q_rows(j), :]
        dst[j] = block
        dst_t[j] = block.T
        return carry

    def halo(j, carry):
        block = halo_ref[j, :BLOCK]
        dst[Q_BLOCKS + j] = block
        dst_t[Q_BLOCKS + j] = block.T
        return carry

    lax.fori_loop(0, Q_BLOCKS, own, 0, unroll=4)
    lax.fori_loop(0, SENDERS, halo, 0, unroll=4)
    slot_col = owner_ranks(gid_ref[...])[2]
    wide = jnp.concatenate([slot_col] * (SENDERS * EXTRA // BLOCK), axis=1)
    hot = (wide == iota((BLOCK, SENDERS * EXTRA), 1)).astype(F32).astype(BF16)
    extra = jnp.concatenate([halo_ref[s, BLOCK:] for s in range(SENDERS)], axis=0)
    rows = (dot(hot, extra) + glob_ref[:, first_col : first_col + COLS].astype(F32)).astype(BF16)
    dst[GLOBAL_BLOCK] = rows
    dst_t[GLOBAL_BLOCK] = rows.T
    dst[EMPTY_BLOCK] = jnp.zeros((BLOCK, COLS), BF16)
    dst_t[EMPTY_BLOCK] = jnp.zeros((BLOCK, COLS), BF16)


def turn_kernel(own_ref, hv_ref, gid_ref, glob_ref, v_ref, vt_ref):
    fill(v_ref, vt_ref, COLS, own_ref, hv_ref, gid_ref, glob_ref)


def stacked(rows):
    lanes = iota((BLOCK, COLS), 1)
    zero = jnp.zeros_like(rows)
    return jnp.concatenate([jnp.where(lanes < HEAD, rows, zero), jnp.where(lanes < HEAD, zero, rows)], axis=0)


def stacked_t(rows):
    turned = rows.T
    subs = iota((COLS, BLOCK), 0)
    zero = jnp.zeros_like(turned)
    return jnp.concatenate([jnp.where(subs < HEAD, turned, zero), jnp.where(subs < HEAD, zero, turned)], axis=1)


def head_rows(turned):
    return jnp.concatenate([turned[:HEAD, :BLOCK], turned[HEAD:, BLOCK:]], axis=0)


def masked_scores(blocks, k_s, turned_q, live_ref):
    keys = jnp.concatenate([k_s[b] for b in blocks], axis=0)
    scores = dot(keys, turned_q)
    row_id = iota((BLOCK, 2 * BLOCK), 0)
    return jnp.concatenate(
        [
            jnp.where(row_id < live_ref[b], scores[u * BLOCK : (u + 1) * BLOCK], NEG)
            for u, b in enumerate(blocks)
        ],
        axis=0,
    )


def block_ids(list_ref, i, g):
    return [list_ref[i * LIST + g * GROUP + u] for u in range(GROUP)]


def q_rows(i):
    return pl.ds(pl.multiple_of(i * BLOCK, BLOCK), BLOCK)


def score_kernel(
    list_ref, groups_ref, live_ref, qt_ref, own_ref, hk_ref, gid_ref, glob_ref, lse_ref, k_s, kt_ref
):
    fill(k_s, kt_ref, 0, own_ref, hk_ref, gid_ref, glob_ref)

    def per_block(i, carry):
        turned_q = qt_ref[i]

        def step(g, state):
            blocks = block_ids(list_ref, i, g)
            new_state = []
            for u in range(GROUP // PAIR):
                top, total = state[u]
                scores = masked_scores(blocks[u * PAIR : (u + 1) * PAIR], k_s, turned_q, live_ref)
                scores = scores.reshape(PAIR * BLOCK // 8, 8, 2 * BLOCK)
                new_top = jnp.maximum(top, jnp.max(scores, axis=0))
                total = total * jnp.exp(top - new_top) + jnp.sum(jnp.exp(scores - new_top[None]), axis=0)
                new_state.append((new_top, total))
            return tuple(new_state)

        init = (jnp.full((8, 2 * BLOCK), NEG, F32), jnp.zeros((8, 2 * BLOCK), F32))
        state = lax.fori_loop(0, groups_ref[i], step, tuple(init for _ in range(GROUP // PAIR)))
        top = jnp.concatenate([t for t, _ in state], axis=0)
        total = jnp.concatenate([t for _, t in state], axis=0)
        best = jnp.max(top, axis=0, keepdims=True)
        denominator = jnp.sum(total * jnp.exp(top - best), axis=0, keepdims=True)
        lse_ref[pl.ds(i, 1), :] = best + jnp.log(denominator)
        return carry

    lax.fori_loop(0, Q_BLOCKS, per_block, 0)


def value_kernel(
    list_ref, groups_ref, live_ref, k_s, vt_s, qt_ref, ct_ref, cs_ref, part_ref, sp_ref, gid_ref,
    own_ref, halo_ref, gout_ref, out_s, delta_ref, lse_ref, acc_s,
):
    clear_blocks(acc_s)
    part = part_ref[...]
    best = part
    for m in range(EXPANDERS):
        best = jnp.maximum(best, sp_ref[m])
    total = jnp.exp(part - best)
    for m in range(EXPANDERS):
        total += jnp.exp(sp_ref[m] - best)
    lse_ref[...] = best + jnp.log(total)

    def per_block(i, carry):
        turned_q = qt_ref[i]
        cot_stack = cs_ref[i]
        lse = lse_ref[pl.ds(i, 1), :]
        out_s[i] = jnp.zeros((COLS, 2 * BLOCK), F32)

        def step(g, carry):
            blocks = block_ids(list_ref, i, g)
            total = None
            for u in range(0, GROUP, PAIR):
                pair = blocks[u : u + PAIR]
                scores = masked_scores(pair, k_s, turned_q, live_ref)
                weight = jnp.exp(scores - lse).astype(BF16)
                term = dot(jnp.concatenate([vt_s[b] for b in pair], axis=1), weight)
                total = term if total is None else total + term
                grads = dot(weight, cot_stack)
                for w, b in enumerate(pair):
                    acc_s[b] += grads[w * BLOCK : (w + 1) * BLOCK]
            out_s[i] += total
            return carry

        lax.fori_loop(0, groups_ref[i], step, 0)
        delta_ref[pl.ds(i, 1), :] = jnp.sum(out_s[i] * ct_ref[i].astype(F32), axis=0, keepdims=True)
        return carry

    lax.fori_loop(0, Q_BLOCKS, per_block, 0)
    store_parts(acc_s, own_ref, halo_ref, gid_ref, gout_ref)


def clear_blocks(acc_s):
    def clear(j, carry):
        acc_s[j] = jnp.zeros((BLOCK, COLS), F32)
        return carry

    lax.fori_loop(0, KEY_BLOCKS, clear, 0, unroll=2)


def store_parts(acc_s, own_ref, halo_ref, gid_ref, gout_ref):
    def own(j, carry):
        own_ref[q_rows(j), :] = acc_s[j]
        return carry

    def halo(j, carry):
        halo_ref[j, :BLOCK] = acc_s[Q_BLOCKS + j].astype(BF16)
        return carry

    lax.fori_loop(0, Q_BLOCKS, own, 0, unroll=2)
    lax.fori_loop(0, SENDERS, halo, 0, unroll=4)
    grads = acc_s[GLOBAL_BLOCK].astype(BF16)
    gout_ref[...] = grads
    slot_row = owner_ranks(gid_ref[...])[1]
    hot = (iota((SENDERS * EXTRA, BLOCK), 0) == slot_row).astype(F32).astype(BF16)
    extra = dot(hot, grads).astype(BF16)
    for s in range(SENDERS):
        halo_ref[s, BLOCK:SLOTS] = extra[s * EXTRA : (s + 1) * EXTRA]


def key_kernel(
    list_ref, groups_ref, live_ref, k_s, kt_s, v_s, qt_ref, qs_ref, ct_ref, lse_ref, delta_ref, back_ref, pair_ref, gid_ref,
    gq_ref, own_ref, halo_ref, gout_ref, acc_s, out_s,
):
    clear_blocks(acc_s)

    def per_block(i, carry):
        turned_q = qt_ref[i]
        q_stack = qs_ref[i]
        turned_cot = ct_ref[i]
        lse = lse_ref[pl.ds(i, 1), :]
        delta = delta_ref[pl.ds(i, 1), :]
        out_s[i] = jnp.zeros((COLS, 2 * BLOCK), F32)

        def step(g, carry):
            blocks = block_ids(list_ref, i, g)
            total = None
            for u in range(0, GROUP, PAIR):
                pair = blocks[u : u + PAIR]
                scores = masked_scores(pair, k_s, turned_q, live_ref)
                dprob = dot(jnp.concatenate([v_s[b] for b in pair], axis=0), turned_cot)
                dscore = (jnp.exp(scores - lse) * (dprob - delta)).astype(BF16)
                term = dot(jnp.concatenate([kt_s[b] for b in pair], axis=1), dscore)
                total = term if total is None else total + term
                grads = dot(dscore, q_stack)
                for w, b in enumerate(pair):
                    acc_s[b] += grads[w * BLOCK : (w + 1) * BLOCK]
            out_s[i] += total
            return carry

        lax.fori_loop(0, groups_ref[i], step, 0)
        return carry

    lax.fori_loop(0, Q_BLOCKS, per_block, 0)
    turned = [turned_weights(back_ref[m, :16]) for m in range(EXPANDERS)]
    for i in range(Q_BLOCKS):
        grad_query = head_rows(out_s[i]).T
        for m in range(EXPANDERS):
            grad_query += dot(turned[m], head_picks(i)) * pair_ref[m * Q_BLOCKS + i].astype(F32)
        gq_ref[i * BLOCK : (i + 1) * BLOCK, :] = (grad_query * (1.0 / math.sqrt(HEAD))).astype(BF16)
    store_parts(acc_s, own_ref, halo_ref, gid_ref, gout_ref)


def scatter_into(acc_s, splits, data):
    subs = packed_iota(0)
    one, zero = jnp.ones((), BF16), jnp.zeros((), BF16)
    bases = [(jnp.where(subs == low, one, zero), jnp.broadcast_to(high, (BLOCK, BLOCK))) for low, high in splits]
    for c in range(NODES_HERE // BLOCK):
        hot = jnp.concatenate([jnp.where(high == jnp.asarray(c, BF16), base, zero) for base, high in bases], axis=1)
        acc_s[c * BLOCK : (c + 1) * BLOCK, :] += dot(hot, data)


def add_halo(acc_s, me_ref, ret_ref, rows_ref, gid_ref):
    def halo(t, carry):
        splits = [split_index(rows_ref[pl.ds(t * GROUP + u, 1), :]) for u in range(GROUP)]
        data = jnp.concatenate([ret_ref[t * GROUP + u, :BLOCK] for u in range(GROUP)], axis=0)
        scatter_into(acc_s, splits, data)
        return carry

    lax.fori_loop(0, SENDERS // GROUP, halo, 0)
    extra = ret_ref[0, BLOCK:SLOTS].astype(F32)
    for s in range(1, SENDERS):
        extra += ret_ref[s, BLOCK:SLOTS].astype(F32)
    high = extra.astype(BF16)
    data = jnp.concatenate([high, (extra - high.astype(F32)).astype(BF16)], axis=0)
    mine = jnp.broadcast_to(mine_columns(gid_ref[...], me_ref[0]), (EXTRA, NODES_HERE))
    hot = (mine == iota((EXTRA, NODES_HERE), 1)).astype(F32)
    hot = jnp.concatenate([hot, hot], axis=0).T.astype(BF16)
    acc_s[...] += dot(hot, data)


def add_partners(acc_s, parts, others, first_col):
    for m, (part, other) in enumerate(zip(parts, others)):
        turned = turned_weights(part)
        index_low = other[NODES_HERE + m * Q_BLOCKS : NODES_HERE + (m + 1) * Q_BLOCKS, :COLS]
        index_high = other[NODES_HERE + m * Q_BLOCKS : NODES_HERE + (m + 1) * Q_BLOCKS, COLS:]
        for t in range(Q_BLOCKS // GROUP):
            splits, data = [], []
            for u in range(GROUP):
                i = t * GROUP + u
                splits.append((index_low[i : i + 1], index_high[i : i + 1]))
                wide = dot(turned, head_picks(i))
                rows = other[i * BLOCK : (i + 1) * BLOCK, first_col : first_col + COLS].astype(F32)
                data.append((wide * rows).astype(BF16))
            scatter_into(acc_s, splits, jnp.concatenate(data, axis=0))


def feature_part(feat_ref, k):
    return pl.ds(pl.multiple_of(((feat_ref[0] + k) % 4) * COLS, COLS), COLS)


def value_back_kernel(
    me_ref, feat_ref, ownv_ref, ret_ref, ownk_ref, rows_ref, o0_ref, o1_ref, o2_ref, o3_ref, gid_ref, wq_ref, wv_ref,
    gq_ref, accv_s, acck_ref, pre_ref,
):
    others = (o0_ref, o1_ref, o2_ref, o3_ref)
    parts = [ret_ref[me_ref[0] ^ (1 << m), SLOTS:] for m in range(EXPANDERS)]
    accv_s[...] = ownv_ref[...]
    add_halo(accv_s, me_ref, ret_ref, rows_ref, gid_ref)
    add_partners(accv_s, [part[16:] for part in parts], others, COLS)
    acck_ref[...] = ownk_ref[...]
    add_partners(acck_ref, [part[:16] for part in parts], others, 0)
    grad_value = accv_s[...].astype(BF16)
    for k in range(4):
        part = feature_part(feat_ref, k)
        pre_ref[k] = dot_nt(gq_ref[...], wq_ref[part, :]) + dot_nt(grad_value, wv_ref[part, :])


def key_back_kernel(
    me_ref, feat_ref, acck_ref, ret_ref, rows_ref, gid_ref, wk_ref, pre_ref, t0_ref, t1_ref, t2_ref, t3_ref, acc_s
):
    acc_s[...] = acck_ref[...]
    add_halo(acc_s, me_ref, ret_ref, rows_ref, gid_ref)
    grad_key = acc_s[...].astype(BF16)
    for k, out in ((1, t1_ref), (2, t2_ref), (3, t3_ref), (0, t0_ref)):
        out[...] = (pre_ref[k] + dot_nt(grad_key, wk_ref[feature_part(feat_ref, k), :])).astype(out.dtype)


def shape(dims, kind=BF16):
    return jax.ShapeDtypeStruct(dims, kind)


def call(kernel, ins, outs, args, scratch=(), name=None, flops=0, out_spaces=None, aliases={}):
    cost = pl.CostEstimate(flops=flops, transcendentals=0, bytes_accessed=4_000_000)
    return pl.pallas_call(
        kernel,
        out_shape=outs,
        in_specs=ins,
        out_specs=out_spaces or tuple(vmem() for _ in outs),
        scratch_shapes=list(scratch),
        compiler_params=params(),
        cost_estimate=cost,
        input_output_aliases=aliases,
        name=name,
    )(*args)


def blocks_of(kind):
    return pltpu.VMEM((KEY_BLOCKS, BLOCK, COLS), kind)


def run_project(me, features, w_query, w_key, w_value, cotangent, rows, exp_list, gids):
    return call(
        project_kernel,
        [smem()] + [vmem()] * 8,
        (
            shape((NODES_HERE, COLS)),
            shape((NODES_HERE, COLS)),
            shape((NODES_HERE, COLS)),
            shape((SENDERS, SLOTS, COLS)),
            shape((SENDERS, SLOTS, COLS)),
            shape((NODES_HERE + EXPANDERS * Q_BLOCKS, 2 * COLS)),
            shape((1,), jnp.int32),
        ),
        (me, features, w_query, w_key, w_value, cotangent, rows, exp_list, gids),
        name="project",
        flops=3_000_000_000,
        out_spaces=(*(vmem() for _ in range(6)), smem()),
        scratch=[pltpu.VMEM((NODES_HERE, 2 * COLS), BF16)],
    )


def run_plan(block_mask, halo_count):
    return call(
        plan_kernel,
        [smem()] * 2,
        (shape((Q_BLOCKS * LIST,), jnp.int32), shape((Q_BLOCKS,), jnp.int32), shape((LIST,), jnp.int32)),
        (block_mask.reshape(-1), halo_count.reshape(-1)),
        name="plan",
        out_spaces=(smem(), smem(), smem()),
    )


def run_partner_keys(exp_rows, swaps, query):
    return call(
        partner_key_kernel,
        [vmem()] * 6,
        (shape((EXPANDERS * Q_BLOCKS, BLOCK, COLS)), shape((EXPANDERS, Q_BLOCKS, 2 * BLOCK), F32)),
        (exp_rows, *swaps, query),
        name="partners",
        flops=5_000_000_000,
    )


def run_finish(me, exp_rows, swaps, cotangent, out_t, scores, lse, local, back_v):
    anywhere = pl.BlockSpec(memory_space=pl.ANY)
    return call(
        finish_kernel,
        [smem()] + [vmem()] * 10 + [anywhere],
        (
            shape((NODES_HERE, COLS)),
            shape((EXPANDERS, PART_ROWS, BLOCK)),
            shape((Q_BLOCKS, 2 * BLOCK), F32),
            shape((SENDERS, BACK, COLS)),
        ),
        (me, exp_rows, *swaps, cotangent, out_t, scores, lse, local, back_v),
        name="finish",
        flops=5_000_000_000,
        out_spaces=(vmem(), vmem(), vmem(), anywhere),
        scratch=[pltpu.SemaphoreType.DMA((EXPANDERS,))],
        aliases={11: 3},
    )


def run_prepare(query, cotangent):
    wide, high = shape((Q_BLOCKS, COLS, 2 * BLOCK)), shape((Q_BLOCKS, 2 * BLOCK, COLS))
    return call(
        prepare_kernel, [vmem()] * 2, (wide, high, wide, high), (query, cotangent), name="prepare", flops=2_000_000_000
    )


def run_scores(plan, turned_q, own, halo_k, gids, glob):
    return call(
        score_kernel,
        [smem()] * 3 + [vmem()] * 5,
        (
            shape((Q_BLOCKS, 2 * BLOCK), F32),
            shape((KEY_BLOCKS, BLOCK, COLS)),
            shape((KEY_BLOCKS, COLS, BLOCK)),
        ),
        (*plan, turned_q, own, halo_k, gids, glob),
        name="scores",
        flops=12_000_000_000,
    )


def run_turn(own, halo_v, gids, glob):
    return call(
        turn_kernel,
        [vmem()] * 4,
        (shape((KEY_BLOCKS, BLOCK, COLS)), shape((KEY_BLOCKS, COLS, BLOCK))),
        (own, halo_v, gids, glob),
        name="turn",
        flops=2_000_000_000,
    )


def run_values(plan, keys, turned_v, prepared, part, scores, gids):
    turned_q, _, turned_cot, cot_stack = prepared
    return call(
        value_kernel,
        [smem()] * 3 + [vmem()] * 8,
        (
            shape((NODES_HERE, COLS), F32),
            shape((SENDERS, BACK, COLS)),
            shape((BLOCK, COLS)),
            shape((Q_BLOCKS, COLS, 2 * BLOCK), F32),
            shape((Q_BLOCKS, 2 * BLOCK), F32),
            shape((Q_BLOCKS, 2 * BLOCK), F32),
        ),
        (*plan, keys, turned_v, turned_q, turned_cot, cot_stack, part, scores, gids),
        scratch=[blocks_of(F32)],
        name="values",
        flops=20_000_000_000,
    )


def run_keys(plan, keys, turned_k, values, prepared, lse, delta, back, pairs, gids):
    turned_q, q_stack, turned_cot, _ = prepared
    return call(
        key_kernel,
        [smem()] * 3 + [vmem()] * 11,
        (
            shape((NODES_HERE, COLS)),
            shape((NODES_HERE, COLS), F32),
            shape((SENDERS, SLOTS, COLS)),
            shape((BLOCK, COLS)),
        ),
        (*plan, keys, turned_k, values, turned_q, q_stack, turned_cot, lse, delta, back, pairs, gids),
        scratch=[blocks_of(F32), pltpu.VMEM((Q_BLOCKS, COLS, 2 * BLOCK), F32)],
        name="keys",
        flops=25_000_000_000,
    )


def run_value_back(me, feat, own_v, returned_v, own_k, rows, others, gids, w_query, w_value, grad_query):
    return call(
        value_back_kernel,
        [smem()] * 2 + [vmem()] * 12,
        (shape((NODES_HERE, COLS), F32), shape((NODES_HERE, COLS), F32), shape((4, NODES_HERE, COLS), F32)),
        (me, feat, own_v, returned_v, own_k, rows, *others, gids, w_query, w_value, grad_query),
        name="value_back",
        flops=12_000_000_000,
    )[1:]


def run_key_back(me, feat, own_k, returned_k, rows, gids, w_key, pre):
    return call(
        key_back_kernel,
        [smem()] * 2 + [vmem()] * 6,
        (shape((NODES_HERE, COLS), F32),) + tuple(shape((NODES_HERE, COLS)) for _ in range(3)),
        (me, feat, own_k, returned_k, rows, gids, w_key, pre),
        scratch=[pltpu.VMEM((NODES_HERE, COLS), F32)],
        name="key_back",
        flops=8_000_000_000,
    )


def ranks(global_ids):
    owner = global_ids // NODES_HERE
    ids = jnp.arange(BLOCK)
    return owner, ((owner[:, None] == owner[None, :]) & (ids[None, :] < ids[:, None])).sum(1)


def more_globals(rounds, global_ids, my_index, own_k, own_v):
    def body(state):
        r, glob = state
        owner, rank = ranks(global_ids)
        slot = rank - r * EXTRA
        here = (slot >= 0) & (slot < EXTRA)
        place = jnp.where((owner == my_index) & here, slot, EXTRA)
        local = jnp.where(here, global_ids % NODES_HERE, 0)
        found = jnp.concatenate([own_k[local], own_v[local]], axis=1)
        rows = jnp.zeros((EXTRA + 1, 2 * COLS), BF16).at[place].set(found)[:EXTRA]
        got = lax.all_to_all(jnp.broadcast_to(rows[None], (SENDERS, *rows.shape)), "dom", 0, 0, tiled=True)
        found = got.reshape(SENDERS * EXTRA, -1)[jnp.clip(owner * EXTRA + slot, 0, SENDERS * EXTRA - 1)]
        return r + 1, jnp.where(here[:, None], found, glob)

    start = (jnp.asarray(1, jnp.int32), jnp.zeros((BLOCK, 2 * COLS), BF16))
    return lax.while_loop(lambda state: state[0] < rounds, body, start)[1]


def more_grads(rounds, global_ids, my_index, part_k, part_v, own_k, own_v):
    def body(state):
        r, own_k, own_v = state
        owner, rank = ranks(global_ids)
        slot = rank - r * EXTRA
        here = (slot >= 0) & (slot < EXTRA)
        part = jnp.concatenate([part_k, part_v], axis=1)
        place = jnp.where(here, owner * EXTRA + slot, SENDERS * EXTRA)
        rows = jnp.zeros((SENDERS * EXTRA + 1, part.shape[1]), BF16).at[place].set(part)[: SENDERS * EXTRA]
        got = lax.all_to_all(rows.reshape(SENDERS, EXTRA, -1), "dom", 0, 0, tiled=True).astype(F32).sum(0)
        take = (owner == my_index) & here
        add = jnp.where(take[:, None], got[jnp.clip(slot, 0, EXTRA - 1)], 0.0)
        local = global_ids % NODES_HERE
        return r + 1, own_k.at[local].add(add[:, :COLS]), own_v.at[local].add(add[:, COLS:])

    start = (jnp.asarray(1, jnp.int32), own_k, own_v)
    return lax.while_loop(lambda state: state[0] < rounds, body, start)[1:]


def on_device(
    features,
    w_query,
    w_key,
    w_value,
    cotangent,
    send_rows,
    halo_count,
    block_mask,
    exp_rows,
    global_ids,
):
    dom_count = lax.axis_size("dom")
    my_index = lax.axis_index("dom")

    def swapped(value, bit):
        return lax.ppermute(value, "dom", [(i, i ^ (1 << bit)) for i in range(dom_count)])

    rows = send_rows[0]
    gids = global_ids.reshape(1, BLOCK)
    me = my_index.reshape(1).astype(jnp.int32)
    feat = lax.axis_index("feat").reshape(1).astype(jnp.int32)

    query, own_keys, own_values, out_k, out_v, away, rounds = run_project(
        me, features, w_query, w_key, w_value, cotangent, rows, exp_rows, gids
    )
    rounds = rounds[0]
    glob = more_globals(rounds, global_ids, my_index, own_keys, own_values)
    out_k, out_v, glob = lax.optimization_barrier((out_k, out_v, glob))
    halo_k = lax.all_to_all(out_k, "dom", 0, 0, tiled=True)
    key_swaps = [swapped(own_keys, m) for m in range(EXPANDERS)]
    plan = run_plan(block_mask, halo_count)
    prepared = run_prepare(query, cotangent)
    halo_v = lax.all_to_all(out_v, "dom", 0, 0, tiled=True)
    part, keys, turned_k = run_scores(plan, prepared[0], own_keys, halo_k, gids, glob)
    own_values_late, part = lax.optimization_barrier((own_values, part))
    part, *key_swaps = lax.optimization_barrier((part, *key_swaps))
    value_swaps = [swapped(own_values_late, m) for m in range(EXPANDERS)]
    pairs, scores = run_partner_keys(exp_rows, key_swaps, query)
    values, turned_v = run_turn(own_values, halo_v, gids, glob)
    away, scores = lax.optimization_barrier((away, scores))
    others = [swapped(away, m) for m in range(EXPANDERS)]
    own_v, back_v, glob_v, out_t, local, lse = run_values(plan, keys, turned_v, prepared, part, scores, gids)
    out_t, *value_swaps = lax.optimization_barrier((out_t, *value_swaps))
    attended, back, delta, back_v = run_finish(
        me, exp_rows, value_swaps, cotangent, out_t, scores, lse, local, back_v
    )
    returned_v = lax.all_to_all(back_v, "dom", 0, 0, tiled=True)
    grad_query, own_k, back_k, glob_k = run_keys(
        plan, keys, turned_k, values, prepared, lse, delta, back, pairs, gids
    )
    own_k, returned_v, *others = lax.optimization_barrier((own_k, returned_v, *others))
    own_k, own_v = more_grads(rounds, global_ids, my_index, glob_k, glob_v, own_k, own_v)
    back_k, own_k, own_v = lax.optimization_barrier((back_k, own_k, own_v))
    returned_k = lax.all_to_all(back_k, "dom", 0, 0, tiled=True)
    own_k, pre = run_value_back(
        me, feat, own_v, returned_v, own_k, rows, others, gids, w_query, w_value, grad_query
    )
    mine, *away = run_key_back(me, feat, own_k, returned_k, rows, gids, w_key, pre)
    for k, term in enumerate(away, 1):
        mine = mine + lax.ppermute(term, "feat", [(i, (i + k) % 4) for i in range(4)]).astype(F32)
    return (attended, mine.astype(BF16))


def solution(mesh):
    return jax.shard_map(
        on_device,
        mesh=mesh,
        in_specs=(
            P("dom", None),
            P(None, "feat"),
            P(None, "feat"),
            P(None, "feat"),
            P("dom", "feat"),
            P("dom", None, None),
            P(None, "dom"),
            P("dom", None),
            P(None, "dom"),
            P(),
        ),
        out_specs=(P("dom", "feat"), P("dom", "feat")),
        check_vma=False,
    )
```

```python
import math

import jax
import jax.numpy as jnp
from jax import lax
from jax.experimental import pallas as pl
from jax.experimental.pallas import tpu as pltpu
from jax.sharding import PartitionSpec as P

HEAD = 64
BLOCK = 128
EXPANDERS = 4
COLS = 128
NODES_HERE = 1024
Q_BLOCKS = NODES_HERE // BLOCK
SENDERS = 32
GLOBAL_BLOCK = Q_BLOCKS + SENDERS
EMPTY_BLOCK = GLOBAL_BLOCK + 1
KEY_BLOCKS = EMPTY_BLOCK + 1
GROUP = 8
PAIR = 4
LIST = 56
EXTRA = 16
SLOTS = BLOCK + EXTRA
PART_ROWS = 32
BACK = SLOTS + PART_ROWS
NEG = -1e30
F32 = jnp.float32
BF16 = jnp.bfloat16


def params():
    return pltpu.CompilerParams(vmem_limit_bytes=20 * 1024 * 1024)


def vmem():
    return pl.BlockSpec(memory_space=pltpu.VMEM)


def smem():
    return pl.BlockSpec(memory_space=pltpu.SMEM)


def iota(shape, dim):
    return lax.broadcasted_iota(jnp.int32, shape, dim)


def dot(a, b):
    return jnp.dot(a, b, preferred_element_type=F32)


def dot_nt(a, b):
    return lax.dot_general(a, b, (((1,), (1,)), ((), ())), preferred_element_type=F32)


def split_index(index):
    return (index & (BLOCK - 1)).astype(F32).astype(BF16), (index >> 7).astype(F32).astype(BF16)


def packed_iota(dim):
    return iota((BLOCK, BLOCK), dim).astype(F32).astype(BF16)


def one_hot_columns(column):
    low, high = split_index(column)
    lanes = jnp.concatenate([packed_iota(1)] * (column.shape[0] // BLOCK), axis=0)
    one, zero = jnp.ones((), BF16), jnp.zeros((), BF16)
    base = jnp.where(low == lanes, one, zero)
    return jnp.concatenate(
        [jnp.where(high == jnp.asarray(c, BF16), base, zero) for c in range(NODES_HERE // BLOCK)], axis=1
    )


def one_hot_of_rows(index_rows):
    columns = [jnp.broadcast_to(row, (BLOCK, BLOCK)).T for row in index_rows]
    return one_hot_columns(jnp.concatenate(columns, axis=0))


def owner_ranks(gid_row):
    owner = jnp.broadcast_to(gid_row >> 10, (BLOCK, BLOCK))
    owner_t = owner.T
    same = owner == owner_t
    subs, lanes = iota((BLOCK, BLOCK), 0), iota((BLOCK, BLOCK), 1)
    row = jnp.sum(jnp.where(jnp.logical_and(same, subs < lanes), 1.0, 0.0), axis=0, keepdims=True)
    col = jnp.sum(jnp.where(jnp.logical_and(same, lanes < subs), 1.0, 0.0), axis=1, keepdims=True)
    row, col = row.astype(jnp.int32), jnp.broadcast_to(col, (BLOCK, BLOCK)).astype(jnp.int32)
    slot_row = jnp.where(row < EXTRA, (gid_row >> 10) * EXTRA + row, -1)
    slot_col = jnp.where(col < EXTRA, owner_t * EXTRA + col, -1)
    return row, slot_row, slot_col


def mine_columns(gid_row, me):
    row, _, _ = owner_ranks(gid_row)
    mine = (gid_row >> 10) == me
    slots = iota((EXTRA, BLOCK), 0)
    hit = jnp.logical_and(jnp.broadcast_to(mine, (EXTRA, BLOCK)), slots == row)
    local = jnp.broadcast_to(gid_row & (NODES_HERE - 1), (EXTRA, BLOCK)) + 1
    return jnp.sum(jnp.where(hit, local, 0).astype(F32), axis=1, keepdims=True).astype(jnp.int32) - 1


def exp_row(exp_ref, m, i):
    return exp_ref[m : m + 1, i * BLOCK : (i + 1) * BLOCK]


def project_kernel(
    me_ref, x_ref, wq_ref, wk_ref, wv_ref, cot_ref, rows_ref, exp_ref, gid_ref, q_ref, k_ref, v_ref, outk_ref, outv_ref,
    away_ref, rounds_ref, kv_ref,
):
    most = jnp.max(owner_ranks(gid_ref[...])[0].astype(F32)).astype(jnp.int32)
    rounds_ref[0] = (most + EXTRA) // EXTRA
    x = x_ref[...]
    keys = dot(x, wk_ref[...]).astype(BF16)
    values = dot(x, wv_ref[...]).astype(BF16)
    k_ref[...] = keys
    v_ref[...] = values
    kv_ref[:, :COLS] = keys
    kv_ref[:, COLS:] = values
    query = (dot(x, wq_ref[...]).astype(BF16).astype(F32) * (1.0 / math.sqrt(HEAD))).astype(BF16)
    q_ref[...] = query
    away_ref[:NODES_HERE, :COLS] = query
    away_ref[:NODES_HERE, COLS:] = cot_ref[...]
    for m in range(EXPANDERS):
        low, high = split_index(jnp.concatenate([exp_row(exp_ref, m, i) for i in range(Q_BLOCKS)], axis=0))
        away_ref[NODES_HERE + m * Q_BLOCKS : NODES_HERE + (m + 1) * Q_BLOCKS, :COLS] = low
        away_ref[NODES_HERE + m * Q_BLOCKS : NODES_HERE + (m + 1) * Q_BLOCKS, COLS:] = high
    mine = jnp.broadcast_to(mine_columns(gid_ref[...], me_ref[0]), (EXTRA, BLOCK))
    lanes = iota((EXTRA, NODES_HERE), 1)
    hot = (jnp.concatenate([mine] * (NODES_HERE // BLOCK), axis=1) == lanes).astype(F32).astype(BF16)
    extra = dot(hot, kv_ref[...]).astype(BF16)

    def gather(t, carry):
        hot = one_hot_of_rows([rows_ref[pl.ds(t * GROUP + u, 1), :] for u in range(GROUP)])
        got = dot(hot, kv_ref[...]).astype(BF16)
        for u in range(GROUP):
            outk_ref[t * GROUP + u, :BLOCK] = got[u * BLOCK : (u + 1) * BLOCK, :COLS]
            outv_ref[t * GROUP + u, :BLOCK] = got[u * BLOCK : (u + 1) * BLOCK, COLS:]
            outk_ref[t * GROUP + u, BLOCK:] = extra[:, :COLS]
            outv_ref[t * GROUP + u, BLOCK:] = extra[:, COLS:]
        return carry

    lax.fori_loop(0, SENDERS // GROUP, gather, 0)


def gather_partner(exp_ref, m, table):
    blocks = []
    for t in range(0, Q_BLOCKS, 4):
        hot = one_hot_of_rows([exp_row(exp_ref, m, t + u) for u in range(4)])
        got = dot(hot, table[...]).astype(BF16)
        blocks += [got[u * BLOCK : (u + 1) * BLOCK] for u in range(4)]
    return blocks


def sum_picks():
    sub = iota((2 * Q_BLOCKS * COLS, 16), 0)
    col = iota((2 * Q_BLOCKS * COLS, 16), 1)
    return (col == (sub >> 8) + jnp.where((sub & (COLS - 1)) < HEAD, 0, 8)).astype(F32).astype(BF16)


def head_sums(a_ref, blocks, picks):
    parts = []
    for i, b in enumerate(blocks):
        prod = a_ref[i * BLOCK : (i + 1) * BLOCK, :].astype(F32) * b.astype(F32)
        high = prod.astype(BF16)
        parts += [high, (prod - high.astype(F32)).astype(BF16)]
    return flat(dot(jnp.concatenate(parts, axis=1), picks).T)


def partner_key_kernel(exp_ref, t0_ref, t1_ref, t2_ref, t3_ref, q_ref, out_ref, sp_ref):
    picks = sum_picks()
    for m, table in enumerate((t0_ref, t1_ref, t2_ref, t3_ref)):
        blocks = gather_partner(exp_ref, m, table)
        for i, block in enumerate(blocks):
            out_ref[m * Q_BLOCKS + i] = block
        sp_ref[m] = head_sums(q_ref, blocks, picks)


def head_picks(i):
    return (iota((16, COLS), 0) == jnp.where(iota((16, COLS), 1) < HEAD, i, 8 + i)).astype(F32).astype(BF16)


def finish_kernel(
    me_ref, exp_ref, t0_ref, t1_ref, t2_ref, t3_ref, cot_ref, out_t_ref, sp_ref, lse_ref, local_ref, _, att_ref, back_ref,
    delta_ref, message_ref, sems,
):
    picks = sum_picks()
    lse = lse_ref[...]
    delta = local_ref[...]
    totals = [head_rows(out_t_ref[i]).T for i in range(Q_BLOCKS)]
    probs, dprobs = [], []
    for m, table in enumerate((t0_ref, t1_ref, t2_ref, t3_ref)):
        blocks = gather_partner(exp_ref, m, table)
        prob = jnp.exp(sp_ref[m] - lse)
        dprob = head_sums(cot_ref, blocks, picks)
        delta += prob * dprob
        weight = tall(prob).astype(BF16)
        back_ref[m, 16:] = weight
        turned = turned_weights(weight)
        for i, block in enumerate(blocks):
            totals[i] += dot(turned, head_picks(i)) * block.astype(F32)
        probs.append(prob)
        dprobs.append(dprob)
    delta_ref[...] = delta
    for m in range(EXPANDERS):
        back_ref[m, :16] = tall(probs[m] * (dprobs[m] - delta)).astype(BF16)
    copies = [
        pltpu.make_async_copy(
            back_ref.at[m], message_ref.at[me_ref[0] ^ (1 << m), pl.ds(SLOTS, PART_ROWS)], sems.at[m]
        )
        for m in range(EXPANDERS)
    ]
    for copy in copies:
        copy.start()
    for i in range(Q_BLOCKS):
        att_ref[i * BLOCK : (i + 1) * BLOCK, :] = totals[i].astype(BF16)
    for copy in copies:
        copy.wait()


def flat(x):
    return jnp.concatenate([x[:8], x[8:]], axis=1)


def tall(x):
    return jnp.concatenate([x[:, :BLOCK], x[:, BLOCK:]], axis=0)


def turned_weights(tall_rows):
    return tall_rows.astype(F32).T.astype(BF16)


def prepare_kernel(q_ref, cot_ref, qt_ref, qs_ref, ct_ref, cs_ref):
    def one(i, carry):
        q = q_ref[q_rows(i), :]
        cot = cot_ref[q_rows(i), :]
        qt_ref[i] = stacked_t(q)
        qs_ref[i] = stacked(q)
        ct_ref[i] = stacked_t(cot)
        cs_ref[i] = stacked(cot)
        return carry

    lax.fori_loop(0, Q_BLOCKS, one, 0, unroll=2)


def plan_kernel(mask_ref, count_ref, list_ref, groups_ref, live_ref):
    for j in range(Q_BLOCKS):
        live_ref[j] = BLOCK
    live_ref[GLOBAL_BLOCK] = BLOCK
    live_ref[EMPTY_BLOCK] = 0

    def copy_count(s, carry):
        live_ref[Q_BLOCKS + s] = count_ref[s]
        return carry

    lax.fori_loop(0, SENDERS, copy_count, 0)

    def per_block(i, carry):
        list_ref[i * LIST] = GLOBAL_BLOCK

        def put(j, n):
            list_ref[i * LIST + n] = j
            used = jnp.logical_and(mask_ref[i * GLOBAL_BLOCK + j] > 0, live_ref[j] > 0)
            return n + used.astype(jnp.int32)

        n = lax.fori_loop(0, GLOBAL_BLOCK, put, 1)
        for extra in range(GROUP):
            list_ref[i * LIST + n + extra] = EMPTY_BLOCK
        groups_ref[i] = (n + GROUP - 1) // GROUP
        return carry

    lax.fori_loop(0, Q_BLOCKS, per_block, 0)


def fill(dst, dst_t, first_col, own_ref, halo_ref, gid_ref, glob_ref):
    def own(j, carry):
        block = own_ref[q_rows(j), :]
        dst[j] = block
        dst_t[j] = block.T
        return carry

    def halo(j, carry):
        block = halo_ref[j, :BLOCK]
        dst[Q_BLOCKS + j] = block
        dst_t[Q_BLOCKS + j] = block.T
        return carry

    lax.fori_loop(0, Q_BLOCKS, own, 0, unroll=4)
    lax.fori_loop(0, SENDERS, halo, 0, unroll=4)
    slot_col = owner_ranks(gid_ref[...])[2]
    wide = jnp.concatenate([slot_col] * (SENDERS * EXTRA // BLOCK), axis=1)
    hot = (wide == iota((BLOCK, SENDERS * EXTRA), 1)).astype(F32).astype(BF16)
    extra = jnp.concatenate([halo_ref[s, BLOCK:] for s in range(SENDERS)], axis=0)
    rows = (dot(hot, extra) + glob_ref[:, first_col : first_col + COLS].astype(F32)).astype(BF16)
    dst[GLOBAL_BLOCK] = rows
    dst_t[GLOBAL_BLOCK] = rows.T
    dst[EMPTY_BLOCK] = jnp.zeros((BLOCK, COLS), BF16)
    dst_t[EMPTY_BLOCK] = jnp.zeros((BLOCK, COLS), BF16)


def turn_kernel(own_ref, hv_ref, gid_ref, glob_ref, v_ref, vt_ref):
    fill(v_ref, vt_ref, COLS, own_ref, hv_ref, gid_ref, glob_ref)


def stacked(rows):
    lanes = iota((BLOCK, COLS), 1)
    zero = jnp.zeros_like(rows)
    return jnp.concatenate([jnp.where(lanes < HEAD, rows, zero), jnp.where(lanes < HEAD, zero, rows)], axis=0)


def stacked_t(rows):
    turned = rows.T
    subs = iota((COLS, BLOCK), 0)
    zero = jnp.zeros_like(turned)
    return jnp.concatenate([jnp.where(subs < HEAD, turned, zero), jnp.where(subs < HEAD, zero, turned)], axis=1)


def head_rows(turned):
    return jnp.concatenate([turned[:HEAD, :BLOCK], turned[HEAD:, BLOCK:]], axis=0)


def masked_scores(blocks, k_s, turned_q, live_ref):
    keys = jnp.concatenate([k_s[b] for b in blocks], axis=0)
    scores = dot(keys, turned_q)
    row_id = iota((BLOCK, 2 * BLOCK), 0)
    return jnp.concatenate(
        [
            jnp.where(row_id < live_ref[b], scores[u * BLOCK : (u + 1) * BLOCK], NEG)
            for u, b in enumerate(blocks)
        ],
        axis=0,
    )


def block_ids(list_ref, i, g):
    return [list_ref[i * LIST + g * GROUP + u] for u in range(GROUP)]


def q_rows(i):
    return pl.ds(pl.multiple_of(i * BLOCK, BLOCK), BLOCK)


def score_kernel(
    list_ref, groups_ref, live_ref, qt_ref, own_ref, hk_ref, gid_ref, glob_ref, lse_ref, k_s, kt_ref
):
    fill(k_s, kt_ref, 0, own_ref, hk_ref, gid_ref, glob_ref)

    def per_block(i, carry):
        turned_q = qt_ref[i]

        def step(g, state):
            blocks = block_ids(list_ref, i, g)
            new_state = []
            for u in range(GROUP // PAIR):
                top, total = state[u]
                scores = masked_scores(blocks[u * PAIR : (u + 1) * PAIR], k_s, turned_q, live_ref)
                scores = scores.reshape(PAIR * BLOCK // 8, 8, 2 * BLOCK)
                new_top = jnp.maximum(top, jnp.max(scores, axis=0))
                total = total * jnp.exp(top - new_top) + jnp.sum(jnp.exp(scores - new_top[None]), axis=0)
                new_state.append((new_top, total))
            return tuple(new_state)

        init = (jnp.full((8, 2 * BLOCK), NEG, F32), jnp.zeros((8, 2 * BLOCK), F32))
        state = lax.fori_loop(0, groups_ref[i], step, tuple(init for _ in range(GROUP // PAIR)))
        top = jnp.concatenate([t for t, _ in state], axis=0)
        total = jnp.concatenate([t for _, t in state], axis=0)
        best = jnp.max(top, axis=0, keepdims=True)
        denominator = jnp.sum(total * jnp.exp(top - best), axis=0, keepdims=True)
        lse_ref[pl.ds(i, 1), :] = best + jnp.log(denominator)
        return carry

    lax.fori_loop(0, Q_BLOCKS, per_block, 0)


def value_kernel(
    list_ref, groups_ref, live_ref, k_s, vt_s, qt_ref, ct_ref, cs_ref, part_ref, sp_ref, gid_ref,
    own_ref, halo_ref, gout_ref, out_s, delta_ref, lse_ref, acc_s,
):
    clear_blocks(acc_s)
    part = part_ref[...]
    best = part
    for m in range(EXPANDERS):
        best = jnp.maximum(best, sp_ref[m])
    total = jnp.exp(part - best)
    for m in range(EXPANDERS):
        total += jnp.exp(sp_ref[m] - best)
    lse_ref[...] = best + jnp.log(total)

    def per_block(i, carry):
        turned_q = qt_ref[i]
        cot_stack = cs_ref[i]
        lse = lse_ref[pl.ds(i, 1), :]
        out_s[i] = jnp.zeros((COLS, 2 * BLOCK), F32)

        def step(g, carry):
            blocks = block_ids(list_ref, i, g)
            total = None
            for u in range(0, GROUP, PAIR):
                pair = blocks[u : u + PAIR]
                scores = masked_scores(pair, k_s, turned_q, live_ref)
                weight = jnp.exp(scores - lse).astype(BF16)
                term = dot(jnp.concatenate([vt_s[b] for b in pair], axis=1), weight)
                total = term if total is None else total + term
                grads = dot(weight, cot_stack)
                for w, b in enumerate(pair):
                    acc_s[b] += grads[w * BLOCK : (w + 1) * BLOCK]
            out_s[i] += total
            return carry

        lax.fori_loop(0, groups_ref[i], step, 0)
        delta_ref[pl.ds(i, 1), :] = jnp.sum(out_s[i] * ct_ref[i].astype(F32), axis=0, keepdims=True)
        return carry

    lax.fori_loop(0, Q_BLOCKS, per_block, 0)
    store_parts(acc_s, own_ref, halo_ref, gid_ref, gout_ref)


def clear_blocks(acc_s):
    def clear(j, carry):
        acc_s[j] = jnp.zeros((BLOCK, COLS), F32)
        return carry

    lax.fori_loop(0, KEY_BLOCKS, clear, 0, unroll=2)


def store_parts(acc_s, own_ref, halo_ref, gid_ref, gout_ref):
    def own(j, carry):
        own_ref[q_rows(j), :] = acc_s[j]
        return carry

    def halo(j, carry):
        halo_ref[j, :BLOCK] = acc_s[Q_BLOCKS + j].astype(BF16)
        return carry

    lax.fori_loop(0, Q_BLOCKS, own, 0, unroll=2)
    lax.fori_loop(0, SENDERS, halo, 0, unroll=4)
    grads = acc_s[GLOBAL_BLOCK].astype(BF16)
    gout_ref[...] = grads
    slot_row = owner_ranks(gid_ref[...])[1]
    hot = (iota((SENDERS * EXTRA, BLOCK), 0) == slot_row).astype(F32).astype(BF16)
    extra = dot(hot, grads).astype(BF16)
    for s in range(SENDERS):
        halo_ref[s, BLOCK:SLOTS] = extra[s * EXTRA : (s + 1) * EXTRA]


def key_kernel(
    list_ref, groups_ref, live_ref, k_s, kt_s, v_s, qt_ref, qs_ref, ct_ref, lse_ref, delta_ref, back_ref, pair_ref, gid_ref,
    gq_ref, own_ref, halo_ref, gout_ref, acc_s, out_s,
):
    clear_blocks(acc_s)

    def per_block(i, carry):
        turned_q = qt_ref[i]
        q_stack = qs_ref[i]
        turned_cot = ct_ref[i]
        lse = lse_ref[pl.ds(i, 1), :]
        delta = delta_ref[pl.ds(i, 1), :]
        out_s[i] = jnp.zeros((COLS, 2 * BLOCK), F32)

        def step(g, carry):
            blocks = block_ids(list_ref, i, g)
            total = None
            for u in range(0, GROUP, PAIR):
                pair = blocks[u : u + PAIR]
                scores = masked_scores(pair, k_s, turned_q, live_ref)
                dprob = dot(jnp.concatenate([v_s[b] for b in pair], axis=0), turned_cot)
                dscore = (jnp.exp(scores - lse) * (dprob - delta)).astype(BF16)
                term = dot(jnp.concatenate([kt_s[b] for b in pair], axis=1), dscore)
                total = term if total is None else total + term
                grads = dot(dscore, q_stack)
                for w, b in enumerate(pair):
                    acc_s[b] += grads[w * BLOCK : (w + 1) * BLOCK]
            out_s[i] += total
            return carry

        lax.fori_loop(0, groups_ref[i], step, 0)
        return carry

    lax.fori_loop(0, Q_BLOCKS, per_block, 0)
    turned = [turned_weights(back_ref[m, :16]) for m in range(EXPANDERS)]
    for i in range(Q_BLOCKS):
        grad_query = head_rows(out_s[i]).T
        for m in range(EXPANDERS):
            grad_query += dot(turned[m], head_picks(i)) * pair_ref[m * Q_BLOCKS + i].astype(F32)
        gq_ref[i * BLOCK : (i + 1) * BLOCK, :] = (grad_query * (1.0 / math.sqrt(HEAD))).astype(BF16)
    store_parts(acc_s, own_ref, halo_ref, gid_ref, gout_ref)


def scatter_into(acc_s, splits, data):
    subs = packed_iota(0)
    one, zero = jnp.ones((), BF16), jnp.zeros((), BF16)
    bases = [(jnp.where(subs == low, one, zero), jnp.broadcast_to(high, (BLOCK, BLOCK))) for low, high in splits]
    for c in range(NODES_HERE // BLOCK):
        hot = jnp.concatenate([jnp.where(high == jnp.asarray(c, BF16), base, zero) for base, high in bases], axis=1)
        acc_s[c * BLOCK : (c + 1) * BLOCK, :] += dot(hot, data)


def add_halo(acc_s, me_ref, ret_ref, rows_ref, gid_ref):
    def halo(t, carry):
        splits = [split_index(rows_ref[pl.ds(t * GROUP + u, 1), :]) for u in range(GROUP)]
        data = jnp.concatenate([ret_ref[t * GROUP + u, :BLOCK] for u in range(GROUP)], axis=0)
        scatter_into(acc_s, splits, data)
        return carry

    lax.fori_loop(0, SENDERS // GROUP, halo, 0)
    extra = ret_ref[0, BLOCK:SLOTS].astype(F32)
    for s in range(1, SENDERS):
        extra += ret_ref[s, BLOCK:SLOTS].astype(F32)
    high = extra.astype(BF16)
    data = jnp.concatenate([high, (extra - high.astype(F32)).astype(BF16)], axis=0)
    mine = jnp.broadcast_to(mine_columns(gid_ref[...], me_ref[0]), (EXTRA, NODES_HERE))
    hot = (mine == iota((EXTRA, NODES_HERE), 1)).astype(F32)
    hot = jnp.concatenate([hot, hot], axis=0).T.astype(BF16)
    acc_s[...] += dot(hot, data)


def add_partners(acc_s, parts, others, first_col):
    for m, (part, other) in enumerate(zip(parts, others)):
        turned = turned_weights(part)
        index_low = other[NODES_HERE + m * Q_BLOCKS : NODES_HERE + (m + 1) * Q_BLOCKS, :COLS]
        index_high = other[NODES_HERE + m * Q_BLOCKS : NODES_HERE + (m + 1) * Q_BLOCKS, COLS:]
        for t in range(Q_BLOCKS // GROUP):
            splits, data = [], []
            for u in range(GROUP):
                i = t * GROUP + u
                splits.append((index_low[i : i + 1], index_high[i : i + 1]))
                wide = dot(turned, head_picks(i))
                rows = other[i * BLOCK : (i + 1) * BLOCK, first_col : first_col + COLS].astype(F32)
                data.append((wide * rows).astype(BF16))
            scatter_into(acc_s, splits, jnp.concatenate(data, axis=0))


def feature_part(feat_ref, k):
    return pl.ds(pl.multiple_of(((feat_ref[0] + k) % 4) * COLS, COLS), COLS)


def value_back_kernel(
    me_ref, feat_ref, ownv_ref, ret_ref, ownk_ref, rows_ref, o0_ref, o1_ref, o2_ref, o3_ref, gid_ref, wq_ref, wv_ref,
    gq_ref, accv_s, acck_ref, pre_ref,
):
    others = (o0_ref, o1_ref, o2_ref, o3_ref)
    parts = [ret_ref[me_ref[0] ^ (1 << m), SLOTS:] for m in range(EXPANDERS)]
    accv_s[...] = ownv_ref[...]
    add_halo(accv_s, me_ref, ret_ref, rows_ref, gid_ref)
    add_partners(accv_s, [part[16:] for part in parts], others, COLS)
    acck_ref[...] = ownk_ref[...]
    add_partners(acck_ref, [part[:16] for part in parts], others, 0)
    grad_value = accv_s[...].astype(BF16)
    for k in range(4):
        part = feature_part(feat_ref, k)
        pre_ref[k] = dot_nt(gq_ref[...], wq_ref[part, :]) + dot_nt(grad_value, wv_ref[part, :])


def key_back_kernel(
    me_ref, feat_ref, acck_ref, ret_ref, rows_ref, gid_ref, wk_ref, pre_ref, t0_ref, t1_ref, t2_ref, t3_ref, acc_s
):
    acc_s[...] = acck_ref[...]
    add_halo(acc_s, me_ref, ret_ref, rows_ref, gid_ref)
    grad_key = acc_s[...].astype(BF16)
    for k, out in ((1, t1_ref), (2, t2_ref), (3, t3_ref), (0, t0_ref)):
        out[...] = (pre_ref[k] + dot_nt(grad_key, wk_ref[feature_part(feat_ref, k), :])).astype(out.dtype)


def shape(dims, kind=BF16):
    return jax.ShapeDtypeStruct(dims, kind)


def call(kernel, ins, outs, args, scratch=(), name=None, flops=0, out_spaces=None, aliases={}):
    cost = pl.CostEstimate(flops=flops, transcendentals=0, bytes_accessed=4_000_000)
    return pl.pallas_call(
        kernel,
        out_shape=outs,
        in_specs=ins,
        out_specs=out_spaces or tuple(vmem() for _ in outs),
        scratch_shapes=list(scratch),
        compiler_params=params(),
        cost_estimate=cost,
        input_output_aliases=aliases,
        name=name,
    )(*args)


def blocks_of(kind):
    return pltpu.VMEM((KEY_BLOCKS, BLOCK, COLS), kind)


def run_project(me, features, w_query, w_key, w_value, cotangent, rows, exp_list, gids):
    return call(
        project_kernel,
        [smem()] + [vmem()] * 8,
        (
            shape((NODES_HERE, COLS)),
            shape((NODES_HERE, COLS)),
            shape((NODES_HERE, COLS)),
            shape((SENDERS, SLOTS, COLS)),
            shape((SENDERS, SLOTS, COLS)),
            shape((NODES_HERE + EXPANDERS * Q_BLOCKS, 2 * COLS)),
            shape((1,), jnp.int32),
        ),
        (me, features, w_query, w_key, w_value, cotangent, rows, exp_list, gids),
        name="project",
        flops=3_000_000_000,
        out_spaces=(*(vmem() for _ in range(6)), smem()),
        scratch=[pltpu.VMEM((NODES_HERE, 2 * COLS), BF16)],
    )


def run_plan(block_mask, halo_count):
    return call(
        plan_kernel,
        [smem()] * 2,
        (shape((Q_BLOCKS * LIST,), jnp.int32), shape((Q_BLOCKS,), jnp.int32), shape((LIST,), jnp.int32)),
        (block_mask.reshape(-1), halo_count.reshape(-1)),
        name="plan",
        out_spaces=(smem(), smem(), smem()),
    )


def run_partner_keys(exp_rows, swaps, query):
    return call(
        partner_key_kernel,
        [vmem()] * 6,
        (shape((EXPANDERS * Q_BLOCKS, BLOCK, COLS)), shape((EXPANDERS, Q_BLOCKS, 2 * BLOCK), F32)),
        (exp_rows, *swaps, query),
        name="partners",
        flops=5_000_000_000,
    )


def run_finish(me, exp_rows, swaps, cotangent, out_t, scores, lse, local, back_v):
    anywhere = pl.BlockSpec(memory_space=pl.ANY)
    return call(
        finish_kernel,
        [smem()] + [vmem()] * 10 + [anywhere],
        (
            shape((NODES_HERE, COLS)),
            shape((EXPANDERS, PART_ROWS, BLOCK)),
            shape((Q_BLOCKS, 2 * BLOCK), F32),
            shape((SENDERS, BACK, COLS)),
        ),
        (me, exp_rows, *swaps, cotangent, out_t, scores, lse, local, back_v),
        name="finish",
        flops=5_000_000_000,
        out_spaces=(vmem(), vmem(), vmem(), anywhere),
        scratch=[pltpu.SemaphoreType.DMA((EXPANDERS,))],
        aliases={11: 3},
    )


def run_prepare(query, cotangent):
    wide, high = shape((Q_BLOCKS, COLS, 2 * BLOCK)), shape((Q_BLOCKS, 2 * BLOCK, COLS))
    return call(
        prepare_kernel, [vmem()] * 2, (wide, high, wide, high), (query, cotangent), name="prepare", flops=2_000_000_000
    )


def run_scores(plan, turned_q, own, halo_k, gids, glob):
    return call(
        score_kernel,
        [smem()] * 3 + [vmem()] * 5,
        (
            shape((Q_BLOCKS, 2 * BLOCK), F32),
            shape((KEY_BLOCKS, BLOCK, COLS)),
            shape((KEY_BLOCKS, COLS, BLOCK)),
        ),
        (*plan, turned_q, own, halo_k, gids, glob),
        name="scores",
        flops=12_000_000_000,
    )


def run_turn(own, halo_v, gids, glob):
    return call(
        turn_kernel,
        [vmem()] * 4,
        (shape((KEY_BLOCKS, BLOCK, COLS)), shape((KEY_BLOCKS, COLS, BLOCK))),
        (own, halo_v, gids, glob),
        name="turn",
        flops=2_000_000_000,
    )


def run_values(plan, keys, turned_v, prepared, part, scores, gids):
    turned_q, _, turned_cot, cot_stack = prepared
    return call(
        value_kernel,
        [smem()] * 3 + [vmem()] * 8,
        (
            shape((NODES_HERE, COLS), F32),
            shape((SENDERS, BACK, COLS)),
            shape((BLOCK, COLS)),
            shape((Q_BLOCKS, COLS, 2 * BLOCK), F32),
            shape((Q_BLOCKS, 2 * BLOCK), F32),
            shape((Q_BLOCKS, 2 * BLOCK), F32),
        ),
        (*plan, keys, turned_v, turned_q, turned_cot, cot_stack, part, scores, gids),
        scratch=[blocks_of(F32)],
        name="values",
        flops=20_000_000_000,
    )


def run_keys(plan, keys, turned_k, values, prepared, lse, delta, back, pairs, gids):
    turned_q, q_stack, turned_cot, _ = prepared
    return call(
        key_kernel,
        [smem()] * 3 + [vmem()] * 11,
        (
            shape((NODES_HERE, COLS)),
            shape((NODES_HERE, COLS), F32),
            shape((SENDERS, SLOTS, COLS)),
            shape((BLOCK, COLS)),
        ),
        (*plan, keys, turned_k, values, turned_q, q_stack, turned_cot, lse, delta, back, pairs, gids),
        scratch=[blocks_of(F32), pltpu.VMEM((Q_BLOCKS, COLS, 2 * BLOCK), F32)],
        name="keys",
        flops=25_000_000_000,
    )


def run_value_back(me, feat, own_v, returned_v, own_k, rows, others, gids, w_query, w_value, grad_query):
    return call(
        value_back_kernel,
        [smem()] * 2 + [vmem()] * 12,
        (shape((NODES_HERE, COLS), F32), shape((NODES_HERE, COLS), F32), shape((4, NODES_HERE, COLS), F32)),
        (me, feat, own_v, returned_v, own_k, rows, *others, gids, w_query, w_value, grad_query),
        name="value_back",
        flops=12_000_000_000,
    )[1:]


def run_key_back(me, feat, own_k, returned_k, rows, gids, w_key, pre):
    return call(
        key_back_kernel,
        [smem()] * 2 + [vmem()] * 6,
        (shape((NODES_HERE, COLS), F32),) + tuple(shape((NODES_HERE, COLS)) for _ in range(3)),
        (me, feat, own_k, returned_k, rows, gids, w_key, pre),
        scratch=[pltpu.VMEM((NODES_HERE, COLS), F32)],
        name="key_back",
        flops=8_000_000_000,
    )


def ranks(global_ids):
    owner = global_ids // NODES_HERE
    ids = jnp.arange(BLOCK)
    return owner, ((owner[:, None] == owner[None, :]) & (ids[None, :] < ids[:, None])).sum(1)


def more_globals(rounds, global_ids, my_index, own_k, own_v):
    def body(state):
        r, glob = state
        owner, rank = ranks(global_ids)
        slot = rank - r * EXTRA
        here = (slot >= 0) & (slot < EXTRA)
        place = jnp.where((owner == my_index) & here, slot, EXTRA)
        local = jnp.where(here, global_ids % NODES_HERE, 0)
        found = jnp.concatenate([own_k[local], own_v[local]], axis=1)
        rows = jnp.zeros((EXTRA + 1, 2 * COLS), BF16).at[place].set(found)[:EXTRA]
        got = lax.all_to_all(jnp.broadcast_to(rows[None], (SENDERS, *rows.shape)), "dom", 0, 0, tiled=True)
        found = got.reshape(SENDERS * EXTRA, -1)[jnp.clip(owner * EXTRA + slot, 0, SENDERS * EXTRA - 1)]
        return r + 1, jnp.where(here[:, None], found, glob)

    start = (jnp.asarray(1, jnp.int32), jnp.zeros((BLOCK, 2 * COLS), BF16))
    return lax.while_loop(lambda state: state[0] < rounds, body, start)[1]


def more_grads(rounds, global_ids, my_index, part_k, part_v, own_k, own_v):
    def body(state):
        r, own_k, own_v = state
        owner, rank = ranks(global_ids)
        slot = rank - r * EXTRA
        here = (slot >= 0) & (slot < EXTRA)
        part = jnp.concatenate([part_k, part_v], axis=1)
        place = jnp.where(here, owner * EXTRA + slot, SENDERS * EXTRA)
        rows = jnp.zeros((SENDERS * EXTRA + 1, part.shape[1]), BF16).at[place].set(part)[: SENDERS * EXTRA]
        got = lax.all_to_all(rows.reshape(SENDERS, EXTRA, -1), "dom", 0, 0, tiled=True).astype(F32).sum(0)
        take = (owner == my_index) & here
        add = jnp.where(take[:, None], got[jnp.clip(slot, 0, EXTRA - 1)], 0.0)
        local = global_ids % NODES_HERE
        return r + 1, own_k.at[local].add(add[:, :COLS]), own_v.at[local].add(add[:, COLS:])

    start = (jnp.asarray(1, jnp.int32), own_k, own_v)
    return lax.while_loop(lambda state: state[0] < rounds, body, start)[1:]


def on_device(
    features,
    w_query,
    w_key,
    w_value,
    cotangent,
    send_rows,
    halo_count,
    block_mask,
    exp_rows,
    global_ids,
):
    dom_count = lax.axis_size("dom")
    my_index = lax.axis_index("dom")

    def swapped(value, bit):
        return lax.ppermute(value, "dom", [(i, i ^ (1 << bit)) for i in range(dom_count)])

    rows = send_rows[0]
    gids = global_ids.reshape(1, BLOCK)
    me = my_index.reshape(1).astype(jnp.int32)
    feat = lax.axis_index("feat").reshape(1).astype(jnp.int32)

    query, own_keys, own_values, out_k, out_v, away, rounds = run_project(
        me, features, w_query, w_key, w_value, cotangent, rows, exp_rows, gids
    )
    rounds = rounds[0]
    glob = more_globals(rounds, global_ids, my_index, own_keys, own_values)
    out_k, out_v, glob = lax.optimization_barrier((out_k, out_v, glob))
    halo_k = lax.all_to_all(out_k, "dom", 0, 0, tiled=True)
    key_swaps = [swapped(own_keys, m) for m in range(EXPANDERS)]
    plan = run_plan(block_mask, halo_count)
    prepared = run_prepare(query, cotangent)
    halo_v = lax.all_to_all(out_v, "dom", 0, 0, tiled=True)
    part, keys, turned_k = run_scores(plan, prepared[0], own_keys, halo_k, gids, glob)
    own_values_late, part = lax.optimization_barrier((own_values, part))
    part, *key_swaps = lax.optimization_barrier((part, *key_swaps))
    value_swaps = [swapped(own_values_late, m) for m in range(EXPANDERS)]
    pairs, scores = run_partner_keys(exp_rows, key_swaps, query)
    values, turned_v = run_turn(own_values, halo_v, gids, glob)
    away, scores = lax.optimization_barrier((away, scores))
    others = [swapped(away, m) for m in range(EXPANDERS)]
    own_v, back_v, glob_v, out_t, local, lse = run_values(plan, keys, turned_v, prepared, part, scores, gids)
    out_t, *value_swaps = lax.optimization_barrier((out_t, *value_swaps))
    attended, back, delta, back_v = run_finish(
        me, exp_rows, value_swaps, cotangent, out_t, scores, lse, local, back_v
    )
    returned_v = lax.all_to_all(back_v, "dom", 0, 0, tiled=True)
    grad_query, own_k, back_k, glob_k = run_keys(
        plan, keys, turned_k, values, prepared, lse, delta, back, pairs, gids
    )
    own_k, returned_v, *others = lax.optimization_barrier((own_k, returned_v, *others))
    own_k, own_v = more_grads(rounds, global_ids, my_index, glob_k, glob_v, own_k, own_v)
    back_k, own_k, own_v = lax.optimization_barrier((back_k, own_k, own_v))
    returned_k = lax.all_to_all(back_k, "dom", 0, 0, tiled=True)
    own_k, pre = run_value_back(
        me, feat, own_v, returned_v, own_k, rows, others, gids, w_query, w_value, grad_query
    )
    mine, *away = run_key_back(me, feat, own_k, returned_k, rows, gids, w_key, pre)
    for k, term in enumerate(away, 1):
        mine = mine + lax.ppermute(term, "feat", [(i, (i + k) % 4) for i in range(4)]).astype(F32)
    return (attended, mine.astype(BF16))


def solution(mesh):
    return jax.shard_map(
        on_device,
        mesh=mesh,
        in_specs=(
            P("dom", None),
            P(None, "feat"),
            P(None, "feat"),
            P(None, "feat"),
            P("dom", "feat"),
            P("dom", None, None),
            P(None, "dom"),
            P("dom", None),
            P(None, "dom"),
            P(),
        ),
        out_specs=(P("dom", "feat"), P("dom", "feat")),
        check_vma=False,
    )
```

```python
import functools
import math

import jax
import jax.numpy as jnp
from jax import lax
from jax.experimental import pallas as pl
from jax.experimental.pallas import tpu as pltpu
from jax.sharding import PartitionSpec as P

HEAD = 64
BLOCK = 128
EXPANDERS = 4
COLS = 128
NODES_HERE = 1024
Q_BLOCKS = NODES_HERE // BLOCK
SENDERS = 32
GLOBAL_BLOCK = Q_BLOCKS + SENDERS
EMPTY_BLOCK = GLOBAL_BLOCK + 1
KEY_BLOCKS = EMPTY_BLOCK + 1
GROUP = 8
PAIR = 4
LIST = 56
EXTRA = 16
SLOTS = BLOCK + EXTRA
PART_ROWS = 32
BACK = SLOTS + PART_ROWS
NEG = -1e30
F32 = jnp.float32
BF16 = jnp.bfloat16


def params(mib):
    return pltpu.CompilerParams(vmem_limit_bytes=mib * 1024 * 1024)


def vmem():
    return pl.BlockSpec(memory_space=pltpu.VMEM)


def smem():
    return pl.BlockSpec(memory_space=pltpu.SMEM)


def iota(shape, dim):
    return lax.broadcasted_iota(jnp.int32, shape, dim)


def dot(a, b):
    return jnp.dot(a, b, preferred_element_type=F32)


def dot_nt(a, b):
    return lax.dot_general(a, b, (((1,), (1,)), ((), ())), preferred_element_type=F32)


def split_index(index):
    return (index & (BLOCK - 1)).astype(F32).astype(BF16), (index >> 7).astype(F32).astype(BF16)


def packed_iota(dim):
    return iota((BLOCK, BLOCK), dim).astype(F32).astype(BF16)


def one_hot_columns(column):
    low, high = split_index(column)
    lanes = jnp.concatenate([packed_iota(1)] * (column.shape[0] // BLOCK), axis=0)
    one, zero = jnp.ones((), BF16), jnp.zeros((), BF16)
    base = jnp.where(low == lanes, one, zero)
    return jnp.concatenate(
        [jnp.where(high == jnp.asarray(c, BF16), base, zero) for c in range(NODES_HERE // BLOCK)], axis=1
    )


def one_hot_of_rows(index_rows):
    columns = [jnp.broadcast_to(row, (BLOCK, BLOCK)).T for row in index_rows]
    return one_hot_columns(jnp.concatenate(columns, axis=0))


def owner_ranks(gid_row):
    owner = jnp.broadcast_to(gid_row >> 10, (BLOCK, BLOCK))
    owner_t = owner.T
    same = owner == owner_t
    subs, lanes = iota((BLOCK, BLOCK), 0), iota((BLOCK, BLOCK), 1)
    row = jnp.sum(jnp.where(jnp.logical_and(same, subs < lanes), 1.0, 0.0), axis=0, keepdims=True)
    col = jnp.sum(jnp.where(jnp.logical_and(same, lanes < subs), 1.0, 0.0), axis=1, keepdims=True)
    row, col = row.astype(jnp.int32), jnp.broadcast_to(col, (BLOCK, BLOCK)).astype(jnp.int32)
    slot_row = jnp.where(row < EXTRA, (gid_row >> 10) * EXTRA + row, -1)
    slot_col = jnp.where(col < EXTRA, owner_t * EXTRA + col, -1)
    return row, slot_row, slot_col


def mine_columns(gid_row, me):
    row, _, _ = owner_ranks(gid_row)
    mine = (gid_row >> 10) == me
    slots = iota((EXTRA, BLOCK), 0)
    hit = jnp.logical_and(jnp.broadcast_to(mine, (EXTRA, BLOCK)), slots == row)
    local = jnp.broadcast_to(gid_row & (NODES_HERE - 1), (EXTRA, BLOCK)) + 1
    return jnp.sum(jnp.where(hit, local, 0).astype(F32), axis=1, keepdims=True).astype(jnp.int32) - 1


def exp_row(exp_ref, m, i):
    return exp_ref[m : m + 1, i * BLOCK : (i + 1) * BLOCK]


def project_kernel(
    me_ref, x_ref, wq_ref, wk_ref, wv_ref, cot_ref, rows_ref, exp_ref, gid_ref, q_ref, k_ref, v_ref, outk_ref, outv_ref,
    away_ref, rounds_ref, kv_ref,
):
    most = jnp.max(owner_ranks(gid_ref[...])[0].astype(F32)).astype(jnp.int32)
    rounds_ref[0] = (most + EXTRA) // EXTRA
    x = x_ref[...]
    keys = dot(x, wk_ref[...]).astype(BF16)
    values = dot(x, wv_ref[...]).astype(BF16)
    k_ref[...] = keys
    v_ref[...] = values
    kv_ref[:, :COLS] = keys
    kv_ref[:, COLS:] = values
    query = (dot(x, wq_ref[...]).astype(BF16).astype(F32) * (1.0 / math.sqrt(HEAD))).astype(BF16)
    q_ref[...] = query
    away_ref[:NODES_HERE, :COLS] = query
    away_ref[:NODES_HERE, COLS:] = cot_ref[...]
    for m in range(EXPANDERS):
        low, high = split_index(jnp.concatenate([exp_row(exp_ref, m, i) for i in range(Q_BLOCKS)], axis=0))
        away_ref[NODES_HERE + m * Q_BLOCKS : NODES_HERE + (m + 1) * Q_BLOCKS, :COLS] = low
        away_ref[NODES_HERE + m * Q_BLOCKS : NODES_HERE + (m + 1) * Q_BLOCKS, COLS:] = high
    mine = jnp.broadcast_to(mine_columns(gid_ref[...], me_ref[0]), (EXTRA, BLOCK))
    lanes = iota((EXTRA, NODES_HERE), 1)
    hot = (jnp.concatenate([mine] * (NODES_HERE // BLOCK), axis=1) == lanes).astype(F32).astype(BF16)
    extra = dot(hot, kv_ref[...]).astype(BF16)

    def gather(t, carry):
        hot = one_hot_of_rows([rows_ref[pl.ds(t * GROUP + u, 1), :] for u in range(GROUP)])
        got = dot(hot, kv_ref[...]).astype(BF16)
        for u in range(GROUP):
            outk_ref[t * GROUP + u, :BLOCK] = got[u * BLOCK : (u + 1) * BLOCK, :COLS]
            outv_ref[t * GROUP + u, :BLOCK] = got[u * BLOCK : (u + 1) * BLOCK, COLS:]
            outk_ref[t * GROUP + u, BLOCK:] = extra[:, :COLS]
            outv_ref[t * GROUP + u, BLOCK:] = extra[:, COLS:]
        return carry

    lax.fori_loop(0, SENDERS // GROUP, gather, 0)


def gather_partner(exp_ref, m, table):
    blocks = []
    for t in range(0, Q_BLOCKS, 4):
        hot = one_hot_of_rows([exp_row(exp_ref, m, t + u) for u in range(4)])
        got = dot(hot, table[...]).astype(BF16)
        blocks += [got[u * BLOCK : (u + 1) * BLOCK] for u in range(4)]
    return blocks


def sum_picks():
    sub = iota((2 * Q_BLOCKS * COLS, 16), 0)
    col = iota((2 * Q_BLOCKS * COLS, 16), 1)
    return (col == (sub >> 8) + jnp.where((sub & (COLS - 1)) < HEAD, 0, 8)).astype(F32).astype(BF16)


def head_sums(a_ref, blocks, picks):
    parts = []
    for i, b in enumerate(blocks):
        prod = a_ref[i * BLOCK : (i + 1) * BLOCK, :].astype(F32) * b.astype(F32)
        high = prod.astype(BF16)
        parts += [high, (prod - high.astype(F32)).astype(BF16)]
    return flat(dot(jnp.concatenate(parts, axis=1), picks).T)


def partner_key_kernel(exp_ref, t0_ref, t1_ref, t2_ref, t3_ref, q_ref, out_ref, sp_ref):
    picks = sum_picks()
    for m, table in enumerate((t0_ref, t1_ref, t2_ref, t3_ref)):
        blocks = gather_partner(exp_ref, m, table)
        for i, block in enumerate(blocks):
            out_ref[m * Q_BLOCKS + i] = block
        sp_ref[m] = head_sums(q_ref, blocks, picks)


def head_picks(i):
    return (iota((16, COLS), 0) == jnp.where(iota((16, COLS), 1) < HEAD, i, 8 + i)).astype(F32).astype(BF16)


def finish_kernel(
    me_ref, exp_ref, t0_ref, t1_ref, t2_ref, t3_ref, cot_ref, sp_ref, lse_ref, local_ref, _, pair_ref, back_ref,
    delta_ref, message_ref, sems,
):
    picks = sum_picks()
    lse = lse_ref[...]
    delta = local_ref[...]
    probs, dprobs = [], []
    for m, table in enumerate((t0_ref, t1_ref, t2_ref, t3_ref)):
        blocks = gather_partner(exp_ref, m, table)
        prob = jnp.exp(sp_ref[m] - lse)
        dprob = head_sums(cot_ref, blocks, picks)
        delta += prob * dprob
        back_ref[m, 16:] = tall(prob).astype(BF16)
        for i, block in enumerate(blocks):
            pair_ref[m * Q_BLOCKS + i] = block
        probs.append(prob)
        dprobs.append(dprob)
    delta_ref[...] = delta
    for m in range(EXPANDERS):
        back_ref[m, :16] = tall(probs[m] * (dprobs[m] - delta)).astype(BF16)
    copies = [
        pltpu.make_async_copy(
            back_ref.at[m], message_ref.at[me_ref[0] ^ (1 << m), pl.ds(SLOTS, PART_ROWS)], sems.at[m]
        )
        for m in range(EXPANDERS)
    ]
    for copy in copies:
        copy.start()
    for copy in copies:
        copy.wait()


def join_partners(out_ref, out_t_ref, part_rows, pair_ref, scale):
    turned = [turned_weights(rows) for rows in part_rows]
    for i in range(Q_BLOCKS):
        total = head_rows(out_t_ref[i]).T
        for m in range(EXPANDERS):
            total += dot(turned[m], head_picks(i)) * pair_ref[m * Q_BLOCKS + i].astype(F32)
        out_ref[i * BLOCK : (i + 1) * BLOCK, :] = (total * scale).astype(BF16)


def attend_kernel(out_t_ref, back_ref, pair_ref, att_ref):
    join_partners(att_ref, out_t_ref, [back_ref[m, 16:] for m in range(EXPANDERS)], pair_ref, 1.0)


def flat(x):
    return jnp.concatenate([x[:8], x[8:]], axis=1)


def tall(x):
    return jnp.concatenate([x[:, :BLOCK], x[:, BLOCK:]], axis=0)


def turned_weights(tall_rows):
    return tall_rows.astype(F32).T.astype(BF16)


def prepare_kernel(q_ref, cot_ref, qt_ref, qs_ref, ct_ref, cs_ref):
    def one(i, carry):
        q = q_ref[q_rows(i), :]
        cot = cot_ref[q_rows(i), :]
        qt_ref[i] = stacked_t(q)
        qs_ref[i] = stacked(q)
        ct_ref[i] = stacked_t(cot)
        cs_ref[i] = stacked(cot)
        return carry

    lax.fori_loop(0, Q_BLOCKS, one, 0, unroll=2)


def plan_kernel(mask_ref, count_ref, list_ref, groups_ref, tail_ref, live_ref):
    for j in range(Q_BLOCKS):
        live_ref[j] = BLOCK
    live_ref[GLOBAL_BLOCK] = BLOCK
    live_ref[EMPTY_BLOCK] = 0

    def copy_count(s, carry):
        live_ref[Q_BLOCKS + s] = count_ref[s]
        return carry

    lax.fori_loop(0, SENDERS, copy_count, 0)

    def per_block(i, carry):
        list_ref[i * LIST] = GLOBAL_BLOCK

        def put(j, n):
            list_ref[i * LIST + n] = j
            used = jnp.logical_and(mask_ref[i * GLOBAL_BLOCK + j] > 0, live_ref[j] > 0)
            return n + used.astype(jnp.int32)

        n = lax.fori_loop(0, GLOBAL_BLOCK, put, 1)
        for extra in range(GROUP):
            list_ref[i * LIST + n + extra] = EMPTY_BLOCK
        groups_ref[i] = (n + PAIR - 1) // GROUP
        tail_ref[i] = jnp.logical_and(n % GROUP > 0, n % GROUP <= PAIR).astype(jnp.int32)
        return carry

    lax.fori_loop(0, Q_BLOCKS, per_block, 0)


def fill(dst, dst_t, first_col, own_ref, halo_ref, gid_ref, glob_ref):
    def own(j, carry):
        block = own_ref[q_rows(j), :]
        dst[j] = block
        dst_t[j] = block.T
        return carry

    def halo(j, carry):
        block = halo_ref[j, :BLOCK]
        dst[Q_BLOCKS + j] = block
        dst_t[Q_BLOCKS + j] = block.T
        return carry

    lax.fori_loop(0, Q_BLOCKS, own, 0, unroll=4)
    lax.fori_loop(0, SENDERS, halo, 0, unroll=4)
    slot_col = owner_ranks(gid_ref[...])[2]
    wide = jnp.concatenate([slot_col] * (SENDERS * EXTRA // BLOCK), axis=1)
    hot = (wide == iota((BLOCK, SENDERS * EXTRA), 1)).astype(F32).astype(BF16)
    extra = jnp.concatenate([halo_ref[s, BLOCK:] for s in range(SENDERS)], axis=0)
    rows = (dot(hot, extra) + glob_ref[:, first_col : first_col + COLS].astype(F32)).astype(BF16)
    dst[GLOBAL_BLOCK] = rows
    dst_t[GLOBAL_BLOCK] = rows.T
    dst[EMPTY_BLOCK] = jnp.zeros((BLOCK, COLS), BF16)
    dst_t[EMPTY_BLOCK] = jnp.zeros((BLOCK, COLS), BF16)


def turn_kernel(own_ref, hv_ref, gid_ref, glob_ref, v_ref, vt_ref):
    fill(v_ref, vt_ref, COLS, own_ref, hv_ref, gid_ref, glob_ref)


def stacked(rows):
    lanes = iota((BLOCK, COLS), 1)
    zero = jnp.zeros_like(rows)
    return jnp.concatenate([jnp.where(lanes < HEAD, rows, zero), jnp.where(lanes < HEAD, zero, rows)], axis=0)


def stacked_t(rows):
    turned = rows.T
    subs = iota((COLS, BLOCK), 0)
    zero = jnp.zeros_like(turned)
    return jnp.concatenate([jnp.where(subs < HEAD, turned, zero), jnp.where(subs < HEAD, zero, turned)], axis=1)


def head_rows(turned):
    return jnp.concatenate([turned[:HEAD, :BLOCK], turned[HEAD:, BLOCK:]], axis=0)


def masked_scores(blocks, k_s, turned_q, live_ref):
    keys = jnp.concatenate([k_s[b] for b in blocks], axis=0)
    scores = dot(keys, turned_q)
    row_id = iota((BLOCK, 2 * BLOCK), 0)
    return jnp.concatenate(
        [
            jnp.where(row_id < live_ref[b], scores[u * BLOCK : (u + 1) * BLOCK], NEG)
            for u, b in enumerate(blocks)
        ],
        axis=0,
    )


def block_ids(list_ref, i, g, size):
    return [list_ref[i * LIST + g * GROUP + u] for u in range(size)]


def q_rows(i):
    return pl.ds(pl.multiple_of(i * BLOCK, BLOCK), BLOCK)


def score_kernel(
    list_ref, groups_ref, tail_ref, live_ref, qt_ref, own_ref, hk_ref, gid_ref, glob_ref, lse_ref, k_s, kt_ref
):
    fill(k_s, kt_ref, 0, own_ref, hk_ref, gid_ref, glob_ref)

    def per_block(i, carry):
        turned_q = qt_ref[i]

        def step(size, g, state):
            blocks = block_ids(list_ref, i, g, size)
            new_state = []
            for u in range(size // PAIR):
                top, total = state[u]
                scores = masked_scores(blocks[u * PAIR : (u + 1) * PAIR], k_s, turned_q, live_ref)
                scores = scores.reshape(PAIR * BLOCK // 8, 8, 2 * BLOCK)
                new_top = jnp.maximum(top, jnp.max(scores, axis=0))
                total = total * jnp.exp(top - new_top) + jnp.sum(jnp.exp(scores - new_top[None]), axis=0)
                new_state.append((new_top, total))
            return tuple(new_state) + tuple(state[size // PAIR :])

        init = (jnp.full((8, 2 * BLOCK), NEG, F32), jnp.zeros((8, 2 * BLOCK), F32))
        state = tuple(init for _ in range(GROUP // PAIR))
        state = lax.fori_loop(0, groups_ref[i], functools.partial(step, GROUP), state)
        state = lax.fori_loop(groups_ref[i], groups_ref[i] + tail_ref[i], functools.partial(step, PAIR), state)
        top = jnp.concatenate([t for t, _ in state], axis=0)
        total = jnp.concatenate([t for _, t in state], axis=0)
        best = jnp.max(top, axis=0, keepdims=True)
        denominator = jnp.sum(total * jnp.exp(top - best), axis=0, keepdims=True)
        lse_ref[pl.ds(i, 1), :] = best + jnp.log(denominator)
        return carry

    lax.fori_loop(0, Q_BLOCKS, per_block, 0)


def value_kernel(
    list_ref, groups_ref, tail_ref, live_ref, k_s, vt_s, qt_ref, ct_ref, cs_ref, part_ref, sp_ref, gid_ref,
    own_ref, halo_ref, gout_ref, out_s, delta_ref, lse_ref, acc_s,
):
    clear_blocks(acc_s)
    part = part_ref[...]
    best = part
    for m in range(EXPANDERS):
        best = jnp.maximum(best, sp_ref[m])
    total = jnp.exp(part - best)
    for m in range(EXPANDERS):
        total += jnp.exp(sp_ref[m] - best)
    lse_ref[...] = best + jnp.log(total)

    def per_block(i, carry):
        turned_q = qt_ref[i]
        cot_stack = cs_ref[i]
        lse = lse_ref[pl.ds(i, 1), :]
        out_s[i] = jnp.zeros((COLS, 2 * BLOCK), F32)

        def step(size, g, carry):
            blocks = block_ids(list_ref, i, g, size)
            total = None
            for u in range(0, size, PAIR):
                pair = blocks[u : u + PAIR]
                scores = masked_scores(pair, k_s, turned_q, live_ref)
                weight = jnp.exp(scores - lse).astype(BF16)
                term = dot(jnp.concatenate([vt_s[b] for b in pair], axis=1), weight)
                total = term if total is None else total + term
                grads = dot(weight, cot_stack)
                for w, b in enumerate(pair):
                    acc_s[b] += grads[w * BLOCK : (w + 1) * BLOCK]
            out_s[i] += total
            return carry

        lax.fori_loop(0, groups_ref[i], functools.partial(step, GROUP), 0)
        lax.fori_loop(groups_ref[i], groups_ref[i] + tail_ref[i], functools.partial(step, PAIR), 0)
        delta_ref[pl.ds(i, 1), :] = jnp.sum(out_s[i] * ct_ref[i].astype(F32), axis=0, keepdims=True)
        return carry

    lax.fori_loop(0, Q_BLOCKS, per_block, 0)
    store_parts(acc_s, own_ref, halo_ref, gid_ref, gout_ref)


def clear_blocks(acc_s):
    def clear(j, carry):
        acc_s[j] = jnp.zeros((BLOCK, COLS), F32)
        return carry

    lax.fori_loop(0, KEY_BLOCKS, clear, 0, unroll=2)


def store_parts(acc_s, own_ref, halo_ref, gid_ref, gout_ref):
    def own(j, carry):
        own_ref[q_rows(j), :] = acc_s[j]
        return carry

    def halo(j, carry):
        halo_ref[j, :BLOCK] = acc_s[Q_BLOCKS + j].astype(BF16)
        return carry

    lax.fori_loop(0, Q_BLOCKS, own, 0, unroll=2)
    lax.fori_loop(0, SENDERS, halo, 0, unroll=4)
    grads = acc_s[GLOBAL_BLOCK].astype(BF16)
    gout_ref[...] = grads
    slot_row = owner_ranks(gid_ref[...])[1]
    hot = (iota((SENDERS * EXTRA, BLOCK), 0) == slot_row).astype(F32).astype(BF16)
    extra = dot(hot, grads).astype(BF16)
    for s in range(SENDERS):
        halo_ref[s, BLOCK:SLOTS] = extra[s * EXTRA : (s + 1) * EXTRA]


def key_kernel(
    list_ref, groups_ref, tail_ref, live_ref, k_s, kt_s, v_s, qt_ref, qs_ref, ct_ref, lse_ref, delta_ref, gid_ref,
    out_s, own_ref, halo_ref, gout_ref, acc_s,
):
    clear_blocks(acc_s)

    def per_block(i, carry):
        turned_q = qt_ref[i]
        q_stack = qs_ref[i]
        turned_cot = ct_ref[i]
        lse = lse_ref[pl.ds(i, 1), :]
        delta = delta_ref[pl.ds(i, 1), :]
        out_s[i] = jnp.zeros((COLS, 2 * BLOCK), F32)

        def step(size, g, carry):
            blocks = block_ids(list_ref, i, g, size)
            total = None
            for u in range(0, size, PAIR):
                pair = blocks[u : u + PAIR]
                scores = masked_scores(pair, k_s, turned_q, live_ref)
                dprob = dot(jnp.concatenate([v_s[b] for b in pair], axis=0), turned_cot)
                dscore = (jnp.exp(scores - lse) * (dprob - delta)).astype(BF16)
                term = dot(jnp.concatenate([kt_s[b] for b in pair], axis=1), dscore)
                total = term if total is None else total + term
                grads = dot(dscore, q_stack)
                for w, b in enumerate(pair):
                    acc_s[b] += grads[w * BLOCK : (w + 1) * BLOCK]
            out_s[i] += total
            return carry

        lax.fori_loop(0, groups_ref[i], functools.partial(step, GROUP), 0)
        lax.fori_loop(groups_ref[i], groups_ref[i] + tail_ref[i], functools.partial(step, PAIR), 0)
        return carry

    lax.fori_loop(0, Q_BLOCKS, per_block, 0)
    store_parts(acc_s, own_ref, halo_ref, gid_ref, gout_ref)


def scatter_into(acc_s, splits, data):
    subs = packed_iota(0)
    one, zero = jnp.ones((), BF16), jnp.zeros((), BF16)
    bases = [(jnp.where(subs == low, one, zero), jnp.broadcast_to(high, (BLOCK, BLOCK))) for low, high in splits]
    for c in range(NODES_HERE // BLOCK):
        hot = jnp.concatenate([jnp.where(high == jnp.asarray(c, BF16), base, zero) for base, high in bases], axis=1)
        acc_s[c * BLOCK : (c + 1) * BLOCK, :] += dot(hot, data)


def add_halo(acc_s, me_ref, ret_ref, rows_ref, gid_ref):
    def halo(t, carry):
        splits = [split_index(rows_ref[pl.ds(t * GROUP + u, 1), :]) for u in range(GROUP)]
        data = jnp.concatenate([ret_ref[t * GROUP + u, :BLOCK] for u in range(GROUP)], axis=0)
        scatter_into(acc_s, splits, data)
        return carry

    lax.fori_loop(0, SENDERS // GROUP, halo, 0)
    extra = ret_ref[0, BLOCK:SLOTS].astype(F32)
    for s in range(1, SENDERS):
        extra += ret_ref[s, BLOCK:SLOTS].astype(F32)
    high = extra.astype(BF16)
    data = jnp.concatenate([high, (extra - high.astype(F32)).astype(BF16)], axis=0)
    mine = jnp.broadcast_to(mine_columns(gid_ref[...], me_ref[0]), (EXTRA, NODES_HERE))
    hot = (mine == iota((EXTRA, NODES_HERE), 1)).astype(F32)
    hot = jnp.concatenate([hot, hot], axis=0).T.astype(BF16)
    acc_s[...] += dot(hot, data)


def add_partners(acc_s, parts, others, first_col):
    for m, (part, other) in enumerate(zip(parts, others)):
        turned = turned_weights(part)
        index_low = other[NODES_HERE + m * Q_BLOCKS : NODES_HERE + (m + 1) * Q_BLOCKS, :COLS]
        index_high = other[NODES_HERE + m * Q_BLOCKS : NODES_HERE + (m + 1) * Q_BLOCKS, COLS:]
        for t in range(Q_BLOCKS // GROUP):
            splits, data = [], []
            for u in range(GROUP):
                i = t * GROUP + u
                splits.append((index_low[i : i + 1], index_high[i : i + 1]))
                wide = dot(turned, head_picks(i))
                rows = other[i * BLOCK : (i + 1) * BLOCK, first_col : first_col + COLS].astype(F32)
                data.append((wide * rows).astype(BF16))
            scatter_into(acc_s, splits, jnp.concatenate(data, axis=0))


def feature_part(feat_ref, k):
    return pl.ds(pl.multiple_of(((feat_ref[0] + k) % 4) * COLS, COLS), COLS)


def value_back_kernel(
    me_ref, feat_ref, ownv_ref, ret_ref, ownk_ref, rows_ref, o0_ref, o1_ref, o2_ref, o3_ref, gid_ref, wq_ref, wv_ref,
    out_t_ref, back_ref, pair_ref, acck_ref, pre_ref, accv_s, gq_ref,
):
    others = (o0_ref, o1_ref, o2_ref, o3_ref)
    parts = [ret_ref[me_ref[0] ^ (1 << m), SLOTS:] for m in range(EXPANDERS)]
    join_partners(
        gq_ref, out_t_ref, [back_ref[m, :16] for m in range(EXPANDERS)], pair_ref, 1.0 / math.sqrt(HEAD)
    )
    accv_s[...] = ownv_ref[...]
    add_halo(accv_s, me_ref, ret_ref, rows_ref, gid_ref)
    add_partners(accv_s, [part[16:] for part in parts], others, COLS)
    acck_ref[...] = ownk_ref[...]
    add_partners(acck_ref, [part[:16] for part in parts], others, 0)
    grad_value = accv_s[...].astype(BF16)
    for k in range(4):
        part = feature_part(feat_ref, k)
        pre_ref[k] = dot_nt(gq_ref[...], wq_ref[part, :]) + dot_nt(grad_value, wv_ref[part, :])


def key_back_kernel(
    me_ref, feat_ref, acck_ref, ret_ref, rows_ref, gid_ref, wk_ref, pre_ref, t0_ref, t1_ref, t2_ref, t3_ref,
    acc_s, own_s, pre_s, sems,
):
    own_copy = pltpu.make_async_copy(acck_ref, own_s, sems.at[0])
    pre_copy = pltpu.make_async_copy(pre_ref, pre_s, sems.at[1])
    own_copy.start()
    pre_copy.start()
    acc_s[...] = jnp.zeros((NODES_HERE, COLS), F32)
    add_halo(acc_s, me_ref, ret_ref, rows_ref, gid_ref)
    own_copy.wait()
    grad_key = (acc_s[...] + own_s[...]).astype(BF16)
    pre_copy.wait()
    for k, out in ((1, t1_ref), (2, t2_ref), (3, t3_ref), (0, t0_ref)):
        out[...] = (pre_s[k] + dot_nt(grad_key, wk_ref[feature_part(feat_ref, k), :])).astype(out.dtype)


def shape(dims, kind=BF16):
    return jax.ShapeDtypeStruct(dims, kind)


def call(kernel, ins, outs, args, scratch=(), name=None, flops=0, out_spaces=None, aliases={}, mib=56):
    cost = pl.CostEstimate(flops=flops, transcendentals=0, bytes_accessed=4_000_000)
    return pl.pallas_call(
        kernel,
        out_shape=outs,
        in_specs=ins,
        out_specs=out_spaces or tuple(vmem() for _ in outs),
        scratch_shapes=list(scratch),
        compiler_params=params(mib),
        cost_estimate=cost,
        input_output_aliases=aliases,
        name=name,
    )(*args)


def blocks_of(kind):
    return pltpu.VMEM((KEY_BLOCKS, BLOCK, COLS), kind)


def run_project(me, features, w_query, w_key, w_value, cotangent, rows, exp_list, gids):
    return call(
        project_kernel,
        [smem()] + [vmem()] * 8,
        (
            shape((NODES_HERE, COLS)),
            shape((NODES_HERE, COLS)),
            shape((NODES_HERE, COLS)),
            shape((SENDERS, SLOTS, COLS)),
            shape((SENDERS, SLOTS, COLS)),
            shape((NODES_HERE + EXPANDERS * Q_BLOCKS, 2 * COLS)),
            shape((1,), jnp.int32),
        ),
        (me, features, w_query, w_key, w_value, cotangent, rows, exp_list, gids),
        name="project",
        mib=56,
        flops=3_000_000_000,
        out_spaces=(*(vmem() for _ in range(6)), smem()),
        scratch=[pltpu.VMEM((NODES_HERE, 2 * COLS), BF16)],
    )


def run_plan(block_mask, halo_count):
    return call(
        plan_kernel,
        [smem()] * 2,
        (
            shape((Q_BLOCKS * LIST,), jnp.int32),
            shape((Q_BLOCKS,), jnp.int32),
            shape((Q_BLOCKS,), jnp.int32),
            shape((LIST,), jnp.int32),
        ),
        (block_mask.reshape(-1), halo_count.reshape(-1)),
        name="plan",
        out_spaces=(smem(), smem(), smem(), smem()),
    )


def run_partner_keys(exp_rows, swaps, query):
    return call(
        partner_key_kernel,
        [vmem()] * 6,
        (shape((EXPANDERS * Q_BLOCKS, BLOCK, COLS)), shape((EXPANDERS, Q_BLOCKS, 2 * BLOCK), F32)),
        (exp_rows, *swaps, query),
        name="partners",
        flops=5_000_000_000,
    )


def run_finish(me, exp_rows, swaps, cotangent, scores, lse, local, back_v):
    anywhere = pl.BlockSpec(memory_space=pl.ANY)
    return call(
        finish_kernel,
        [smem()] + [vmem()] * 9 + [anywhere],
        (
            shape((EXPANDERS * Q_BLOCKS, BLOCK, COLS)),
            shape((EXPANDERS, PART_ROWS, BLOCK)),
            shape((Q_BLOCKS, 2 * BLOCK), F32),
            shape((SENDERS, BACK, COLS)),
        ),
        (me, exp_rows, *swaps, cotangent, scores, lse, local, back_v),
        name="finish",
        flops=5_000_000_000,
        out_spaces=(vmem(), vmem(), vmem(), anywhere),
        scratch=[pltpu.SemaphoreType.DMA((EXPANDERS,))],
        aliases={10: 3},
    )


def run_attend(out_t, back, value_pairs):
    return call(
        attend_kernel,
        [vmem()] * 3,
        (shape((NODES_HERE, COLS)),),
        (out_t, back, value_pairs),
        name="attend",
        flops=2_000_000_000,
    )[0]


def run_prepare(query, cotangent):
    wide, high = shape((Q_BLOCKS, COLS, 2 * BLOCK)), shape((Q_BLOCKS, 2 * BLOCK, COLS))
    return call(
        prepare_kernel, [vmem()] * 2, (wide, high, wide, high), (query, cotangent), name="prepare", flops=2_000_000_000
    )


def run_scores(plan, turned_q, own, halo_k, gids, glob):
    return call(
        score_kernel,
        [smem()] * 4 + [vmem()] * 5,
        (
            shape((Q_BLOCKS, 2 * BLOCK), F32),
            shape((KEY_BLOCKS, BLOCK, COLS)),
            shape((KEY_BLOCKS, COLS, BLOCK)),
        ),
        (*plan, turned_q, own, halo_k, gids, glob),
        name="scores",
        flops=12_000_000_000,
    )


def run_turn(own, halo_v, gids, glob):
    return call(
        turn_kernel,
        [vmem()] * 4,
        (shape((KEY_BLOCKS, BLOCK, COLS)), shape((KEY_BLOCKS, COLS, BLOCK))),
        (own, halo_v, gids, glob),
        name="turn",
        flops=2_000_000_000,
    )


def run_values(plan, keys, turned_v, prepared, part, scores, gids):
    turned_q, _, turned_cot, cot_stack = prepared
    return call(
        value_kernel,
        [smem()] * 4 + [vmem()] * 8,
        (
            shape((NODES_HERE, COLS), F32),
            shape((SENDERS, BACK, COLS)),
            shape((BLOCK, COLS)),
            shape((Q_BLOCKS, COLS, 2 * BLOCK), F32),
            shape((Q_BLOCKS, 2 * BLOCK), F32),
            shape((Q_BLOCKS, 2 * BLOCK), F32),
        ),
        (*plan, keys, turned_v, turned_q, turned_cot, cot_stack, part, scores, gids),
        scratch=[blocks_of(F32)],
        name="values",
        flops=20_000_000_000,
    )


def run_keys(plan, keys, turned_k, values, prepared, lse, delta, gids):
    turned_q, q_stack, turned_cot, _ = prepared
    return call(
        key_kernel,
        [smem()] * 4 + [vmem()] * 9,
        (
            shape((Q_BLOCKS, COLS, 2 * BLOCK), F32),
            shape((NODES_HERE, COLS), F32),
            shape((SENDERS, SLOTS, COLS)),
            shape((BLOCK, COLS)),
        ),
        (*plan, keys, turned_k, values, turned_q, q_stack, turned_cot, lse, delta, gids),
        scratch=[blocks_of(F32)],
        name="keys",
        mib=56,
        flops=25_000_000_000,
    )


def run_value_back(me, feat, own_v, returned_v, own_k, rows, others, gids, w_query, w_value, out_t, back, pairs):
    return call(
        value_back_kernel,
        [smem()] * 2 + [vmem()] * 14,
        (shape((NODES_HERE, COLS), F32), shape((4, NODES_HERE, COLS), F32)),
        (me, feat, own_v, returned_v, own_k, rows, *others, gids, w_query, w_value, out_t, back, pairs),
        scratch=[pltpu.VMEM((NODES_HERE, COLS), F32), pltpu.VMEM((NODES_HERE, COLS), BF16)],
        name="value_back",
        mib=56,
        flops=12_000_000_000,
    )


def run_key_back(me, feat, own_k, returned_k, rows, gids, w_key, pre):
    anywhere = pl.BlockSpec(memory_space=pl.ANY)
    return call(
        key_back_kernel,
        [smem()] * 2 + [anywhere] + [vmem()] * 4 + [anywhere],
        (shape((NODES_HERE, COLS), F32),) + tuple(shape((NODES_HERE, COLS)) for _ in range(3)),
        (me, feat, own_k, returned_k, rows, gids, w_key, pre),
        scratch=[
            pltpu.VMEM((NODES_HERE, COLS), F32),
            pltpu.VMEM((NODES_HERE, COLS), F32),
            pltpu.VMEM((4, NODES_HERE, COLS), F32),
            pltpu.SemaphoreType.DMA((2,)),
        ],
        name="key_back",
        mib=56,
        flops=8_000_000_000,
    )


def ranks(global_ids):
    owner = global_ids // NODES_HERE
    ids = jnp.arange(BLOCK)
    return owner, ((owner[:, None] == owner[None, :]) & (ids[None, :] < ids[:, None])).sum(1)


def more_globals(rounds, global_ids, my_index, own_k, own_v):
    def body(state):
        r, glob = state
        owner, rank = ranks(global_ids)
        slot = rank - r * EXTRA
        here = (slot >= 0) & (slot < EXTRA)
        place = jnp.where((owner == my_index) & here, slot, EXTRA)
        local = jnp.where(here, global_ids % NODES_HERE, 0)
        found = jnp.concatenate([own_k[local], own_v[local]], axis=1)
        rows = jnp.zeros((EXTRA + 1, 2 * COLS), BF16).at[place].set(found)[:EXTRA]
        got = lax.all_to_all(jnp.broadcast_to(rows[None], (SENDERS, *rows.shape)), "dom", 0, 0, tiled=True)
        found = got.reshape(SENDERS * EXTRA, -1)[jnp.clip(owner * EXTRA + slot, 0, SENDERS * EXTRA - 1)]
        return r + 1, jnp.where(here[:, None], found, glob)

    start = (jnp.asarray(1, jnp.int32), jnp.zeros((BLOCK, 2 * COLS), BF16))
    return lax.while_loop(lambda state: state[0] < rounds, body, start)[1]


def more_grads(rounds, global_ids, my_index, part_k, part_v, own_k, own_v):
    def body(state):
        r, own_k, own_v = state
        owner, rank = ranks(global_ids)
        slot = rank - r * EXTRA
        here = (slot >= 0) & (slot < EXTRA)
        part = jnp.concatenate([part_k, part_v], axis=1)
        place = jnp.where(here, owner * EXTRA + slot, SENDERS * EXTRA)
        rows = jnp.zeros((SENDERS * EXTRA + 1, part.shape[1]), BF16).at[place].set(part)[: SENDERS * EXTRA]
        got = lax.all_to_all(rows.reshape(SENDERS, EXTRA, -1), "dom", 0, 0, tiled=True).astype(F32).sum(0)
        take = (owner == my_index) & here
        add = jnp.where(take[:, None], got[jnp.clip(slot, 0, EXTRA - 1)], 0.0)
        local = global_ids % NODES_HERE
        return r + 1, own_k.at[local].add(add[:, :COLS]), own_v.at[local].add(add[:, COLS:])

    start = (jnp.asarray(1, jnp.int32), own_k, own_v)
    return lax.while_loop(lambda state: state[0] < rounds, body, start)[1:]


def on_device(
    features,
    w_query,
    w_key,
    w_value,
    cotangent,
    send_rows,
    halo_count,
    block_mask,
    exp_rows,
    global_ids,
):
    dom_count = lax.axis_size("dom")
    my_index = lax.axis_index("dom")

    def swapped(value, bit):
        return lax.ppermute(value, "dom", [(i, i ^ (1 << bit)) for i in range(dom_count)])

    rows = send_rows[0]
    gids = global_ids.reshape(1, BLOCK)
    me = my_index.reshape(1).astype(jnp.int32)
    feat = lax.axis_index("feat").reshape(1).astype(jnp.int32)

    query, own_keys, own_values, out_k, out_v, away, rounds = run_project(
        me, features, w_query, w_key, w_value, cotangent, rows, exp_rows, gids
    )
    rounds = rounds[0]
    glob = more_globals(rounds, global_ids, my_index, own_keys, own_values)
    out_k, out_v, glob = lax.optimization_barrier((out_k, out_v, glob))
    halo_k = lax.all_to_all(out_k, "dom", 0, 0, tiled=True)
    key_swaps = [swapped(own_keys, m) for m in range(EXPANDERS)]
    plan = run_plan(block_mask, halo_count)
    prepared = run_prepare(query, cotangent)
    halo_v = lax.all_to_all(out_v, "dom", 0, 0, tiled=True)
    part, keys, turned_k = run_scores(plan, prepared[0], own_keys, halo_k, gids, glob)
    own_values_late, part = lax.optimization_barrier((own_values, part))
    part, *key_swaps = lax.optimization_barrier((part, *key_swaps))
    value_swaps = [swapped(own_values_late, m) for m in range(EXPANDERS)]
    pairs, scores = run_partner_keys(exp_rows, key_swaps, query)
    values, turned_v = run_turn(own_values, halo_v, gids, glob)
    away, scores = lax.optimization_barrier((away, scores))
    others = [swapped(away, m) for m in range(EXPANDERS)]
    own_v, back_v, glob_v, out_t, local, lse = run_values(plan, keys, turned_v, prepared, part, scores, gids)
    local, *value_swaps = lax.optimization_barrier((local, *value_swaps))
    value_pairs, back, delta, back_v = run_finish(
        me, exp_rows, value_swaps, cotangent, scores, lse, local, back_v
    )
    returned_v = lax.all_to_all(back_v, "dom", 0, 0, tiled=True)
    query_t, own_k, back_k, glob_k = run_keys(plan, keys, turned_k, values, prepared, lse, delta, gids)
    own_k, returned_v, *others = lax.optimization_barrier((own_k, returned_v, *others))
    own_k, own_v = more_grads(rounds, global_ids, my_index, glob_k, glob_v, own_k, own_v)
    back_k, own_k, own_v = lax.optimization_barrier((back_k, own_k, own_v))
    returned_k = lax.all_to_all(back_k, "dom", 0, 0, tiled=True)
    own_k, pre = run_value_back(
        me, feat, own_v, returned_v, own_k, rows, others, gids, w_query, w_value, query_t, back, pairs
    )
    mine, *away = run_key_back(me, feat, own_k, returned_k, rows, gids, w_key, pre)
    out_t, mine = lax.optimization_barrier((out_t, mine))
    attended = run_attend(out_t, back, value_pairs)
    for k in (2, 1, 3):
        mine = mine + lax.ppermute(away[k - 1], "feat", [(i, (i + k) % 4) for i in range(4)]).astype(F32)
    return (attended, mine.astype(BF16))


def solution(mesh):
    return jax.shard_map(
        on_device,
        mesh=mesh,
        in_specs=(
            P("dom", None),
            P(None, "feat"),
            P(None, "feat"),
            P(None, "feat"),
            P("dom", "feat"),
            P("dom", None, None),
            P(None, "dom"),
            P("dom", None),
            P(None, "dom"),
            P(),
        ),
        out_specs=(P("dom", "feat"), P("dom", "feat")),
        check_vma=False,
    )
```

```python
import functools
import math

import jax
import jax.numpy as jnp
from jax import lax
from jax.experimental import pallas as pl
from jax.experimental.pallas import tpu as pltpu
from jax.sharding import PartitionSpec as P

HEAD = 64
BLOCK = 128
EXPANDERS = 4
COLS = 128
NODES_HERE = 1024
Q_BLOCKS = NODES_HERE // BLOCK
SENDERS = 32
GLOBAL_BLOCK = Q_BLOCKS + SENDERS
EMPTY_BLOCK = GLOBAL_BLOCK + 1
KEY_BLOCKS = EMPTY_BLOCK + 1
GROUP = 8
PAIR = 8
SCORE_PAIR = 4
ITEMS = 2
MAX_ITEMS = 64
LIST = 56
EXTRA = 16
SLOTS = BLOCK + EXTRA
PART_ROWS = 32
BACK = SLOTS + PART_ROWS
NEG = -1e30
F32 = jnp.float32
BF16 = jnp.bfloat16


def params(mib):
    return pltpu.CompilerParams(vmem_limit_bytes=mib * 1024 * 1024)


def vmem():
    return pl.BlockSpec(memory_space=pltpu.VMEM)


def smem():
    return pl.BlockSpec(memory_space=pltpu.SMEM)


def iota(shape, dim):
    return lax.broadcasted_iota(jnp.int32, shape, dim)


def dot(a, b):
    return jnp.dot(a, b, preferred_element_type=F32)


def dot_nt(a, b):
    return lax.dot_general(a, b, (((1,), (1,)), ((), ())), preferred_element_type=F32)


def split_index(index):
    return (index & (BLOCK - 1)).astype(F32).astype(BF16), (index >> 7).astype(F32).astype(BF16)


def packed_iota(dim):
    return iota((BLOCK, BLOCK), dim).astype(F32).astype(BF16)


def one_hot_columns(column):
    low, high = split_index(column)
    lanes = jnp.concatenate([packed_iota(1)] * (column.shape[0] // BLOCK), axis=0)
    one, zero = jnp.ones((), BF16), jnp.zeros((), BF16)
    base = jnp.where(low == lanes, one, zero)
    return jnp.concatenate(
        [jnp.where(high == jnp.asarray(c, BF16), base, zero) for c in range(NODES_HERE // BLOCK)], axis=1
    )


def one_hot_of_rows(index_rows):
    columns = [jnp.broadcast_to(row, (BLOCK, BLOCK)).T for row in index_rows]
    return one_hot_columns(jnp.concatenate(columns, axis=0))


def owner_ranks(gid_row):
    owner = jnp.broadcast_to(gid_row >> 10, (BLOCK, BLOCK))
    owner_t = owner.T
    same = owner == owner_t
    subs, lanes = iota((BLOCK, BLOCK), 0), iota((BLOCK, BLOCK), 1)
    row = jnp.sum(jnp.where(jnp.logical_and(same, subs < lanes), 1.0, 0.0), axis=0, keepdims=True)
    col = jnp.sum(jnp.where(jnp.logical_and(same, lanes < subs), 1.0, 0.0), axis=1, keepdims=True)
    row, col = row.astype(jnp.int32), jnp.broadcast_to(col, (BLOCK, BLOCK)).astype(jnp.int32)
    slot_row = jnp.where(row < EXTRA, (gid_row >> 10) * EXTRA + row, -1)
    slot_col = jnp.where(col < EXTRA, owner_t * EXTRA + col, -1)
    return row, slot_row, slot_col


def mine_columns(gid_row, me):
    row, _, _ = owner_ranks(gid_row)
    mine = (gid_row >> 10) == me
    slots = iota((EXTRA, BLOCK), 0)
    hit = jnp.logical_and(jnp.broadcast_to(mine, (EXTRA, BLOCK)), slots == row)
    local = jnp.broadcast_to(gid_row & (NODES_HERE - 1), (EXTRA, BLOCK)) + 1
    return jnp.sum(jnp.where(hit, local, 0).astype(F32), axis=1, keepdims=True).astype(jnp.int32) - 1


def exp_row(exp_ref, m, i):
    return exp_ref[m : m + 1, i * BLOCK : (i + 1) * BLOCK]


def project_kernel(
    me_ref, x_ref, wq_ref, wk_ref, wv_ref, cot_ref, rows_ref, exp_ref, gid_ref, q_ref, k_ref, v_ref, outk_ref, outv_ref,
    away_ref, rounds_ref, kv_ref, msgk_s, msgv_s, sems,
):
    most = jnp.max(owner_ranks(gid_ref[...])[0].astype(F32)).astype(jnp.int32)
    rounds_ref[0] = (most + EXTRA) // EXTRA
    x = x_ref[...]
    keys = dot(x, wk_ref[...]).astype(BF16)
    values = dot(x, wv_ref[...]).astype(BF16)
    k_ref[...] = keys
    v_ref[...] = values
    kv_ref[:, :COLS] = keys
    kv_ref[:, COLS:] = values
    query = (dot(x, wq_ref[...]).astype(BF16).astype(F32) * (1.0 / math.sqrt(HEAD))).astype(BF16)
    q_ref[...] = query
    away_ref[:NODES_HERE, :COLS] = query
    away_ref[:NODES_HERE, COLS:] = cot_ref[...]
    for m in range(EXPANDERS):
        low, high = split_index(jnp.concatenate([exp_row(exp_ref, m, i) for i in range(Q_BLOCKS)], axis=0))
        away_ref[NODES_HERE + m * Q_BLOCKS : NODES_HERE + (m + 1) * Q_BLOCKS, :COLS] = low
        away_ref[NODES_HERE + m * Q_BLOCKS : NODES_HERE + (m + 1) * Q_BLOCKS, COLS:] = high
    mine = jnp.broadcast_to(mine_columns(gid_ref[...], me_ref[0]), (EXTRA, BLOCK))
    lanes = iota((EXTRA, NODES_HERE), 1)
    hot = (jnp.concatenate([mine] * (NODES_HERE // BLOCK), axis=1) == lanes).astype(F32).astype(BF16)
    extra = dot(hot, kv_ref[...]).astype(BF16)

    def sends(t):
        here = pl.ds(t * GROUP, GROUP)
        return (
            pltpu.make_async_copy(msgk_s.at[here], outk_ref.at[here], sems.at[0, t]),
            pltpu.make_async_copy(msgv_s.at[here], outv_ref.at[here], sems.at[1, t]),
        )

    def gather(t, carry):
        hot = one_hot_of_rows([rows_ref[pl.ds(t * GROUP + u, 1), :] for u in range(GROUP)])
        got = dot(hot, kv_ref[...]).astype(BF16)
        for u in range(GROUP):
            msgk_s[t * GROUP + u, :BLOCK] = got[u * BLOCK : (u + 1) * BLOCK, :COLS]
            msgv_s[t * GROUP + u, :BLOCK] = got[u * BLOCK : (u + 1) * BLOCK, COLS:]
            msgk_s[t * GROUP + u, BLOCK:] = extra[:, :COLS]
            msgv_s[t * GROUP + u, BLOCK:] = extra[:, COLS:]
        for send in sends(t):
            send.start()
        return carry

    lax.fori_loop(0, SENDERS // GROUP, gather, 0)
    for t in range(SENDERS // GROUP):
        for send in sends(t):
            send.wait()


def gather_partner(exp_ref, m, table):
    blocks = []
    for t in range(0, Q_BLOCKS, 4):
        hot = one_hot_of_rows([exp_row(exp_ref, m, t + u) for u in range(4)])
        got = dot(hot, table[...]).astype(BF16)
        blocks += [got[u * BLOCK : (u + 1) * BLOCK] for u in range(4)]
    return blocks


def sum_picks():
    sub = iota((2 * Q_BLOCKS * COLS, 16), 0)
    col = iota((2 * Q_BLOCKS * COLS, 16), 1)
    return (col == (sub >> 8) + jnp.where((sub & (COLS - 1)) < HEAD, 0, 8)).astype(F32).astype(BF16)


def head_sums(a_ref, blocks, picks):
    parts = []
    for i, b in enumerate(blocks):
        prod = a_ref[i * BLOCK : (i + 1) * BLOCK, :].astype(F32) * b.astype(F32)
        high = prod.astype(BF16)
        parts += [high, (prod - high.astype(F32)).astype(BF16)]
    return flat(dot(jnp.concatenate(parts, axis=1), picks).T)


def partner_key_kernel(exp_ref, t0_ref, t1_ref, t2_ref, t3_ref, q_ref, out_ref, sp_ref):
    picks = sum_picks()
    for m, table in enumerate((t0_ref, t1_ref, t2_ref, t3_ref)):
        blocks = gather_partner(exp_ref, m, table)
        for i, block in enumerate(blocks):
            out_ref[m * Q_BLOCKS + i] = block
        sp_ref[m] = head_sums(q_ref, blocks, picks)


def head_picks(i):
    return (iota((16, COLS), 0) == jnp.where(iota((16, COLS), 1) < HEAD, i, 8 + i)).astype(F32).astype(BF16)


def finish_kernel(
    me_ref, exp_ref, t0_ref, t1_ref, t2_ref, t3_ref, cot_ref, sp_ref, lse_ref, local_ref, _, pair_ref, back_ref,
    delta_ref, message_ref, sems,
):
    picks = sum_picks()
    lse = lse_ref[...]
    delta = local_ref[...]
    probs, dprobs = [], []
    for m, table in enumerate((t0_ref, t1_ref, t2_ref, t3_ref)):
        blocks = gather_partner(exp_ref, m, table)
        prob = jnp.exp(sp_ref[m] - lse)
        dprob = head_sums(cot_ref, blocks, picks)
        delta += prob * dprob
        back_ref[m, 16:] = tall(prob).astype(BF16)
        for i, block in enumerate(blocks):
            pair_ref[m * Q_BLOCKS + i] = block
        probs.append(prob)
        dprobs.append(dprob)
    delta_ref[...] = delta
    for m in range(EXPANDERS):
        back_ref[m, :16] = tall(probs[m] * (dprobs[m] - delta)).astype(BF16)
    copies = [
        pltpu.make_async_copy(
            back_ref.at[m], message_ref.at[me_ref[0] ^ (1 << m), pl.ds(SLOTS, PART_ROWS)], sems.at[m]
        )
        for m in range(EXPANDERS)
    ]
    for copy in copies:
        copy.start()
    for copy in copies:
        copy.wait()


def join_partners(out_ref, out_t_ref, part_rows, pair_ref, scale):
    turned = [turned_weights(rows) for rows in part_rows]
    for i in range(Q_BLOCKS):
        total = head_rows(out_t_ref[i]).T
        for m in range(EXPANDERS):
            total += dot(turned[m], head_picks(i)) * pair_ref[m * Q_BLOCKS + i].astype(F32)
        out_ref[i * BLOCK : (i + 1) * BLOCK, :] = (total * scale).astype(BF16)


def attend_kernel(out_t_ref, back_ref, pair_ref, att_ref):
    join_partners(att_ref, out_t_ref, [back_ref[m, 16:] for m in range(EXPANDERS)], pair_ref, 1.0)


def flat(x):
    return jnp.concatenate([x[:8], x[8:]], axis=1)


def tall(x):
    return jnp.concatenate([x[:, :BLOCK], x[:, BLOCK:]], axis=0)


def turned_weights(tall_rows):
    return tall_rows.astype(F32).T.astype(BF16)


def prepare_kernel(q_ref, cot_ref, qt_ref, qs_ref, ct_ref, cs_ref):
    def one(i, carry):
        q = q_ref[q_rows(i), :]
        cot = cot_ref[q_rows(i), :]
        qt_ref[i] = stacked_t(q)
        qs_ref[i] = stacked(q)
        ct_ref[i] = stacked_t(cot)
        cs_ref[i] = stacked(cot)
        return carry

    lax.fori_loop(0, Q_BLOCKS, one, 0, unroll=2)


def plan_kernel(mask_ref, halo_ref, list_ref, where_ref, block_ref, count_ref, live_ref):
    for j in range(Q_BLOCKS):
        live_ref[j] = BLOCK
    live_ref[GLOBAL_BLOCK] = BLOCK
    live_ref[EMPTY_BLOCK] = 0

    def copy_count(s, carry):
        live_ref[Q_BLOCKS + s] = halo_ref[s]
        return carry

    lax.fori_loop(0, SENDERS, copy_count, 0)

    def per_block(i, items):
        list_ref[i * LIST] = GLOBAL_BLOCK

        def put(j, n):
            list_ref[i * LIST + n] = j
            used = jnp.logical_and(mask_ref[i * GLOBAL_BLOCK + j] > 0, live_ref[j] > 0)
            return n + used.astype(jnp.int32)

        n = lax.fori_loop(0, GLOBAL_BLOCK, put, 1)
        for extra in range(GROUP):
            list_ref[i * LIST + n + extra] = EMPTY_BLOCK
        groups = (n + GROUP - 1) // GROUP

        def item(g, carry):
            where_ref[items + g] = i * LIST + g * GROUP
            block_ref[items + g] = i
            return carry

        lax.fori_loop(0, groups, item, 0)
        return items + groups

    items = lax.fori_loop(0, Q_BLOCKS, per_block, 0)
    for u in range(GROUP):
        list_ref[Q_BLOCKS * LIST + u] = EMPTY_BLOCK
    for u in range(ITEMS - 1):
        where_ref[items + u] = Q_BLOCKS * LIST
        block_ref[items + u] = 0
    count_ref[0] = (items + ITEMS - 1) // ITEMS


def fill(dst, dst_t, first_col,  own_ref, halo_ref, gid_ref, glob_ref):
    def put(j, block):
        if dst is not None:
            dst[j] = block
        if dst_t is not None:
            dst_t[j] = block.T

    def own(j, carry):
        put(j, own_ref[q_rows(j), :])
        return carry

    def halo(j, carry):
        put(Q_BLOCKS + j, halo_ref[j, :BLOCK])
        return carry

    lax.fori_loop(0, Q_BLOCKS, own, 0, unroll=4)
    lax.fori_loop(0, SENDERS, halo, 0, unroll=4)
    slot_col = owner_ranks(gid_ref[...])[2]
    wide = jnp.concatenate([slot_col] * (SENDERS * EXTRA // BLOCK), axis=1)
    hot = (wide == iota((BLOCK, SENDERS * EXTRA), 1)).astype(F32).astype(BF16)
    extra = jnp.concatenate([halo_ref[s, BLOCK:] for s in range(SENDERS)], axis=0)
    rows = (dot(hot, extra) + glob_ref[:, first_col : first_col + COLS].astype(F32)).astype(BF16)
    put(GLOBAL_BLOCK, rows)
    put(EMPTY_BLOCK, jnp.zeros((BLOCK, COLS), BF16))


def stacked(rows):
    lanes = iota((BLOCK, COLS), 1)
    zero = jnp.zeros_like(rows)
    return jnp.concatenate([jnp.where(lanes < HEAD, rows, zero), jnp.where(lanes < HEAD, zero, rows)], axis=0)


def stacked_t(rows):
    turned = rows.T
    subs = iota((COLS, BLOCK), 0)
    zero = jnp.zeros_like(turned)
    return jnp.concatenate([jnp.where(subs < HEAD, turned, zero), jnp.where(subs < HEAD, zero, turned)], axis=1)


def head_rows(turned):
    return jnp.concatenate([turned[:HEAD, :BLOCK], turned[HEAD:, BLOCK:]], axis=0)


def masked_scores(blocks, k_s, turned_q, live_ref):
    keys = jnp.concatenate([k_s[b] for b in blocks], axis=0)
    scores = dot(keys, turned_q)
    row_id = iota((BLOCK, 2 * BLOCK), 0)
    return jnp.concatenate(
        [
            jnp.where(row_id < live_ref[b], scores[u * BLOCK : (u + 1) * BLOCK], NEG)
            for u, b in enumerate(blocks)
        ],
        axis=0,
    )


def item_of(t, u, list_ref, where_ref, block_ref):
    where = where_ref[t * ITEMS + u]
    return block_ref[t * ITEMS + u], [list_ref[where + b] for b in range(GROUP)]


def q_rows(i):
    return pl.ds(pl.multiple_of(i * BLOCK, BLOCK), BLOCK)


def score_kernel(
    list_ref, where_ref, block_ref, count_ref, live_ref, qt_ref, own_ref, hk_ref, gid_ref, glob_ref, lse_ref, k_s, kt_ref,
    top_s, total_s,
):
    fill(k_s, kt_ref, 0, own_ref, hk_ref, gid_ref, glob_ref)

    top_s[...] = jnp.full((Q_BLOCKS, 8, 2 * BLOCK), NEG, F32)
    total_s[...] = jnp.zeros((Q_BLOCKS, 8, 2 * BLOCK), F32)

    def step(t, carry):
        for item in range(ITEMS):
            i, blocks = item_of(t, item, list_ref, where_ref, block_ref)
            turned_q = qt_ref[i]
            parts = []
            for u in range(0, GROUP, SCORE_PAIR):
                scores = masked_scores(blocks[u : u + SCORE_PAIR], k_s, turned_q, live_ref)
                scores = scores.reshape(SCORE_PAIR * BLOCK // 8, 8, 2 * BLOCK)
                top = jnp.max(scores, axis=0)
                parts.append((top, jnp.sum(jnp.exp(scores - top[None]), axis=0)))
            parts.append((top_s[i], total_s[i]))
            best = functools.reduce(jnp.maximum, [top for top, _ in parts])
            top_s[i] = best
            total_s[i] = sum(total * jnp.exp(top - best) for top, total in parts)
        return carry

    lax.fori_loop(0, count_ref[0], step, 0)
    for i in range(Q_BLOCKS):
        top = top_s[i]
        best = jnp.max(top, axis=0, keepdims=True)
        denominator = jnp.sum(total_s[i] * jnp.exp(top - best), axis=0, keepdims=True)
        lse_ref[i : i + 1, :] = best + jnp.log(denominator)


def value_kernel(
    list_ref, where_ref, block_ref, count_ref, live_ref, k_s, ownv_ref, hv_ref, glob_ref, qt_ref, ct_ref, cs_ref, part_ref,
    sp_ref, gid_ref, own_ref, halo_ref, gout_ref, out_s, delta_ref, lse_ref, acc_s, vt_s,
):
    fill(None, vt_s, COLS, ownv_ref, hv_ref, gid_ref, glob_ref)
    clear_blocks(acc_s)
    part = part_ref[...]
    best = part
    for m in range(EXPANDERS):
        best = jnp.maximum(best, sp_ref[m])
    total = jnp.exp(part - best)
    for m in range(EXPANDERS):
        total += jnp.exp(sp_ref[m] - best)
    lse_ref[...] = best + jnp.log(total)

    out_s[...] = jnp.zeros((Q_BLOCKS, COLS, 2 * BLOCK), F32)

    def step(t, carry):
        for item in range(ITEMS):
            i, blocks = item_of(t, item, list_ref, where_ref, block_ref)
            turned_q = qt_ref[i]
            cot_stack = cs_ref[i]
            lse = lse_ref[pl.ds(i, 1), :]
            for u in range(0, GROUP, PAIR):
                pair = blocks[u : u + PAIR]
                scores = masked_scores(pair, k_s, turned_q, live_ref)
                weight = jnp.exp(scores - lse).astype(BF16)
                out_s[i] += dot(jnp.concatenate([vt_s[b] for b in pair], axis=1), weight)
                grads = dot(weight, cot_stack)
                for w, b in enumerate(pair):
                    acc_s[b] += grads[w * BLOCK : (w + 1) * BLOCK]
        return carry

    lax.fori_loop(0, count_ref[0], step, 0)
    for i in range(Q_BLOCKS):
        delta_ref[i : i + 1, :] = jnp.sum(out_s[i] * ct_ref[i].astype(F32), axis=0, keepdims=True)
    store_parts(acc_s, own_ref, halo_ref, gid_ref, gout_ref)


def clear_blocks(acc_s):
    def clear(j, carry):
        acc_s[j] = jnp.zeros((BLOCK, COLS), F32)
        return carry

    lax.fori_loop(0, KEY_BLOCKS, clear, 0, unroll=2)


def store_parts(acc_s, own_ref, halo_ref, gid_ref, gout_ref):
    def own(j, carry):
        own_ref[q_rows(j), :] = acc_s[j]
        return carry

    def halo(j, carry):
        halo_ref[j, :BLOCK] = acc_s[Q_BLOCKS + j].astype(BF16)
        return carry

    lax.fori_loop(0, Q_BLOCKS, own, 0, unroll=2)
    lax.fori_loop(0, SENDERS, halo, 0, unroll=4)
    grads = acc_s[GLOBAL_BLOCK].astype(BF16)
    gout_ref[...] = grads
    slot_row = owner_ranks(gid_ref[...])[1]
    hot = (iota((SENDERS * EXTRA, BLOCK), 0) == slot_row).astype(F32).astype(BF16)
    extra = dot(hot, grads).astype(BF16)
    for s in range(SENDERS):
        halo_ref[s, BLOCK:SLOTS] = extra[s * EXTRA : (s + 1) * EXTRA]


def key_kernel(
    list_ref, where_ref, block_ref, count_ref, live_ref, k_s, kt_s, ownv_ref, hv_ref, glob_ref, qt_ref, qs_ref, ct_ref, lse_ref,
    delta_ref, gid_ref, out_s, own_ref, halo_ref, gout_ref, acc_s, v_s,
):
    fill(v_s, None, COLS, ownv_ref, hv_ref, gid_ref, glob_ref)
    clear_blocks(acc_s)

    out_s[...] = jnp.zeros((Q_BLOCKS, COLS, 2 * BLOCK), F32)

    def step(t, carry):
        for item in range(ITEMS):
            i, blocks = item_of(t, item, list_ref, where_ref, block_ref)
            turned_q = qt_ref[i]
            q_stack = qs_ref[i]
            turned_cot = ct_ref[i]
            lse = lse_ref[pl.ds(i, 1), :]
            delta = delta_ref[pl.ds(i, 1), :]
            for u in range(0, GROUP, PAIR):
                pair = blocks[u : u + PAIR]
                scores = masked_scores(pair, k_s, turned_q, live_ref)
                dprob = dot(jnp.concatenate([v_s[b] for b in pair], axis=0), turned_cot)
                dscore = (jnp.exp(scores - lse) * (dprob - delta)).astype(BF16)
                out_s[i] += dot(jnp.concatenate([kt_s[b] for b in pair], axis=1), dscore)
                grads = dot(dscore, q_stack)
                for w, b in enumerate(pair):
                    acc_s[b] += grads[w * BLOCK : (w + 1) * BLOCK]
        return carry

    lax.fori_loop(0, count_ref[0], step, 0)
    store_parts(acc_s, own_ref, halo_ref, gid_ref, gout_ref)


def scatter_into(acc_s, splits, data):
    subs = packed_iota(0)
    one, zero = jnp.ones((), BF16), jnp.zeros((), BF16)
    bases = [(jnp.where(subs == low, one, zero), jnp.broadcast_to(high, (BLOCK, BLOCK))) for low, high in splits]
    for c in range(NODES_HERE // BLOCK):
        hot = jnp.concatenate([jnp.where(high == jnp.asarray(c, BF16), base, zero) for base, high in bases], axis=1)
        acc_s[c * BLOCK : (c + 1) * BLOCK, :] += dot(hot, data)


def add_halo(acc_s, me_ref, ret_ref, rows_ref, gid_ref, more_ref):
    def halo(t, carry):
        splits = [split_index(rows_ref[pl.ds(t * GROUP + u, 1), :]) for u in range(GROUP)]
        data = jnp.concatenate([ret_ref[t * GROUP + u, :BLOCK] for u in range(GROUP)], axis=0)
        scatter_into(acc_s, splits, data)
        return carry

    lax.fori_loop(0, SENDERS // GROUP, halo, 0)
    extra = ret_ref[0, BLOCK:SLOTS].astype(F32)
    for s in range(1, SENDERS):
        extra += ret_ref[s, BLOCK:SLOTS].astype(F32)
    high = extra.astype(BF16)
    data = jnp.concatenate([high, (extra - high.astype(F32)).astype(BF16)], axis=0)
    mine = jnp.broadcast_to(mine_columns(gid_ref[...], me_ref[0]), (EXTRA, NODES_HERE))
    hot = (mine == iota((EXTRA, NODES_HERE), 1)).astype(F32)
    hot = jnp.concatenate([hot, hot], axis=0).T.astype(BF16)
    acc_s[...] += dot(hot, data)
    gids = gid_ref[...]
    local = jnp.where((gids >> 10) == me_ref[0], gids & (NODES_HERE - 1), NODES_HERE)
    more = more_ref[...]
    high = more.astype(BF16)
    low = (more - high.astype(F32)).astype(BF16)
    scatter_into(acc_s, [split_index(local)] * 2, jnp.concatenate([high, low], axis=0))


def add_partners(acc_s, parts, others, first_col):
    for m, (part, other) in enumerate(zip(parts, others)):
        turned = turned_weights(part)
        index_low = other[NODES_HERE + m * Q_BLOCKS : NODES_HERE + (m + 1) * Q_BLOCKS, :COLS]
        index_high = other[NODES_HERE + m * Q_BLOCKS : NODES_HERE + (m + 1) * Q_BLOCKS, COLS:]
        for t in range(Q_BLOCKS // GROUP):
            splits, data = [], []
            for u in range(GROUP):
                i = t * GROUP + u
                splits.append((index_low[i : i + 1], index_high[i : i + 1]))
                wide = dot(turned, head_picks(i))
                rows = other[i * BLOCK : (i + 1) * BLOCK, first_col : first_col + COLS].astype(F32)
                data.append((wide * rows).astype(BF16))
            scatter_into(acc_s, splits, jnp.concatenate(data, axis=0))


def feature_part(feat_ref, k):
    return pl.ds(pl.multiple_of(((feat_ref[0] + k) % 4) * COLS, COLS), COLS)


def value_back_kernel(
    me_ref, feat_ref, ownv_ref, ret_ref, ownk_ref, rows_ref, o0_ref, o1_ref, o2_ref, o3_ref, gid_ref, wq_ref, wv_ref,
    out_t_ref, back_ref, pair_ref, more_ref, acck_ref, pre_ref, accv_s, gq_ref,
):
    others = (o0_ref, o1_ref, o2_ref, o3_ref)
    parts = [ret_ref[me_ref[0] ^ (1 << m), SLOTS:] for m in range(EXPANDERS)]
    join_partners(
        gq_ref, out_t_ref, [back_ref[m, :16] for m in range(EXPANDERS)], pair_ref, 1.0 / math.sqrt(HEAD)
    )
    accv_s[...] = ownv_ref[...]
    add_halo(accv_s, me_ref, ret_ref, rows_ref, gid_ref, more_ref)
    add_partners(accv_s, [part[16:] for part in parts], others, COLS)
    acck_ref[...] = ownk_ref[...]
    add_partners(acck_ref, [part[:16] for part in parts], others, 0)
    grad_value = accv_s[...].astype(BF16)
    for k in range(4):
        part = feature_part(feat_ref, k)
        pre_ref[k] = dot_nt(gq_ref[...], wq_ref[part, :]) + dot_nt(grad_value, wv_ref[part, :])


def key_back_kernel(
    me_ref, feat_ref, acck_ref, ret_ref, rows_ref, gid_ref, wk_ref, pre_ref, more_ref, t0_ref, t1_ref, t2_ref, t3_ref,
    acc_s, own_s, pre_s, sems,
):
    own_copy = pltpu.make_async_copy(acck_ref, own_s, sems.at[0])
    pre_copy = pltpu.make_async_copy(pre_ref, pre_s, sems.at[1])
    own_copy.start()
    pre_copy.start()
    acc_s[...] = jnp.zeros((NODES_HERE, COLS), F32)
    add_halo(acc_s, me_ref, ret_ref, rows_ref, gid_ref, more_ref)
    own_copy.wait()
    grad_key = (acc_s[...] + own_s[...]).astype(BF16)
    pre_copy.wait()
    for k, out in ((1, t1_ref), (2, t2_ref), (3, t3_ref), (0, t0_ref)):
        out[...] = (pre_s[k] + dot_nt(grad_key, wk_ref[feature_part(feat_ref, k), :])).astype(out.dtype)


def shape(dims, kind=BF16):
    return jax.ShapeDtypeStruct(dims, kind)


def call(kernel, ins, outs, args, scratch=(), name=None, flops=0, out_spaces=None, aliases={}, mib=56):
    cost = pl.CostEstimate(flops=flops, transcendentals=0, bytes_accessed=4_000_000)
    return pl.pallas_call(
        kernel,
        out_shape=outs,
        in_specs=ins,
        out_specs=out_spaces or tuple(vmem() for _ in outs),
        scratch_shapes=list(scratch),
        compiler_params=params(mib),
        cost_estimate=cost,
        input_output_aliases=aliases,
        name=name,
    )(*args)


def blocks_of(kind):
    return pltpu.VMEM((KEY_BLOCKS, BLOCK, COLS), kind)


def run_project(me, features, w_query, w_key, w_value, cotangent, rows, exp_list, gids):
    anywhere = pl.BlockSpec(memory_space=pl.ANY)
    return call(
        project_kernel,
        [smem()] + [vmem()] * 8,
        (
            shape((NODES_HERE, COLS)),
            shape((NODES_HERE, COLS)),
            shape((NODES_HERE, COLS)),
            shape((SENDERS, SLOTS, COLS)),
            shape((SENDERS, SLOTS, COLS)),
            shape((NODES_HERE + EXPANDERS * Q_BLOCKS, 2 * COLS)),
            shape((1,), jnp.int32),
        ),
        (me, features, w_query, w_key, w_value, cotangent, rows, exp_list, gids),
        name="project",
        mib=56,
        flops=3_000_000_000,
        out_spaces=(vmem(), vmem(), vmem(), anywhere, anywhere, vmem(), smem()),
        scratch=[
            pltpu.VMEM((NODES_HERE, 2 * COLS), BF16),
            pltpu.VMEM((SENDERS, SLOTS, COLS), BF16),
            pltpu.VMEM((SENDERS, SLOTS, COLS), BF16),
            pltpu.SemaphoreType.DMA((2, SENDERS // GROUP)),
        ],
    )


def run_plan(block_mask, halo_count):
    sizes = (Q_BLOCKS * LIST + GROUP, MAX_ITEMS, MAX_ITEMS, 1, KEY_BLOCKS)
    return call(
        plan_kernel,
        [smem()] * 2,
        tuple(shape((size,), jnp.int32) for size in sizes),
        (block_mask.reshape(-1), halo_count.reshape(-1)),
        name="plan",
        out_spaces=tuple(smem() for _ in sizes),
    )


def run_partner_keys(exp_rows, swaps, query):
    return call(
        partner_key_kernel,
        [vmem()] * 6,
        (shape((EXPANDERS * Q_BLOCKS, BLOCK, COLS)), shape((EXPANDERS, Q_BLOCKS, 2 * BLOCK), F32)),
        (exp_rows, *swaps, query),
        name="partners",
        flops=5_000_000_000,
    )


def run_finish(me, exp_rows, swaps, cotangent, scores, lse, local, back_v):
    anywhere = pl.BlockSpec(memory_space=pl.ANY)
    return call(
        finish_kernel,
        [smem()] + [vmem()] * 9 + [anywhere],
        (
            shape((EXPANDERS * Q_BLOCKS, BLOCK, COLS)),
            shape((EXPANDERS, PART_ROWS, BLOCK)),
            shape((Q_BLOCKS, 2 * BLOCK), F32),
            shape((SENDERS, BACK, COLS)),
        ),
        (me, exp_rows, *swaps, cotangent, scores, lse, local, back_v),
        name="finish",
        flops=5_000_000_000,
        out_spaces=(vmem(), vmem(), vmem(), anywhere),
        scratch=[pltpu.SemaphoreType.DMA((EXPANDERS,))],
        aliases={10: 3},
    )


def run_attend(out_t, back, value_pairs):
    return call(
        attend_kernel,
        [vmem()] * 3,
        (shape((NODES_HERE, COLS)),),
        (out_t, back, value_pairs),
        name="attend",
        flops=2_000_000_000,
    )[0]


def run_prepare(query, cotangent):
    wide, high = shape((Q_BLOCKS, COLS, 2 * BLOCK)), shape((Q_BLOCKS, 2 * BLOCK, COLS))
    return call(
        prepare_kernel, [vmem()] * 2, (wide, high, wide, high), (query, cotangent), name="prepare", flops=2_000_000_000
    )


def run_scores(plan, turned_q, own, halo_k, gids, glob):
    return call(
        score_kernel,
        [smem()] * 5 + [vmem()] * 5,
        (
            shape((Q_BLOCKS, 2 * BLOCK), F32),
            shape((KEY_BLOCKS, BLOCK, COLS)),
            shape((KEY_BLOCKS, COLS, BLOCK)),
        ),
        (*plan, turned_q, own, halo_k, gids, glob),
        scratch=[pltpu.VMEM((Q_BLOCKS, 8, 2 * BLOCK), F32)] * 2,
        name="scores",
        flops=12_000_000_000,
    )


def run_values(plan, keys, own_values, halo_v, glob, prepared, part, scores, gids):
    turned_q, _, turned_cot, cot_stack = prepared
    return call(
        value_kernel,
        [smem()] * 5 + [vmem()] * 10,
        (
            shape((NODES_HERE, COLS), F32),
            shape((SENDERS, BACK, COLS)),
            shape((BLOCK, COLS)),
            shape((Q_BLOCKS, COLS, 2 * BLOCK), F32),
            shape((Q_BLOCKS, 2 * BLOCK), F32),
            shape((Q_BLOCKS, 2 * BLOCK), F32),
        ),
        (*plan, keys, own_values, halo_v, glob, turned_q, turned_cot, cot_stack, part, scores, gids),
        scratch=[blocks_of(F32), blocks_of(BF16)],
        name="values",
        flops=20_000_000_000,
    )


def run_keys(plan, keys, turned_k, own_values, halo_v, glob, prepared, lse, delta, gids):
    turned_q, q_stack, turned_cot, _ = prepared
    return call(
        key_kernel,
        [smem()] * 5 + [vmem()] * 11,
        (
            shape((Q_BLOCKS, COLS, 2 * BLOCK), F32),
            shape((NODES_HERE, COLS), F32),
            shape((SENDERS, SLOTS, COLS)),
            shape((BLOCK, COLS)),
        ),
        (*plan, keys, turned_k, own_values, halo_v, glob, turned_q, q_stack, turned_cot, lse, delta, gids),
        scratch=[blocks_of(F32), blocks_of(BF16)],
        name="keys",
        mib=56,
        flops=25_000_000_000,
    )


def run_value_back(me, feat, own_v, returned_v, own_k, rows, others, gids, w_query, w_value, out_t, back, pairs, more):
    return call(
        value_back_kernel,
        [smem()] * 2 + [vmem()] * 15,
        (shape((NODES_HERE, COLS), F32), shape((4, NODES_HERE, COLS), F32)),
        (me, feat, own_v, returned_v, own_k, rows, *others, gids, w_query, w_value, out_t, back, pairs, more),
        scratch=[pltpu.VMEM((NODES_HERE, COLS), F32), pltpu.VMEM((NODES_HERE, COLS), BF16)],
        name="value_back",
        mib=56,
        flops=12_000_000_000,
    )


def run_key_back(me, feat, own_k, returned_k, rows, gids, w_key, pre, more):
    anywhere = pl.BlockSpec(memory_space=pl.ANY)
    return call(
        key_back_kernel,
        [smem()] * 2 + [anywhere] + [vmem()] * 4 + [anywhere, vmem()],
        (shape((NODES_HERE, COLS), F32),) + tuple(shape((NODES_HERE, COLS)) for _ in range(3)),
        (me, feat, own_k, returned_k, rows, gids, w_key, pre, more),
        scratch=[
            pltpu.VMEM((NODES_HERE, COLS), F32),
            pltpu.VMEM((NODES_HERE, COLS), F32),
            pltpu.VMEM((4, NODES_HERE, COLS), F32),
            pltpu.SemaphoreType.DMA((2,)),
        ],
        name="key_back",
        mib=56,
        flops=8_000_000_000,
    )


def ranks(global_ids):
    owner = global_ids // NODES_HERE
    ids = jnp.arange(BLOCK)
    return owner, ((owner[:, None] == owner[None, :]) & (ids[None, :] < ids[:, None])).sum(1)


def more_globals(rounds, global_ids, my_index, own_k, own_v):
    def body(state):
        r, glob = state
        owner, rank = ranks(global_ids + jnp.minimum(r, 0))
        slot = rank - r * EXTRA
        here = (slot >= 0) & (slot < EXTRA)
        place = jnp.where((owner == my_index) & here, slot, EXTRA)
        local = jnp.where(here, global_ids % NODES_HERE, 0)
        found = jnp.concatenate([own_k[local], own_v[local]], axis=1)
        rows = jnp.zeros((EXTRA + 1, 2 * COLS), BF16).at[place].set(found)[:EXTRA]
        got = lax.all_to_all(jnp.broadcast_to(rows[None], (SENDERS, *rows.shape)), "dom", 0, 0, tiled=True)
        found = got.reshape(SENDERS * EXTRA, -1)[jnp.clip(owner * EXTRA + slot, 0, SENDERS * EXTRA - 1)]
        return r + 1, jnp.where(here[:, None], found, glob)

    start = (jnp.asarray(1, jnp.int32), jnp.zeros((BLOCK, 2 * COLS), BF16))
    return lax.while_loop(lambda state: state[0] < rounds, body, start)[1]


def more_grads(rounds, global_ids, my_index, part_k, part_v):
    def body(state):
        r, more_k, more_v = state
        owner, rank = ranks(global_ids + jnp.minimum(r, 0))
        slot = rank - r * EXTRA
        here = (slot >= 0) & (slot < EXTRA)
        place = jnp.where(here, owner * EXTRA + slot, SENDERS * EXTRA)

        def summed(part):
            rows = jnp.zeros((SENDERS * EXTRA + 1, COLS), BF16).at[place].set(part)[: SENDERS * EXTRA]
            got = lax.all_to_all(rows.reshape(SENDERS, EXTRA, -1), "dom", 0, 0, tiled=True).astype(F32).sum(0)
            return jnp.where(((owner == my_index) & here)[:, None], got[jnp.clip(slot, 0, EXTRA - 1)], 0.0)

        return r + 1, more_k + summed(part_k), more_v + summed(part_v)

    zeros = jnp.zeros((BLOCK, COLS), F32)
    start = (jnp.asarray(1, jnp.int32), zeros, zeros)
    return lax.while_loop(lambda state: state[0] < rounds, body, start)[1:]


def on_device(
    features,
    w_query,
    w_key,
    w_value,
    cotangent,
    send_rows,
    halo_count,
    block_mask,
    exp_rows,
    global_ids,
):
    dom_count = lax.axis_size("dom")
    my_index = lax.axis_index("dom")

    def swapped(value, bit):
        return lax.ppermute(value, "dom", [(i, i ^ (1 << bit)) for i in range(dom_count)])

    rows = send_rows[0]
    gids = global_ids.reshape(1, BLOCK)
    me = my_index.reshape(1).astype(jnp.int32)
    feat = lax.axis_index("feat").reshape(1).astype(jnp.int32)

    query, own_keys, own_values, out_k, out_v, away, rounds = run_project(
        me, features, w_query, w_key, w_value, cotangent, rows, exp_rows, gids
    )
    rounds = rounds[0]
    glob = more_globals(rounds, global_ids, my_index, own_keys, own_values)
    out_k, out_v, glob = lax.optimization_barrier((out_k, out_v, glob))
    halo_k = lax.all_to_all(out_k, "dom", 0, 0, tiled=True)
    key_swaps = [swapped(own_keys, m) for m in range(EXPANDERS)]
    plan = run_plan(block_mask, halo_count)
    prepared = run_prepare(query, cotangent)
    own_values_late, *prepared = lax.optimization_barrier((own_values, *prepared))
    value_swaps = [swapped(own_values_late, m) for m in range(EXPANDERS)]
    halo_v = lax.all_to_all(out_v, "dom", 0, 0, tiled=True)
    part, keys, turned_k = run_scores(plan, prepared[0], own_keys, halo_k, gids, glob)
    part, *key_swaps = lax.optimization_barrier((part, *key_swaps))
    pairs, scores = run_partner_keys(exp_rows, key_swaps, query)
    away, scores = lax.optimization_barrier((away, scores))
    others = [swapped(away, m) for m in range(EXPANDERS)]
    own_v, back_v, glob_v, out_t, local, lse = run_values(
        plan, keys, own_values, halo_v, glob, prepared, part, scores, gids
    )
    local, *value_swaps = lax.optimization_barrier((local, *value_swaps))
    value_pairs, back, delta, back_v = run_finish(
        me, exp_rows, value_swaps, cotangent, scores, lse, local, back_v
    )
    returned_v = lax.all_to_all(back_v, "dom", 0, 0, tiled=True)
    query_t, own_k, back_k, glob_k = run_keys(
        plan, keys, turned_k, own_values, halo_v, glob, prepared, lse, delta, gids
    )
    glob_k, returned_v, *others = lax.optimization_barrier((glob_k, returned_v, *others))
    more_k, more_v = more_grads(rounds, global_ids, my_index, glob_k, glob_v)
    back_k, more_k, more_v = lax.optimization_barrier((back_k, more_k, more_v))
    returned_k = lax.all_to_all(back_k, "dom", 0, 0, tiled=True)
    own_k, pre = run_value_back(
        me, feat, own_v, returned_v, own_k, rows, others, gids, w_query, w_value, query_t, back, pairs, more_v
    )
    mine, *away = run_key_back(me, feat, own_k, returned_k, rows, gids, w_key, pre, more_k)
    out_t, mine = lax.optimization_barrier((out_t, mine))
    attended = run_attend(out_t, back, value_pairs)
    for k in (2, 1, 3):
        mine = mine + lax.ppermute(away[k - 1], "feat", [(i, (i + k) % 4) for i in range(4)]).astype(F32)
    return (attended, mine.astype(BF16))


def solution(mesh):
    return jax.shard_map(
        on_device,
        mesh=mesh,
        in_specs=(
            P("dom", None),
            P(None, "feat"),
            P(None, "feat"),
            P(None, "feat"),
            P("dom", "feat"),
            P("dom", None, None),
            P(None, "dom"),
            P("dom", None),
            P(None, "dom"),
            P(),
        ),
        out_specs=(P("dom", "feat"), P("dom", "feat")),
        check_vma=False,
    )
```

```python
import functools
import math

import jax
import jax.numpy as jnp
from jax import lax
from jax.experimental import pallas as pl
from jax.experimental.pallas import tpu as pltpu
from jax.sharding import PartitionSpec as P

HEAD = 64
BLOCK = 128
EXPANDERS = 4
COLS = 128
NODES_HERE = 1024
Q_BLOCKS = NODES_HERE // BLOCK
SENDERS = 32
GLOBAL_BLOCK = Q_BLOCKS + SENDERS
EMPTY_BLOCK = GLOBAL_BLOCK + 1
KEY_BLOCKS = EMPTY_BLOCK + 1
GROUP = 8
PAIR = 8
SCORE_PAIR = 4
ITEMS = 2
MAX_ITEMS = 64
TOGETHER = (0, 3)
LIST = 56
EXTRA = 16
SLOTS = BLOCK + EXTRA
PART_ROWS = 32
BACK = SLOTS + PART_ROWS
NEG = -1e30
F32 = jnp.float32
BF16 = jnp.bfloat16


def params(mib):
    return pltpu.CompilerParams(vmem_limit_bytes=mib * 1024 * 1024)


def vmem():
    return pl.BlockSpec(memory_space=pltpu.VMEM)


def smem():
    return pl.BlockSpec(memory_space=pltpu.SMEM)


def iota(shape, dim):
    return lax.broadcasted_iota(jnp.int32, shape, dim)


def dot(a, b):
    return jnp.dot(a, b, preferred_element_type=F32)


def dot_nt(a, b):
    return lax.dot_general(a, b, (((1,), (1,)), ((), ())), preferred_element_type=F32)


def split_index(index):
    return (index & (BLOCK - 1)).astype(F32).astype(BF16), (index >> 7).astype(F32).astype(BF16)


def packed_iota(dim):
    return iota((BLOCK, BLOCK), dim).astype(F32).astype(BF16)


def one_hot_columns(column):
    low, high = split_index(column)
    lanes = jnp.concatenate([packed_iota(1)] * (column.shape[0] // BLOCK), axis=0)
    one, zero = jnp.ones((), BF16), jnp.zeros((), BF16)
    base = jnp.where(low == lanes, one, zero)
    return jnp.concatenate(
        [jnp.where(high == jnp.asarray(c, BF16), base, zero) for c in range(NODES_HERE // BLOCK)], axis=1
    )


def one_hot_of_rows(index_rows):
    columns = [jnp.broadcast_to(row, (BLOCK, BLOCK)).T for row in index_rows]
    return one_hot_columns(jnp.concatenate(columns, axis=0))


def owner_ranks(gid_row):
    owner = jnp.broadcast_to(gid_row >> 10, (BLOCK, BLOCK))
    owner_t = owner.T
    same = owner == owner_t
    subs, lanes = iota((BLOCK, BLOCK), 0), iota((BLOCK, BLOCK), 1)
    row = jnp.sum(jnp.where(jnp.logical_and(same, subs < lanes), 1.0, 0.0), axis=0, keepdims=True)
    col = jnp.sum(jnp.where(jnp.logical_and(same, lanes < subs), 1.0, 0.0), axis=1, keepdims=True)
    row, col = row.astype(jnp.int32), jnp.broadcast_to(col, (BLOCK, BLOCK)).astype(jnp.int32)
    slot_row = jnp.where(row < EXTRA, (gid_row >> 10) * EXTRA + row, -1)
    slot_col = jnp.where(col < EXTRA, owner_t * EXTRA + col, -1)
    return row, slot_row, slot_col


def mine_columns(gid_row, me):
    row, _, _ = owner_ranks(gid_row)
    mine = (gid_row >> 10) == me
    slots = iota((EXTRA, BLOCK), 0)
    hit = jnp.logical_and(jnp.broadcast_to(mine, (EXTRA, BLOCK)), slots == row)
    local = jnp.broadcast_to(gid_row & (NODES_HERE - 1), (EXTRA, BLOCK)) + 1
    return jnp.sum(jnp.where(hit, local, 0).astype(F32), axis=1, keepdims=True).astype(jnp.int32) - 1


def exp_row(exp_ref, m, i):
    return exp_ref[m : m + 1, i * BLOCK : (i + 1) * BLOCK]


def project_kernel(
    me_ref, x_ref, wq_ref, wk_ref, wv_ref, cot_ref, rows_ref, exp_ref, gid_ref, q_ref, k_ref, v_ref, kv_ref, outk_ref, outv_ref,
    away_ref, rounds_ref, msgk_s, msgv_s, sems,
):
    most = jnp.max(owner_ranks(gid_ref[...])[0].astype(F32)).astype(jnp.int32)
    rounds_ref[0] = (most + EXTRA) // EXTRA
    x = x_ref[...]
    keys = dot(x, wk_ref[...]).astype(BF16)
    values = dot(x, wv_ref[...]).astype(BF16)
    k_ref[...] = keys
    v_ref[...] = values
    kv_ref[:, :COLS] = keys
    kv_ref[:, COLS:] = values
    query = (dot(x, wq_ref[...]).astype(BF16).astype(F32) * (1.0 / math.sqrt(HEAD))).astype(BF16)
    q_ref[...] = query
    away_ref[:NODES_HERE, :COLS] = query
    away_ref[:NODES_HERE, COLS:] = cot_ref[...]
    for m in range(EXPANDERS):
        low, high = split_index(jnp.concatenate([exp_row(exp_ref, m, i) for i in range(Q_BLOCKS)], axis=0))
        away_ref[NODES_HERE + m * Q_BLOCKS : NODES_HERE + (m + 1) * Q_BLOCKS, :COLS] = low
        away_ref[NODES_HERE + m * Q_BLOCKS : NODES_HERE + (m + 1) * Q_BLOCKS, COLS:] = high
    mine = jnp.broadcast_to(mine_columns(gid_ref[...], me_ref[0]), (EXTRA, BLOCK))
    lanes = iota((EXTRA, NODES_HERE), 1)
    hot = (jnp.concatenate([mine] * (NODES_HERE // BLOCK), axis=1) == lanes).astype(F32).astype(BF16)
    extra = dot(hot, kv_ref[...]).astype(BF16)

    def sends(t):
        here = pl.ds(t * GROUP, GROUP)
        return (
            pltpu.make_async_copy(msgk_s.at[here], outk_ref.at[here], sems.at[0, t]),
            pltpu.make_async_copy(msgv_s.at[here], outv_ref.at[here], sems.at[1, t]),
        )

    def gather(t, carry):
        hot = one_hot_of_rows([rows_ref[pl.ds(t * GROUP + u, 1), :] for u in range(GROUP)])
        got = dot(hot, kv_ref[...]).astype(BF16)
        for u in range(GROUP):
            msgk_s[t * GROUP + u, :BLOCK] = got[u * BLOCK : (u + 1) * BLOCK, :COLS]
            msgv_s[t * GROUP + u, :BLOCK] = got[u * BLOCK : (u + 1) * BLOCK, COLS:]
            msgk_s[t * GROUP + u, BLOCK:] = extra[:, :COLS]
            msgv_s[t * GROUP + u, BLOCK:] = extra[:, COLS:]
        for send in sends(t):
            send.start()
        return carry

    lax.fori_loop(0, SENDERS // GROUP, gather, 0)
    for t in range(SENDERS // GROUP):
        for send in sends(t):
            send.wait()


def gather_partner(exp_ref, m, table, first_col=0):
    blocks = []
    for t in range(0, Q_BLOCKS, 4):
        hot = one_hot_of_rows([exp_row(exp_ref, m, t + u) for u in range(4)])
        got = dot(hot, table[:, first_col : first_col + COLS]).astype(BF16)
        blocks += [got[u * BLOCK : (u + 1) * BLOCK] for u in range(4)]
    return blocks


def sum_picks():
    sub = iota((2 * Q_BLOCKS * COLS, 16), 0)
    col = iota((2 * Q_BLOCKS * COLS, 16), 1)
    return (col == (sub >> 8) + jnp.where((sub & (COLS - 1)) < HEAD, 0, 8)).astype(F32).astype(BF16)


def head_sums(a_ref, blocks, picks):
    parts = []
    for i, b in enumerate(blocks):
        prod = a_ref[i * BLOCK : (i + 1) * BLOCK, :].astype(F32) * b.astype(F32)
        high = prod.astype(BF16)
        parts += [high, (prod - high.astype(F32)).astype(BF16)]
    return flat(dot(jnp.concatenate(parts, axis=1), picks).T)


def partner_key_kernel(exp_ref, t0_ref, t1_ref, t2_ref, t3_ref, q_ref, out_ref, sp_ref):
    picks = sum_picks()
    for m, table in enumerate((t0_ref, t1_ref, t2_ref, t3_ref)):
        blocks = gather_partner(exp_ref, m, table)
        for i, block in enumerate(blocks):
            out_ref[m * Q_BLOCKS + i] = block
        sp_ref[m] = head_sums(q_ref, blocks, picks)


def head_picks(i):
    return (iota((16, COLS), 0) == jnp.where(iota((16, COLS), 1) < HEAD, i, 8 + i)).astype(F32).astype(BF16)


def finish_kernel(
    me_ref, exp_ref, t0_ref, t1_ref, t2_ref, t3_ref, cot_ref, sp_ref, lse_ref, local_ref, _, pair_ref, back_ref,
    delta_ref, message_ref, sems,
):
    picks = sum_picks()
    lse = lse_ref[...]
    delta = local_ref[...]
    probs, dprobs = [], []
    for m, table in enumerate((t0_ref, t1_ref, t2_ref, t3_ref)):
        blocks = gather_partner(exp_ref, m, table, table.shape[1] - COLS)
        prob = jnp.exp(sp_ref[m] - lse)
        dprob = head_sums(cot_ref, blocks, picks)
        delta += prob * dprob
        back_ref[m, 16:] = tall(prob).astype(BF16)
        for i, block in enumerate(blocks):
            pair_ref[m * Q_BLOCKS + i] = block
        probs.append(prob)
        dprobs.append(dprob)
    delta_ref[...] = delta
    for m in range(EXPANDERS):
        back_ref[m, :16] = tall(probs[m] * (dprobs[m] - delta)).astype(BF16)
    copies = [
        pltpu.make_async_copy(
            back_ref.at[m], message_ref.at[me_ref[0] ^ (1 << m), pl.ds(SLOTS, PART_ROWS)], sems.at[m]
        )
        for m in range(EXPANDERS)
    ]
    for copy in copies:
        copy.start()
    for copy in copies:
        copy.wait()


def join_partners(out_ref, out_t_ref, part_rows, pair_ref, scale):
    turned = [turned_weights(rows) for rows in part_rows]
    for i in range(Q_BLOCKS):
        total = head_rows(out_t_ref[i]).T
        for m in range(EXPANDERS):
            total += dot(turned[m], head_picks(i)) * pair_ref[m * Q_BLOCKS + i].astype(F32)
        out_ref[i * BLOCK : (i + 1) * BLOCK, :] = (total * scale).astype(BF16)


def attend_kernel(out_t_ref, back_ref, pair_ref, att_ref):
    join_partners(att_ref, out_t_ref, [back_ref[m, 16:] for m in range(EXPANDERS)], pair_ref, 1.0)


def flat(x):
    return jnp.concatenate([x[:8], x[8:]], axis=1)


def tall(x):
    return jnp.concatenate([x[:, :BLOCK], x[:, BLOCK:]], axis=0)


def turned_weights(tall_rows):
    return tall_rows.astype(F32).T.astype(BF16)


def prepare_kernel(q_ref, cot_ref, qt_ref, qs_ref, ct_ref, cs_ref):
    def one(i, carry):
        q = q_ref[q_rows(i), :]
        cot = cot_ref[q_rows(i), :]
        qt_ref[i] = stacked_t(q)
        qs_ref[i] = stacked(q)
        ct_ref[i] = stacked_t(cot)
        cs_ref[i] = stacked(cot)
        return carry

    lax.fori_loop(0, Q_BLOCKS, one, 0, unroll=2)


def plan_kernel(mask_ref, halo_ref, list_ref, where_ref, block_ref, count_ref, live_ref):
    for j in range(Q_BLOCKS):
        live_ref[j] = BLOCK
    live_ref[GLOBAL_BLOCK] = BLOCK
    live_ref[EMPTY_BLOCK] = 0

    def copy_count(s, carry):
        live_ref[Q_BLOCKS + s] = halo_ref[s]
        return carry

    lax.fori_loop(0, SENDERS, copy_count, 0)

    def per_block(i, items):
        list_ref[i * LIST] = GLOBAL_BLOCK

        def put(j, n):
            list_ref[i * LIST + n] = j
            used = jnp.logical_and(mask_ref[i * GLOBAL_BLOCK + j] > 0, live_ref[j] > 0)
            return n + used.astype(jnp.int32)

        n = lax.fori_loop(0, GLOBAL_BLOCK, put, 1)
        for extra in range(GROUP):
            list_ref[i * LIST + n + extra] = EMPTY_BLOCK
        groups = (n + GROUP - 1) // GROUP

        def item(g, carry):
            where_ref[items + g] = i * LIST + g * GROUP
            block_ref[items + g] = i
            return carry

        lax.fori_loop(0, groups, item, 0)
        return items + groups

    items = lax.fori_loop(0, Q_BLOCKS, per_block, 0)
    for u in range(GROUP):
        list_ref[Q_BLOCKS * LIST + u] = EMPTY_BLOCK
    for u in range(ITEMS - 1):
        where_ref[items + u] = Q_BLOCKS * LIST
        block_ref[items + u] = 0
    count_ref[0] = (items + ITEMS - 1) // ITEMS


def fill(dst, dst_t, first_col,  own_ref, halo_ref, gid_ref, glob_ref):
    def put(j, block):
        if dst is not None:
            dst[j] = block
        if dst_t is not None:
            dst_t[j] = block.T

    def own(j, carry):
        put(j, own_ref[q_rows(j), :])
        return carry

    def halo(j, carry):
        put(Q_BLOCKS + j, halo_ref[j, :BLOCK])
        return carry

    lax.fori_loop(0, Q_BLOCKS, own, 0, unroll=4)
    lax.fori_loop(0, SENDERS, halo, 0, unroll=4)
    slot_col = owner_ranks(gid_ref[...])[2]
    wide = jnp.concatenate([slot_col] * (SENDERS * EXTRA // BLOCK), axis=1)
    hot = (wide == iota((BLOCK, SENDERS * EXTRA), 1)).astype(F32).astype(BF16)
    extra = jnp.concatenate([halo_ref[s, BLOCK:] for s in range(SENDERS)], axis=0)
    rows = (dot(hot, extra) + glob_ref[:, first_col : first_col + COLS].astype(F32)).astype(BF16)
    put(GLOBAL_BLOCK, rows)
    put(EMPTY_BLOCK, jnp.zeros((BLOCK, COLS), BF16))


def stacked(rows):
    lanes = iota((BLOCK, COLS), 1)
    zero = jnp.zeros_like(rows)
    return jnp.concatenate([jnp.where(lanes < HEAD, rows, zero), jnp.where(lanes < HEAD, zero, rows)], axis=0)


def stacked_t(rows):
    turned = rows.T
    subs = iota((COLS, BLOCK), 0)
    zero = jnp.zeros_like(turned)
    return jnp.concatenate([jnp.where(subs < HEAD, turned, zero), jnp.where(subs < HEAD, zero, turned)], axis=1)


def head_rows(turned):
    return jnp.concatenate([turned[:HEAD, :BLOCK], turned[HEAD:, BLOCK:]], axis=0)


def masked_scores(blocks, k_s, turned_q, live_ref):
    keys = jnp.concatenate([k_s[b] for b in blocks], axis=0)
    scores = dot(keys, turned_q)
    row_id = iota((BLOCK, 2 * BLOCK), 0)
    return jnp.concatenate(
        [
            jnp.where(row_id < live_ref[b], scores[u * BLOCK : (u + 1) * BLOCK], NEG)
            for u, b in enumerate(blocks)
        ],
        axis=0,
    )


def item_of(t, u, list_ref, where_ref, block_ref):
    where = where_ref[t * ITEMS + u]
    return block_ref[t * ITEMS + u], [list_ref[where + b] for b in range(GROUP)]


def q_rows(i):
    return pl.ds(pl.multiple_of(i * BLOCK, BLOCK), BLOCK)


def score_kernel(
    list_ref, where_ref, block_ref, count_ref, live_ref, qt_ref, own_ref, hk_ref, gid_ref, glob_ref, lse_ref, k_s, kt_ref,
    top_s, total_s,
):
    fill(k_s, kt_ref, 0, own_ref, hk_ref, gid_ref, glob_ref)

    top_s[...] = jnp.full((Q_BLOCKS, 8, 2 * BLOCK), NEG, F32)
    total_s[...] = jnp.zeros((Q_BLOCKS, 8, 2 * BLOCK), F32)

    def step(t, carry):
        for item in range(ITEMS):
            i, blocks = item_of(t, item, list_ref, where_ref, block_ref)
            turned_q = qt_ref[i]
            parts = []
            for u in range(0, GROUP, SCORE_PAIR):
                scores = masked_scores(blocks[u : u + SCORE_PAIR], k_s, turned_q, live_ref)
                scores = scores.reshape(SCORE_PAIR * BLOCK // 8, 8, 2 * BLOCK)
                top = jnp.max(scores, axis=0)
                parts.append((top, jnp.sum(jnp.exp(scores - top[None]), axis=0)))
            parts.append((top_s[i], total_s[i]))
            best = functools.reduce(jnp.maximum, [top for top, _ in parts])
            top_s[i] = best
            total_s[i] = sum(total * jnp.exp(top - best) for top, total in parts)
        return carry

    lax.fori_loop(0, count_ref[0], step, 0)
    for i in range(Q_BLOCKS):
        top = top_s[i]
        best = jnp.max(top, axis=0, keepdims=True)
        denominator = jnp.sum(total_s[i] * jnp.exp(top - best), axis=0, keepdims=True)
        lse_ref[i : i + 1, :] = best + jnp.log(denominator)


def value_kernel(
    list_ref, where_ref, block_ref, count_ref, live_ref, k_s, ownv_ref, hv_ref, glob_ref, qt_ref, ct_ref, cs_ref, part_ref,
    sp_ref, gid_ref, own_ref, halo_ref, gout_ref, out_s, delta_ref, lse_ref, acc_s, vt_s,
):
    fill(None, vt_s, COLS, ownv_ref, hv_ref, gid_ref, glob_ref)
    clear_blocks(acc_s)
    part = part_ref[...]
    best = part
    for m in range(EXPANDERS):
        best = jnp.maximum(best, sp_ref[m])
    total = jnp.exp(part - best)
    for m in range(EXPANDERS):
        total += jnp.exp(sp_ref[m] - best)
    lse_ref[...] = best + jnp.log(total)

    out_s[...] = jnp.zeros((Q_BLOCKS, COLS, 2 * BLOCK), F32)

    def step(t, carry):
        for item in range(ITEMS):
            i, blocks = item_of(t, item, list_ref, where_ref, block_ref)
            turned_q = qt_ref[i]
            cot_stack = cs_ref[i]
            lse = lse_ref[pl.ds(i, 1), :]
            for u in range(0, GROUP, PAIR):
                pair = blocks[u : u + PAIR]
                scores = masked_scores(pair, k_s, turned_q, live_ref)
                weight = jnp.exp(scores - lse).astype(BF16)
                out_s[i] += dot(jnp.concatenate([vt_s[b] for b in pair], axis=1), weight)
                grads = dot(weight, cot_stack)
                for w, b in enumerate(pair):
                    acc_s[b] += grads[w * BLOCK : (w + 1) * BLOCK]
        return carry

    lax.fori_loop(0, count_ref[0], step, 0)
    for i in range(Q_BLOCKS):
        delta_ref[i : i + 1, :] = jnp.sum(out_s[i] * ct_ref[i].astype(F32), axis=0, keepdims=True)
    store_parts(acc_s, own_ref, halo_ref, gid_ref, gout_ref)


def clear_blocks(acc_s):
    def clear(j, carry):
        acc_s[j] = jnp.zeros((BLOCK, COLS), F32)
        return carry

    lax.fori_loop(0, KEY_BLOCKS, clear, 0, unroll=2)


def store_parts(acc_s, own_ref, halo_ref, gid_ref, gout_ref):
    def own(j, carry):
        own_ref[q_rows(j), :] = acc_s[j]
        return carry

    def halo(j, carry):
        halo_ref[j, :BLOCK] = acc_s[Q_BLOCKS + j].astype(BF16)
        return carry

    lax.fori_loop(0, Q_BLOCKS, own, 0, unroll=2)
    lax.fori_loop(0, SENDERS, halo, 0, unroll=4)
    grads = acc_s[GLOBAL_BLOCK].astype(BF16)
    gout_ref[...] = grads
    slot_row = owner_ranks(gid_ref[...])[1]
    hot = (iota((SENDERS * EXTRA, BLOCK), 0) == slot_row).astype(F32).astype(BF16)
    extra = dot(hot, grads).astype(BF16)
    for s in range(SENDERS):
        halo_ref[s, BLOCK:SLOTS] = extra[s * EXTRA : (s + 1) * EXTRA]


def key_kernel(
    list_ref, where_ref, block_ref, count_ref, live_ref, k_s, kt_s, ownv_ref, hv_ref, glob_ref, qt_ref, qs_ref, ct_ref, lse_ref,
    delta_ref, gid_ref, out_s, own_ref, halo_ref, gout_ref, acc_s, v_s,
):
    fill(v_s, None, COLS, ownv_ref, hv_ref, gid_ref, glob_ref)
    clear_blocks(acc_s)

    out_s[...] = jnp.zeros((Q_BLOCKS, COLS, 2 * BLOCK), F32)

    def step(t, carry):
        for item in range(ITEMS):
            i, blocks = item_of(t, item, list_ref, where_ref, block_ref)
            turned_q = qt_ref[i]
            q_stack = qs_ref[i]
            turned_cot = ct_ref[i]
            lse = lse_ref[pl.ds(i, 1), :]
            delta = delta_ref[pl.ds(i, 1), :]
            for u in range(0, GROUP, PAIR):
                pair = blocks[u : u + PAIR]
                scores = masked_scores(pair, k_s, turned_q, live_ref)
                dprob = dot(jnp.concatenate([v_s[b] for b in pair], axis=0), turned_cot)
                dscore = (jnp.exp(scores - lse) * (dprob - delta)).astype(BF16)
                out_s[i] += dot(jnp.concatenate([kt_s[b] for b in pair], axis=1), dscore)
                grads = dot(dscore, q_stack)
                for w, b in enumerate(pair):
                    acc_s[b] += grads[w * BLOCK : (w + 1) * BLOCK]
        return carry

    lax.fori_loop(0, count_ref[0], step, 0)
    store_parts(acc_s, own_ref, halo_ref, gid_ref, gout_ref)


def scatter_into(acc_s, splits, data):
    subs = packed_iota(0)
    one, zero = jnp.ones((), BF16), jnp.zeros((), BF16)
    bases = [(jnp.where(subs == low, one, zero), jnp.broadcast_to(high, (BLOCK, BLOCK))) for low, high in splits]
    for c in range(NODES_HERE // BLOCK):
        hot = jnp.concatenate([jnp.where(high == jnp.asarray(c, BF16), base, zero) for base, high in bases], axis=1)
        acc_s[c * BLOCK : (c + 1) * BLOCK, :] += dot(hot, data)


def add_halo(acc_s, me_ref, ret_ref, rows_ref, gid_ref, more_ref):
    def halo(t, carry):
        splits = [split_index(rows_ref[pl.ds(t * GROUP + u, 1), :]) for u in range(GROUP)]
        data = jnp.concatenate([ret_ref[t * GROUP + u, :BLOCK] for u in range(GROUP)], axis=0)
        scatter_into(acc_s, splits, data)
        return carry

    lax.fori_loop(0, SENDERS // GROUP, halo, 0)
    extra = ret_ref[0, BLOCK:SLOTS].astype(F32)
    for s in range(1, SENDERS):
        extra += ret_ref[s, BLOCK:SLOTS].astype(F32)
    high = extra.astype(BF16)
    data = jnp.concatenate([high, (extra - high.astype(F32)).astype(BF16)], axis=0)
    mine = jnp.broadcast_to(mine_columns(gid_ref[...], me_ref[0]), (EXTRA, NODES_HERE))
    hot = (mine == iota((EXTRA, NODES_HERE), 1)).astype(F32)
    hot = jnp.concatenate([hot, hot], axis=0).T.astype(BF16)
    acc_s[...] += dot(hot, data)
    gids = gid_ref[...]
    local = jnp.where((gids >> 10) == me_ref[0], gids & (NODES_HERE - 1), NODES_HERE)
    more = more_ref[...]
    high = more.astype(BF16)
    low = (more - high.astype(F32)).astype(BF16)
    scatter_into(acc_s, [split_index(local)] * 2, jnp.concatenate([high, low], axis=0))


def add_partners(acc_s, parts, others, first_col):
    for m, (part, other) in enumerate(zip(parts, others)):
        turned = turned_weights(part)
        index_low = other[NODES_HERE + m * Q_BLOCKS : NODES_HERE + (m + 1) * Q_BLOCKS, :COLS]
        index_high = other[NODES_HERE + m * Q_BLOCKS : NODES_HERE + (m + 1) * Q_BLOCKS, COLS:]
        for t in range(Q_BLOCKS // GROUP):
            splits, data = [], []
            for u in range(GROUP):
                i = t * GROUP + u
                splits.append((index_low[i : i + 1], index_high[i : i + 1]))
                wide = dot(turned, head_picks(i))
                rows = other[i * BLOCK : (i + 1) * BLOCK, first_col : first_col + COLS].astype(F32)
                data.append((wide * rows).astype(BF16))
            scatter_into(acc_s, splits, jnp.concatenate(data, axis=0))


def feature_part(feat_ref, k):
    return pl.ds(pl.multiple_of(((feat_ref[0] + k) % 4) * COLS, COLS), COLS)


def value_back_kernel(
    me_ref, feat_ref, ownv_ref, ret_ref, ownk_ref, rows_ref, o0_ref, o1_ref, o2_ref, o3_ref, gid_ref, wq_ref, wv_ref,
    out_t_ref, back_ref, pair_ref, more_ref, acck_ref, pre_ref, accv_s, gq_ref,
):
    others = (o0_ref, o1_ref, o2_ref, o3_ref)
    parts = [ret_ref[me_ref[0] ^ (1 << m), SLOTS:] for m in range(EXPANDERS)]
    join_partners(
        gq_ref, out_t_ref, [back_ref[m, :16] for m in range(EXPANDERS)], pair_ref, 1.0 / math.sqrt(HEAD)
    )
    accv_s[...] = ownv_ref[...]
    add_halo(accv_s, me_ref, ret_ref, rows_ref, gid_ref, more_ref)
    add_partners(accv_s, [part[16:] for part in parts], others, COLS)
    acck_ref[...] = ownk_ref[...]
    add_partners(acck_ref, [part[:16] for part in parts], others, 0)
    grad_value = accv_s[...].astype(BF16)
    for k in range(4):
        part = feature_part(feat_ref, k)
        pre_ref[k] = dot_nt(gq_ref[...], wq_ref[part, :]) + dot_nt(grad_value, wv_ref[part, :])


def key_back_kernel(
    me_ref, feat_ref, acck_ref, ret_ref, rows_ref, gid_ref, wk_ref, pre_ref, more_ref, t0_ref, t1_ref, t2_ref, t3_ref,
    acc_s, own_s, pre_s, sems,
):
    own_copy = pltpu.make_async_copy(acck_ref, own_s, sems.at[0])
    pre_copy = pltpu.make_async_copy(pre_ref, pre_s, sems.at[1])
    own_copy.start()
    pre_copy.start()
    acc_s[...] = jnp.zeros((NODES_HERE, COLS), F32)
    add_halo(acc_s, me_ref, ret_ref, rows_ref, gid_ref, more_ref)
    own_copy.wait()
    grad_key = (acc_s[...] + own_s[...]).astype(BF16)
    pre_copy.wait()
    for k, out in ((1, t1_ref), (2, t2_ref), (3, t3_ref), (0, t0_ref)):
        out[...] = (pre_s[k] + dot_nt(grad_key, wk_ref[feature_part(feat_ref, k), :])).astype(out.dtype)


def shape(dims, kind=BF16):
    return jax.ShapeDtypeStruct(dims, kind)


def call(kernel, ins, outs, args, scratch=(), name=None, flops=0, out_spaces=None, aliases={}, mib=56):
    cost = pl.CostEstimate(flops=flops, transcendentals=0, bytes_accessed=4_000_000)
    return pl.pallas_call(
        kernel,
        out_shape=outs,
        in_specs=ins,
        out_specs=out_spaces or tuple(vmem() for _ in outs),
        scratch_shapes=list(scratch),
        compiler_params=params(mib),
        cost_estimate=cost,
        input_output_aliases=aliases,
        name=name,
    )(*args)


def blocks_of(kind):
    return pltpu.VMEM((KEY_BLOCKS, BLOCK, COLS), kind)


def run_project(me, features, w_query, w_key, w_value, cotangent, rows, exp_list, gids):
    anywhere = pl.BlockSpec(memory_space=pl.ANY)
    return call(
        project_kernel,
        [smem()] + [vmem()] * 8,
        (
            shape((NODES_HERE, COLS)),
            shape((NODES_HERE, COLS)),
            shape((NODES_HERE, COLS)),
            shape((NODES_HERE, 2 * COLS)),
            shape((SENDERS, SLOTS, COLS)),
            shape((SENDERS, SLOTS, COLS)),
            shape((NODES_HERE + EXPANDERS * Q_BLOCKS, 2 * COLS)),
            shape((1,), jnp.int32),
        ),
        (me, features, w_query, w_key, w_value, cotangent, rows, exp_list, gids),
        name="project",
        mib=56,
        flops=3_000_000_000,
        out_spaces=(vmem(), vmem(), vmem(), vmem(), anywhere, anywhere, vmem(), smem()),
        scratch=[
            pltpu.VMEM((SENDERS, SLOTS, COLS), BF16),
            pltpu.VMEM((SENDERS, SLOTS, COLS), BF16),
            pltpu.SemaphoreType.DMA((2, SENDERS // GROUP)),
        ],
    )


def run_plan(block_mask, halo_count):
    sizes = (Q_BLOCKS * LIST + GROUP, MAX_ITEMS, MAX_ITEMS, 1, KEY_BLOCKS)
    return call(
        plan_kernel,
        [smem()] * 2,
        tuple(shape((size,), jnp.int32) for size in sizes),
        (block_mask.reshape(-1), halo_count.reshape(-1)),
        name="plan",
        out_spaces=tuple(smem() for _ in sizes),
    )


def run_partner_keys(exp_rows, swaps, query):
    return call(
        partner_key_kernel,
        [vmem()] * 6,
        (shape((EXPANDERS * Q_BLOCKS, BLOCK, COLS)), shape((EXPANDERS, Q_BLOCKS, 2 * BLOCK), F32)),
        (exp_rows, *swaps, query),
        name="partners",
        flops=5_000_000_000,
    )


def run_finish(me, exp_rows, swaps, cotangent, scores, lse, local, back_v):
    anywhere = pl.BlockSpec(memory_space=pl.ANY)
    return call(
        finish_kernel,
        [smem()] + [vmem()] * 9 + [anywhere],
        (
            shape((EXPANDERS * Q_BLOCKS, BLOCK, COLS)),
            shape((EXPANDERS, PART_ROWS, BLOCK)),
            shape((Q_BLOCKS, 2 * BLOCK), F32),
            shape((SENDERS, BACK, COLS)),
        ),
        (me, exp_rows, *swaps, cotangent, scores, lse, local, back_v),
        name="finish",
        flops=5_000_000_000,
        out_spaces=(vmem(), vmem(), vmem(), anywhere),
        scratch=[pltpu.SemaphoreType.DMA((EXPANDERS,))],
        aliases={10: 3},
    )


def run_attend(out_t, back, value_pairs):
    return call(
        attend_kernel,
        [vmem()] * 3,
        (shape((NODES_HERE, COLS)),),
        (out_t, back, value_pairs),
        name="attend",
        flops=2_000_000_000,
    )[0]


def run_prepare(query, cotangent):
    wide, high = shape((Q_BLOCKS, COLS, 2 * BLOCK)), shape((Q_BLOCKS, 2 * BLOCK, COLS))
    return call(
        prepare_kernel, [vmem()] * 2, (wide, high, wide, high), (query, cotangent), name="prepare", flops=2_000_000_000
    )


def run_scores(plan, turned_q, own, halo_k, gids, glob):
    return call(
        score_kernel,
        [smem()] * 5 + [vmem()] * 5,
        (
            shape((Q_BLOCKS, 2 * BLOCK), F32),
            shape((KEY_BLOCKS, BLOCK, COLS)),
            shape((KEY_BLOCKS, COLS, BLOCK)),
        ),
        (*plan, turned_q, own, halo_k, gids, glob),
        scratch=[pltpu.VMEM((Q_BLOCKS, 8, 2 * BLOCK), F32)] * 2,
        name="scores",
        flops=12_000_000_000,
    )


def run_values(plan, keys, own_values, halo_v, glob, prepared, part, scores, gids):
    turned_q, _, turned_cot, cot_stack = prepared
    return call(
        value_kernel,
        [smem()] * 5 + [vmem()] * 10,
        (
            shape((NODES_HERE, COLS), F32),
            shape((SENDERS, BACK, COLS)),
            shape((BLOCK, COLS)),
            shape((Q_BLOCKS, COLS, 2 * BLOCK), F32),
            shape((Q_BLOCKS, 2 * BLOCK), F32),
            shape((Q_BLOCKS, 2 * BLOCK), F32),
        ),
        (*plan, keys, own_values, halo_v, glob, turned_q, turned_cot, cot_stack, part, scores, gids),
        scratch=[blocks_of(F32), blocks_of(BF16)],
        name="values",
        flops=20_000_000_000,
    )


def run_keys(plan, keys, turned_k, own_values, halo_v, glob, prepared, lse, delta, gids):
    turned_q, q_stack, turned_cot, _ = prepared
    return call(
        key_kernel,
        [smem()] * 5 + [vmem()] * 11,
        (
            shape((Q_BLOCKS, COLS, 2 * BLOCK), F32),
            shape((NODES_HERE, COLS), F32),
            shape((SENDERS, SLOTS, COLS)),
            shape((BLOCK, COLS)),
        ),
        (*plan, keys, turned_k, own_values, halo_v, glob, turned_q, q_stack, turned_cot, lse, delta, gids),
        scratch=[blocks_of(F32), blocks_of(BF16)],
        name="keys",
        mib=56,
        flops=25_000_000_000,
    )


def run_value_back(me, feat, own_v, returned_v, own_k, rows, others, gids, w_query, w_value, out_t, back, pairs, more):
    return call(
        value_back_kernel,
        [smem()] * 2 + [vmem()] * 15,
        (shape((NODES_HERE, COLS), F32), shape((4, NODES_HERE, COLS), F32)),
        (me, feat, own_v, returned_v, own_k, rows, *others, gids, w_query, w_value, out_t, back, pairs, more),
        scratch=[pltpu.VMEM((NODES_HERE, COLS), F32), pltpu.VMEM((NODES_HERE, COLS), BF16)],
        name="value_back",
        mib=56,
        flops=12_000_000_000,
    )


def run_key_back(me, feat, own_k, returned_k, rows, gids, w_key, pre, more):
    anywhere = pl.BlockSpec(memory_space=pltpu.HBM)
    return call(
        key_back_kernel,
        [smem()] * 2 + [anywhere] + [vmem()] * 4 + [anywhere, vmem()],
        (shape((NODES_HERE, COLS), F32),) + tuple(shape((NODES_HERE, COLS)) for _ in range(3)),
        (me, feat, own_k, returned_k, rows, gids, w_key, pre, more),
        scratch=[
            pltpu.VMEM((NODES_HERE, COLS), F32),
            pltpu.VMEM((NODES_HERE, COLS), F32),
            pltpu.VMEM((4, NODES_HERE, COLS), F32),
            pltpu.SemaphoreType.DMA((2,)),
        ],
        name="key_back",
        mib=20,
        flops=8_000_000_000,
    )


def ranks(global_ids):
    owner = global_ids // NODES_HERE
    ids = jnp.arange(BLOCK)
    return owner, ((owner[:, None] == owner[None, :]) & (ids[None, :] < ids[:, None])).sum(1)


def more_globals(rounds, global_ids, my_index, own_k, own_v):
    def body(state):
        r, glob = state
        ids = global_ids + jnp.minimum(r, 0)
        owner, rank = ranks(ids)
        slot = rank - r * EXTRA
        here = (slot >= 0) & (slot < EXTRA)
        place = jnp.where((owner == my_index) & here, slot, EXTRA)
        local = jnp.where(here, ids % NODES_HERE, 0)
        found = jnp.concatenate([own_k[local], own_v[local]], axis=1)
        rows = jnp.zeros((EXTRA + 1, 2 * COLS), BF16).at[place].set(found)[:EXTRA]
        got = lax.all_to_all(jnp.broadcast_to(rows[None], (SENDERS, *rows.shape)), "dom", 0, 0, tiled=True)
        found = got.reshape(SENDERS * EXTRA, -1)[jnp.clip(owner * EXTRA + slot, 0, SENDERS * EXTRA - 1)]
        return r + 1, jnp.where(here[:, None], found, glob)

    start = (jnp.asarray(1, jnp.int32), jnp.zeros((BLOCK, 2 * COLS), BF16))
    return lax.while_loop(lambda state: state[0] < rounds, body, start)[1]


def more_grads(rounds, global_ids, my_index, part_k, part_v):
    def body(state):
        r, more_k, more_v = state
        ids = global_ids + jnp.minimum(r, 0)
        owner, rank = ranks(ids)
        slot = rank - r * EXTRA
        here = (slot >= 0) & (slot < EXTRA)
        place = jnp.where(here, owner * EXTRA + slot, SENDERS * EXTRA)

        def summed(part):
            rows = jnp.zeros((SENDERS * EXTRA + 1, COLS), BF16).at[place].set(part)[: SENDERS * EXTRA]
            got = lax.all_to_all(rows.reshape(SENDERS, EXTRA, -1), "dom", 0, 0, tiled=True).astype(F32).sum(0)
            return jnp.where(((owner == my_index) & here)[:, None], got[jnp.clip(slot, 0, EXTRA - 1)], 0.0)

        return r + 1, more_k + summed(part_k), more_v + summed(part_v)

    zeros = jnp.zeros((BLOCK, COLS), F32)
    start = (jnp.asarray(1, jnp.int32), zeros, zeros)
    return lax.while_loop(lambda state: state[0] < rounds, body, start)[1:]


def on_device(
    features,
    w_query,
    w_key,
    w_value,
    cotangent,
    send_rows,
    halo_count,
    block_mask,
    exp_rows,
    global_ids,
):
    dom_count = lax.axis_size("dom")
    my_index = lax.axis_index("dom")

    def swapped(value, bit):
        return lax.ppermute(value, "dom", [(i, i ^ (1 << bit)) for i in range(dom_count)])

    rows = send_rows[0]
    gids = global_ids.reshape(1, BLOCK)
    me = my_index.reshape(1).astype(jnp.int32)
    feat = lax.axis_index("feat").reshape(1).astype(jnp.int32)

    query, own_keys, own_values, paired, out_k, out_v, away, rounds = run_project(
        me, features, w_query, w_key, w_value, cotangent, rows, exp_rows, gids
    )
    rounds = rounds[0]
    glob = more_globals(rounds, global_ids, my_index, own_keys, own_values)
    out_k, out_v, glob = lax.optimization_barrier((out_k, out_v, glob))
    halo_k = lax.all_to_all(out_k, "dom", 0, 0, tiled=True)
    key_swaps = [swapped(paired if m in TOGETHER else own_keys, m) for m in range(EXPANDERS)]
    plan = run_plan(block_mask, halo_count)
    prepared = run_prepare(query, cotangent)
    own_values_late, *prepared = lax.optimization_barrier((own_values, *prepared))
    value_swaps = {m: swapped(own_values_late, m) for m in range(EXPANDERS) if m not in TOGETHER}
    halo_v = lax.all_to_all(out_v, "dom", 0, 0, tiled=True)
    part, keys, turned_k = run_scores(plan, prepared[0], own_keys, halo_k, gids, glob)
    part, *key_swaps = lax.optimization_barrier((part, *key_swaps))
    pairs, scores = run_partner_keys(exp_rows, key_swaps, query)
    away, scores = lax.optimization_barrier((away, scores))
    others = [swapped(away, m) for m in range(EXPANDERS)]
    own_v, back_v, glob_v, out_t, local, lse = run_values(
        plan, keys, own_values, halo_v, glob, prepared, part, scores, gids
    )
    local, value_swaps = lax.optimization_barrier((local, value_swaps))
    value_swaps = [value_swaps.get(m, key_swaps[m]) for m in range(EXPANDERS)]
    value_pairs, back, delta, back_v = run_finish(
        me, exp_rows, value_swaps, cotangent, scores, lse, local, back_v
    )
    returned_v = lax.all_to_all(back_v, "dom", 0, 0, tiled=True)
    query_t, own_k, back_k, glob_k = run_keys(
        plan, keys, turned_k, own_values, halo_v, glob, prepared, lse, delta, gids
    )
    glob_k, returned_v, *others = lax.optimization_barrier((glob_k, returned_v, *others))
    more_k, more_v = more_grads(rounds, global_ids, my_index, glob_k, glob_v)
    back_k, more_k, more_v = lax.optimization_barrier((back_k, more_k, more_v))
    returned_k = lax.all_to_all(back_k, "dom", 0, 0, tiled=True)
    own_k, pre = run_value_back(
        me, feat, own_v, returned_v, own_k, rows, others, gids, w_query, w_value, query_t, back, pairs, more_v
    )
    mine, *away = run_key_back(me, feat, own_k, returned_k, rows, gids, w_key, pre, more_k)
    out_t, mine = lax.optimization_barrier((out_t, mine))
    attended = run_attend(out_t, back, value_pairs)
    for k in (2, 1, 3):
        mine = mine + lax.ppermute(away[k - 1], "feat", [(i, (i + k) % 4) for i in range(4)]).astype(F32)
    return (attended, mine.astype(BF16))


def solution(mesh):
    return jax.shard_map(
        on_device,
        mesh=mesh,
        in_specs=(
            P("dom", None),
            P(None, "feat"),
            P(None, "feat"),
            P(None, "feat"),
            P("dom", "feat"),
            P("dom", None, None),
            P(None, "dom"),
            P("dom", None),
            P(None, "dom"),
            P(),
        ),
        out_specs=(P("dom", "feat"), P("dom", "feat")),
        check_vma=False,
    )
```

```python
import functools
import math

import jax
import jax.numpy as jnp
from jax import lax
from jax.experimental import pallas as pl
from jax.experimental.pallas import tpu as pltpu
from jax.sharding import PartitionSpec as P

HEAD = 64
BLOCK = 128
EXPANDERS = 4
COLS = 128
NODES_HERE = 1024
Q_BLOCKS = NODES_HERE // BLOCK
SENDERS = 32
GLOBAL_BLOCK = Q_BLOCKS + SENDERS
EMPTY_BLOCK = GLOBAL_BLOCK + 1
KEY_BLOCKS = EMPTY_BLOCK + 1
GROUP = 8
PAIR = 8
SCORE_PAIR = 4
ITEMS = 2
MAX_ITEMS = 64
TOGETHER = (0, 3)
LIST = 56
EXTRA = 16
SLOTS = BLOCK + EXTRA
PART_ROWS = 32
BACK = SLOTS + PART_ROWS
NEG = -1e30
F32 = jnp.float32
BF16 = jnp.bfloat16


def params(mib):
    return pltpu.CompilerParams(vmem_limit_bytes=mib * 1024 * 1024)


def vmem():
    return pl.BlockSpec(memory_space=pltpu.VMEM)


def anywhere():
    return pl.BlockSpec(memory_space=pl.ANY)


def start_copies(pairs, sems):
    copies = [pltpu.make_async_copy(src, dst, sems.at[n]) for n, (src, dst) in enumerate(pairs)]
    for copy in copies:
        copy.start()
    return copies


def wait_all(copies):
    for copy in copies:
        copy.wait()


def smem():
    return pl.BlockSpec(memory_space=pltpu.SMEM)


def iota(shape, dim):
    return lax.broadcasted_iota(jnp.int32, shape, dim)


def dot(a, b):
    return jnp.dot(a, b, preferred_element_type=F32)


def dot_nt(a, b):
    return lax.dot_general(a, b, (((1,), (1,)), ((), ())), preferred_element_type=F32)


def split_index(index):
    return (index & (BLOCK - 1)).astype(F32).astype(BF16), (index >> 7).astype(F32).astype(BF16)


def packed_iota(dim):
    return iota((BLOCK, BLOCK), dim).astype(F32).astype(BF16)


def one_hot_columns(column):
    low, high = split_index(column)
    lanes = jnp.concatenate([packed_iota(1)] * (column.shape[0] // BLOCK), axis=0)
    one, zero = jnp.ones((), BF16), jnp.zeros((), BF16)
    base = jnp.where(low == lanes, one, zero)
    return jnp.concatenate(
        [jnp.where(high == jnp.asarray(c, BF16), base, zero) for c in range(NODES_HERE // BLOCK)], axis=1
    )


def one_hot_of_rows(index_rows):
    columns = [jnp.broadcast_to(row, (BLOCK, BLOCK)).T for row in index_rows]
    return one_hot_columns(jnp.concatenate(columns, axis=0))


def owner_ranks(gid_row):
    owner = jnp.broadcast_to(gid_row >> 10, (BLOCK, BLOCK))
    owner_t = owner.T
    same = owner == owner_t
    subs, lanes = iota((BLOCK, BLOCK), 0), iota((BLOCK, BLOCK), 1)
    row = jnp.sum(jnp.where(jnp.logical_and(same, subs < lanes), 1.0, 0.0), axis=0, keepdims=True)
    col = jnp.sum(jnp.where(jnp.logical_and(same, lanes < subs), 1.0, 0.0), axis=1, keepdims=True)
    row, col = row.astype(jnp.int32), jnp.broadcast_to(col, (BLOCK, BLOCK)).astype(jnp.int32)
    slot_row = jnp.where(row < EXTRA, (gid_row >> 10) * EXTRA + row, -1)
    slot_col = jnp.where(col < EXTRA, owner_t * EXTRA + col, -1)
    return row, slot_row, slot_col


def mine_columns(gid_row, me):
    row, _, _ = owner_ranks(gid_row)
    mine = (gid_row >> 10) == me
    slots = iota((EXTRA, BLOCK), 0)
    hit = jnp.logical_and(jnp.broadcast_to(mine, (EXTRA, BLOCK)), slots == row)
    local = jnp.broadcast_to(gid_row & (NODES_HERE - 1), (EXTRA, BLOCK)) + 1
    return jnp.sum(jnp.where(hit, local, 0).astype(F32), axis=1, keepdims=True).astype(jnp.int32) - 1


def exp_row(exp_ref, m, i):
    return exp_ref[m : m + 1, i * BLOCK : (i + 1) * BLOCK]


def project_kernel(
    me_ref, x_ref, wq_ref, wk_ref, wv_ref, cot_ref, rows_ref, exp_ref, gid_ref, q_ref, k_ref, v_ref, kv_ref, outk_ref, outv_ref,
    away_ref, rounds_ref, msgk_s, msgv_s, sems,
):
    most = jnp.max(owner_ranks(gid_ref[...])[0].astype(F32)).astype(jnp.int32)
    rounds_ref[0] = (most + EXTRA) // EXTRA
    x = x_ref[...]
    keys = dot(x, wk_ref[...]).astype(BF16)
    values = dot(x, wv_ref[...]).astype(BF16)
    k_ref[...] = keys
    v_ref[...] = values
    kv_ref[:, :COLS] = keys
    kv_ref[:, COLS:] = values
    query = (dot(x, wq_ref[...]).astype(BF16).astype(F32) * (1.0 / math.sqrt(HEAD))).astype(BF16)
    q_ref[...] = query
    away_ref[:NODES_HERE, :COLS] = query
    away_ref[:NODES_HERE, COLS:] = cot_ref[...]
    for m in range(EXPANDERS):
        low, high = split_index(jnp.concatenate([exp_row(exp_ref, m, i) for i in range(Q_BLOCKS)], axis=0))
        away_ref[NODES_HERE + m * Q_BLOCKS : NODES_HERE + (m + 1) * Q_BLOCKS, :COLS] = low
        away_ref[NODES_HERE + m * Q_BLOCKS : NODES_HERE + (m + 1) * Q_BLOCKS, COLS:] = high
    mine = jnp.broadcast_to(mine_columns(gid_ref[...], me_ref[0]), (EXTRA, BLOCK))
    lanes = iota((EXTRA, NODES_HERE), 1)
    hot = (jnp.concatenate([mine] * (NODES_HERE // BLOCK), axis=1) == lanes).astype(F32).astype(BF16)
    extra = dot(hot, kv_ref[...]).astype(BF16)

    def sends(t):
        here = pl.ds(t * GROUP, GROUP)
        return (
            pltpu.make_async_copy(msgk_s.at[here], outk_ref.at[here], sems.at[0, t]),
            pltpu.make_async_copy(msgv_s.at[here], outv_ref.at[here], sems.at[1, t]),
        )

    def gather(t, carry):
        hot = one_hot_of_rows([rows_ref[pl.ds(t * GROUP + u, 1), :] for u in range(GROUP)])
        got = dot(hot, kv_ref[...]).astype(BF16)
        for u in range(GROUP):
            msgk_s[t * GROUP + u, :BLOCK] = got[u * BLOCK : (u + 1) * BLOCK, :COLS]
            msgv_s[t * GROUP + u, :BLOCK] = got[u * BLOCK : (u + 1) * BLOCK, COLS:]
            msgk_s[t * GROUP + u, BLOCK:] = extra[:, :COLS]
            msgv_s[t * GROUP + u, BLOCK:] = extra[:, COLS:]
        for send in sends(t):
            send.start()
        return carry

    lax.fori_loop(0, SENDERS // GROUP, gather, 0)
    for t in range(SENDERS // GROUP):
        for send in sends(t):
            send.wait()


def gather_partner(exp_ref, m, table, first_col=0):
    blocks = []
    for t in range(0, Q_BLOCKS, 4):
        hot = one_hot_of_rows([exp_row(exp_ref, m, t + u) for u in range(4)])
        got = dot(hot, table[:, first_col : first_col + COLS]).astype(BF16)
        blocks += [got[u * BLOCK : (u + 1) * BLOCK] for u in range(4)]
    return blocks


def sum_picks():
    sub = iota((2 * Q_BLOCKS * COLS, 16), 0)
    col = iota((2 * Q_BLOCKS * COLS, 16), 1)
    return (col == (sub >> 8) + jnp.where((sub & (COLS - 1)) < HEAD, 0, 8)).astype(F32).astype(BF16)


def head_sums(a_ref, blocks, picks):
    parts = []
    for i, b in enumerate(blocks):
        prod = a_ref[i * BLOCK : (i + 1) * BLOCK, :].astype(F32) * b.astype(F32)
        high = prod.astype(BF16)
        parts += [high, (prod - high.astype(F32)).astype(BF16)]
    return flat(dot(jnp.concatenate(parts, axis=1), picks).T)


def partner_key_kernel(exp_ref, t0_ref, t1_ref, t2_ref, t3_ref, q_ref, out_ref, sp_ref, pair_s, sems):
    picks = sum_picks()
    copies = []
    for m, table in enumerate((t0_ref, t1_ref, t2_ref, t3_ref)):
        blocks = gather_partner(exp_ref, m, table)
        for i, block in enumerate(blocks):
            pair_s[m * Q_BLOCKS + i] = block
        here = pl.ds(m * Q_BLOCKS, Q_BLOCKS)
        copies += start_copies([(pair_s.at[here], out_ref.at[here])], sems.at[pl.ds(m, 1)])
        sp_ref[m] = head_sums(q_ref, blocks, picks)
    wait_all(copies)


def head_picks(i):
    return (iota((16, COLS), 0) == jnp.where(iota((16, COLS), 1) < HEAD, i, 8 + i)).astype(F32).astype(BF16)


def finish_kernel(
    me_ref, exp_ref, t0_ref, t1_ref, t2_ref, t3_ref, cot_ref, sp_ref, lse_ref, local_ref, _, pair_ref, back_ref,
    delta_ref, message_ref, sems,
):
    picks = sum_picks()
    lse = lse_ref[...]
    delta = local_ref[...]
    probs, dprobs = [], []
    for m, table in enumerate((t0_ref, t1_ref, t2_ref, t3_ref)):
        blocks = gather_partner(exp_ref, m, table, table.shape[1] - COLS)
        prob = jnp.exp(sp_ref[m] - lse)
        dprob = head_sums(cot_ref, blocks, picks)
        delta += prob * dprob
        back_ref[m, 16:] = tall(prob).astype(BF16)
        for i, block in enumerate(blocks):
            pair_ref[m * Q_BLOCKS + i] = block
        probs.append(prob)
        dprobs.append(dprob)
    delta_ref[...] = delta
    for m in range(EXPANDERS):
        back_ref[m, :16] = tall(probs[m] * (dprobs[m] - delta)).astype(BF16)
    copies = [
        pltpu.make_async_copy(
            back_ref.at[m], message_ref.at[me_ref[0] ^ (1 << m), pl.ds(SLOTS, PART_ROWS)], sems.at[m]
        )
        for m in range(EXPANDERS)
    ]
    for copy in copies:
        copy.start()
    for copy in copies:
        copy.wait()


def join_partners(out_ref, out_t_ref, part_rows, pair_ref, scale):
    turned = [turned_weights(rows) for rows in part_rows]
    for i in range(Q_BLOCKS):
        total = head_rows(out_t_ref[i]).T
        for m in range(EXPANDERS):
            total += dot(turned[m], head_picks(i)) * pair_ref[m * Q_BLOCKS + i].astype(F32)
        out_ref[i * BLOCK : (i + 1) * BLOCK, :] = (total * scale).astype(BF16)


def attend_kernel(out_t_ref, back_ref, pair_ref, att_ref):
    join_partners(att_ref, out_t_ref, [back_ref[m, 16:] for m in range(EXPANDERS)], pair_ref, 1.0)


def flat(x):
    return jnp.concatenate([x[:8], x[8:]], axis=1)


def tall(x):
    return jnp.concatenate([x[:, :BLOCK], x[:, BLOCK:]], axis=0)


def turned_weights(tall_rows):
    return tall_rows.astype(F32).T.astype(BF16)


def prepare_kernel(q_ref, cot_ref, qt_ref, qs_ref, ct_ref, cs_ref):
    def one(i, carry):
        q = q_ref[q_rows(i), :]
        cot = cot_ref[q_rows(i), :]
        qt_ref[i] = stacked_t(q)
        qs_ref[i] = stacked(q)
        ct_ref[i] = stacked_t(cot)
        cs_ref[i] = stacked(cot)
        return carry

    lax.fori_loop(0, Q_BLOCKS, one, 0, unroll=2)


def plan_kernel(mask_ref, halo_ref, list_ref, where_ref, block_ref, count_ref, live_ref):
    for j in range(Q_BLOCKS):
        live_ref[j] = BLOCK
    live_ref[GLOBAL_BLOCK] = BLOCK
    live_ref[EMPTY_BLOCK] = 0

    def copy_count(s, carry):
        live_ref[Q_BLOCKS + s] = halo_ref[s]
        return carry

    lax.fori_loop(0, SENDERS, copy_count, 0)

    def per_block(i, items):
        list_ref[i * LIST] = GLOBAL_BLOCK

        def put(j, n):
            list_ref[i * LIST + n] = j
            used = jnp.logical_and(mask_ref[i * GLOBAL_BLOCK + j] > 0, live_ref[j] > 0)
            return n + used.astype(jnp.int32)

        n = lax.fori_loop(0, GLOBAL_BLOCK, put, 1)
        for extra in range(GROUP):
            list_ref[i * LIST + n + extra] = EMPTY_BLOCK
        groups = (n + GROUP - 1) // GROUP

        def item(g, carry):
            where_ref[items + g] = i * LIST + g * GROUP
            block_ref[items + g] = i
            return carry

        lax.fori_loop(0, groups, item, 0)
        return items + groups

    items = lax.fori_loop(0, Q_BLOCKS, per_block, 0)
    for u in range(GROUP):
        list_ref[Q_BLOCKS * LIST + u] = EMPTY_BLOCK
    for u in range(ITEMS - 1):
        where_ref[items + u] = Q_BLOCKS * LIST
        block_ref[items + u] = 0
    count_ref[0] = (items + ITEMS - 1) // ITEMS


def fill(dst, dst_t, first_col,  own_ref, halo_ref, gid_ref, glob_ref):
    def put(j, block):
        if dst is not None:
            dst[j] = block
        if dst_t is not None:
            dst_t[j] = block.T

    def own(j, carry):
        put(j, own_ref[q_rows(j), :])
        return carry

    def halo(j, carry):
        put(Q_BLOCKS + j, halo_ref[j, :BLOCK])
        return carry

    lax.fori_loop(0, Q_BLOCKS, own, 0, unroll=4)
    lax.fori_loop(0, SENDERS, halo, 0, unroll=4)
    slot_col = owner_ranks(gid_ref[...])[2]
    wide = jnp.concatenate([slot_col] * (SENDERS * EXTRA // BLOCK), axis=1)
    hot = (wide == iota((BLOCK, SENDERS * EXTRA), 1)).astype(F32).astype(BF16)
    extra = jnp.concatenate([halo_ref[s, BLOCK:] for s in range(SENDERS)], axis=0)
    rows = (dot(hot, extra) + glob_ref[:, first_col : first_col + COLS].astype(F32)).astype(BF16)
    put(GLOBAL_BLOCK, rows)
    put(EMPTY_BLOCK, jnp.zeros((BLOCK, COLS), BF16))


def stacked(rows):
    lanes = iota((BLOCK, COLS), 1)
    zero = jnp.zeros_like(rows)
    return jnp.concatenate([jnp.where(lanes < HEAD, rows, zero), jnp.where(lanes < HEAD, zero, rows)], axis=0)


def stacked_t(rows):
    turned = rows.T
    subs = iota((COLS, BLOCK), 0)
    zero = jnp.zeros_like(turned)
    return jnp.concatenate([jnp.where(subs < HEAD, turned, zero), jnp.where(subs < HEAD, zero, turned)], axis=1)


def head_rows(turned):
    return jnp.concatenate([turned[:HEAD, :BLOCK], turned[HEAD:, BLOCK:]], axis=0)


def masked_scores(blocks, k_s, turned_q, live_ref):
    keys = jnp.concatenate([k_s[b] for b in blocks], axis=0)
    scores = dot(keys, turned_q)
    row_id = iota((BLOCK, 2 * BLOCK), 0)
    return jnp.concatenate(
        [
            jnp.where(row_id < live_ref[b], scores[u * BLOCK : (u + 1) * BLOCK], NEG)
            for u, b in enumerate(blocks)
        ],
        axis=0,
    )


def item_of(t, u, list_ref, where_ref, block_ref):
    where = where_ref[t * ITEMS + u]
    return block_ref[t * ITEMS + u], [list_ref[where + b] for b in range(GROUP)]


def q_rows(i):
    return pl.ds(pl.multiple_of(i * BLOCK, BLOCK), BLOCK)


def score_kernel(
    list_ref, where_ref, block_ref, count_ref, live_ref, qt_ref, own_ref, hk_ref, gid_ref, glob_ref, lse_ref, k_ref, kt_ref,
    top_s, total_s, k_s, kt_s, sems,
):
    fill(k_s, kt_s, 0, own_ref, hk_ref, gid_ref, glob_ref)
    copies = start_copies([(k_s, k_ref), (kt_s, kt_ref)], sems)

    top_s[...] = jnp.full((Q_BLOCKS, 8, 2 * BLOCK), NEG, F32)
    total_s[...] = jnp.zeros((Q_BLOCKS, 8, 2 * BLOCK), F32)

    def step(t, carry):
        for item in range(ITEMS):
            i, blocks = item_of(t, item, list_ref, where_ref, block_ref)
            turned_q = qt_ref[i]
            parts = []
            for u in range(0, GROUP, SCORE_PAIR):
                scores = masked_scores(blocks[u : u + SCORE_PAIR], k_s, turned_q, live_ref)
                scores = scores.reshape(SCORE_PAIR * BLOCK // 8, 8, 2 * BLOCK)
                top = jnp.max(scores, axis=0)
                parts.append((top, jnp.sum(jnp.exp(scores - top[None]), axis=0)))
            parts.append((top_s[i], total_s[i]))
            best = functools.reduce(jnp.maximum, [top for top, _ in parts])
            top_s[i] = best
            total_s[i] = sum(total * jnp.exp(top - best) for top, total in parts)
        return carry

    lax.fori_loop(0, count_ref[0], step, 0)
    for i in range(Q_BLOCKS):
        top = top_s[i]
        best = jnp.max(top, axis=0, keepdims=True)
        denominator = jnp.sum(total_s[i] * jnp.exp(top - best), axis=0, keepdims=True)
        lse_ref[i : i + 1, :] = best + jnp.log(denominator)
    wait_all(copies)


def value_kernel(
    list_ref, where_ref, block_ref, count_ref, live_ref, k_in, ownv_ref, hv_ref, glob_ref, qt_in, ct_in, cs_in, part_ref,
    sp_ref, gid_ref, own_ref, halo_ref, gout_ref, out_ref, delta_ref, lse_ref, acc_s, vt_s, k_s, qt_ref, ct_ref, cs_ref,
    in_sems, out_s, halo_s, sems,
):
    loads = start_copies([(k_in, k_s), (qt_in, qt_ref), (cs_in, cs_ref), (ct_in, ct_ref)], in_sems)
    fill(None, vt_s, COLS, ownv_ref, hv_ref, gid_ref, glob_ref)
    clear_blocks(acc_s)
    part = part_ref[...]
    best = part
    for m in range(EXPANDERS):
        best = jnp.maximum(best, sp_ref[m])
    total = jnp.exp(part - best)
    for m in range(EXPANDERS):
        total += jnp.exp(sp_ref[m] - best)
    lse_ref[...] = best + jnp.log(total)
    wait_all(loads)

    out_s[...] = jnp.zeros((Q_BLOCKS, COLS, 2 * BLOCK), F32)

    def step(t, carry):
        for item in range(ITEMS):
            i, blocks = item_of(t, item, list_ref, where_ref, block_ref)
            turned_q = qt_ref[i]
            cot_stack = cs_ref[i]
            lse = lse_ref[pl.ds(i, 1), :]
            for u in range(0, GROUP, PAIR):
                pair = blocks[u : u + PAIR]
                scores = masked_scores(pair, k_s, turned_q, live_ref)
                weight = jnp.exp(scores - lse).astype(BF16)
                out_s[i] += dot(jnp.concatenate([vt_s[b] for b in pair], axis=1), weight)
                grads = dot(weight, cot_stack)
                for w, b in enumerate(pair):
                    acc_s[b] += grads[w * BLOCK : (w + 1) * BLOCK]
        return carry

    lax.fori_loop(0, count_ref[0], step, 0)
    out_copy = pltpu.make_async_copy(out_s, out_ref, sems.at[1 + SENDERS // GROUP])
    out_copy.start()
    for i in range(Q_BLOCKS):
        delta_ref[i : i + 1, :] = jnp.sum(out_s[i] * ct_ref[i].astype(F32), axis=0, keepdims=True)
    wait_all(store_parts(acc_s, own_ref, halo_ref, gid_ref, gout_ref, halo_s, sems) + [out_copy])


def clear_blocks(acc_s):
    def clear(j, carry):
        acc_s[j] = jnp.zeros((BLOCK, COLS), F32)
        return carry

    lax.fori_loop(0, KEY_BLOCKS, clear, 0, unroll=2)


def store_parts(acc_s, own_ref, halo_ref, gid_ref, gout_ref, halo_s, sems):
    copies = start_copies([(acc_s.at[pl.ds(0, Q_BLOCKS)], own_ref)], sems)
    grads = acc_s[GLOBAL_BLOCK].astype(BF16)
    gout_ref[...] = grads
    slot_row = owner_ranks(gid_ref[...])[1]
    hot = (iota((SENDERS * EXTRA, BLOCK), 0) == slot_row).astype(F32).astype(BF16)
    extra = dot(hot, grads).astype(BF16)
    for t in range(SENDERS // GROUP):
        for s in range(t * GROUP, (t + 1) * GROUP):
            halo_s[s, :BLOCK] = acc_s[Q_BLOCKS + s].astype(BF16)
            halo_s[s, BLOCK:] = extra[s * EXTRA : (s + 1) * EXTRA]
        here = pl.ds(t * GROUP, GROUP)
        copy = pltpu.make_async_copy(halo_s.at[here], halo_ref.at[here, pl.ds(0, SLOTS)], sems.at[1 + t])
        copy.start()
        copies.append(copy)
    return copies


def part_scratch():
    return [pltpu.VMEM((SENDERS, SLOTS, COLS), BF16), pltpu.SemaphoreType.DMA((2 + SENDERS // GROUP,))]


def key_kernel(
    list_ref, where_ref, block_ref, count_ref, live_ref, k_in, kt_in, ownv_ref, hv_ref, glob_ref, qt_in, qs_in, ct_in, lse_ref,
    delta_ref, gid_ref, out_ref, own_ref, halo_ref, gout_ref, acc_s, v_s, k_s, kt_s, qt_ref, qs_ref, ct_ref, in_sems,
    out_s, halo_s, sems,
):
    loads = start_copies(
        [(k_in, k_s), (qt_in, qt_ref), (ct_in, ct_ref), (kt_in, kt_s), (qs_in, qs_ref)], in_sems
    )
    fill(v_s, None, COLS, ownv_ref, hv_ref, gid_ref, glob_ref)
    clear_blocks(acc_s)
    wait_all(loads)

    out_s[...] = jnp.zeros((Q_BLOCKS, COLS, 2 * BLOCK), F32)

    def step(t, carry):
        for item in range(ITEMS):
            i, blocks = item_of(t, item, list_ref, where_ref, block_ref)
            turned_q = qt_ref[i]
            q_stack = qs_ref[i]
            turned_cot = ct_ref[i]
            lse = lse_ref[pl.ds(i, 1), :]
            delta = delta_ref[pl.ds(i, 1), :]
            for u in range(0, GROUP, PAIR):
                pair = blocks[u : u + PAIR]
                scores = masked_scores(pair, k_s, turned_q, live_ref)
                dprob = dot(jnp.concatenate([v_s[b] for b in pair], axis=0), turned_cot)
                dscore = (jnp.exp(scores - lse) * (dprob - delta)).astype(BF16)
                out_s[i] += dot(jnp.concatenate([kt_s[b] for b in pair], axis=1), dscore)
                grads = dot(dscore, q_stack)
                for w, b in enumerate(pair):
                    acc_s[b] += grads[w * BLOCK : (w + 1) * BLOCK]
        return carry

    lax.fori_loop(0, count_ref[0], step, 0)
    out_copy = pltpu.make_async_copy(out_s, out_ref, sems.at[1 + SENDERS // GROUP])
    out_copy.start()
    wait_all(store_parts(acc_s, own_ref, halo_ref, gid_ref, gout_ref, halo_s, sems) + [out_copy])


def scatter_into(acc_s, splits, data):
    subs = packed_iota(0)
    one, zero = jnp.ones((), BF16), jnp.zeros((), BF16)
    bases = [(jnp.where(subs == low, one, zero), jnp.broadcast_to(high, (BLOCK, BLOCK))) for low, high in splits]
    for c in range(NODES_HERE // BLOCK):
        hot = jnp.concatenate([jnp.where(high == jnp.asarray(c, BF16), base, zero) for base, high in bases], axis=1)
        acc_s[c * BLOCK : (c + 1) * BLOCK, :] += dot(hot, data)


def add_halo(acc_s, me_ref, ret_ref, rows_ref, gid_ref, more_ref):
    def halo(t, carry):
        splits = [split_index(rows_ref[pl.ds(t * GROUP + u, 1), :]) for u in range(GROUP)]
        data = jnp.concatenate([ret_ref[t * GROUP + u, :BLOCK] for u in range(GROUP)], axis=0)
        scatter_into(acc_s, splits, data)
        return carry

    lax.fori_loop(0, SENDERS // GROUP, halo, 0)
    extra = ret_ref[0, BLOCK:SLOTS].astype(F32)
    for s in range(1, SENDERS):
        extra += ret_ref[s, BLOCK:SLOTS].astype(F32)
    high = extra.astype(BF16)
    data = jnp.concatenate([high, (extra - high.astype(F32)).astype(BF16)], axis=0)
    mine = jnp.broadcast_to(mine_columns(gid_ref[...], me_ref[0]), (EXTRA, NODES_HERE))
    hot = (mine == iota((EXTRA, NODES_HERE), 1)).astype(F32)
    hot = jnp.concatenate([hot, hot], axis=0).T.astype(BF16)
    acc_s[...] += dot(hot, data)
    gids = gid_ref[...]
    local = jnp.where((gids >> 10) == me_ref[0], gids & (NODES_HERE - 1), NODES_HERE)
    more = more_ref[...]
    high = more.astype(BF16)
    low = (more - high.astype(F32)).astype(BF16)
    scatter_into(acc_s, [split_index(local)] * 2, jnp.concatenate([high, low], axis=0))


def add_partners(acc_s, parts, others, first_col):
    for m, (part, other) in enumerate(zip(parts, others)):
        turned = turned_weights(part)
        index_low = other[NODES_HERE + m * Q_BLOCKS : NODES_HERE + (m + 1) * Q_BLOCKS, :COLS]
        index_high = other[NODES_HERE + m * Q_BLOCKS : NODES_HERE + (m + 1) * Q_BLOCKS, COLS:]
        for t in range(Q_BLOCKS // GROUP):
            splits, data = [], []
            for u in range(GROUP):
                i = t * GROUP + u
                splits.append((index_low[i : i + 1], index_high[i : i + 1]))
                wide = dot(turned, head_picks(i))
                rows = other[i * BLOCK : (i + 1) * BLOCK, first_col : first_col + COLS].astype(F32)
                data.append((wide * rows).astype(BF16))
            scatter_into(acc_s, splits, jnp.concatenate(data, axis=0))


def feature_part(feat_ref, k):
    return pl.ds(pl.multiple_of(((feat_ref[0] + k) % 4) * COLS, COLS), COLS)


def value_back_kernel(
    me_ref, feat_ref, ownv_ref, ret_ref, ownk_ref, rows_ref, o0_ref, o1_ref, o2_ref, o3_ref, gid_ref, wq_ref, wv_ref,
    out_t_ref, back_ref, pair_ref, more_ref, acck_ref, pre_ref, accv_s, gq_ref,
):
    others = (o0_ref, o1_ref, o2_ref, o3_ref)
    parts = [ret_ref[me_ref[0] ^ (1 << m), SLOTS:] for m in range(EXPANDERS)]
    join_partners(
        gq_ref, out_t_ref, [back_ref[m, :16] for m in range(EXPANDERS)], pair_ref, 1.0 / math.sqrt(HEAD)
    )
    accv_s[...] = ownv_ref[...]
    add_halo(accv_s, me_ref, ret_ref, rows_ref, gid_ref, more_ref)
    add_partners(accv_s, [part[16:] for part in parts], others, COLS)
    acck_ref[...] = ownk_ref[...]
    add_partners(acck_ref, [part[:16] for part in parts], others, 0)
    grad_value = accv_s[...].astype(BF16)
    for k in range(4):
        part = feature_part(feat_ref, k)
        pre_ref[k] = dot_nt(gq_ref[...], wq_ref[part, :]) + dot_nt(grad_value, wv_ref[part, :])


def key_back_kernel(
    me_ref, feat_ref, acck_ref, ret_ref, rows_ref, gid_ref, wk_ref, pre_ref, more_ref, t0_ref, t1_ref, t2_ref, t3_ref,
    acc_s, own_s, pre_s, sems,
):
    own_copy = pltpu.make_async_copy(acck_ref, own_s, sems.at[0])
    pre_copy = pltpu.make_async_copy(pre_ref, pre_s, sems.at[1])
    own_copy.start()
    pre_copy.start()
    acc_s[...] = jnp.zeros((NODES_HERE, COLS), F32)
    add_halo(acc_s, me_ref, ret_ref, rows_ref, gid_ref, more_ref)
    own_copy.wait()
    grad_key = (acc_s[...] + own_s[...]).astype(BF16)
    pre_copy.wait()
    for k, out in ((1, t1_ref), (2, t2_ref), (3, t3_ref), (0, t0_ref)):
        out[...] = (pre_s[k] + dot_nt(grad_key, wk_ref[feature_part(feat_ref, k), :])).astype(out.dtype)


def shape(dims, kind=BF16):
    return jax.ShapeDtypeStruct(dims, kind)


def call(kernel, ins, outs, args, scratch=(), name=None, flops=0, out_spaces=None, aliases={}, mib=56):
    cost = pl.CostEstimate(flops=flops, transcendentals=0, bytes_accessed=4_000_000)
    return pl.pallas_call(
        kernel,
        out_shape=outs,
        in_specs=ins,
        out_specs=out_spaces or tuple(vmem() for _ in outs),
        scratch_shapes=list(scratch),
        compiler_params=params(mib),
        cost_estimate=cost,
        input_output_aliases=aliases,
        name=name,
    )(*args)


def blocks_of(kind):
    return pltpu.VMEM((KEY_BLOCKS, BLOCK, COLS), kind)


def run_project(me, features, w_query, w_key, w_value, cotangent, rows, exp_list, gids):
    return call(
        project_kernel,
        [smem()] + [vmem()] * 8,
        (
            shape((NODES_HERE, COLS)),
            shape((NODES_HERE, COLS)),
            shape((NODES_HERE, COLS)),
            shape((NODES_HERE, 2 * COLS)),
            shape((SENDERS, SLOTS, COLS)),
            shape((SENDERS, SLOTS, COLS)),
            shape((NODES_HERE + EXPANDERS * Q_BLOCKS, 2 * COLS)),
            shape((1,), jnp.int32),
        ),
        (me, features, w_query, w_key, w_value, cotangent, rows, exp_list, gids),
        name="project",
        mib=56,
        flops=3_000_000_000,
        out_spaces=(vmem(), vmem(), vmem(), vmem(), anywhere(), anywhere(), vmem(), smem()),
        scratch=[
            pltpu.VMEM((SENDERS, SLOTS, COLS), BF16),
            pltpu.VMEM((SENDERS, SLOTS, COLS), BF16),
            pltpu.SemaphoreType.DMA((2, SENDERS // GROUP)),
        ],
    )


def run_plan(block_mask, halo_count):
    sizes = (Q_BLOCKS * LIST + GROUP, MAX_ITEMS, MAX_ITEMS, 1, KEY_BLOCKS)
    return call(
        plan_kernel,
        [smem()] * 2,
        tuple(shape((size,), jnp.int32) for size in sizes),
        (block_mask.reshape(-1), halo_count.reshape(-1)),
        name="plan",
        out_spaces=tuple(smem() for _ in sizes),
    )


def run_partner_keys(exp_rows, swaps, query):
    return call(
        partner_key_kernel,
        [vmem()] * 6,
        (shape((EXPANDERS * Q_BLOCKS, BLOCK, COLS)), shape((EXPANDERS, Q_BLOCKS, 2 * BLOCK), F32)),
        (exp_rows, *swaps, query),
        name="partners",
        out_spaces=(anywhere(), vmem()),
        scratch=[
            pltpu.VMEM((EXPANDERS * Q_BLOCKS, BLOCK, COLS), BF16),
            pltpu.SemaphoreType.DMA((EXPANDERS,)),
        ],
        flops=5_000_000_000,
    )


def run_finish(me, exp_rows, swaps, cotangent, scores, lse, local, back_v):
    anywhere = pl.BlockSpec(memory_space=pl.ANY)
    return call(
        finish_kernel,
        [smem()] + [vmem()] * 9 + [anywhere],
        (
            shape((EXPANDERS * Q_BLOCKS, BLOCK, COLS)),
            shape((EXPANDERS, PART_ROWS, BLOCK)),
            shape((Q_BLOCKS, 2 * BLOCK), F32),
            shape((SENDERS, BACK, COLS)),
        ),
        (me, exp_rows, *swaps, cotangent, scores, lse, local, back_v),
        name="finish",
        flops=5_000_000_000,
        out_spaces=(vmem(), vmem(), vmem(), anywhere),
        scratch=[pltpu.SemaphoreType.DMA((EXPANDERS,))],
        aliases={10: 3},
    )


def run_attend(out_t, back, value_pairs):
    return call(
        attend_kernel,
        [vmem()] * 3,
        (shape((NODES_HERE, COLS)),),
        (out_t, back, value_pairs),
        name="attend",
        flops=2_000_000_000,
    )[0]


def run_prepare(query, cotangent):
    wide, high = shape((Q_BLOCKS, COLS, 2 * BLOCK)), shape((Q_BLOCKS, 2 * BLOCK, COLS))
    return call(
        prepare_kernel, [vmem()] * 2, (wide, high, wide, high), (query, cotangent), name="prepare", flops=2_000_000_000
    )


def run_scores(plan, turned_q, own, halo_k, gids, glob):
    return call(
        score_kernel,
        [smem()] * 5 + [vmem()] * 5,
        (
            shape((Q_BLOCKS, 2 * BLOCK), F32),
            shape((KEY_BLOCKS, BLOCK, COLS)),
            shape((KEY_BLOCKS, COLS, BLOCK)),
        ),
        (*plan, turned_q, own, halo_k, gids, glob),
        scratch=[pltpu.VMEM((Q_BLOCKS, 8, 2 * BLOCK), F32)] * 2
        + [blocks_of(BF16), blocks_of(BF16), pltpu.SemaphoreType.DMA((2,))],
        out_spaces=(vmem(), anywhere(), anywhere()),
        name="scores",
        flops=12_000_000_000,
    )


def run_values(plan, keys, own_values, halo_v, glob, prepared, part, scores, gids):
    turned_q, _, turned_cot, cot_stack = prepared
    return call(
        value_kernel,
        [smem()] * 5 + [anywhere()] + [vmem()] * 3 + [anywhere()] * 3 + [vmem()] * 3,
        (
            shape((Q_BLOCKS, BLOCK, COLS), F32),
            shape((SENDERS, BACK, COLS)),
            shape((BLOCK, COLS)),
            shape((Q_BLOCKS, COLS, 2 * BLOCK), F32),
            shape((Q_BLOCKS, 2 * BLOCK), F32),
            shape((Q_BLOCKS, 2 * BLOCK), F32),
        ),
        (*plan, keys, own_values, halo_v, glob, turned_q, turned_cot, cot_stack, part, scores, gids),
        scratch=[
            blocks_of(F32), blocks_of(BF16), blocks_of(BF16), pltpu.VMEM((Q_BLOCKS, COLS, 2 * BLOCK), BF16), pltpu.VMEM((Q_BLOCKS, COLS, 2 * BLOCK), BF16),
            pltpu.VMEM((Q_BLOCKS, 2 * BLOCK, COLS), BF16), pltpu.SemaphoreType.DMA((4,)), pltpu.VMEM((Q_BLOCKS, COLS, 2 * BLOCK), F32),
            *part_scratch(),
        ],
        out_spaces=(anywhere(), anywhere(), vmem(), anywhere(), vmem(), vmem()),
        name="values",
        flops=20_000_000_000,
    )


def run_keys(plan, keys, turned_k, own_values, halo_v, glob, prepared, lse, delta, gids):
    turned_q, q_stack, turned_cot, _ = prepared
    return call(
        key_kernel,
        [smem()] * 5 + [anywhere()] * 2 + [vmem()] * 3 + [anywhere()] * 3 + [vmem()] * 3,
        (
            shape((Q_BLOCKS, COLS, 2 * BLOCK), F32),
            shape((Q_BLOCKS, BLOCK, COLS), F32),
            shape((SENDERS, SLOTS, COLS)),
            shape((BLOCK, COLS)),
        ),
        (*plan, keys, turned_k, own_values, halo_v, glob, turned_q, q_stack, turned_cot, lse, delta, gids),
        scratch=[
            blocks_of(F32), blocks_of(BF16), blocks_of(BF16), blocks_of(BF16), pltpu.VMEM((Q_BLOCKS, COLS, 2 * BLOCK), BF16),
            pltpu.VMEM((Q_BLOCKS, 2 * BLOCK, COLS), BF16), pltpu.VMEM((Q_BLOCKS, COLS, 2 * BLOCK), BF16), pltpu.SemaphoreType.DMA((5,)), pltpu.VMEM((Q_BLOCKS, COLS, 2 * BLOCK), F32),
            *part_scratch(),
        ],
        out_spaces=(anywhere(), anywhere(), anywhere(), vmem()),
        name="keys",
        mib=56,
        flops=25_000_000_000,
    )


def run_value_back(me, feat, own_v, returned_v, own_k, rows, others, gids, w_query, w_value, out_t, back, pairs, more):
    return call(
        value_back_kernel,
        [smem()] * 2 + [vmem()] * 15,
        (shape((NODES_HERE, COLS), F32), shape((4, NODES_HERE, COLS), F32)),
        (me, feat, own_v.reshape(NODES_HERE, COLS), returned_v, own_k.reshape(NODES_HERE, COLS), rows, *others, gids, w_query, w_value, out_t, back, pairs, more),
        scratch=[pltpu.VMEM((NODES_HERE, COLS), F32), pltpu.VMEM((NODES_HERE, COLS), BF16)],
        name="value_back",
        mib=56,
        flops=12_000_000_000,
    )


def run_key_back(me, feat, own_k, returned_k, rows, gids, w_key, pre, more):
    anywhere = pl.BlockSpec(memory_space=pltpu.HBM)
    return call(
        key_back_kernel,
        [smem()] * 2 + [anywhere] + [vmem()] * 4 + [anywhere, vmem()],
        (shape((NODES_HERE, COLS), F32),) + tuple(shape((NODES_HERE, COLS)) for _ in range(3)),
        (me, feat, own_k, returned_k, rows, gids, w_key, pre, more),
        scratch=[
            pltpu.VMEM((NODES_HERE, COLS), F32),
            pltpu.VMEM((NODES_HERE, COLS), F32),
            pltpu.VMEM((4, NODES_HERE, COLS), F32),
            pltpu.SemaphoreType.DMA((2,)),
        ],
        name="key_back",
        mib=20,
        flops=8_000_000_000,
    )


def ranks(global_ids):
    owner = global_ids // NODES_HERE
    ids = jnp.arange(BLOCK)
    return owner, ((owner[:, None] == owner[None, :]) & (ids[None, :] < ids[:, None])).sum(1)


def more_globals(rounds, global_ids, my_index, own_k, own_v):
    def body(state):
        r, glob = state
        ids = global_ids + jnp.minimum(r, 0)
        owner, rank = ranks(ids)
        slot = rank - r * EXTRA
        here = (slot >= 0) & (slot < EXTRA)
        place = jnp.where((owner == my_index) & here, slot, EXTRA)
        local = jnp.where(here, ids % NODES_HERE, 0)
        found = jnp.concatenate([own_k[local], own_v[local]], axis=1)
        rows = jnp.zeros((EXTRA + 1, 2 * COLS), BF16).at[place].set(found)[:EXTRA]
        got = lax.all_to_all(jnp.broadcast_to(rows[None], (SENDERS, *rows.shape)), "dom", 0, 0, tiled=True)
        found = got.reshape(SENDERS * EXTRA, -1)[jnp.clip(owner * EXTRA + slot, 0, SENDERS * EXTRA - 1)]
        return r + 1, jnp.where(here[:, None], found, glob)

    start = (jnp.asarray(1, jnp.int32), jnp.zeros((BLOCK, 2 * COLS), BF16))
    return lax.while_loop(lambda state: state[0] < rounds, body, start)[1]


def more_grads(rounds, global_ids, my_index, part_k, part_v):
    def body(state):
        r, more_k, more_v = state
        ids = global_ids + jnp.minimum(r, 0)
        owner, rank = ranks(ids)
        slot = rank - r * EXTRA
        here = (slot >= 0) & (slot < EXTRA)
        place = jnp.where(here, owner * EXTRA + slot, SENDERS * EXTRA)

        def summed(part):
            rows = jnp.zeros((SENDERS * EXTRA + 1, COLS), BF16).at[place].set(part)[: SENDERS * EXTRA]
            got = lax.all_to_all(rows.reshape(SENDERS, EXTRA, -1), "dom", 0, 0, tiled=True).astype(F32).sum(0)
            return jnp.where(((owner == my_index) & here)[:, None], got[jnp.clip(slot, 0, EXTRA - 1)], 0.0)

        return r + 1, more_k + summed(part_k), more_v + summed(part_v)

    zeros = jnp.zeros((BLOCK, COLS), F32)
    start = (jnp.asarray(1, jnp.int32), zeros, zeros)
    return lax.while_loop(lambda state: state[0] < rounds, body, start)[1:]


def on_device(
    features,
    w_query,
    w_key,
    w_value,
    cotangent,
    send_rows,
    halo_count,
    block_mask,
    exp_rows,
    global_ids,
):
    dom_count = lax.axis_size("dom")
    my_index = lax.axis_index("dom")

    def swapped(value, bit):
        return lax.ppermute(value, "dom", [(i, i ^ (1 << bit)) for i in range(dom_count)])

    rows = send_rows[0]
    gids = global_ids.reshape(1, BLOCK)
    me = my_index.reshape(1).astype(jnp.int32)
    feat = lax.axis_index("feat").reshape(1).astype(jnp.int32)

    query, own_keys, own_values, paired, out_k, out_v, away, rounds = run_project(
        me, features, w_query, w_key, w_value, cotangent, rows, exp_rows, gids
    )
    rounds = rounds[0]
    glob = more_globals(rounds, global_ids, my_index, own_keys, own_values)
    out_k, out_v, glob = lax.optimization_barrier((out_k, out_v, glob))
    halo_k = lax.all_to_all(out_k, "dom", 0, 0, tiled=True)
    key_swaps = [swapped(paired if m in TOGETHER else own_keys, m) for m in range(EXPANDERS)]
    plan = run_plan(block_mask, halo_count)
    prepared = run_prepare(query, cotangent)
    own_values_late, *prepared = lax.optimization_barrier((own_values, *prepared))
    value_swaps = {m: swapped(own_values_late, m) for m in range(EXPANDERS) if m not in TOGETHER}
    halo_v = lax.all_to_all(out_v, "dom", 0, 0, tiled=True)
    part, keys, turned_k = run_scores(plan, prepared[0], own_keys, halo_k, gids, glob)
    part, *key_swaps = lax.optimization_barrier((part, *key_swaps))
    pairs, scores = run_partner_keys(exp_rows, key_swaps, query)
    away, scores = lax.optimization_barrier((away, scores))
    others = [swapped(away, m) for m in range(EXPANDERS)]
    own_v, back_v, glob_v, out_t, local, lse = run_values(
        plan, keys, own_values, halo_v, glob, prepared, part, scores, gids
    )
    local, value_swaps = lax.optimization_barrier((local, value_swaps))
    value_swaps = [value_swaps.get(m, key_swaps[m]) for m in range(EXPANDERS)]
    value_pairs, back, delta, back_v = run_finish(
        me, exp_rows, value_swaps, cotangent, scores, lse, local, back_v
    )
    returned_v = lax.all_to_all(back_v, "dom", 0, 0, tiled=True)
    query_t, own_k, back_k, glob_k = run_keys(
        plan, keys, turned_k, own_values, halo_v, glob, prepared, lse, delta, gids
    )
    glob_k, returned_v, *others = lax.optimization_barrier((glob_k, returned_v, *others))
    more_k, more_v = more_grads(rounds, global_ids, my_index, glob_k, glob_v)
    back_k, more_k, more_v = lax.optimization_barrier((back_k, more_k, more_v))
    returned_k = lax.all_to_all(back_k, "dom", 0, 0, tiled=True)
    own_k, pre = run_value_back(
        me, feat, own_v, returned_v, own_k, rows, others, gids, w_query, w_value, query_t, back, pairs, more_v
    )
    mine, *away = run_key_back(me, feat, own_k, returned_k, rows, gids, w_key, pre, more_k)
    out_t, mine = lax.optimization_barrier((out_t, mine))
    attended = run_attend(out_t, back, value_pairs)
    for k in (2, 1, 3):
        mine = mine + lax.ppermute(away[k - 1], "feat", [(i, (i + k) % 4) for i in range(4)]).astype(F32)
    return (attended, mine.astype(BF16))


def solution(mesh):
    return jax.shard_map(
        on_device,
        mesh=mesh,
        in_specs=(
            P("dom", None),
            P(None, "feat"),
            P(None, "feat"),
            P(None, "feat"),
            P("dom", "feat"),
            P("dom", None, None),
            P(None, "dom"),
            P("dom", None),
            P(None, "dom"),
            P(),
        ),
        out_specs=(P("dom", "feat"), P("dom", "feat")),
        check_vma=False,
    )
```

```python
import functools
import math

import jax
import jax.numpy as jnp
from jax import lax
from jax.experimental import pallas as pl
from jax.experimental.pallas import tpu as pltpu
from jax.sharding import PartitionSpec as P

HEAD = 64
BLOCK = 128
EXPANDERS = 4
COLS = 128
NODES_HERE = 1024
Q_BLOCKS = NODES_HERE // BLOCK
SENDERS = 32
GLOBAL_BLOCK = Q_BLOCKS + SENDERS
EMPTY_BLOCK = GLOBAL_BLOCK + 1
KEY_BLOCKS = EMPTY_BLOCK + 1
GROUP = 8
PAIR = 8
SCORE_PAIR = 4
ITEMS = 2
MAX_ITEMS = 64
TOGETHER = (0, 3)
LIST = 56
EXTRA = 16
SLOTS = BLOCK + EXTRA
PART_ROWS = 32
BACK = SLOTS + PART_ROWS
NEG = -1e30
F32 = jnp.float32
BF16 = jnp.bfloat16


def params(mib):
    return pltpu.CompilerParams(vmem_limit_bytes=mib * 1024 * 1024)


def vmem():
    return pl.BlockSpec(memory_space=pltpu.VMEM)


def anywhere():
    return pl.BlockSpec(memory_space=pl.ANY)


def start_copies(pairs, sems):
    copies = [pltpu.make_async_copy(src, dst, sems.at[n]) for n, (src, dst) in enumerate(pairs)]
    for copy in copies:
        copy.start()
    return copies


def wait_all(copies):
    for copy in copies:
        copy.wait()


def smem():
    return pl.BlockSpec(memory_space=pltpu.SMEM)


def iota(shape, dim):
    return lax.broadcasted_iota(jnp.int32, shape, dim)


def dot(a, b):
    return jnp.dot(a, b, preferred_element_type=F32)


def dot_nt(a, b):
    return lax.dot_general(a, b, (((1,), (1,)), ((), ())), preferred_element_type=F32)


def split_index(index):
    return (index & (BLOCK - 1)).astype(F32).astype(BF16), (index >> 7).astype(F32).astype(BF16)


def packed_iota(dim):
    return iota((BLOCK, BLOCK), dim).astype(F32).astype(BF16)


def one_hot_columns(column):
    low, high = split_index(column)
    lanes = jnp.concatenate([packed_iota(1)] * (column.shape[0] // BLOCK), axis=0)
    one, zero = jnp.ones((), BF16), jnp.zeros((), BF16)
    base = jnp.where(low == lanes, one, zero)
    return jnp.concatenate(
        [jnp.where(high == jnp.asarray(c, BF16), base, zero) for c in range(NODES_HERE // BLOCK)], axis=1
    )


def one_hot_of_rows(index_rows):
    columns = [jnp.broadcast_to(row, (BLOCK, BLOCK)).T for row in index_rows]
    return one_hot_columns(jnp.concatenate(columns, axis=0))


def owner_ranks(gid_row):
    owner = jnp.broadcast_to(gid_row >> 10, (BLOCK, BLOCK))
    owner_t = owner.T
    same = owner == owner_t
    subs, lanes = iota((BLOCK, BLOCK), 0), iota((BLOCK, BLOCK), 1)
    row = jnp.sum(jnp.where(jnp.logical_and(same, subs < lanes), 1.0, 0.0), axis=0, keepdims=True)
    col = jnp.sum(jnp.where(jnp.logical_and(same, lanes < subs), 1.0, 0.0), axis=1, keepdims=True)
    row, col = row.astype(jnp.int32), jnp.broadcast_to(col, (BLOCK, BLOCK)).astype(jnp.int32)
    slot_row = jnp.where(row < EXTRA, (gid_row >> 10) * EXTRA + row, -1)
    slot_col = jnp.where(col < EXTRA, owner_t * EXTRA + col, -1)
    return row, slot_row, slot_col


def mine_columns(gid_row, me):
    row, _, _ = owner_ranks(gid_row)
    mine = (gid_row >> 10) == me
    slots = iota((EXTRA, BLOCK), 0)
    hit = jnp.logical_and(jnp.broadcast_to(mine, (EXTRA, BLOCK)), slots == row)
    local = jnp.broadcast_to(gid_row & (NODES_HERE - 1), (EXTRA, BLOCK)) + 1
    return jnp.sum(jnp.where(hit, local, 0).astype(F32), axis=1, keepdims=True).astype(jnp.int32) - 1


def exp_row(exp_ref, m, i):
    return exp_ref[m : m + 1, i * BLOCK : (i + 1) * BLOCK]


def project_kernel(
    me_ref, x_ref, wq_ref, wk_ref, wv_ref, cot_ref, rows_ref, exp_ref, gid_ref, q_out, k_out, v_out, kv_out, outk_ref, outv_ref,
    away_out, rounds_ref, msgk_s, msgv_s, sems, q_ref, k_ref, v_ref, kv_ref, away_ref, out_sems,
):
    most = jnp.max(owner_ranks(gid_ref[...])[0].astype(F32)).astype(jnp.int32)
    rounds_ref[0] = (most + EXTRA) // EXTRA
    x = x_ref[...]
    keys = dot(x, wk_ref[...]).astype(BF16)
    values = dot(x, wv_ref[...]).astype(BF16)
    k_ref[...] = keys
    v_ref[...] = values
    kv_ref[:, :COLS] = keys
    kv_ref[:, COLS:] = values
    query = (dot(x, wq_ref[...]).astype(BF16).astype(F32) * (1.0 / math.sqrt(HEAD))).astype(BF16)
    q_ref[...] = query
    away_ref[:NODES_HERE, :COLS] = query
    away_ref[:NODES_HERE, COLS:] = cot_ref[...]
    for m in range(EXPANDERS):
        low, high = split_index(jnp.concatenate([exp_row(exp_ref, m, i) for i in range(Q_BLOCKS)], axis=0))
        away_ref[NODES_HERE + m * Q_BLOCKS : NODES_HERE + (m + 1) * Q_BLOCKS, :COLS] = low
        away_ref[NODES_HERE + m * Q_BLOCKS : NODES_HERE + (m + 1) * Q_BLOCKS, COLS:] = high
    copies = start_copies(
        [(k_ref, k_out), (kv_ref, kv_out), (v_ref, v_out), (q_ref, q_out), (away_ref, away_out)], out_sems
    )
    mine = jnp.broadcast_to(mine_columns(gid_ref[...], me_ref[0]), (EXTRA, BLOCK))
    lanes = iota((EXTRA, NODES_HERE), 1)
    hot = (jnp.concatenate([mine] * (NODES_HERE // BLOCK), axis=1) == lanes).astype(F32).astype(BF16)
    extra = dot(hot, kv_ref[...]).astype(BF16)

    def sends(t):
        here = pl.ds(t * GROUP, GROUP)
        return (
            pltpu.make_async_copy(msgk_s.at[here], outk_ref.at[here], sems.at[0, t]),
            pltpu.make_async_copy(msgv_s.at[here], outv_ref.at[here], sems.at[1, t]),
        )

    def gather(t, carry):
        hot = one_hot_of_rows([rows_ref[pl.ds(t * GROUP + u, 1), :] for u in range(GROUP)])
        got = dot(hot, kv_ref[...]).astype(BF16)
        for u in range(GROUP):
            msgk_s[t * GROUP + u, :BLOCK] = got[u * BLOCK : (u + 1) * BLOCK, :COLS]
            msgv_s[t * GROUP + u, :BLOCK] = got[u * BLOCK : (u + 1) * BLOCK, COLS:]
            msgk_s[t * GROUP + u, BLOCK:] = extra[:, :COLS]
            msgv_s[t * GROUP + u, BLOCK:] = extra[:, COLS:]
        for send in sends(t):
            send.start()
        return carry

    lax.fori_loop(0, SENDERS // GROUP, gather, 0)
    for t in range(SENDERS // GROUP):
        for send in sends(t):
            send.wait()
    wait_all(copies)


def gather_partner(exp_ref, m, table, first_col=0):
    blocks = []
    for t in range(0, Q_BLOCKS, 4):
        hot = one_hot_of_rows([exp_row(exp_ref, m, t + u) for u in range(4)])
        got = dot(hot, table[:, first_col : first_col + COLS]).astype(BF16)
        blocks += [got[u * BLOCK : (u + 1) * BLOCK] for u in range(4)]
    return blocks


def sum_picks():
    sub = iota((2 * Q_BLOCKS * COLS, 16), 0)
    col = iota((2 * Q_BLOCKS * COLS, 16), 1)
    return (col == (sub >> 8) + jnp.where((sub & (COLS - 1)) < HEAD, 0, 8)).astype(F32).astype(BF16)


def head_sums(a_ref, blocks, picks):
    parts = []
    for i, b in enumerate(blocks):
        prod = a_ref[i * BLOCK : (i + 1) * BLOCK, :].astype(F32) * b.astype(F32)
        high = prod.astype(BF16)
        parts += [high, (prod - high.astype(F32)).astype(BF16)]
    return flat(dot(jnp.concatenate(parts, axis=1), picks).T)


def partner_key_kernel(exp_ref, t0_ref, t1_ref, t2_ref, t3_ref, q_ref, out_ref, sp_ref, pair_s, sems):
    picks = sum_picks()
    copies = []
    for m, table in enumerate((t0_ref, t1_ref, t2_ref, t3_ref)):
        blocks = gather_partner(exp_ref, m, table)
        for i, block in enumerate(blocks):
            pair_s[m * Q_BLOCKS + i] = block
        here = pl.ds(m * Q_BLOCKS, Q_BLOCKS)
        copies += start_copies([(pair_s.at[here], out_ref.at[here])], sems.at[pl.ds(m, 1)])
        sp_ref[m] = head_sums(q_ref, blocks, picks)
    wait_all(copies)


def head_picks(i):
    return (iota((16, COLS), 0) == jnp.where(iota((16, COLS), 1) < HEAD, i, 8 + i)).astype(F32).astype(BF16)


def finish_kernel(
    me_ref, exp_ref, t0_ref, t1_ref, t2_ref, t3_ref, cot_ref, sp_ref, lse_ref, local_ref, _, pair_ref, back_ref,
    delta_ref, message_ref, sems,
):
    picks = sum_picks()
    lse = lse_ref[...]
    delta = local_ref[...]
    probs, dprobs = [], []
    for m, table in enumerate((t0_ref, t1_ref, t2_ref, t3_ref)):
        blocks = gather_partner(exp_ref, m, table, table.shape[1] - COLS)
        prob = jnp.exp(sp_ref[m] - lse)
        dprob = head_sums(cot_ref, blocks, picks)
        delta += prob * dprob
        back_ref[m, 16:] = tall(prob).astype(BF16)
        for i, block in enumerate(blocks):
            pair_ref[m * Q_BLOCKS + i] = block
        probs.append(prob)
        dprobs.append(dprob)
    delta_ref[...] = delta
    for m in range(EXPANDERS):
        back_ref[m, :16] = tall(probs[m] * (dprobs[m] - delta)).astype(BF16)
    copies = [
        pltpu.make_async_copy(
            back_ref.at[m], message_ref.at[me_ref[0] ^ (1 << m), pl.ds(SLOTS, PART_ROWS)], sems.at[m]
        )
        for m in range(EXPANDERS)
    ]
    for copy in copies:
        copy.start()
    for copy in copies:
        copy.wait()


def join_partners(out_ref, out_t_ref, part_rows, pair_ref, scale):
    turned = [turned_weights(rows) for rows in part_rows]
    for i in range(Q_BLOCKS):
        total = head_rows(out_t_ref[i]).T
        for m in range(EXPANDERS):
            total += dot(turned[m], head_picks(i)) * pair_ref[m * Q_BLOCKS + i].astype(F32)
        out_ref[i * BLOCK : (i + 1) * BLOCK, :] = (total * scale).astype(BF16)


def attend_kernel(out_t_ref, back_ref, pair_ref, att_ref):
    join_partners(att_ref, out_t_ref, [back_ref[m, 16:] for m in range(EXPANDERS)], pair_ref, 1.0)


def flat(x):
    return jnp.concatenate([x[:8], x[8:]], axis=1)


def tall(x):
    return jnp.concatenate([x[:, :BLOCK], x[:, BLOCK:]], axis=0)


def turned_weights(tall_rows):
    return tall_rows.astype(F32).T.astype(BF16)


def prepare_kernel(q_ref, cot_ref, qt_ref, qs_ref, ct_ref, cs_ref):
    def one(i, carry):
        q = q_ref[q_rows(i), :]
        cot = cot_ref[q_rows(i), :]
        qt_ref[i] = stacked_t(q)
        qs_ref[i] = stacked(q)
        ct_ref[i] = stacked_t(cot)
        cs_ref[i] = stacked(cot)
        return carry

    lax.fori_loop(0, Q_BLOCKS, one, 0, unroll=2)


def plan_kernel(mask_ref, halo_ref, list_ref, where_ref, block_ref, count_ref, live_ref):
    for j in range(Q_BLOCKS):
        live_ref[j] = BLOCK
    live_ref[GLOBAL_BLOCK] = BLOCK
    live_ref[EMPTY_BLOCK] = 0

    def copy_count(s, carry):
        live_ref[Q_BLOCKS + s] = halo_ref[s]
        return carry

    lax.fori_loop(0, SENDERS, copy_count, 0)

    def per_block(i, items):
        list_ref[i * LIST] = GLOBAL_BLOCK

        def put(j, n):
            list_ref[i * LIST + n] = j
            used = jnp.logical_and(mask_ref[i * GLOBAL_BLOCK + j] > 0, live_ref[j] > 0)
            return n + used.astype(jnp.int32)

        n = lax.fori_loop(0, GLOBAL_BLOCK, put, 1)
        for extra in range(GROUP):
            list_ref[i * LIST + n + extra] = EMPTY_BLOCK
        groups = (n + GROUP - 1) // GROUP

        def item(g, carry):
            where_ref[items + g] = i * LIST + g * GROUP
            block_ref[items + g] = i
            return carry

        lax.fori_loop(0, groups, item, 0)
        return items + groups

    items = lax.fori_loop(0, Q_BLOCKS, per_block, 0)
    for u in range(GROUP):
        list_ref[Q_BLOCKS * LIST + u] = EMPTY_BLOCK
    for u in range(ITEMS - 1):
        where_ref[items + u] = Q_BLOCKS * LIST
        block_ref[items + u] = 0
    count_ref[0] = (items + ITEMS - 1) // ITEMS


def fill(dst, dst_t, first_col,  own_ref, halo_ref, gid_ref, glob_ref):
    def put(j, block):
        if dst is not None:
            dst[j] = block
        if dst_t is not None:
            dst_t[j] = block.T

    def own(j, carry):
        put(j, own_ref[q_rows(j), :])
        return carry

    def halo(j, carry):
        put(Q_BLOCKS + j, halo_ref[j, :BLOCK])
        return carry

    lax.fori_loop(0, Q_BLOCKS, own, 0, unroll=4)
    lax.fori_loop(0, SENDERS, halo, 0, unroll=4)
    slot_col = owner_ranks(gid_ref[...])[2]
    wide = jnp.concatenate([slot_col] * (SENDERS * EXTRA // BLOCK), axis=1)
    hot = (wide == iota((BLOCK, SENDERS * EXTRA), 1)).astype(F32).astype(BF16)
    extra = jnp.concatenate([halo_ref[s, BLOCK:] for s in range(SENDERS)], axis=0)
    rows = (dot(hot, extra) + glob_ref[:, first_col : first_col + COLS].astype(F32)).astype(BF16)
    put(GLOBAL_BLOCK, rows)
    put(EMPTY_BLOCK, jnp.zeros((BLOCK, COLS), BF16))


def stacked(rows):
    lanes = iota((BLOCK, COLS), 1)
    zero = jnp.zeros_like(rows)
    return jnp.concatenate([jnp.where(lanes < HEAD, rows, zero), jnp.where(lanes < HEAD, zero, rows)], axis=0)


def stacked_t(rows):
    turned = rows.T
    subs = iota((COLS, BLOCK), 0)
    zero = jnp.zeros_like(turned)
    return jnp.concatenate([jnp.where(subs < HEAD, turned, zero), jnp.where(subs < HEAD, zero, turned)], axis=1)


def head_rows(turned):
    return jnp.concatenate([turned[:HEAD, :BLOCK], turned[HEAD:, BLOCK:]], axis=0)


def masked_scores(blocks, k_s, turned_q, live_ref):
    keys = jnp.concatenate([k_s[b] for b in blocks], axis=0)
    scores = dot(keys, turned_q)
    row_id = iota((BLOCK, 2 * BLOCK), 0)
    return jnp.concatenate(
        [
            jnp.where(row_id < live_ref[b], scores[u * BLOCK : (u + 1) * BLOCK], NEG)
            for u, b in enumerate(blocks)
        ],
        axis=0,
    )


def item_of(t, u, list_ref, where_ref, block_ref):
    where = where_ref[t * ITEMS + u]
    return block_ref[t * ITEMS + u], [list_ref[where + b] for b in range(GROUP)]


def q_rows(i):
    return pl.ds(pl.multiple_of(i * BLOCK, BLOCK), BLOCK)


def score_kernel(
    list_ref, where_ref, block_ref, count_ref, live_ref, qt_ref, own_ref, hk_ref, gid_ref, glob_ref, lse_ref, k_ref, kt_ref,
    top_s, total_s, k_s, kt_s, sems,
):
    fill(k_s, kt_s, 0, own_ref, hk_ref, gid_ref, glob_ref)
    copies = start_copies([(k_s, k_ref), (kt_s, kt_ref)], sems)

    top_s[...] = jnp.full((Q_BLOCKS, 8, 2 * BLOCK), NEG, F32)
    total_s[...] = jnp.zeros((Q_BLOCKS, 8, 2 * BLOCK), F32)

    def step(t, carry):
        for item in range(ITEMS):
            i, blocks = item_of(t, item, list_ref, where_ref, block_ref)
            turned_q = qt_ref[i]
            parts = []
            for u in range(0, GROUP, SCORE_PAIR):
                scores = masked_scores(blocks[u : u + SCORE_PAIR], k_s, turned_q, live_ref)
                scores = scores.reshape(SCORE_PAIR * BLOCK // 8, 8, 2 * BLOCK)
                top = jnp.max(scores, axis=0)
                parts.append((top, jnp.sum(jnp.exp(scores - top[None]), axis=0)))
            parts.append((top_s[i], total_s[i]))
            best = functools.reduce(jnp.maximum, [top for top, _ in parts])
            top_s[i] = best
            total_s[i] = sum(total * jnp.exp(top - best) for top, total in parts)
        return carry

    lax.fori_loop(0, count_ref[0], step, 0)
    for i in range(Q_BLOCKS):
        top = top_s[i]
        best = jnp.max(top, axis=0, keepdims=True)
        denominator = jnp.sum(total_s[i] * jnp.exp(top - best), axis=0, keepdims=True)
        lse_ref[i : i + 1, :] = best + jnp.log(denominator)
    wait_all(copies)


def value_kernel(
    list_ref, where_ref, block_ref, count_ref, live_ref, k_in, ownv_ref, hv_ref, glob_ref, qt_in, ct_in, cs_in, part_ref,
    sp_ref, gid_ref, own_ref, halo_ref, gout_ref, out_ref, delta_ref, lse_ref, acc_s, vt_s, k_s, qt_ref, ct_ref, cs_ref,
    in_sems, out_s, halo_s, sems,
):
    loads = start_copies([(k_in, k_s), (qt_in, qt_ref), (cs_in, cs_ref), (ct_in, ct_ref)], in_sems)
    fill(None, vt_s, COLS, ownv_ref, hv_ref, gid_ref, glob_ref)
    clear_blocks(acc_s)
    part = part_ref[...]
    best = part
    for m in range(EXPANDERS):
        best = jnp.maximum(best, sp_ref[m])
    total = jnp.exp(part - best)
    for m in range(EXPANDERS):
        total += jnp.exp(sp_ref[m] - best)
    lse_ref[...] = best + jnp.log(total)
    wait_all(loads)

    out_s[...] = jnp.zeros((Q_BLOCKS, COLS, 2 * BLOCK), F32)

    def step(t, carry):
        for item in range(ITEMS):
            i, blocks = item_of(t, item, list_ref, where_ref, block_ref)
            turned_q = qt_ref[i]
            cot_stack = cs_ref[i]
            lse = lse_ref[pl.ds(i, 1), :]
            for u in range(0, GROUP, PAIR):
                pair = blocks[u : u + PAIR]
                scores = masked_scores(pair, k_s, turned_q, live_ref)
                weight = jnp.exp(scores - lse).astype(BF16)
                out_s[i] += dot(jnp.concatenate([vt_s[b] for b in pair], axis=1), weight)
                grads = dot(weight, cot_stack)
                for w, b in enumerate(pair):
                    acc_s[b] += grads[w * BLOCK : (w + 1) * BLOCK]
        return carry

    lax.fori_loop(0, count_ref[0], step, 0)
    out_copy = pltpu.make_async_copy(out_s, out_ref, sems.at[1 + SENDERS // GROUP])
    out_copy.start()
    for i in range(Q_BLOCKS):
        delta_ref[i : i + 1, :] = jnp.sum(out_s[i] * ct_ref[i].astype(F32), axis=0, keepdims=True)
    wait_all(store_parts(acc_s, own_ref, halo_ref, gid_ref, gout_ref, halo_s, sems) + [out_copy])


def clear_blocks(acc_s):
    def clear(j, carry):
        acc_s[j] = jnp.zeros((BLOCK, COLS), F32)
        return carry

    lax.fori_loop(0, KEY_BLOCKS, clear, 0, unroll=2)


def store_parts(acc_s, own_ref, halo_ref, gid_ref, gout_ref, halo_s, sems):
    copies = start_copies([(acc_s.at[pl.ds(0, Q_BLOCKS)], own_ref)], sems)
    grads = acc_s[GLOBAL_BLOCK].astype(BF16)
    gout_ref[...] = grads
    slot_row = owner_ranks(gid_ref[...])[1]
    hot = (iota((SENDERS * EXTRA, BLOCK), 0) == slot_row).astype(F32).astype(BF16)
    extra = dot(hot, grads).astype(BF16)
    for t in range(SENDERS // GROUP):
        for s in range(t * GROUP, (t + 1) * GROUP):
            halo_s[s, :BLOCK] = acc_s[Q_BLOCKS + s].astype(BF16)
            halo_s[s, BLOCK:] = extra[s * EXTRA : (s + 1) * EXTRA]
        here = pl.ds(t * GROUP, GROUP)
        copy = pltpu.make_async_copy(halo_s.at[here], halo_ref.at[here, pl.ds(0, SLOTS)], sems.at[1 + t])
        copy.start()
        copies.append(copy)
    return copies


def part_scratch():
    return [pltpu.VMEM((SENDERS, SLOTS, COLS), BF16), pltpu.SemaphoreType.DMA((2 + SENDERS // GROUP,))]


def key_kernel(
    list_ref, where_ref, block_ref, count_ref, live_ref, k_in, kt_in, ownv_ref, hv_ref, glob_ref, qt_in, qs_in, ct_in, lse_ref,
    delta_ref, gid_ref, out_ref, own_ref, halo_ref, gout_ref, acc_s, v_s, k_s, kt_s, qt_ref, qs_ref, ct_ref, in_sems,
    out_s, halo_s, sems,
):
    loads = start_copies(
        [(k_in, k_s), (qt_in, qt_ref), (ct_in, ct_ref), (kt_in, kt_s), (qs_in, qs_ref)], in_sems
    )
    fill(v_s, None, COLS, ownv_ref, hv_ref, gid_ref, glob_ref)
    clear_blocks(acc_s)
    wait_all(loads)

    out_s[...] = jnp.zeros((Q_BLOCKS, COLS, 2 * BLOCK), F32)

    def step(t, carry):
        for item in range(ITEMS):
            i, blocks = item_of(t, item, list_ref, where_ref, block_ref)
            turned_q = qt_ref[i]
            q_stack = qs_ref[i]
            turned_cot = ct_ref[i]
            lse = lse_ref[pl.ds(i, 1), :]
            delta = delta_ref[pl.ds(i, 1), :]
            for u in range(0, GROUP, PAIR):
                pair = blocks[u : u + PAIR]
                scores = masked_scores(pair, k_s, turned_q, live_ref)
                dprob = dot(jnp.concatenate([v_s[b] for b in pair], axis=0), turned_cot)
                dscore = (jnp.exp(scores - lse) * (dprob - delta)).astype(BF16)
                out_s[i] += dot(jnp.concatenate([kt_s[b] for b in pair], axis=1), dscore)
                grads = dot(dscore, q_stack)
                for w, b in enumerate(pair):
                    acc_s[b] += grads[w * BLOCK : (w + 1) * BLOCK]
        return carry

    lax.fori_loop(0, count_ref[0], step, 0)
    out_copy = pltpu.make_async_copy(out_s, out_ref, sems.at[1 + SENDERS // GROUP])
    out_copy.start()
    wait_all(store_parts(acc_s, own_ref, halo_ref, gid_ref, gout_ref, halo_s, sems) + [out_copy])


def scatter_into(acc_s, splits, data):
    subs = packed_iota(0)
    one, zero = jnp.ones((), BF16), jnp.zeros((), BF16)
    bases = [(jnp.where(subs == low, one, zero), jnp.broadcast_to(high, (BLOCK, BLOCK))) for low, high in splits]
    for c in range(NODES_HERE // BLOCK):
        hot = jnp.concatenate([jnp.where(high == jnp.asarray(c, BF16), base, zero) for base, high in bases], axis=1)
        acc_s[c * BLOCK : (c + 1) * BLOCK, :] += dot(hot, data)


def add_halo(acc_s, me_ref, ret_ref, rows_ref, gid_ref, more_ref):
    def halo(t, carry):
        splits = [split_index(rows_ref[pl.ds(t * GROUP + u, 1), :]) for u in range(GROUP)]
        data = jnp.concatenate([ret_ref[t * GROUP + u, :BLOCK] for u in range(GROUP)], axis=0)
        scatter_into(acc_s, splits, data)
        return carry

    lax.fori_loop(0, SENDERS // GROUP, halo, 0)
    extra = ret_ref[0, BLOCK:SLOTS].astype(F32)
    for s in range(1, SENDERS):
        extra += ret_ref[s, BLOCK:SLOTS].astype(F32)
    high = extra.astype(BF16)
    data = jnp.concatenate([high, (extra - high.astype(F32)).astype(BF16)], axis=0)
    mine = jnp.broadcast_to(mine_columns(gid_ref[...], me_ref[0]), (EXTRA, NODES_HERE))
    hot = (mine == iota((EXTRA, NODES_HERE), 1)).astype(F32)
    hot = jnp.concatenate([hot, hot], axis=0).T.astype(BF16)
    acc_s[...] += dot(hot, data)
    gids = gid_ref[...]
    local = jnp.where((gids >> 10) == me_ref[0], gids & (NODES_HERE - 1), NODES_HERE)
    more = more_ref[...]
    high = more.astype(BF16)
    low = (more - high.astype(F32)).astype(BF16)
    scatter_into(acc_s, [split_index(local)] * 2, jnp.concatenate([high, low], axis=0))


def add_partners(acc_s, parts, others, first_col):
    for m, (part, other) in enumerate(zip(parts, others)):
        turned = turned_weights(part)
        index_low = other[NODES_HERE + m * Q_BLOCKS : NODES_HERE + (m + 1) * Q_BLOCKS, :COLS]
        index_high = other[NODES_HERE + m * Q_BLOCKS : NODES_HERE + (m + 1) * Q_BLOCKS, COLS:]
        for t in range(Q_BLOCKS // GROUP):
            splits, data = [], []
            for u in range(GROUP):
                i = t * GROUP + u
                splits.append((index_low[i : i + 1], index_high[i : i + 1]))
                wide = dot(turned, head_picks(i))
                rows = other[i * BLOCK : (i + 1) * BLOCK, first_col : first_col + COLS].astype(F32)
                data.append((wide * rows).astype(BF16))
            scatter_into(acc_s, splits, jnp.concatenate(data, axis=0))


def feature_part(feat_ref, k):
    return pl.ds(pl.multiple_of(((feat_ref[0] + k) % 4) * COLS, COLS), COLS)


def value_back_kernel(
    me_ref, feat_ref, ownv_ref, ret_ref, ownk_ref, rows_ref, o0_ref, o1_ref, o2_ref, o3_ref, gid_ref, wq_ref, wv_ref,
    out_t_ref, back_ref, pair_ref, more_ref, pre_ref, accv_s, gq_ref,
):
    others = (o0_ref, o1_ref, o2_ref, o3_ref)
    parts = [ret_ref[me_ref[0] ^ (1 << m), SLOTS:] for m in range(EXPANDERS)]
    join_partners(
        gq_ref, out_t_ref, [back_ref[m, :16] for m in range(EXPANDERS)], pair_ref, 1.0 / math.sqrt(HEAD)
    )
    accv_s[...] = ownv_ref[...]
    add_halo(accv_s, me_ref, ret_ref, rows_ref, gid_ref, more_ref)
    add_partners(accv_s, [part[16:] for part in parts], others, COLS)
    acck_ref = pre_ref.at[4]
    acck_ref[...] = ownk_ref[...]
    add_partners(acck_ref, [part[:16] for part in parts], others, 0)
    grad_value = accv_s[...].astype(BF16)
    for k in range(4):
        part = feature_part(feat_ref, k)
        pre_ref[k] = dot_nt(gq_ref[...], wq_ref[part, :]) + dot_nt(grad_value, wv_ref[part, :])


def key_back_kernel(
    me_ref, feat_ref, ret_ref, rows_ref, gid_ref, wk_ref, pre_ref, more_ref, t0_ref, t1_ref, t2_ref, t3_ref,
    acc_s, pre_s, sems,
):
    copies = start_copies([(pre_ref, pre_s)], sems)
    acc_s[...] = jnp.zeros((NODES_HERE, COLS), F32)
    add_halo(acc_s, me_ref, ret_ref, rows_ref, gid_ref, more_ref)
    wait_all(copies)
    grad_key = (acc_s[...] + pre_s[4]).astype(BF16)
    for k, out in ((1, t1_ref), (2, t2_ref), (3, t3_ref), (0, t0_ref)):
        out[...] = (pre_s[k] + dot_nt(grad_key, wk_ref[feature_part(feat_ref, k), :])).astype(out.dtype)


def shape(dims, kind=BF16):
    return jax.ShapeDtypeStruct(dims, kind)


def call(kernel, ins, outs, args, scratch=(), name=None, flops=0, out_spaces=None, aliases={}, mib=56):
    cost = pl.CostEstimate(flops=flops, transcendentals=0, bytes_accessed=4_000_000)
    return pl.pallas_call(
        kernel,
        out_shape=outs,
        in_specs=ins,
        out_specs=out_spaces or tuple(vmem() for _ in outs),
        scratch_shapes=list(scratch),
        compiler_params=params(mib),
        cost_estimate=cost,
        input_output_aliases=aliases,
        name=name,
    )(*args)


def blocks_of(kind):
    return pltpu.VMEM((KEY_BLOCKS, BLOCK, COLS), kind)


def run_project(me, features, w_query, w_key, w_value, cotangent, rows, exp_list, gids):
    return call(
        project_kernel,
        [smem()] + [vmem()] * 8,
        (
            shape((NODES_HERE, COLS)),
            shape((NODES_HERE, COLS)),
            shape((NODES_HERE, COLS)),
            shape((NODES_HERE, 2 * COLS)),
            shape((SENDERS, SLOTS, COLS)),
            shape((SENDERS, SLOTS, COLS)),
            shape((NODES_HERE + EXPANDERS * Q_BLOCKS, 2 * COLS)),
            shape((1,), jnp.int32),
        ),
        (me, features, w_query, w_key, w_value, cotangent, rows, exp_list, gids),
        name="project",
        mib=56,
        flops=3_000_000_000,
        out_spaces=(*(anywhere() for _ in range(7)), smem()),
        scratch=[
            pltpu.VMEM((SENDERS, SLOTS, COLS), BF16),
            pltpu.VMEM((SENDERS, SLOTS, COLS), BF16),
            pltpu.SemaphoreType.DMA((2, SENDERS // GROUP)),
            pltpu.VMEM((NODES_HERE, COLS), BF16),
            pltpu.VMEM((NODES_HERE, COLS), BF16),
            pltpu.VMEM((NODES_HERE, COLS), BF16),
            pltpu.VMEM((NODES_HERE, 2 * COLS), BF16),
            pltpu.VMEM((NODES_HERE + EXPANDERS * Q_BLOCKS, 2 * COLS), BF16),
            pltpu.SemaphoreType.DMA((5,)),
        ],
    )


def run_plan(block_mask, halo_count):
    sizes = (Q_BLOCKS * LIST + GROUP, MAX_ITEMS, MAX_ITEMS, 1, KEY_BLOCKS)
    return call(
        plan_kernel,
        [smem()] * 2,
        tuple(shape((size,), jnp.int32) for size in sizes),
        (block_mask.reshape(-1), halo_count.reshape(-1)),
        name="plan",
        out_spaces=tuple(smem() for _ in sizes),
    )


def run_partner_keys(exp_rows, swaps, query):
    return call(
        partner_key_kernel,
        [vmem()] * 6,
        (shape((EXPANDERS * Q_BLOCKS, BLOCK, COLS)), shape((EXPANDERS, Q_BLOCKS, 2 * BLOCK), F32)),
        (exp_rows, *swaps, query),
        name="partners",
        out_spaces=(anywhere(), vmem()),
        scratch=[
            pltpu.VMEM((EXPANDERS * Q_BLOCKS, BLOCK, COLS), BF16),
            pltpu.SemaphoreType.DMA((EXPANDERS,)),
        ],
        flops=5_000_000_000,
    )


def run_finish(me, exp_rows, swaps, cotangent, scores, lse, local, back_v):
    anywhere = pl.BlockSpec(memory_space=pl.ANY)
    return call(
        finish_kernel,
        [smem()] + [vmem()] * 9 + [anywhere],
        (
            shape((EXPANDERS * Q_BLOCKS, BLOCK, COLS)),
            shape((EXPANDERS, PART_ROWS, BLOCK)),
            shape((Q_BLOCKS, 2 * BLOCK), F32),
            shape((SENDERS, BACK, COLS)),
        ),
        (me, exp_rows, *swaps, cotangent, scores, lse, local, back_v),
        name="finish",
        flops=5_000_000_000,
        out_spaces=(vmem(), vmem(), vmem(), anywhere),
        scratch=[pltpu.SemaphoreType.DMA((EXPANDERS,))],
        aliases={10: 3},
    )


def run_attend(out_t, back, value_pairs):
    return call(
        attend_kernel,
        [vmem()] * 3,
        (shape((NODES_HERE, COLS)),),
        (out_t, back, value_pairs),
        name="attend",
        flops=2_000_000_000,
    )[0]


def run_prepare(query, cotangent):
    wide, high = shape((Q_BLOCKS, COLS, 2 * BLOCK)), shape((Q_BLOCKS, 2 * BLOCK, COLS))
    return call(
        prepare_kernel, [vmem()] * 2, (wide, high, wide, high), (query, cotangent), name="prepare", flops=2_000_000_000
    )


def run_scores(plan, turned_q, own, halo_k, gids, glob):
    return call(
        score_kernel,
        [smem()] * 5 + [vmem()] * 5,
        (
            shape((Q_BLOCKS, 2 * BLOCK), F32),
            shape((KEY_BLOCKS, BLOCK, COLS)),
            shape((KEY_BLOCKS, COLS, BLOCK)),
        ),
        (*plan, turned_q, own, halo_k, gids, glob),
        scratch=[pltpu.VMEM((Q_BLOCKS, 8, 2 * BLOCK), F32)] * 2
        + [blocks_of(BF16), blocks_of(BF16), pltpu.SemaphoreType.DMA((2,))],
        out_spaces=(vmem(), anywhere(), anywhere()),
        name="scores",
        flops=12_000_000_000,
    )


def run_values(plan, keys, own_values, halo_v, glob, prepared, part, scores, gids):
    turned_q, _, turned_cot, cot_stack = prepared
    return call(
        value_kernel,
        [smem()] * 5 + [anywhere()] + [vmem()] * 3 + [anywhere()] * 3 + [vmem()] * 3,
        (
            shape((Q_BLOCKS, BLOCK, COLS), F32),
            shape((SENDERS, BACK, COLS)),
            shape((BLOCK, COLS)),
            shape((Q_BLOCKS, COLS, 2 * BLOCK), F32),
            shape((Q_BLOCKS, 2 * BLOCK), F32),
            shape((Q_BLOCKS, 2 * BLOCK), F32),
        ),
        (*plan, keys, own_values, halo_v, glob, turned_q, turned_cot, cot_stack, part, scores, gids),
        scratch=[
            blocks_of(F32), blocks_of(BF16), blocks_of(BF16), pltpu.VMEM((Q_BLOCKS, COLS, 2 * BLOCK), BF16), pltpu.VMEM((Q_BLOCKS, COLS, 2 * BLOCK), BF16),
            pltpu.VMEM((Q_BLOCKS, 2 * BLOCK, COLS), BF16), pltpu.SemaphoreType.DMA((4,)), pltpu.VMEM((Q_BLOCKS, COLS, 2 * BLOCK), F32),
            *part_scratch(),
        ],
        out_spaces=(anywhere(), anywhere(), vmem(), anywhere(), vmem(), vmem()),
        name="values",
        flops=20_000_000_000,
    )


def run_keys(plan, keys, turned_k, own_values, halo_v, glob, prepared, lse, delta, gids):
    turned_q, q_stack, turned_cot, _ = prepared
    return call(
        key_kernel,
        [smem()] * 5 + [anywhere()] * 2 + [vmem()] * 3 + [anywhere()] * 3 + [vmem()] * 3,
        (
            shape((Q_BLOCKS, COLS, 2 * BLOCK), F32),
            shape((Q_BLOCKS, BLOCK, COLS), F32),
            shape((SENDERS, SLOTS, COLS)),
            shape((BLOCK, COLS)),
        ),
        (*plan, keys, turned_k, own_values, halo_v, glob, turned_q, q_stack, turned_cot, lse, delta, gids),
        scratch=[
            blocks_of(F32), blocks_of(BF16), blocks_of(BF16), blocks_of(BF16), pltpu.VMEM((Q_BLOCKS, COLS, 2 * BLOCK), BF16),
            pltpu.VMEM((Q_BLOCKS, 2 * BLOCK, COLS), BF16), pltpu.VMEM((Q_BLOCKS, COLS, 2 * BLOCK), BF16), pltpu.SemaphoreType.DMA((5,)), pltpu.VMEM((Q_BLOCKS, COLS, 2 * BLOCK), F32),
            *part_scratch(),
        ],
        out_spaces=(anywhere(), anywhere(), anywhere(), vmem()),
        name="keys",
        mib=56,
        flops=25_000_000_000,
    )


def run_value_back(me, feat, own_v, returned_v, own_k, rows, others, gids, w_query, w_value, out_t, back, pairs, more):
    return call(
        value_back_kernel,
        [smem()] * 2 + [vmem()] * 15,
        (shape((5, NODES_HERE, COLS), F32),),
        (me, feat, own_v.reshape(NODES_HERE, COLS), returned_v, own_k.reshape(NODES_HERE, COLS), rows, *others, gids, w_query, w_value, out_t, back, pairs, more),
        scratch=[pltpu.VMEM((NODES_HERE, COLS), F32), pltpu.VMEM((NODES_HERE, COLS), BF16)],
        name="value_back",
        mib=56,
        flops=12_000_000_000,
    )[0]


def run_key_back(me, feat, returned_k, rows, gids, w_key, pre, more):
    anywhere = pl.BlockSpec(memory_space=pltpu.HBM)
    return call(
        key_back_kernel,
        [smem()] * 2 + [vmem()] * 4 + [anywhere, vmem()],
        (shape((NODES_HERE, COLS), F32),) + tuple(shape((NODES_HERE, COLS)) for _ in range(3)),
        (me, feat, returned_k, rows, gids, w_key, pre, more),
        scratch=[
            pltpu.VMEM((NODES_HERE, COLS), F32),
            pltpu.VMEM((5, NODES_HERE, COLS), F32),
            pltpu.SemaphoreType.DMA((1,)),
        ],
        name="key_back",
        mib=20,
        flops=8_000_000_000,
    )


def ranks(global_ids):
    owner = global_ids // NODES_HERE
    ids = jnp.arange(BLOCK)
    return owner, ((owner[:, None] == owner[None, :]) & (ids[None, :] < ids[:, None])).sum(1)


def more_globals(rounds, global_ids, my_index, own_k, own_v):
    def body(state):
        r, glob = state
        ids = global_ids + jnp.minimum(r, 0)
        owner, rank = ranks(ids)
        slot = rank - r * EXTRA
        here = (slot >= 0) & (slot < EXTRA)
        place = jnp.where((owner == my_index) & here, slot, EXTRA)
        local = jnp.where(here, ids % NODES_HERE, 0)
        found = jnp.concatenate([own_k[local], own_v[local]], axis=1)
        rows = jnp.zeros((EXTRA + 1, 2 * COLS), BF16).at[place].set(found)[:EXTRA]
        got = lax.all_to_all(jnp.broadcast_to(rows[None], (SENDERS, *rows.shape)), "dom", 0, 0, tiled=True)
        found = got.reshape(SENDERS * EXTRA, -1)[jnp.clip(owner * EXTRA + slot, 0, SENDERS * EXTRA - 1)]
        return r + 1, jnp.where(here[:, None], found, glob)

    start = (jnp.asarray(1, jnp.int32), jnp.zeros((BLOCK, 2 * COLS), BF16))
    return lax.while_loop(lambda state: state[0] < rounds, body, start)[1]


def more_grads(rounds, global_ids, my_index, part_k, part_v):
    def body(state):
        r, more_k, more_v = state
        ids = global_ids + jnp.minimum(r, 0)
        owner, rank = ranks(ids)
        slot = rank - r * EXTRA
        here = (slot >= 0) & (slot < EXTRA)
        place = jnp.where(here, owner * EXTRA + slot, SENDERS * EXTRA)

        def summed(part):
            rows = jnp.zeros((SENDERS * EXTRA + 1, COLS), BF16).at[place].set(part)[: SENDERS * EXTRA]
            got = lax.all_to_all(rows.reshape(SENDERS, EXTRA, -1), "dom", 0, 0, tiled=True).astype(F32).sum(0)
            return jnp.where(((owner == my_index) & here)[:, None], got[jnp.clip(slot, 0, EXTRA - 1)], 0.0)

        return r + 1, more_k + summed(part_k), more_v + summed(part_v)

    zeros = jnp.zeros((BLOCK, COLS), F32)
    start = (jnp.asarray(1, jnp.int32), zeros, zeros)
    return lax.while_loop(lambda state: state[0] < rounds, body, start)[1:]


def on_device(
    features,
    w_query,
    w_key,
    w_value,
    cotangent,
    send_rows,
    halo_count,
    block_mask,
    exp_rows,
    global_ids,
):
    dom_count = lax.axis_size("dom")
    my_index = lax.axis_index("dom")

    def swapped(value, bit):
        return lax.ppermute(value, "dom", [(i, i ^ (1 << bit)) for i in range(dom_count)])

    rows = send_rows[0]
    gids = global_ids.reshape(1, BLOCK)
    me = my_index.reshape(1).astype(jnp.int32)
    feat = lax.axis_index("feat").reshape(1).astype(jnp.int32)

    query, own_keys, own_values, paired, out_k, out_v, away, rounds = run_project(
        me, features, w_query, w_key, w_value, cotangent, rows, exp_rows, gids
    )
    rounds = rounds[0]
    glob = more_globals(rounds, global_ids, my_index, own_keys, own_values)
    out_k, out_v, glob = lax.optimization_barrier((out_k, out_v, glob))
    halo_k = lax.all_to_all(out_k, "dom", 0, 0, tiled=True)
    key_swaps = [swapped(paired if m in TOGETHER else own_keys, m) for m in range(EXPANDERS)]
    plan = run_plan(block_mask, halo_count)
    prepared = run_prepare(query, cotangent)
    own_values_late, *prepared = lax.optimization_barrier((own_values, *prepared))
    value_swaps = {m: swapped(own_values_late, m) for m in range(EXPANDERS) if m not in TOGETHER}
    halo_v = lax.all_to_all(out_v, "dom", 0, 0, tiled=True)
    part, keys, turned_k = run_scores(plan, prepared[0], own_keys, halo_k, gids, glob)
    part, *key_swaps = lax.optimization_barrier((part, *key_swaps))
    pairs, scores = run_partner_keys(exp_rows, key_swaps, query)
    away, scores = lax.optimization_barrier((away, scores))
    others = [swapped(away, m) for m in range(EXPANDERS)]
    own_v, back_v, glob_v, out_t, local, lse = run_values(
        plan, keys, own_values, halo_v, glob, prepared, part, scores, gids
    )
    local, value_swaps = lax.optimization_barrier((local, value_swaps))
    value_swaps = [value_swaps.get(m, key_swaps[m]) for m in range(EXPANDERS)]
    value_pairs, back, delta, back_v = run_finish(
        me, exp_rows, value_swaps, cotangent, scores, lse, local, back_v
    )
    returned_v = lax.all_to_all(back_v, "dom", 0, 0, tiled=True)
    query_t, own_k, back_k, glob_k = run_keys(
        plan, keys, turned_k, own_values, halo_v, glob, prepared, lse, delta, gids
    )
    glob_k, returned_v, *others = lax.optimization_barrier((glob_k, returned_v, *others))
    more_k, more_v = more_grads(rounds, global_ids, my_index, glob_k, glob_v)
    back_k, more_k, more_v = lax.optimization_barrier((back_k, more_k, more_v))
    returned_k = lax.all_to_all(back_k, "dom", 0, 0, tiled=True)
    pre = run_value_back(
        me, feat, own_v, returned_v, own_k, rows, others, gids, w_query, w_value, query_t, back, pairs, more_v
    )
    mine, *away = run_key_back(me, feat, returned_k, rows, gids, w_key, pre, more_k)
    out_t, mine = lax.optimization_barrier((out_t, mine))
    attended = run_attend(out_t, back, value_pairs)
    for k in (2, 1, 3):
        mine = mine + lax.ppermute(away[k - 1], "feat", [(i, (i + k) % 4) for i in range(4)]).astype(F32)
    return (attended, mine.astype(BF16))


def solution(mesh):
    return jax.shard_map(
        on_device,
        mesh=mesh,
        in_specs=(
            P("dom", None),
            P(None, "feat"),
            P(None, "feat"),
            P(None, "feat"),
            P("dom", "feat"),
            P("dom", None, None),
            P(None, "dom"),
            P("dom", None),
            P(None, "dom"),
            P(),
        ),
        out_specs=(P("dom", "feat"), P("dom", "feat")),
        check_vma=False,
    )
```
